32 devices in a mesh: ctx: 16 (over z, y, x), wsh: 2 (over core).
Axes of the slice: x: 2, y: 2, z: 4, core: 2. Of those that a mesh axis runs over, the one named last changes fastest.
Arguments:
- tokens: bfloat16 [8, 2048, 512], P('wsh', 'ctx'), may hold values from -6 to 6
- routes: int32 [8, 2048, 2], P('wsh', 'ctx'), may hold values from 0 to 7, all different within a row
- block_order: int32 [16], replicated, may hold values from 0 to 15, each once
- norm_gain1: bfloat16 [512], P('wsh'), may hold values from 0.5 to 1.5
- router_w: bfloat16 [512, 8], P('wsh'), may hold values from -0.1875 to 0.1875
- query_w: bfloat16 [512, 512], P('wsh'), may hold values from -0.25 to 0.25
- kv_w: bfloat16 [512, 128], P('wsh'), may hold values from -0.25 to 0.25
- out_w: bfloat16 [512, 512], P('wsh'), may hold values from -6 to 6
- norm_gain2: bfloat16 [512], P('wsh'), may hold values from 0.5 to 1.5
- up_w: bfloat16 [512, 2048], P('wsh'), may hold values from -0.25 to 0.25
- down_w: bfloat16 [2048, 512], P('wsh'), may hold values from -0.125 to 0.125
- cotangent: bfloat16 [8, 2048, 512], P('wsh', 'ctx'), may hold values from -6 to 6
Outputs:
- layer_out: float32 [8, 2048, 512], P('wsh', 'ctx')
- input_grad: float32 [8, 2048, 512], P('wsh', 'ctx')
- grad_gain1: float32 [512], P('wsh')
- grad_router: float32 [512, 8], P('wsh')
- grad_query: float32 [512, 512], P('wsh')
- grad_kv: float32 [512, 128], P('wsh')
- grad_out: float32 [512, 512], P('wsh')
- grad_gain2: float32 [512], P('wsh')
- grad_up: float32 [512, 2048], P('wsh')
- grad_down: float32 [2048, 512], P('wsh')
The draws below stay inside these ranges and needn't reach their ends.
Inputs may be any that keep to these rules, and one draw needn't show every extreme that they name: `routes`: each token names 2 different experts. A permutation: index p of ctx holds, of every sequence, block block_order[p] and block 31 - block_order[p], as the first step says.
All inputs are finite; a program needn't handle non-finite values.
Results may differ from the reference program's by a relative error of at most 0.013.
Values may be sent and summed in bfloat16 or wider, within the bound.
No kernel may reach another device: no remote copies, remote signals or barrier semaphores. Data moves between devices by JAX's collectives and lax.ppermute only.
A program may use at most 192 MiB of HBM per device.

```python
import math
import jax
import jax.numpy as jnp
from jax import lax

D = 512
EXPERTS = 8
HEAD = 64
FF = 2048
TOP = 2
BLK = 64
PAIRS = 16
LEN = 2048
SEQS = 8


def block_scale(stream_key, shape, split, least, largest):
    def one(position, parts):
        heights = jax.random.uniform(jax.random.fold_in(jax.random.fold_in(stream_key, 6), position), (parts,), jnp.float32, least / len(split), largest / len(split))
        return jnp.repeat(jnp.exp(heights), shape[position] // parts).reshape((-1,) + (1,) * (len(shape) - position - 1))

    loudness = one(*split[0])
    for cut in split[1:]:
        loudness = loudness * one(*cut)
    return loudness


def distinct(stream_key, rows, number_of, top, lift):
    sequence = jax.random.permutation(jax.random.fold_in(stream_key, 1), number_of)
    boost = sequence
    for power in range(3):
        boost = boost * boost // number_of
    boost = boost * lift // number_of
    tickets = jax.random.randint(jax.random.fold_in(stream_key, 2), (rows, number_of), 0, 4096) + boost
    sure = jax.random.permutation(jax.random.fold_in(stream_key, 3), rows)[jnp.arange(number_of) % rows]
    tickets = jnp.where(jnp.arange(rows)[:, None] == sure[None, :], 1 << 14, tickets)
    score = tickets * number_of + jnp.arange(number_of)
    return lax.top_k(score.astype(jnp.int32), top)[1].astype(jnp.int32)


def normal_values(stream_key, dims, width, reach, shards=(), kind=jnp.bfloat16):
    entries = jax.random.normal(stream_key, dims, jnp.float32) * width
    if len(shards) > 0:
        entries = block_scale(stream_key, dims, shards, -0.22, 0.18) * entries
    return jnp.clip(entries, min=-reach, max=reach).astype(kind)


def setup_inputs(seed: int = 0) -> dict:
    keys = jax.random.split(jax.random.key(seed), 13)
    return {
        "tokens": normal_values(keys[0], (SEQS, LEN, D), 1.0, 6.0, ((0, 2), (1, 16))),
        "routes": distinct(keys[1], SEQS * LEN, EXPERTS, TOP, 2048).reshape((SEQS, LEN, TOP)),
        "block_order": jax.random.permutation(keys[2], PAIRS).astype(jnp.int32),
        "norm_gain1": jnp.clip(1.0 + 0.1 * jax.random.normal(keys[3], (D,), jnp.float32), 0.5, 1.5).astype(jnp.bfloat16),
        "router_w": normal_values(keys[4], (D, EXPERTS), (2 * D) ** -0.5, 0.1875, ((0, 2),)),
        "query_w": normal_values(keys[5], (D, EXPERTS * HEAD), D ** -0.5, 0.25, ((0, 2),)),
        "kv_w": normal_values(keys[6], (D, 2 * HEAD), D ** -0.5, 0.25, ((0, 2),)),
        "out_w": normal_values(keys[7], (EXPERTS * HEAD, D), (LEN ** 0.5 / 24), 6.0, ((0, 2),)),
        "norm_gain2": jnp.clip(1.0 + 0.1 * jax.random.normal(keys[8], (D,), jnp.float32), 0.5, 1.5).astype(jnp.bfloat16),
        "up_w": normal_values(keys[9], (D, FF), D ** -0.5, 0.25, ((0, 2),)),
        "down_w": normal_values(keys[10], (FF, D), FF ** -0.5, 0.125, ((0, 2),)),
        "cotangent": normal_values(keys[11], (SEQS, LEN, D), 1.0, 6.0, ((0, 2), (1, 16))),
    }


HIGHEST = lax.Precision.HIGHEST

@jax.custom_vjp
def low(v):
    return lax.optimization_barrier(v.astype(jnp.bfloat16)).astype(jnp.float32)

@jax.custom_vjp
def low_back(v):
    return v

def low_keep(v):
    return (low(v), None)

def low_pass(kept, grad):
    return (grad,)

def back_keep(v):
    return (v, None)

def back_low(kept, grad):
    return (low(grad),)
low.defvjp(low_keep, low_pass)
low_back.defvjp(back_keep, back_low)

def smooth_unit(values_in):
    return jax.nn.gelu(values_in, approximate=False)

def normalize(inputs, gain_vec):
    centre = inputs - lax.optimization_barrier(jnp.mean(inputs, axis=-1, keepdims=True))
    spread = lax.optimization_barrier(jnp.mean(centre * centre, axis=-1, keepdims=True))
    return centre * lax.rsqrt(spread + 1e-05) * gain_vec

def gating(logits, expert_hot):
    chosen = lax.optimization_barrier(jnp.sum(expert_hot * logits[..., None, :], axis=-1))
    return jax.nn.softmax(chosen, axis=-1)

def attention(queries, keys_all, values_all, places):
    query_span = math.gcd(LEN, 512)
    block_count = LEN // query_span

    @jax.checkpoint
    def one_block(item_now):
        query_rows, row_places = item_now
        scores = low_back(jnp.einsum('tsh,kh->tsk', query_rows, keys_all, precision=HIGHEST))
        allowed = places[None, None, :] <= row_places[:, None, None]
        top_score = lax.optimization_barrier(jnp.max(jnp.where(allowed, scores, -1e+30), axis=-1, keepdims=True))
        raised = jnp.exp(jnp.where(allowed, scores - top_score, -1e+30))
        shares = raised / lax.optimization_barrier(jnp.sum(raised, axis=-1, keepdims=True))
        return low_back(jnp.einsum('tsk,kh->tsh', low(shares), values_all, precision=HIGHEST))
    result = lax.map(one_block, (queries.reshape(block_count, query_span, TOP, HEAD), places.reshape(block_count, query_span)))
    return result.reshape(LEN, TOP, HEAD)

def block_layer(inputs, expert_hot, places, gain_one, router, query_mat, kv_mat, out_mat, gain_two, up_mat, down_mat):
    normed = low(normalize(inputs, gain_one))
    gate_values = gating(jnp.dot(normed, router, precision=HIGHEST), expert_hot)
    query_all = jnp.dot(normed, query_mat, precision=HIGHEST).reshape(LEN, EXPERTS, HEAD)
    queries = low_back(low(jnp.einsum('tse,teh->tsh', expert_hot, query_all, precision=HIGHEST) * 0.125))
    keyval = low_back(low(jnp.dot(normed, kv_mat, precision=HIGHEST)))
    attended = attention(queries, keyval[:, :HEAD], keyval[:, HEAD:], places)
    weighted = gate_values[..., None] * attended
    mixed_heads = low(jnp.einsum('tse,tsh->teh', expert_hot, weighted, precision=HIGHEST).reshape(LEN, EXPERTS * HEAD))
    hidden = inputs + low_back(jnp.dot(mixed_heads, out_mat, precision=HIGHEST))
    normed_two = low(normalize(hidden, gain_two))
    pre_act = low_back(jnp.dot(normed_two, up_mat, precision=HIGHEST))
    activated = low(smooth_unit(pre_act))
    return hidden + low_back(jnp.dot(activated, down_mat, precision=HIGHEST))

def reference(tokens, routes, block_order, norm_gain1, router_w, query_w, kv_w, out_w, norm_gain2, up_w, down_w, cotangent):
    order_int = block_order.astype(jnp.int32)
    routes_int = routes.astype(jnp.int32)
    offsets = jnp.arange(BLK, dtype=jnp.int32)
    front_rows = (order_int[:, None] * BLK + offsets[None, :]).astype(jnp.int32)
    back_rows = ((2 * PAIRS - 1 - order_int)[:, None] * BLK + offsets[None, :]).astype(jnp.int32)
    places = jnp.concatenate([front_rows, back_rows], axis=1).reshape(LEN).astype(jnp.int32)
    weights = tuple((w.astype(jnp.float32) for w in (norm_gain1, router_w, query_w, kv_w, out_w, norm_gain2, up_w, down_w)))

    def advance(totals, item_now):
        seq_tokens, seq_routes, seq_cotangent = item_now
        expert_hot = (seq_routes[..., None] == jnp.arange(EXPERTS, dtype=jnp.int32)).astype(jnp.float32)

        def forward(inputs, *params):
            return block_layer(inputs, expert_hot, places, *params)
        result, pull_back = jax.vjp(forward, seq_tokens.astype(jnp.float32), *weights)
        pulled = pull_back(seq_cotangent.astype(jnp.float32))
        totals = tuple(((a + b).astype(jnp.float32) for a, b in zip(totals, pulled[1:])))
        return (totals, (result.astype(jnp.float32), pulled[0].astype(jnp.float32)))
    initial = tuple((jnp.zeros(w.shape, jnp.float32) for w in weights))
    totals, outputs = lax.scan(advance, initial, (tokens.astype(jnp.float32), routes_int, cotangent.astype(jnp.float32)))
    return (outputs[0], outputs[1], totals[0], totals[1], totals[2], totals[3], totals[4], totals[5], totals[6], totals[7])
```

```python
import math

import jax
import jax.numpy as jnp
from jax import lax
from jax.sharding import PartitionSpec as P

HIGHEST = lax.Precision.HIGHEST
BF = jnp.bfloat16
F32 = jnp.float32


def factors(size):
    out = []
    while size > 1:
        step = 4 if size % 4 == 0 else 2
        out.append(step)
        size //= step
    return out


def swap(values, mask, size):
    return lax.ppermute(values, "ctx", [(i, i ^ mask) for i in range(size)])


def smooth_unit(values_in):
    return jax.nn.gelu(values_in, approximate=False)


def normalize(inputs, gain_vec):
    centre = inputs - jnp.mean(inputs, axis=-1, keepdims=True)
    spread = jnp.mean(centre * centre, axis=-1, keepdims=True)
    return centre * lax.rsqrt(spread + 1e-05) * gain_vec


def gating(logits, expert_hot):
    chosen = jnp.sum(expert_hot * logits[..., None, :], axis=-1)
    return jax.nn.softmax(chosen, axis=-1)


def tile_scores(queries, kv_all, query_places, key_places, first_row, width):
    head = queries.shape[-1]
    tile = lax.dynamic_slice_in_dim(kv_all, first_row, width, 1)
    places = lax.dynamic_slice_in_dim(key_places, first_row, width, 0)
    keys_tile = tile[..., :head]
    values_tile = tile[..., head:]
    scores = jnp.einsum("btsh,bkh->btsk", queries, keys_tile, preferred_element_type=jnp.float32)
    allowed = places[None, None, None, :] <= query_places[None, :, None, None]
    return (keys_tile, values_tile, scores, allowed)


def log_totals(queries, kv_all, query_places, key_places):
    rows = kv_all.shape[1]
    width = math.gcd(rows, 2048)

    def log_advance(carry, index):
        top_score, total = carry
        unused_keys, unused_values, scores, allowed = tile_scores(
            queries, kv_all, query_places, key_places, index * width, width
        )
        fresh = jnp.maximum(top_score, jnp.max(jnp.where(allowed, scores, -1e30), axis=-1))
        shares = jnp.where(allowed, jnp.exp(scores - fresh[..., None]), 0.0)
        total = total * jnp.exp(top_score - fresh) + jnp.sum(shares, axis=-1)
        return ((fresh, total), None)

    shape = queries.shape[:-1]
    initial = (jnp.full(shape, -1e30, jnp.float32), jnp.zeros(shape, jnp.float32))
    carry, unused = lax.scan(log_advance, initial, jnp.arange(rows // width, dtype=jnp.int32))
    return carry[0] + jnp.log(carry[1])


def attend(queries, kv_all, query_places, key_places, log_total):
    rows = kv_all.shape[1]
    width = math.gcd(rows, 2048)

    def attend_advance(carry, index):
        unused_keys, values_tile, scores, allowed = tile_scores(
            queries, kv_all, query_places, key_places, index * width, width
        )
        shares = jnp.where(allowed, jnp.exp(scores - log_total[..., None]), 0.0).astype(
            jnp.bfloat16
        )
        return (
            carry
            + jnp.einsum("btsk,bkh->btsh", shares, values_tile, preferred_element_type=jnp.float32),
            None,
        )

    summed, unused = lax.scan(
        attend_advance,
        jnp.zeros(queries.shape, jnp.float32),
        jnp.arange(rows // width, dtype=jnp.int32),
    )
    return summed


def key_range_grads(
    queries, back_attended, kv_all, query_places, key_places, log_total, row_delta, begin, row_count
):
    width = math.gcd(row_count, 2048)

    def key_advance(carry, index):
        back_query, back_kv = carry
        keys_tile, values_tile, scores, allowed = tile_scores(
            queries, kv_all, query_places, key_places, begin + index * width, width
        )
        shares = jnp.where(allowed, jnp.exp(scores - log_total[..., None]), 0.0)
        back_shares = jnp.einsum(
            "btsh,bkh->btsk", back_attended, values_tile, preferred_element_type=jnp.float32
        )
        back_scores = (shares * (back_shares - row_delta[..., None])).astype(jnp.bfloat16)
        back_query = back_query + jnp.einsum(
            "btsk,bkh->btsh", back_scores, keys_tile, preferred_element_type=jnp.float32
        )
        back_keys = jnp.einsum(
            "btsk,btsh->bkh", back_scores, queries, preferred_element_type=jnp.float32
        )
        back_values = jnp.einsum(
            "btsk,btsh->bkh",
            shares.astype(jnp.bfloat16),
            back_attended,
            preferred_element_type=jnp.float32,
        )
        back_kv = lax.dynamic_update_slice_in_dim(
            back_kv, jnp.concatenate([back_keys, back_values], axis=-1), index * width, 1
        )
        return ((back_query, back_kv), None)

    head = queries.shape[-1]
    kv_start = jnp.zeros((queries.shape[0], row_count, 2 * head), jnp.float32)
    carry, unused = lax.scan(
        key_advance,
        (jnp.zeros(queries.shape, jnp.float32), kv_start),
        jnp.arange(row_count // width, dtype=jnp.int32),
    )
    return carry


def pick(parts, index):
    return lax.dynamic_index_in_dim(parts, index, 0, False)


def spread_out(parts, place, stride, size):
    count = parts.shape[0]
    slots = [pick(parts, place)]
    for k in range(1, count):
        slots.append(swap(pick(parts, place ^ k), k * stride, size))
    return jnp.stack(slots)


def bring_back(slots, place, stride, size):
    count = slots.shape[0]
    out = jnp.zeros(slots.shape, slots.dtype)
    for k in range(count):
        got = slots[0] if k == 0 else swap(slots[k], k * stride, size)
        out = lax.dynamic_update_index_in_dim(out, got, place ^ k, 0)
    return out


def gather_masked(rows, span, size):
    stride = 1
    for step in factors(span):
        rows = jnp.concatenate(
            [rows] + [swap(rows, j * stride, size) for j in range(1, step)], axis=0
        )
        stride *= step
    return rows


def scatter_masked(rows, span, size):
    steps = factors(span)
    stride = span
    for step in reversed(steps):
        stride //= step
        parts = rows.reshape((step, rows.shape[0] // step) + rows.shape[1:])
        total = parts[0]
        for j in range(1, step):
            total = total + swap(parts[j].astype(BF), j * stride, size).astype(F32)
        rows = total
    return rows


def reduce_all(rows, size):
    here = lax.axis_index("ctx")
    stride = 1
    for step in factors(size):
        digit = (here // stride) % step
        parts = rows.reshape(step, rows.shape[0] // step, rows.shape[1])
        total = pick(parts, digit).astype(F32)
        for j in range(1, step):
            total = total + swap(pick(parts, digit ^ j), j * stride, size).astype(F32)
        rows = total.astype(BF)
        stride *= step
    for step in reversed(factors(size)):
        stride //= step
        digit = (here // stride) % step
        out = jnp.zeros((step,) + rows.shape, rows.dtype)
        for j in range(step):
            got = rows if j == 0 else swap(rows, j * stride, size)
            out = lax.dynamic_update_index_in_dim(out, got, digit ^ j, 0)
        rows = out.reshape(step * rows.shape[0], rows.shape[1])
    return rows


def total_grads(grads, size, width=512):
    core = lax.axis_index("wsh")
    halves = [g.reshape(2, -1, width) if g.size >= 2 * width else g.reshape(2, 1, -1) for g in grads]
    mine = [pick(h, core) for h in halves]
    theirs = [pick(h, 1 - core).astype(BF) for h in halves]
    mine = [jnp.pad(h, ((0, 0), (0, width - h.shape[1]))) for h in mine]
    theirs = [jnp.pad(h, ((0, 0), (0, width - h.shape[1]))) for h in theirs]
    packed = jnp.concatenate(theirs, axis=0)
    own = jnp.concatenate(mine, axis=0)
    rows = own.shape[0]
    unit = 16 * size
    extra = -rows % unit
    packed = jnp.pad(packed, ((0, extra), (0, 0)))
    own = jnp.pad(own, ((0, extra), (0, 0)))
    own = own + lax.ppermute(packed, "wsh", [(0, 1), (1, 0)]).astype(F32)
    done = reduce_all(own.astype(BF), size)
    out = []
    at = 0
    for g, h in zip(grads, halves):
        count, wide = h.shape[1:]
        piece = done[at : at + count, :wide].astype(F32)
        at += count
        out.append(piece.reshape((g.shape[0] // 2,) + g.shape[1:]))
    return out


def whole(half):
    core = lax.axis_index("wsh")
    other = lax.ppermute(half, "wsh", [(0, 1), (1, 0)])
    both = jnp.stack([half, other])
    return jnp.concatenate([pick(both, core), pick(both, 1 - core)], axis=0)


def on_device(
    tokens,
    routes,
    block_order,
    norm_gain1,
    router_w,
    query_w,
    kv_w,
    out_w,
    norm_gain2,
    up_w,
    down_w,
    cotangent,
):
    size = lax.axis_size("ctx")
    count, local, width = tokens.shape
    rest = size // count
    here = lax.axis_index("ctx")
    place, other = here // rest, here % rest
    router, query_mat, kv_mat, out_mat, up_mat, down_mat = (
        whole(w) for w in (router_w, query_w, kv_w, out_w, up_w, down_w)
    )
    gain_one = whole(norm_gain1).astype(F32)
    gain_two = whole(norm_gain2).astype(F32)
    experts = router.shape[1]
    head = kv_mat.shape[1] // 2
    block = local // 2

    inputs = spread_out(tokens, place, rest, size).reshape(count * local, width).astype(F32)
    my_routes = spread_out(routes, place, rest, size).reshape(count * local, 2)
    my_cot = spread_out(cotangent, place, rest, size).reshape(count * local, width)

    slots = jnp.arange(count, dtype=jnp.int32)
    masks = jnp.arange(rest, dtype=jnp.int32)
    pair = (place ^ slots)[None, :] * rest + (other ^ masks)[:, None]
    first = block_order[pair.reshape(-1)]
    offsets = jnp.arange(block, dtype=jnp.int32)
    front = first[:, None] * block + offsets[None, :]
    back = (2 * size - 1 - first)[:, None] * block + offsets[None, :]
    key_places = jnp.concatenate([front, back], axis=1).reshape(-1)
    query_places = key_places[: count * local]

    expert_hot = (my_routes[..., None] == jnp.arange(experts, dtype=jnp.int32)).astype(F32)
    normed, norm_pull_one = jax.vjp(normalize, inputs, gain_one)
    normed_low = normed.astype(BF)
    logits = jnp.dot(normed_low, router, preferred_element_type=F32)
    gate_values, gate_pull = jax.vjp(lambda v: gating(v, expert_hot), logits)
    query_all = jnp.dot(normed_low, query_mat, preferred_element_type=F32).reshape(-1, experts, head)
    queries = (jnp.einsum("tse,teh->tsh", expert_hot, query_all, precision=HIGHEST) * 0.125).astype(BF)
    keyval = jnp.dot(normed_low, kv_mat, preferred_element_type=F32).astype(BF)
    kv_all = gather_masked(keyval, rest, size)
    queries, kv_all = queries[None], kv_all[None]
    log_total = log_totals(queries, kv_all, query_places, key_places)
    attended = attend(queries, kv_all, query_places, key_places, log_total)[0]
    weighted = gate_values[..., None] * attended
    mixed = (
        jnp.einsum("tse,tsh->teh", expert_hot, weighted, precision=HIGHEST)
        .reshape(-1, experts * head)
        .astype(BF)
    )
    hidden = inputs + jnp.dot(mixed, out_mat, preferred_element_type=F32)
    normed_two, norm_pull_two = jax.vjp(normalize, hidden, gain_two)
    two_low = normed_two.astype(BF)
    pre_act = jnp.dot(two_low, up_mat, preferred_element_type=F32)
    act_values, act_pull = jax.vjp(smooth_unit, pre_act)
    activated = act_values.astype(BF)
    layer_part = hidden + jnp.dot(activated, down_mat, preferred_element_type=F32)
    grad_down = jnp.einsum("tf,td->fd", activated, my_cot, preferred_element_type=F32)
    back_act = jnp.einsum("td,fd->tf", my_cot, down_mat, preferred_element_type=F32)
    (back_pre_f,) = act_pull(back_act)
    back_pre = back_pre_f.astype(BF)
    grad_up = jnp.einsum("td,tf->df", two_low, back_pre, preferred_element_type=F32)
    back_two = jnp.einsum("tf,df->td", back_pre, up_mat, preferred_element_type=F32)
    hidden_part, grad_gain2 = norm_pull_two(back_two)
    back_hidden = my_cot.astype(F32) + hidden_part
    back_branch = back_hidden.astype(BF)
    grad_out = jnp.einsum("tk,td->kd", mixed, back_branch, preferred_element_type=F32)
    early = total_grads([grad_up, grad_down, grad_out, grad_gain2], size)

    back_mixed = jnp.einsum("td,kd->tk", back_branch, out_mat, preferred_element_type=F32).reshape(
        -1, experts, head
    )
    back_slots = jnp.einsum("tse,teh->tsh", expert_hot, back_mixed, precision=HIGHEST)
    back_gates = jnp.sum(back_slots * attended, axis=-1)
    back_attended = (gate_values[..., None] * back_slots).astype(BF)
    (back_logits,) = gate_pull(back_gates)
    row_delta = jnp.sum(back_attended.astype(F32) * attended, axis=-1)
    back_query, full_kv = key_range_grads(
        queries,
        back_attended[None],
        kv_all,
        query_places,
        key_places,
        log_total,
        row_delta[None],
        0,
        kv_all.shape[1],
    )
    back_query = back_query[0].astype(BF)
    back_kv = scatter_masked(full_kv[0], rest, size).astype(BF)
    back_qall = (
        (jnp.einsum("tse,tsh->teh", expert_hot.astype(BF), back_query, preferred_element_type=F32) * 0.125)
        .reshape(-1, experts * head)
        .astype(BF)
    )
    grad_query = jnp.einsum("td,tk->dk", normed_low, back_qall, preferred_element_type=F32)
    grad_kv = jnp.einsum("td,tk->dk", normed_low, back_kv, preferred_element_type=F32)
    grad_router = jnp.einsum("td,te->de", normed_low.astype(F32), back_logits, precision=HIGHEST)
    back_normed = jnp.einsum("tk,dk->td", back_qall, query_mat, preferred_element_type=F32)
    back_normed = back_normed + jnp.einsum("tk,dk->td", back_kv, kv_mat, preferred_element_type=F32)
    back_normed = back_normed + jnp.einsum(
        "te,de->td", back_logits, router.astype(F32), precision=HIGHEST
    )
    input_part, grad_gain1 = norm_pull_one(back_normed)
    input_part = back_hidden + input_part
    late = total_grads([grad_query, grad_kv, grad_router, grad_gain1], size)

    layer_out = bring_back(layer_part.reshape(count, local, width).astype(BF), place, rest, size)
    input_grad = bring_back(input_part.reshape(count, local, width).astype(BF), place, rest, size)
    return (
        layer_out.astype(F32),
        input_grad.astype(F32),
        late[3],
        late[2],
        late[0],
        late[1],
        early[2],
        early[3],
        early[0],
        early[1],
    )


def solution(mesh):
    placed = (
        P("wsh", "ctx", None),
        P("wsh", "ctx", None),
        P(),
        P("wsh"),
        P("wsh", None),
        P("wsh", None),
        P("wsh", None),
        P("wsh", None),
        P("wsh"),
        P("wsh", None),
        P("wsh", None),
        P("wsh", "ctx", None),
    )
    return jax.shard_map(
        on_device,
        mesh=mesh,
        in_specs=placed,
        out_specs=(
            P("wsh", "ctx", None),
            P("wsh", "ctx", None),
            P("wsh"),
            P("wsh", None),
            P("wsh", None),
            P("wsh", None),
            P("wsh", None),
            P("wsh"),
            P("wsh", None),
            P("wsh", None),
        ),
        check_vma=False,
    )
```

```python
import functools
import math

import jax
import jax.numpy as jnp
from jax import lax
from jax.experimental import pallas as pl
from jax.experimental.pallas import tpu as pltpu
from jax.sharding import PartitionSpec as P

BF = jnp.bfloat16
F32 = jnp.float32
I32 = jnp.int32
NONE = -1e30
TWO = 2


def factors(size):
    out = []
    while size > 1:
        step = 4 if size % 4 == 0 else 2
        out.append(step)
        size //= step
    return out


def swap(values, mask, size):
    return lax.ppermute(values, "ctx", [(i, i ^ mask) for i in range(size)])


def trade(values):
    return lax.ppermute(values, "wsh", [(0, 1), (1, 0)])


def pick(parts, index):
    return lax.dynamic_index_in_dim(parts, index, 0, False)


def mm(a, b, left=1, right=0):
    return lax.dot_general(a, b, (((left,), (right,)), ((), ())), preferred_element_type=F32)


def call(body, outs, args, scratch=(), smem=(), flops=0, mib=40):
    whole = pl.BlockSpec(memory_space=pltpu.VMEM)
    scalars = pl.BlockSpec(memory_space=pltpu.SMEM)
    moved = sum(math.prod(s) * jnp.dtype(d).itemsize for s, d in outs)
    moved += sum(a.size * a.dtype.itemsize for a in args)
    return pl.pallas_call(
        body,
        out_shape=[jax.ShapeDtypeStruct(s, d) for s, d in outs],
        in_specs=[scalars if i in smem else whole for i in range(len(args))],
        out_specs=[whole] * len(outs),
        scratch_shapes=[pltpu.VMEM(s, d) for s, d in scratch],
        compiler_params=pltpu.CompilerParams(vmem_limit_bytes=mib << 20),
        cost_estimate=pl.CostEstimate(flops=int(flops), bytes_accessed=int(moved), transcendentals=0),
    )(*args)


def join(slots):
    half = slots[0].shape[0] // 2
    return jnp.concatenate([s[:half] for s in slots] + [s[half:] for s in slots], axis=0)


def slot_rows(rows, k, count):
    half = rows.shape[0] // (2 * count)
    low = k * half
    high = rows.shape[0] // 2 + k * half
    return jnp.concatenate([rows[low : low + half], rows[high : high + half]], axis=0)


def centred(rows):
    centre = rows - jnp.mean(rows, axis=-1, keepdims=True)
    scale = lax.rsqrt(jnp.mean(centre * centre, axis=-1, keepdims=True) + 1e-05)
    return centre * scale, scale


def fill(scratch, own, other, core):
    half = own.shape[0]
    scratch[pl.ds(pl.multiple_of(core * half, half), half), :] = own[...]
    scratch[pl.ds(pl.multiple_of((1 - core) * half, half), half), :] = other[...]


def gain_row(own, other, core):
    part = core.astype(F32)
    a, b = own[...].astype(F32), other[...].astype(F32)
    return jnp.concatenate([a + part * (b - a), b + part * (a - b)], axis=1)


def pick_gain(own, other, core):
    a, b = own[...].astype(F32), other[...].astype(F32)
    first = jnp.where(core == 0, a, b)
    second = jnp.where(core == 0, b, a)
    return jnp.concatenate([first, second], axis=1)


def route_rows(pieces):
    lane = lax.broadcasted_iota(I32, (8, 128), 1)
    low = lane < 64
    rolled = [pltpu.roll(p, 64, 1) for p in pieces]
    count = len(pieces)
    front = [jnp.where(low, pieces[i], rolled[i + 1]) for i in range(0, count, 2)]
    back = [jnp.where(low, rolled[i], pieces[i + 1]) for i in range(0, count, 2)]
    return jnp.concatenate(front + back, axis=1)


def project_body(count, rest, experts, head, *refs):
    tok, others = refs[0], refs[1:count]
    (routes0, *routes_x) = refs[count : 2 * count]
    g_own, g_other, q_own, q_other, k_own, k_other, r_own, r_other = refs[2 * count : 2 * count + 8]
    kv_out, qt_out, nt_out, gate_out, route_out, wq, wk, wr = refs[2 * count + 8 :]
    core = lax.axis_index("wsh")
    place = lax.axis_index("ctx") // rest
    fill(wq, q_own, q_other, core)
    fill(wk, k_own, k_other, core)
    wr[...] = jnp.zeros_like(wr)
    half = r_own.shape[0]
    wr[pl.ds(pl.multiple_of(core * half, half), half), :experts] = r_own[...].astype(F32)
    wr[pl.ds(pl.multiple_of((1 - core) * half, half), half), :experts] = r_other[...].astype(F32)
    rows = join([tok[place]] + [o[...] for o in others]).astype(F32)
    unit, _ = centred(rows)
    normed = (unit * pick_gain(g_own, g_other, core)).astype(BF)
    nt_out[...] = normed.T
    kv_out[...] = mm(normed, wk[...]).astype(BF)
    routes = route_rows([routes0[place]] + [r[...] for r in routes_x])
    route_out[...] = routes
    logits = mm(normed, wr[...].astype(BF)).T
    queries = (mm(normed, wq[...]) * 0.125).T
    chosen = []
    for s in range(TWO):
        route = routes[s : s + 1]
        total = jnp.zeros((head, rows.shape[0]), F32)
        value = jnp.zeros((1, rows.shape[0]), F32)
        for e in range(experts):
            here = route == e
            total = jnp.where(here, queries[e * head : (e + 1) * head], total)
            value = jnp.where(here, logits[e : e + 1], value)
        qt_out[s * head : (s + 1) * head, :] = total.astype(BF)
        chosen.append(value)
    top = jnp.maximum(chosen[0], chosen[1])
    raised = [jnp.exp(c - top) for c in chosen]
    total = raised[0] + raised[1]
    gate_out[...] = jnp.concatenate([r / total for r in raised], axis=0)


def places(order, count, rest, block, width, part):
    me = lax.axis_index("ctx")
    place, other = me // rest, me % rest
    size = count * rest
    lane = lax.broadcasted_iota(I32, (1, width), 1)
    out = jnp.zeros((1, width), I32)
    for k in range(count):
        first = order[(place ^ k) * rest + other]
        base = jnp.where(part == 0, first, 2 * size - 1 - first) * block
        out = jnp.where(lane // block == k, lane - k * block + base, out)
    return out


def key_bases(order, count, rest, block, chunk, part):
    me = lax.axis_index("ctx")
    place, other = me // rest, me % rest
    size = count * rest
    out = []
    for k in range(count):
        first = order[(place ^ k) * rest + (other ^ chunk)]
        out.append((first if part == 0 else 2 * size - 1 - first) * block)
    return out


def masked(scores, gap, bases, block):
    parts = [
        jnp.where(gap <= -base, scores[k * block : (k + 1) * block], NONE)
        for k, base in enumerate(bases)
    ]
    return jnp.concatenate(parts, axis=0)


def scored(kv, side, h, gap, order, count, rest, block, chunk, half):
    first = mm(kv[:half], side)
    if h == 0:
        return masked(first, gap, key_bases(order, count, rest, block, chunk, 0), block)
    second = mm(kv[half:], side)
    second = masked(second, gap, key_bases(order, count, rest, block, chunk, 1), block)
    return jnp.concatenate([first, second], axis=0)


def load_keys(kv_refs, kv_all, kv_turned):
    rows = kv_refs[0].shape[0]
    for c, ref in enumerate(kv_refs):
        kv_all[c * rows : (c + 1) * rows, :] = ref[...]
        kv_turned[:, c * rows : (c + 1) * rows] = ref[...].T


def attend_body(count, rest, experts, head, pieces, *refs):
    order = refs[0]
    kv_refs = refs[1 : 1 + pieces]
    qt, gates, routes, tok = refs[1 + pieces : 5 + pieces]
    others = refs[5 + pieces : 4 + pieces + count]
    g_own, g_other, o_own, o_other = refs[4 + pieces + count : 8 + pieces + count]
    att_out, log_out, mixed_out, hidden_out, two_out, turned_out, kv_all, kv_turned, wo = refs[
        8 + pieces + count :
    ]
    core = lax.axis_index("wsh")
    place = lax.axis_index("ctx") // rest
    total = qt.shape[1]
    half = total // 2
    block = half // count
    load_keys(kv_refs, kv_all, kv_turned)
    fill(wo, o_own, o_other, core)
    for h in range(2):
        gap = lax.broadcasted_iota(I32, (block, half), 0) - places(order, count, rest, block, half, h)
        for s in range(TWO):
            side = qt[s * head : (s + 1) * head, h * half : (h + 1) * half]
            side = jnp.concatenate([side, jnp.zeros_like(side)], axis=0)
            reach = half * (h + 1)

            def step(chunk, carry, side=side, h=h, gap=gap, reach=reach):
                top, norm, summed = carry
                at = pl.multiple_of(chunk * total, total)
                kv = kv_all[pl.ds(at, total), :]
                scores = scored(kv, side, h, gap, order, count, rest, block, chunk, half)
                fresh = jnp.maximum(top, jnp.max(scores, axis=0, keepdims=True))
                shares = jnp.exp(scores - fresh)
                fade = jnp.exp(top - fresh)
                norm = norm * fade + jnp.sum(shares, axis=0, keepdims=True)
                values = kv_turned[head:, pl.ds(at, reach)]
                summed = summed * fade + mm(values, shares.astype(BF))
                return fresh, norm, summed

            start = (
                jnp.full((1, half), NONE, F32),
                jnp.zeros((1, half), F32),
                jnp.zeros((head, half), F32),
            )
            top, norm, summed = lax.fori_loop(0, rest, step, start, unroll=rest <= 4)
            log_out[s : s + 1, h * half : (h + 1) * half] = top + jnp.log(norm)
            att_out[s * head : (s + 1) * head, h * half : (h + 1) * half] = summed / norm
    for e in range(experts):
        part = jnp.zeros((head, total), F32)
        for s in range(TWO):
            gate = jnp.where(routes[s : s + 1] == e, gates[s : s + 1], 0.0)
            part = part + gate * att_out[s * head : (s + 1) * head, :]
        mixed_out[e * head : (e + 1) * head, :] = part.astype(BF)
    rows = join([tok[place]] + [o[...] for o in others]).astype(F32)
    hidden = rows + mm(mixed_out[...].T, wo[...])
    hidden_out[...] = hidden
    unit, _ = centred(hidden)
    two = (unit * pick_gain(g_own, g_other, core)).astype(BF)
    two_out[...] = two
    turned_out[...] = two.T


def feed_body(count, rest, first, tile, *refs):
    two, turned, cot = refs[:3]
    others = refs[3 : 2 + count]
    u_own, u_other, down, layer_in = refs[2 + count : 6 + count]
    at = 6 + count
    back_in = None
    if not first:
        back_in = refs[at]
        at += 1
    if first:
        layer_out, back_out, send, keep = refs[at : at + 4]
        up, cots = refs[at + 4 :]
    else:
        outs = refs[at : at + count + 4]
        layer_pieces, back_out, keep_down, keep, send = outs[:count], *outs[count:]
        up, cots, layer_out = refs[at + count + 4 :]
    core = lax.axis_index("wsh")
    place = lax.axis_index("ctx") // rest
    side = (1 - core) if first else core
    width = down.shape[0]
    half = u_own.shape[0]
    lanes = pl.ds(pl.multiple_of(side * width, width), width)
    up[pl.ds(pl.multiple_of(core * half, half), half), :] = u_own[:, lanes]
    up[pl.ds(pl.multiple_of((1 - core) * half, half), half), :] = u_other[:, lanes]
    cots[...] = join([cot[place]] + [o[...] for o in others])
    layer_out[...] = layer_in[...]
    if first:
        back_out[...] = jnp.zeros_like(back_out)
    else:
        back_out[...] = back_in[...]
    mine = pl.ds(pl.multiple_of(core * half, half), half)
    theirs = pl.ds(pl.multiple_of((1 - core) * half, half), half)
    dim = up.shape[0]
    per = dim // tile

    def step(j, carry):
        cols = pl.ds(pl.multiple_of(j * tile, tile), tile)
        up_j = up[:, cols]
        down_j = down[cols, :]
        pre = mm(two[...], up_j)
        back = mm(cots[...], down_j, 1, 1)
        phi = 0.5 * (1.0 + lax.erf(pre * math.sqrt(0.5)))
        bell = jnp.exp(pre * pre * -0.5) * (1.0 / math.sqrt(2.0 * math.pi))
        act = (pre * phi).astype(BF)
        back_pre = (back * (phi + pre * bell)).astype(BF)
        layer_out[...] += mm(act, down_j)
        back_out[...] += mm(back_pre, up_j, 1, 1)
        grad = mm(act.T, cots[...]).astype(BF)
        grad_mine = mm(turned[mine, :], back_pre).astype(BF)
        grad_theirs = mm(turned[theirs, :], back_pre).astype(BF)
        rows = pl.ds(pl.multiple_of((j // per) * half, half), half)
        lane = pl.ds(pl.multiple_of((j % per) * tile, tile), tile)
        keep[rows, lane] = grad_mine
        if first:
            send[cols, :] = grad
            lower = pl.ds(pl.multiple_of(width + (j // per) * half, half), half)
            send[lower, lane] = grad_theirs
        else:
            keep_down[cols, :] = grad
            send[rows, lane] = grad_theirs
        return carry

    lax.fori_loop(0, width // tile, step, 0)
    if not first:
        for k in range(count):
            layer_pieces[k][...] = slot_rows(layer_out[...], k, count).astype(layer_pieces[k].dtype)


def turn_body(count, rest, experts, head, *refs):
    hidden, back_two, cot = refs[:3]
    others = refs[3 : 2 + count]
    mixed, o_own, o_other, g_own, g_other, gates, routes, att = refs[2 + count : 10 + count]
    back_hidden_out, keep, send, grad_att_out, delta_out, logit_out, gain_out, wo = refs[10 + count :]
    core = lax.axis_index("wsh")
    place = lax.axis_index("ctx") // rest
    fill(wo, o_own, o_other, core)
    half = o_own.shape[0]
    unit, scale = centred(hidden[...])
    back = back_two[...]
    side = back * pick_gain(g_own, g_other, core)
    part = scale * (
        side
        - jnp.mean(side, axis=-1, keepdims=True)
        - unit * jnp.mean(side * unit, axis=-1, keepdims=True)
    )
    gain_out[...] = jnp.broadcast_to(jnp.sum(back * unit, axis=0, keepdims=True), gain_out.shape)
    cots = join([cot[place]] + [o[...] for o in others]).astype(F32)
    back_hidden = cots + part
    back_hidden_out[...] = back_hidden
    branch = back_hidden.astype(BF)
    keep[...] = mm(mixed[pl.ds(pl.multiple_of(core * half, half), half), :], branch).astype(BF)
    send[...] = mm(mixed[pl.ds(pl.multiple_of((1 - core) * half, half), half), :], branch).astype(BF)
    back_mixed = mm(wo[...], branch, 1, 1)
    grads = []
    for s in range(TWO):
        total = jnp.zeros((head, branch.shape[0]), F32)
        for e in range(experts):
            total = jnp.where(routes[s : s + 1] == e, back_mixed[e * head : (e + 1) * head], total)
        att_s = att[s * head : (s + 1) * head, :]
        grads.append(jnp.sum(total * att_s, axis=0, keepdims=True))
        low = (gates[s : s + 1] * total).astype(BF)
        grad_att_out[s * head : (s + 1) * head, :] = low
        delta_out[s : s + 1, :] = jnp.sum(low.astype(F32) * att_s, axis=0, keepdims=True)
    mean = gates[0:1] * grads[0] + gates[1:2] * grads[1]
    row = lax.broadcasted_iota(I32, logit_out.shape, 0)
    logit = jnp.zeros(logit_out.shape, F32)
    for s in range(TWO):
        value = gates[s : s + 1] * (grads[s] - mean)
        logit = logit + jnp.where(row == routes[s : s + 1], value, 0.0)
    logit_out[...] = logit


def attend_back_body(count, rest, head, pieces, split, *refs):
    order = refs[0]
    kv_refs = refs[1 : 1 + pieces]
    qt, grad_att, logs, delta = refs[1 + pieces : 5 + pieces]
    grad_q_out = refs[5 + pieces]
    outs = refs[6 + pieces : 6 + pieces + split]
    kv_all, kv_turned, sides, turned, grad_kv, grad_q = refs[6 + pieces + split :]
    total = qt.shape[1]
    half = total // 2
    block = half // count
    load_keys(kv_refs, kv_all, kv_turned)
    blank = jnp.zeros((head, total), BF)
    for s in range(TWO):
        q_side = jnp.concatenate([qt[s * head : (s + 1) * head, :], blank], axis=0)
        g_side = jnp.concatenate([blank, grad_att[s * head : (s + 1) * head, :]], axis=0)
        sides[2 * s], sides[2 * s + 1] = q_side, g_side
        turned[2 * s], turned[2 * s + 1] = q_side.T, g_side.T
    grad_q[...] = jnp.zeros_like(grad_q)
    gaps = [
        lax.broadcasted_iota(I32, (block, half), 0) - places(order, count, rest, block, half, h)
        for h in range(2)
    ]

    def step(chunk, carry):
        at = pl.multiple_of(chunk * total, total)
        kv = kv_all[pl.ds(at, total), :]
        front = jnp.zeros((half, 2 * head), F32)
        back = jnp.zeros((half, 2 * head), F32)
        for h in range(2):
            cols = slice(h * half, (h + 1) * half)
            reach = half * (h + 1)
            for s in range(TWO):
                scores = scored(
                    kv, sides[2 * s, :, cols], h, gaps[h], order, count, rest, block, chunk, half
                )
                shares = jnp.exp(scores - logs[s : s + 1, cols])
                back_shares = mm(kv[:reach], sides[2 * s + 1, :, cols])
                back_scores = (shares * (back_shares - delta[s : s + 1, cols])).astype(BF)
                grad = mm(back_scores, turned[2 * s, cols, :]) + mm(
                    shares.astype(BF), turned[2 * s + 1, cols, :]
                )
                front = front + grad[:half]
                if h == 1:
                    back = back + grad[half:]
                rows = slice(s * head, (s + 1) * head)
                grad_q[rows, cols] += mm(kv_turned[:head, pl.ds(at, reach)], back_scores)
        grad_kv[pl.ds(at, half), :] = front
        grad_kv[pl.ds(at + half, half), :] = back
        return carry

    lax.fori_loop(0, rest, step, 0)
    grad_q_out[...] = grad_q[...].astype(BF)
    rows = outs[0].shape[0]
    for i, out in enumerate(outs):
        out[...] = grad_kv[i * rows : (i + 1) * rows, :].astype(out.dtype)


def unproject_body(count, rest, experts, head, terms, *refs):
    kv_terms = refs[:terms]
    grad_q, normed_t, routes, logit, tok = refs[terms : terms + 5]
    others = refs[terms + 5 : terms + 4 + count]
    at = terms + 4 + count
    back_hidden, q_own, q_other, k_own, k_other, r_own, r_other, g_own, g_other, gain_two = refs[
        at : at + 10
    ]
    at += 10
    pieces = refs[at : at + count]
    keep, send, wq, wk, wr, bqt, gains, routers = refs[at + count :]
    core = lax.axis_index("wsh")
    place = lax.axis_index("ctx") // rest
    fill(wq, q_own, q_other, core)
    fill(wk, k_own, k_other, core)
    wr[...] = jnp.zeros_like(wr)
    half = r_own.shape[0]
    wr[pl.ds(pl.multiple_of(core * half, half), half), :experts] = r_own[...].astype(F32)
    wr[pl.ds(pl.multiple_of((1 - core) * half, half), half), :experts] = r_other[...].astype(F32)
    back_kv = kv_terms[0][...].astype(F32)
    for term in kv_terms[1:]:
        back_kv = back_kv + term[...].astype(F32)
    back_kv = back_kv.astype(BF)
    total = back_kv.shape[0]
    for e in range(experts):
        part = jnp.zeros((head, total), F32)
        for s in range(TWO):
            value = grad_q[s * head : (s + 1) * head, :].astype(F32) * 0.125
            part = jnp.where(routes[s : s + 1] == e, value, part)
        bqt[e * head : (e + 1) * head, :] = part.astype(BF)
    back_q = bqt[...].T
    logits = logit[...]
    parts = []
    left = logits
    for _ in range(3):
        low = left.astype(BF)
        parts.append(low)
        left = left - low.astype(F32)
    router = parts_dot(parts, normed_t[...])
    routers[...] = router
    back = mm(back_q, wq[...], 1, 1) + mm(back_kv, wk[...], 1, 1)
    wr_turned = wr[...].T.astype(BF)
    for low in parts:
        padded = jnp.concatenate([low.astype(F32), jnp.zeros((120, total), F32)], axis=0)
        back = back + mm(padded.T.astype(BF), wr_turned)
    rows = join([tok[place]] + [o[...] for o in others]).astype(F32)
    unit, scale = centred(rows)
    side = back * pick_gain(g_own, g_other, core)
    grad = back_hidden[...] + scale * (
        side
        - jnp.mean(side, axis=-1, keepdims=True)
        - unit * jnp.mean(side * unit, axis=-1, keepdims=True)
    )
    for k in range(count):
        pieces[k][...] = slot_rows(grad, k, count).astype(pieces[k].dtype)
    gains[0:1, :] = jnp.sum(back * unit, axis=0, keepdims=True)
    gains[1:2, :] = gain_two[0:1, :]
    for out, which in ((keep, core), (send, 1 - core)):
        mine = pl.ds(pl.multiple_of(which * half, half), half)
        turned = normed_t[mine, :]
        out[:half, :] = mm(turned, back_q).astype(out.dtype)
        grad_k = mm(turned, back_kv).astype(out.dtype)
        step = half // 4
        for j in range(4):
            out[half : half + step, j * 128 : (j + 1) * 128] = grad_k[j * step : (j + 1) * step]
        at = half + step
        blank = jnp.zeros((experts, half), F32)
        out[at : at + 8, :] = jnp.concatenate([routers[:, mine], blank], axis=1).astype(out.dtype)
        gain = jnp.concatenate([gains[0:1, mine], gains[1:2, mine]], axis=1)
        out[at + 8 : at + 16, :] = jnp.broadcast_to(gain, (8, 2 * half)).astype(out.dtype)
        out[at + 16 :, :] = jnp.zeros((out.shape[0] - at - 16, 2 * half), out.dtype)


def parts_dot(parts, normed_t):
    out = None
    for low in parts:
        value = mm(low, normed_t, 1, 1)
        out = value if out is None else out + value
    return out


def place_of(strides):
    me = lax.axis_index("ctx")
    return [(me // stride) % step for stride, step in strides]


def first_body(layout, rows, stride, step, n_in, *refs):
    ins, outs, total = refs[:n_in], refs[n_in : n_in + step], refs[n_in + step]
    at = 0
    for terms in layout:
        height = terms[0][2]
        value = None
        for index, begin, count in terms:
            part = ins[index][begin : begin + count, :].astype(F32)
            value = part if value is None else value + part
        total[at : at + height, :] = value
        at += height
    if at < total.shape[0]:
        total[at:, :] = jnp.zeros((total.shape[0] - at, total.shape[1]), F32)
    digit = (lax.axis_index("ctx") // stride) % step
    for j in range(step):
        begin = pl.multiple_of((digit ^ j) * rows, 8)
        outs[j][...] = total[pl.ds(begin, rows), :].astype(outs[j].dtype)


def final_body(strides, dest, n_in, *refs):
    ins = refs[:n_in]
    outs, total = refs[n_in:-1], refs[-1]
    me = lax.axis_index("ctx")
    shift = 0
    blocks = 1
    for stride, step in strides:
        shift = shift * step + (me // stride) % step
        blocks *= step
    rows = total.shape[0] // blocks
    per = blocks // n_in
    for i, ref in enumerate(ins):
        for b in range(per):
            begin = pl.multiple_of(((i * per + b) ^ shift) * rows, 8)
            total[pl.ds(begin, rows), :] = ref[b * rows : (b + 1) * rows, :].astype(F32)
    dest(total, outs)


def reduce_rows(args, layout, height, size, dest, outs):
    strides = []
    stride = 1
    for step in factors(size):
        strides.append((stride, step))
        stride *= step
    width = 512
    unit = 8 * size
    height = -(-height // unit) * unit
    rows = height
    terms = None
    for i, (stride, step) in enumerate(strides):
        full, rows = rows, rows // step
        if i > 0:
            args = terms
            layout = [[(index, 0, full) for index in range(len(terms))]]
        pieces = call(
            functools.partial(first_body, layout, rows, stride, step, len(args)),
            [((rows, width), F32)] + [((rows, width), BF)] * (step - 1),
            args,
            scratch=[((full, width), F32)],
        )
        terms = [pieces[0]] + [swap(pieces[j], j * stride, size) for j in range(1, step)]
    done = functools.reduce(lambda a, b: a + b.astype(F32), terms).astype(BF)
    for i, (stride, step) in reversed(list(enumerate(strides))):
        got = [done] + [swap(done, j * stride, size) for j in range(1, step)]
        if i > 0:
            done = jnp.concatenate(got, axis=0)
    return call(
        functools.partial(final_body, strides, dest, len(got)),
        outs,
        got,
        scratch=[((height, width), F32)],
    )


def down_dest(total, outs):
    outs[0][...] = total[: outs[0].shape[0], :]


def up_dest(total, outs):
    up, out = outs
    half = up.shape[0]
    core = lax.axis_index("wsh")
    tiles = up.shape[1] // 512
    for i in range(tiles):
        side, inner = i // (tiles // 2), i % (tiles // 2)
        tile = (core if side == 0 else 1 - core) * (tiles // 2) + inner
        up[:, pl.ds(pl.multiple_of(tile * 512, 512), 512)] = total[i * half : (i + 1) * half, :]
    out[...] = total[tiles * half : tiles * half + out.shape[0], :]


def late_dest(total, outs):
    query, kv, router, gains = outs
    half = query.shape[0]
    step = half // 4
    query[...] = total[:half, :]
    for j in range(4):
        kv[j * step : (j + 1) * step, :] = total[half : half + step, j * 128 : (j + 1) * 128]
    at = half + step
    experts = router.shape[1]
    block = jnp.concatenate([total[at : at + 8, :half], jnp.zeros((120, half), F32)], axis=0)
    router[...] = block.T[:, :experts]
    gains[0:1, :] = total[at + 8 : at + 9, :half]
    gains[1:2, :] = total[at + 8 : at + 9, half:]


def place_body(rest, *refs):
    place = lax.axis_index("ctx") // rest
    for k, ref in enumerate(refs[:-1]):
        refs[-1][place ^ k] = ref[...].astype(F32)


def on_device(
    tokens,
    routes,
    block_order,
    norm_gain1,
    router_w,
    query_w,
    kv_w,
    out_w,
    norm_gain2,
    up_w,
    down_w,
    cotangent,
):
    size = lax.axis_size("ctx")
    count, local, dim = tokens.shape
    rest = size // count
    place = lax.axis_index("ctx") // rest
    total = count * local
    experts = router_w.shape[1]
    head = kv_w.shape[1] // 2
    feed = up_w.shape[1]

    def away(parts):
        return [swap(pick(parts, place ^ k), k * rest, size) for k in range(1, count)]

    tok_x = away(tokens)
    routes_all = jnp.pad(routes.transpose(0, 2, 1), ((0, 0), (0, 6), (0, 0)))
    routes_x = away(routes_all)
    gains = jnp.stack([norm_gain1, norm_gain2])
    gains_x = trade(gains)
    g1, g2 = gains[0:1], gains[1:2]
    g1x, g2x = gains_x[0:1], gains_x[1:2]
    query_x, kv_x, router_x = trade(query_w), trade(kv_w), trade(router_w)
    cot_x = away(cotangent)
    out_x, up_x, down_x = trade(out_w), trade(up_w), trade(down_w)

    kv, qt, normed_t, gates, route = call(
        functools.partial(project_body, count, rest, experts, head),
        [
            ((total, 2 * head), BF),
            ((TWO * head, total), BF),
            ((dim, total), BF),
            ((TWO, total), F32),
            ((8, total), I32),
        ],
        [tokens, *tok_x, routes_all, *routes_x, g1, g1x, query_w, query_x, kv_w, kv_x, router_w, router_x],
        scratch=[((dim, experts * head), BF), ((dim, 2 * head), BF), ((dim, 128), F32)],
        flops=2 * total * dim * (experts * head + 256),
    )

    steps = factors(rest)
    stride = 1
    have = kv
    for i, step in enumerate(steps):
        kv_pieces = [have] + [swap(have, j * stride, size) for j in range(1, step)]
        stride *= step
        if i + 1 < len(steps):
            have = jnp.concatenate(kv_pieces, axis=0)
    span = rest * total
    att, logs, mixed, hidden, two, two_t = call(
        functools.partial(attend_body, count, rest, experts, head, len(kv_pieces)),
        [
            ((TWO * head, total), F32),
            ((TWO, total), F32),
            ((experts * head, total), BF),
            ((total, dim), F32),
            ((total, dim), BF),
            ((dim, total), BF),
        ],
        [block_order, *kv_pieces, qt, gates, route, tokens, *tok_x, g2, g2x, out_w, out_x],
        scratch=[((span, 2 * head), BF), ((2 * head, span), BF), ((experts * head, dim), BF)],
        smem=(0,),
        flops=8 * total * span * head,
    )

    tile = 256
    wide = feed // 2
    tall = dim // 2
    upper = wide * tall // dim
    flops = 12 * total * dim * wide
    feed_scratch = [((dim, wide), BF), ((total, dim), BF)]
    layer, back_two, send_one, keep_one = call(
        functools.partial(feed_body, count, rest, True, tile),
        [
            ((total, dim), F32),
            ((total, dim), F32),
            ((wide + upper, dim), BF),
            ((upper, dim), BF),
        ],
        [two, two_t, cotangent, *cot_x, up_w, up_x, down_x, hidden],
        scratch=feed_scratch,
        flops=flops,
    )
    recv_one = trade(send_one)
    *layer_pieces, back_two, keep_down, keep_two, send_two = call(
        functools.partial(feed_body, count, rest, False, tile),
        [((local, dim), F32)]
        + [((local, dim), BF)] * (count - 1)
        + [
            ((total, dim), F32),
            ((wide, dim), BF),
            ((upper, dim), BF),
            ((upper, dim), BF),
        ],
        [two, two_t, cotangent, *cot_x, up_w, up_x, down_w, layer, back_two],
        scratch=feed_scratch + [((total, dim), F32)],
        flops=flops,
    )
    recv_two = trade(send_two)
    (grad_down,) = reduce_rows(
        [keep_down, recv_one],
        [[(0, 0, wide), (1, 0, wide)]],
        wide,
        size,
        down_dest,
        [((wide, dim), F32)],
    )
    layer_got = layer_pieces[:1] + [swap(layer_pieces[k], k * rest, size) for k in range(1, count)]
    (layer_out,) = call(
        functools.partial(place_body, rest), [((count, local, dim), F32)], layer_got
    )

    back_hidden, keep_out, send_out, grad_att, delta, logit, gain_two = call(
        functools.partial(turn_body, count, rest, experts, head),
        [
            ((total, dim), F32),
            ((tall, dim), BF),
            ((tall, dim), BF),
            ((TWO * head, total), BF),
            ((TWO, total), F32),
            ((experts, total), F32),
            ((8, dim), F32),
        ],
        [hidden, back_two, cotangent, *cot_x, mixed, out_w, out_x, g2, g2x, gates, route, att],
        scratch=[((experts * head, dim), BF)],
        flops=6 * total * dim * dim,
    )
    recv_out = trade(send_out)
    grad_up, grad_out = reduce_rows(
        [keep_two, recv_one, keep_one, recv_two, keep_out, recv_out],
        [
            [(0, 0, upper), (1, wide, upper)],
            [(2, 0, upper), (3, 0, upper)],
            [(4, 0, tall), (5, 0, tall)],
        ],
        2 * upper + tall,
        size,
        up_dest,
        [((tall, feed), F32), ((tall, dim), F32)],
    )

    split = steps[-1]
    share = span // split
    grad_q, *kv_terms = call(
        functools.partial(attend_back_body, count, rest, head, len(kv_pieces), split),
        [((TWO * head, total), BF), ((share, 2 * head), F32)] + [((share, 2 * head), BF)] * (split - 1),
        [block_order, *kv_pieces, qt, grad_att, logs, delta],
        scratch=[
            ((span, 2 * head), BF),
            ((2 * head, span), BF),
            ((2 * TWO, 2 * head, total), BF),
            ((2 * TWO, total, 2 * head), BF),
            ((span, 2 * head), F32),
            ((TWO * head, total), F32),
        ],
        smem=(0,),
        flops=20 * total * span * head,
    )
    stride = rest
    for i, step in reversed(list(enumerate(steps))):
        stride //= step
        if i + 1 < len(steps):
            summed = functools.reduce(lambda a, b: a + b.astype(F32), terms)
            kv_terms = jnp.split(summed, step, axis=0)
        terms = [kv_terms[0]] + [
            swap(kv_terms[j].astype(BF), j * stride, size) for j in range(1, step)
        ]

    height = -(-(tall + tall // 4 + 16) // (8 * size)) * 8 * size
    *input_pieces, keep_late, send_late = call(
        functools.partial(unproject_body, count, rest, experts, head, len(terms)),
        [((local, dim), F32)]
        + [((local, dim), BF)] * (count - 1)
        + [((height, dim), F32), ((height, dim), BF)],
        [
            *terms,
            grad_q,
            normed_t,
            route,
            logit,
            tokens,
            *tok_x,
            back_hidden,
            query_w,
            query_x,
            kv_w,
            kv_x,
            router_w,
            router_x,
            g1,
            g1x,
            gain_two,
        ],
        scratch=[
            ((dim, experts * head), BF),
            ((dim, 2 * head), BF),
            ((dim, 128), F32),
            ((experts * head, total), BF),
            ((8, dim), F32),
            ((8, dim), F32),
        ],
        flops=8 * total * dim * dim,
    )
    recv_late = trade(send_late)
    grad_query, grad_kv, grad_router, grad_gains = reduce_rows(
        [keep_late, recv_late],
        [[(0, 0, height), (1, 0, height)]],
        height,
        size,
        late_dest,
        [((tall, experts * head), F32), ((tall, 2 * head), F32), ((tall, experts), F32), ((2, tall), F32)],
    )
    input_got = input_pieces[:1] + [swap(input_pieces[k], k * rest, size) for k in range(1, count)]
    (input_grad,) = call(
        functools.partial(place_body, rest), [((count, local, dim), F32)], input_got
    )
    return (
        layer_out,
        input_grad,
        grad_gains[0],
        grad_router,
        grad_query,
        grad_kv,
        grad_out,
        grad_gains[1],
        grad_up,
        grad_down,
    )


def solution(mesh):
    placed = (
        P("wsh", "ctx", None),
        P("wsh", "ctx", None),
        P(),
        P("wsh"),
        P("wsh", None),
        P("wsh", None),
        P("wsh", None),
        P("wsh", None),
        P("wsh"),
        P("wsh", None),
        P("wsh", None),
        P("wsh", "ctx", None),
    )
    return jax.shard_map(
        on_device,
        mesh=mesh,
        in_specs=placed,
        out_specs=(
            P("wsh", "ctx", None),
            P("wsh", "ctx", None),
            P("wsh"),
            P("wsh", None),
            P("wsh", None),
            P("wsh", None),
            P("wsh", None),
            P("wsh"),
            P("wsh", None),
            P("wsh", None),
        ),
        check_vma=False,
    )
```

```python
import functools
import math

import jax
import jax.numpy as jnp
from jax import lax
from jax.experimental import pallas as pl
from jax.experimental.pallas import tpu as pltpu
from jax.sharding import PartitionSpec as P

BF = jnp.bfloat16
F32 = jnp.float32
I32 = jnp.int32
NONE = -1e30
TWO = 2


def factors(size):
    out = []
    while size > 1:
        step = 4 if size % 4 == 0 else 2
        out.append(step)
        size //= step
    return out


def swap(values, mask, size):
    return lax.ppermute(values, "ctx", [(i, i ^ mask) for i in range(size)])


def groups_of(stride, step, size):
    out = []
    for i in range(size):
        if (i // stride) % step == 0:
            out.append([i + j * stride for j in range(step)])
    return out


def exchange(parts, stride, size):
    step = parts.shape[0]
    groups = groups_of(stride, step, size)
    return lax.all_to_all(parts, "ctx", 0, 0, tiled=True, axis_index_groups=groups)


def trade(values):
    return lax.ppermute(values, "wsh", [(0, 1), (1, 0)])


def pick(parts, index):
    return lax.dynamic_index_in_dim(parts, index, 0, False)


def mm(a, b, left=1, right=0):
    return lax.dot_general(a, b, (((left,), (right,)), ((), ())), preferred_element_type=F32)


class Order:
    last = None
    rest = None
    leave = None


def after(value, *earlier):
    return lax.optimization_barrier((value, *earlier))[0]


class Far:
    def __init__(self, value):
        self.value = value


class Ahead:
    def __init__(self, value, shape=None, view=None):
        self.value, self.view = value, view
        self.shape = value.shape if shape is None else shape


def loading_body(body, plan, n_out, far_out, late, views, n_scratch, *refs):
    n_in, n_pre = len(plan), len(views)
    ins, pre_in = list(refs[:n_in]), refs[n_in : n_in + n_pre]
    at = n_in + n_pre
    outs, pre_out = list(refs[at : at + n_out]), refs[at + n_out : at + n_out + n_pre]
    at += n_out + n_pre
    own = refs[at : at + n_scratch]
    held, sems = refs[at + n_scratch : -1], refs[-1]
    first, second, ahead, slot = [], [], [], 0
    for i in range(n_in):
        if plan[i]:
            copy = pltpu.make_async_copy(ins[i], held[slot], sems.at[slot])
            (second if i in late else first).append(copy)
            ins[i] = held[slot]
            slot += 1
    leaving = {}
    for i in range(n_out):
        if far_out[i]:
            leaving[i] = pltpu.make_async_copy(held[slot], outs[i], sems.at[slot])
            outs[i] = held[slot]
            slot += 1
    for view, source, target in zip(views, pre_in, pre_out):
        source = source if view is None else view(source)
        ahead.append(pltpu.make_async_copy(source, target, sems.at[slot]))
        slot += 1
    for copy in first + second + ahead:
        copy.start()
    for copy in first:
        copy.wait()

    def rest():
        for copy in second:
            copy.wait()

    gone = []

    def leave(*which):
        for i in which:
            if far_out[i]:
                gone.append(i)
                leaving[i].start()

    Order.rest, Order.leave = rest, leave
    body(*ins, *outs, *own)
    leave(*[i for i in range(n_out) if i not in gone])
    for i in gone:
        leaving[i].wait()
    for copy in ahead:
        copy.wait()


def call(body, outs, args, scratch=(), smem=(), late=(), ahead=(), mib=14):
    whole = pl.BlockSpec(memory_space=pltpu.VMEM)
    scalars = pl.BlockSpec(memory_space=pltpu.SMEM)
    distant = pl.BlockSpec(memory_space=pltpu.HBM)
    plan = [isinstance(a, Far) for a in args]
    args = [
        pltpu.with_memory_space_constraint(a.value, pltpu.HBM) if isinstance(a, Far) else a
        for a in args
    ]
    far_out = [len(o) > 2 for o in outs]
    if Order.last is not None:
        args[0] = after(args[0], Order.last)
    held = [(a.shape, a.dtype) for a, far in zip(args, plan) if far]
    held += [o[:2] for o, far in zip(outs, far_out) if far]
    need = sum(math.prod(s) * jnp.dtype(d).itemsize for s, d in [*held, *scratch])
    run = pl.pallas_call(
        functools.partial(
            loading_body,
            body,
            plan,
            len(outs),
            far_out,
            late,
            [a.view for a in ahead],
            len(scratch),
        ),
        out_shape=[
            pltpu.HBM(o[0], o[1]) if far else jax.ShapeDtypeStruct(o[0], o[1])
            for o, far in zip(outs, far_out)
        ]
        + [jax.ShapeDtypeStruct(a.shape, a.value.dtype) for a in ahead],
        in_specs=[
            scalars if i in smem else distant if plan[i] else whole for i in range(len(args))
        ]
        + [distant] * len(ahead),
        out_specs=[distant if far else whole for far in far_out] + [whole] * len(ahead),
        scratch_shapes=[pltpu.VMEM(s, d) for s, d in [*scratch, *held]]
        + [pltpu.SemaphoreType.DMA((max(len(held) + len(ahead), 1),))],
        compiler_params=pltpu.CompilerParams(vmem_limit_bytes=(mib << 20) + need),
        cost_estimate=pl.CostEstimate(flops=1, bytes_accessed=1, transcendentals=0),
    )
    moved = [pltpu.with_memory_space_constraint(a.value, pltpu.HBM) for a in ahead]
    got = list(run(*args, *moved))
    Order.last = got[0]
    return got


def far(values):
    return [Far(v) for v in values]


def join(slots):
    half = slots[0].shape[0] // 2
    return jnp.concatenate([s[:half] for s in slots] + [s[half:] for s in slots], axis=0)


def slot_rows(rows, k, count):
    half = rows.shape[0] // (2 * count)
    low = k * half
    high = rows.shape[0] // 2 + k * half
    return jnp.concatenate([rows[low : low + half], rows[high : high + half]], axis=0)


def centred(rows):
    centre = rows - jnp.mean(rows, axis=-1, keepdims=True)
    scale = lax.rsqrt(jnp.mean(centre * centre, axis=-1, keepdims=True) + 1e-05)
    return centre * scale, scale


def fill(scratch, own, other, core):
    half = own.shape[0]
    scratch[pl.ds(pl.multiple_of(core * half, half), half), :] = own[...]
    scratch[pl.ds(pl.multiple_of((1 - core) * half, half), half), :] = other[...]


def pick_gain(own, other, which, core):
    a = own[which : which + 1, :].astype(F32)
    b = other[which : which + 1, :].astype(F32)
    first = jnp.where(core == 0, a, b)
    second = jnp.where(core == 0, b, a)
    return jnp.concatenate([first, second], axis=1)


def route_rows(pieces):
    lane = lax.broadcasted_iota(I32, (8, 128), 1)
    low = lane < 64
    rolled = [pltpu.roll(p, 64, 1) for p in pieces]
    count = len(pieces)
    front = [jnp.where(low, pieces[i], rolled[i + 1]) for i in range(0, count, 2)]
    back = [jnp.where(low, rolled[i], pieces[i + 1]) for i in range(0, count, 2)]
    return jnp.concatenate(front + back, axis=1)


def pack_body(count, rest, *refs):
    tok, routes = refs[:2]
    place = lax.axis_index("ctx") // rest
    local, dim = tok.shape[1:]
    for k, out in enumerate(refs[2:]):
        out[:local, :] = tok[place ^ (k + 1)]
        out[local:, :] = jnp.zeros((8, dim), BF)
        out[local : local + TWO, :128] = routes[place ^ (k + 1)].astype(F32).astype(BF)


def pack_weights_body(query, kv, router, packed):
    half, cols = query.shape
    packed[half:, :] = jnp.zeros((8, packed.shape[1]), BF)
    packed[:half, :cols] = query[...]
    packed[:half, cols:] = kv[...]
    packed[half:, :half] = router[...]


def fill_router(wr, own, packed, core):
    half = own.shape[1]
    wr[...] = jnp.zeros_like(wr)
    experts = own.shape[0]
    mine = pl.ds(pl.multiple_of(core * half, half), half)
    theirs = pl.ds(pl.multiple_of((1 - core) * half, half), half)
    wr[:experts, mine] = own[...].astype(F32)
    wr[:experts, theirs] = packed[half:, :half].astype(F32)


def keys_body(count, rest, *refs):
    toks = refs[:count]
    routes, g_own, g_other, k_own, packed = refs[count : count + 5]
    kv_out, normed_out, tok_out, gain_out, wk, tail_out = refs[count + 5 :]
    core = lax.axis_index("wsh")
    place = lax.axis_index("ctx") // rest
    half = k_own.shape[0]
    local = toks[0].shape[0]
    keys = k_own.shape[1]
    fill(wk, k_own, packed.at[:half, packed.shape[1] - keys :], core)
    rows = join([t[:local] for t in toks])
    tok_out[...] = rows
    Order.leave(2, 4)
    tail_out[...] = jnp.zeros_like(tail_out)
    tail_out[:TWO, :] = routes[place].astype(F32)
    for k in range(1, count):
        tail_out[8 * k : 8 * k + 8, :] = toks[k][local : local + 8, :128].astype(F32)
    rows = rows.astype(F32)
    unit, _ = centred(rows)
    gain_out[...] = jnp.zeros_like(gain_out)
    for which in range(TWO):
        gain_out[which : which + 1, :] = pick_gain(g_own, g_other, which, core)
    normed = (unit * gain_out[0:1, :]).astype(BF)
    normed_out[...] = normed
    kv = mm(normed, wk[...]).astype(BF)
    for i in range(kv_out.shape[0]):
        kv_out[i] = kv


def project_body(count, experts, head, *refs):
    normed_ref, tails, q_own, r_own, packed = refs[:5]
    qt_out, qt_far, nt_out, gate_out, gate_far, route_out, route_far, wq, wr = refs[5:]
    core = lax.axis_index("wsh")
    half, cols = q_own.shape
    fill(wq, q_own, packed.at[:half, :cols], core)
    fill_router(wr, r_own, packed, core)
    normed = normed_ref[...]
    nt_out[...] = normed.T
    Order.leave(2, 7, 8)
    routes = route_rows([tails[8 * k : 8 * k + 8, :] for k in range(count)])
    route_out[...] = routes
    route_far[...] = routes
    logits = mm(wr[...].astype(BF), normed, 1, 1)
    queries = (mm(normed, wq[...]) * 0.125).T
    chosen = []
    for s in range(TWO):
        route = routes[s : s + 1]
        total = jnp.zeros((head, normed.shape[0]), F32)
        value = jnp.zeros((1, normed.shape[0]), F32)
        for e in range(experts):
            here = route == e
            total = jnp.where(here, queries[e * head : (e + 1) * head], total)
            value = jnp.where(here, logits[e : e + 1], value)
        qt_out[s * head : (s + 1) * head, :] = total.astype(BF)
        chosen.append(value)
    qt_far[...] = qt_out[...]
    top = jnp.maximum(chosen[0], chosen[1])
    raised = [jnp.exp(c - top) for c in chosen]
    total = raised[0] + raised[1]
    gate_out[...] = jnp.concatenate([r / total for r in raised], axis=0)
    gate_far[...] = gate_out[...]


def places(order, count, rest, block, width, part):
    me = lax.axis_index("ctx")
    place, other = me // rest, me % rest
    size = count * rest
    lane = lax.broadcasted_iota(I32, (1, width), 1)
    out = jnp.zeros((1, width), I32)
    for k in range(count):
        first = order[(place ^ k) * rest + other]
        base = jnp.where(part == 0, first, 2 * size - 1 - first) * block
        out = jnp.where(lane // block == k, lane - k * block + base, out)
    return out


def key_bases(order, count, rest, block, chunk, part):
    me = lax.axis_index("ctx")
    place = me // rest
    size = count * rest
    out = []
    for k in range(count):
        first = order[(place ^ k) * rest + chunk]
        out.append((first if part == 0 else 2 * size - 1 - first) * block)
    return out


def masked(scores, gap, bases, block):
    parts = [
        jnp.where(gap <= -base, scores[k * block : (k + 1) * block], NONE)
        for k, base in enumerate(bases)
    ]
    return jnp.concatenate(parts, axis=0)


def scored(kv, side, h, gap, order, count, rest, block, chunk, half):
    first = mm(kv[:half], side)
    if h == 0:
        return masked(first, gap, key_bases(order, count, rest, block, chunk, 0), block)
    second = mm(kv[half:], side)
    second = masked(second, gap, key_bases(order, count, rest, block, chunk, 1), block)
    return jnp.concatenate([first, second], axis=0)


def turn_keys(kv, kv_turned):
    rows = kv.shape[1]
    for c in range(kv.shape[0]):
        kv_turned[:, c * rows : (c + 1) * rows] = kv[c].T


def attend_body(count, rest, experts, head, *refs):
    order, kv_ref, qt, gates, routes = refs[:5]
    tok, gains, o_own, o_other = refs[5:9]
    att_out, log_out, mixed_out, hidden_out, two_out, turned_out, kv_out, wo_out, kv_turned = refs[9:]
    kv_out[...] = kv_ref[...]
    Order.leave(6)
    core = lax.axis_index("wsh")
    other = lax.axis_index("ctx") % rest
    total = qt.shape[1]
    half = total // 2
    block = half // count
    turn_keys(kv_ref, kv_turned)
    for h in range(2):
        gap = lax.broadcasted_iota(I32, (block, half), 0) - places(order, count, rest, block, half, h)
        for s in range(TWO):
            side = qt[s * head : (s + 1) * head, h * half : (h + 1) * half]
            side = jnp.concatenate([side, jnp.zeros_like(side)], axis=0)
            reach = half * (h + 1)

            def step(turn, carry, side=side, h=h, gap=gap, reach=reach):
                top, norm, summed = carry
                chunk = turn ^ other
                at = pl.multiple_of(chunk * total, total)
                kv = kv_ref[chunk]
                scores = scored(kv, side, h, gap, order, count, rest, block, chunk, half)
                fresh = jnp.maximum(top, jnp.max(scores, axis=0, keepdims=True))
                shares = jnp.exp(scores - fresh)
                fade = jnp.exp(top - fresh)
                norm = norm * fade + jnp.sum(shares, axis=0, keepdims=True)
                values = kv_turned[head:, pl.ds(at, reach)]
                summed = summed * fade + mm(values, shares.astype(BF))
                return fresh, norm, summed

            start = (
                jnp.full((1, half), NONE, F32),
                jnp.zeros((1, half), F32),
                jnp.zeros((head, half), F32),
            )
            top, norm, summed = lax.fori_loop(0, rest, step, start, unroll=rest <= 4)
            log_out[s : s + 1, h * half : (h + 1) * half] = top + jnp.log(norm)
            att_out[s * head : (s + 1) * head, h * half : (h + 1) * half] = summed / norm
    Order.rest()
    fill(wo_out, o_own, o_other, core)
    Order.leave(0, 1, 7)
    for e in range(experts):
        part = jnp.zeros((head, total), F32)
        for s in range(TWO):
            gate = jnp.where(routes[s : s + 1] == e, gates[s : s + 1], 0.0)
            part = part + gate * att_out[s * head : (s + 1) * head, :]
        mixed_out[e * head : (e + 1) * head, :] = part.astype(BF)
    Order.leave(2)
    hidden = tok[...].astype(F32) + mm(mixed_out[...].T, wo_out[...])
    hidden_out[...] = hidden
    unit, _ = centred(hidden)
    two = (unit * gains[1:2, :]).astype(BF)
    two_out[...] = two
    turned_out[...] = two.T


def feed_body(count, rest, first, tile, *refs):
    two, turned = refs[:2]
    if first:
        slots = refs[2 : 2 + count]
        u_own, u_other, down, layer_in = refs[2 + count : 6 + count]
        layer_out, back_out, send, keep, cots, cot_far, send_up, up = refs[6 + count :]
    else:
        cots, u_own, u_other, down, layer_in, back_in = refs[2:8]
        outs = refs[8 : 12 + count]
        layer_pieces, back_out, keep_down, keep, send = outs[:count], *outs[count:]
        up, layer_out = refs[12 + count :]
    core = lax.axis_index("wsh")
    side = (1 - core) if first else core
    width = down.shape[0]
    half = u_own.shape[0]
    lanes = pl.ds(pl.multiple_of(side * width, width), width)
    up[pl.ds(pl.multiple_of(core * half, half), half), :] = u_own[...]
    up[pl.ds(pl.multiple_of((1 - core) * half, half), half), :] = u_other[:, lanes]
    if first:
        cots[...] = join([o[...] for o in slots])
        cot_far[...] = cots[...]
        Order.leave(5)
    layer_out[...] = layer_in[...]
    if first:
        back_out[...] = jnp.zeros_like(back_out)
    else:
        back_out[...] = back_in[...]
    mine = pl.ds(pl.multiple_of(core * half, half), half)
    theirs = pl.ds(pl.multiple_of((1 - core) * half, half), half)
    dim = up.shape[0]
    per = dim // tile

    def step(j, carry):
        cols = pl.ds(pl.multiple_of(j * tile, tile), tile)
        up_j = up[:, cols]
        down_j = down[cols, :]
        pre = mm(two[...], up_j)
        back = mm(cots[...], down_j, 1, 1)
        phi = 0.5 * (1.0 + lax.erf(pre * math.sqrt(0.5)))
        bell = jnp.exp(pre * pre * -0.5) * (1.0 / math.sqrt(2.0 * math.pi))
        act = (pre * phi).astype(BF)
        back_pre = (back * (phi + pre * bell)).astype(BF)
        layer_out[...] += mm(act, down_j)
        back_out[...] += mm(back_pre, up_j, 1, 1)
        grad = mm(act.T, cots[...]).astype(BF)
        grad_mine = mm(turned[mine, :], back_pre).astype(BF)
        grad_theirs = mm(turned[theirs, :], back_pre).astype(BF)
        rows = pl.ds(pl.multiple_of((j // per) * half, half), half)
        lane = pl.ds(pl.multiple_of((j % per) * tile, tile), tile)
        keep[rows, lane] = grad_mine
        if first:
            send[cols, :] = grad
            send_up[rows, lane] = grad_theirs
        else:
            keep_down[cols, :] = grad
            send[rows, lane] = grad_theirs
        return carry

    lax.fori_loop(0, width // tile, step, 0)
    if not first:
        for k in range(count):
            layer_pieces[k][...] = slot_rows(layer_out[...], k, count).astype(layer_pieces[k].dtype)


def turn_body(count, rest, experts, head, *refs):
    hidden, back_two, cot, wo, gain, gates, routes, att = refs[:8]
    back_hidden_out, branch_out, grad_att_out, delta_out, logit_out, gain_out = refs[8:]
    unit, scale = centred(hidden[...])
    back = back_two[...]
    side = back * gain[1:2, :]
    part = scale * (
        side
        - jnp.mean(side, axis=-1, keepdims=True)
        - unit * jnp.mean(side * unit, axis=-1, keepdims=True)
    )
    gain_out[...] = jnp.broadcast_to(jnp.sum(back * unit, axis=0, keepdims=True), gain_out.shape)
    back_hidden = cot[...].astype(F32) + part
    back_hidden_out[...] = back_hidden
    branch = back_hidden.astype(BF)
    branch_out[...] = branch
    Order.leave(0, 1, 5)
    back_mixed = mm(wo[...], branch, 1, 1)
    grads = []
    for s in range(TWO):
        total = jnp.zeros((head, branch.shape[0]), F32)
        for e in range(experts):
            total = jnp.where(routes[s : s + 1] == e, back_mixed[e * head : (e + 1) * head], total)
        att_s = att[s * head : (s + 1) * head, :]
        grads.append(jnp.sum(total * att_s, axis=0, keepdims=True))
        low = (gates[s : s + 1] * total).astype(BF)
        grad_att_out[s * head : (s + 1) * head, :] = low
        delta_out[s : s + 1, :] = jnp.sum(low.astype(F32) * att_s, axis=0, keepdims=True)
    mean = gates[0:1] * grads[0] + gates[1:2] * grads[1]
    row = lax.broadcasted_iota(I32, logit_out.shape, 0)
    logit = jnp.zeros(logit_out.shape, F32)
    for s in range(TWO):
        value = gates[s : s + 1] * (grads[s] - mean)
        logit = logit + jnp.where(row.astype(F32) == routes[s : s + 1], value, 0.0)
    logit_out[...] = logit


def attend_back_body(count, rest, head, split, *refs):
    order, kv_ref, qt, grad_att, logs, delta, grad_q_out = refs[:7]
    outs = refs[7 : 7 + split]
    kv_turned, sides, turned, grad_kv, grad_q = refs[7 + split :]
    total = qt.shape[1]
    half = total // 2
    block = half // count
    turn_keys(kv_ref, kv_turned)
    blank = jnp.zeros((head, total), BF)
    for s in range(TWO):
        q_side = jnp.concatenate([qt[s * head : (s + 1) * head, :], blank], axis=0)
        g_side = jnp.concatenate([blank, grad_att[s * head : (s + 1) * head, :]], axis=0)
        sides[2 * s], sides[2 * s + 1] = q_side, g_side
        turned[2 * s], turned[2 * s + 1] = q_side.T, g_side.T
    grad_q[...] = jnp.zeros_like(grad_q)
    gaps = [
        lax.broadcasted_iota(I32, (block, half), 0) - places(order, count, rest, block, half, h)
        for h in range(2)
    ]

    def step(chunk, carry):
        at = pl.multiple_of(chunk * total, total)
        kv = kv_ref[chunk]
        front = jnp.zeros((half, 2 * head), F32)
        back = jnp.zeros((half, 2 * head), F32)
        for h in range(2):
            cols = slice(h * half, (h + 1) * half)
            reach = half * (h + 1)
            for s in range(TWO):
                scores = scored(
                    kv, sides[2 * s, :, cols], h, gaps[h], order, count, rest, block, chunk, half
                )
                shares = jnp.exp(scores - logs[s : s + 1, cols])
                back_shares = mm(kv[:reach], sides[2 * s + 1, :, cols])
                back_scores = (shares * (back_shares - delta[s : s + 1, cols])).astype(BF)
                grad = mm(back_scores, turned[2 * s, cols, :]) + mm(
                    shares.astype(BF), turned[2 * s + 1, cols, :]
                )
                front = front + grad[:half]
                if h == 1:
                    back = back + grad[half:]
                rows = slice(s * head, (s + 1) * head)
                grad_q[rows, cols] += mm(kv_turned[:head, pl.ds(at, reach)], back_scores)
        grad_kv[pl.ds(at, half), :] = front
        grad_kv[pl.ds(at + half, half), :] = back
        return carry

    lax.fori_loop(0, rest, step, 0)
    grad_q_out[...] = grad_q[...].astype(BF)
    rows = outs[0].shape[0]
    digit = (lax.axis_index("ctx") % rest) // (rest // split)
    for i, out in enumerate(outs):
        begin = pl.multiple_of((digit ^ i) * rows, rows)
        out[...] = grad_kv[pl.ds(begin, rows), :].astype(out.dtype)


def query_body(experts, head, *refs):
    grad_q, normed_t, routes, mixed, branch, wq, wr, logit, tok = refs[:9]
    keep_out, keep, send, back_out, unit_out, scale_out, routers, bqt = refs[9:]
    core = lax.axis_index("wsh")
    total = grad_q.shape[1]
    for e in range(experts):
        part = jnp.zeros((head, total), F32)
        for s in range(TWO):
            value = grad_q[s * head : (s + 1) * head, :].astype(F32) * 0.125
            part = jnp.where(routes[s : s + 1] == e, value, part)
        bqt[e * head : (e + 1) * head, :] = part.astype(BF)
    back_q = bqt[...].T
    half = keep.shape[0]
    mine = pl.ds(pl.multiple_of(core * half, half), half)
    theirs = pl.ds(pl.multiple_of((1 - core) * half, half), half)
    send[:half, :] = mm(mixed[theirs, :], branch[...]).astype(BF)
    send[half:, :] = mm(normed_t[theirs, :], back_q).astype(BF)
    keep_out[...] = mm(mixed[mine, :], branch[...]).astype(BF)
    keep[...] = mm(normed_t[mine, :], back_q).astype(BF)
    parts = []
    left = logit[...]
    for _ in range(3):
        low = left.astype(BF)
        parts.append(low)
        left = left - low.astype(F32)
    routers[...] = parts_dot(parts, normed_t[...])
    back = mm(back_q, wq[...], 1, 1)
    wr_turned = wr[...].astype(BF)
    for low in parts:
        padded = jnp.concatenate([low.astype(F32), jnp.zeros((120, total), F32)], axis=0)
        back = back + mm(padded.T.astype(BF), wr_turned)
    back_out[...] = back
    unit, scale = centred(tok[...].astype(F32))
    unit_out[...] = unit
    scale_out[...] = jnp.broadcast_to(scale, scale_out.shape)


def unproject_body(count, terms, *refs):
    kv_terms = refs[:terms]
    back_part, unit_ref, scale_ref, routers, normed_t, back_hidden, wk, gain, gain_two, sent = refs[
        terms : terms + 10
    ]
    at = terms + 10
    pieces = refs[at : at + count]
    keep, send, gains = refs[at + count :]
    core = lax.axis_index("wsh")
    half = back_part.shape[1] // 2
    back_kv = kv_terms[0][...].astype(F32)
    for term in kv_terms[1:]:
        back_kv = back_kv + term[...].astype(F32)
    back_kv = back_kv.astype(BF)
    back = back_part[...] + mm(back_kv, wk[...], 1, 1)
    unit, scale = unit_ref[...], scale_ref[:, 0:1]
    side = back * gain[0:1, :]
    grad = back_hidden[...] + scale * (
        side
        - jnp.mean(side, axis=-1, keepdims=True)
        - unit * jnp.mean(side * unit, axis=-1, keepdims=True)
    )
    gains[0:1, :] = jnp.sum(back * unit, axis=0, keepdims=True)
    gains[1:2, :] = gain_two[0:1, :]
    step = half // 4
    experts = routers.shape[0]
    high = sent.shape[0]
    send[:high, :] = sent[...]
    for out, which in ((keep, core), (send.at[high:, :], 1 - core)):
        mine = pl.ds(pl.multiple_of(which * half, half), half)
        grad_k = mm(normed_t[mine, :], back_kv).astype(out.dtype)
        for j in range(4):
            out[:step, j * 128 : (j + 1) * 128] = grad_k[j * step : (j + 1) * step]
        blank = jnp.zeros((experts, half), F32)
        out[step : step + 8, :] = jnp.concatenate([routers[:, mine], blank], axis=1).astype(out.dtype)
        gain_pair = jnp.concatenate([gains[0:1, mine], gains[1:2, mine]], axis=1)
        out[step + 8 :, :] = jnp.broadcast_to(gain_pair, (8, 2 * half)).astype(out.dtype)
    for k in range(count):
        pieces[k][...] = slot_rows(grad, k, count).astype(pieces[k].dtype)


def parts_dot(parts, normed_t):
    out = None
    for low in parts:
        value = mm(low, normed_t, 1, 1)
        out = value if out is None else out + value
    return out


def sum_layout(layout, ins, total):
    at = 0
    for terms in layout:
        height = terms[0][2]
        value = None
        for index, begin, count in terms:
            part = ins[index][begin : begin + count, :].astype(F32)
            value = part if value is None else value + part
        total[at : at + height, :] = value
        at += height
    if at < total.shape[0]:
        total[at:, :] = jnp.zeros((total.shape[0] - at, total.shape[1]), F32)


def cut_rows(total, outs, stride, step):
    rows = outs[0].shape[0]
    digit = (lax.axis_index("ctx") // stride) % step
    for j in range(step):
        begin = pl.multiple_of((digit ^ j) * rows, 8)
        outs[j][...] = total[pl.ds(begin, rows), :].astype(outs[j].dtype)


def start_body(layout, whole, stride, step, n_in, *refs):
    ins, outs, total = refs[:n_in], refs[n_in:-1], refs[-1]
    sum_layout(layout, ins, total)
    if whole:
        rows = total.shape[0] // step
        for j in range(step):
            outs[0][j] = total[j * rows : (j + 1) * rows, :].astype(BF)
    else:
        cut_rows(total, outs, stride, step)


def terms_of(ref):
    return [ref.at[j] for j in range(ref.shape[0])] if len(ref.shape) == 3 else [ref]


def middle_body(chunks, stride, step, n_in, riders, *refs):
    ins, riding = refs[:n_in], refs[n_in : n_in + riders]
    refs = refs[n_in + riders :]
    outs, totals = refs[:step], refs[step:]
    digit = (lax.axis_index("ctx") // stride) % step
    at, low = 0, 0
    for count, total in zip(chunks, totals):
        value = None
        for ref in ins[at : at + count]:
            for term in terms_of(ref):
                part = term[...].astype(F32)
                value = part if value is None else value + part
        total[...] = value
        rows = total.shape[0] // step
        for j in range(step):
            begin = pl.multiple_of((digit ^ j) * rows, 8)
            outs[j][low : low + rows, :] = total[pl.ds(begin, rows), :].astype(outs[j].dtype)
        low += rows
        at += count
    for j in range(1, step if riders else 1):
        outs[j][low:, :] = riding[j - 1][...]


def copies_body(slices, n_in, *refs):
    ins, out = refs[:n_in], refs[-1]
    for j in range(out.shape[0]):
        at = 0
        for begin, rows in slices:
            for ref in ins:
                out[j, at : at + rows, :] = ref[begin : begin + rows, :]
                at += rows


def final_body(strides, parts, dests, n_out, *refs):
    got, outs, totals = refs[0], refs[1 : 1 + n_out], refs[1 + n_out :]
    me = lax.axis_index("ctx")
    shift, per = 0, 1
    for stride, step in strides[1:]:
        shift = shift * step + (me // stride) % step
        per *= step
    at, used = 0, 0
    for height, total, (dest, many) in zip(parts, totals, dests):
        rows = height // per
        for i in range(got.shape[0]):
            for b in range(per):
                begin = pl.multiple_of((i * per + (b ^ shift)) * rows, 8)
                piece = got[i, at + b * rows : at + (b + 1) * rows, :]
                total[pl.ds(begin, rows), :] = piece.astype(F32)
        at += height
        dest(total, outs[used : used + many])
        used += many


WIDTH = 512


def cut_up(chunks, heights, strides, at, size, riders=()):
    stride, step = strides[at]
    total = sum(heights) // step
    more = riders[0].shape[0] if riders else 0
    n_in = sum(len(c) for c in chunks)
    pieces = call(
        functools.partial(middle_body, [len(c) for c in chunks], stride, step, n_in, len(riders)),
        [((total, WIDTH), F32)] + [((total + more, WIDTH), BF)] * (step - 1),
        [t for c in chunks for t in c] + far(riders),
        scratch=[((h, WIDTH), F32) for h in heights],
    )
    return pieces[:1] + [swap(pieces[j], j * stride, size) for j in range(1, step)]


def spread(done, strides, at, size):
    stride, step = strides[at]
    return [done] + [swap(done, j * stride, size) for j in range(1, step)]


def settle(terms):
    return call(add_body, [(terms[0].shape, BF)], terms)[0]


def add_body(*refs):
    rows = refs[-1].shape[0]
    value = refs[0][:rows, :].astype(F32)
    for ref in refs[1:-1]:
        value = value + ref[:rows, :].astype(F32)
    refs[-1][...] = value.astype(refs[-1].dtype)


def early_dest(total, outs):
    down, tile = outs
    wide = down.shape[0]
    down[...] = total[:wide, :]
    tile[...] = total[wide : wide + tile.shape[0], :]


def both_final_body(strides, parts, got, tile, *refs):
    outs, totals = refs[:7], refs[7:]

    def main(total, outs):
        (up,) = outs
        half = up.shape[0]
        core = lax.axis_index("wsh")
        tiles = up.shape[1] // WIDTH
        for i in range(tiles):
            side, inner = i // (tiles // 2), i % (tiles // 2)
            at = (core if side == 0 else 1 - core) * (tiles // 2) + inner
            rows = tile[...] if i == 0 else total[(i - 1) * half : i * half, :]
            up[:, pl.ds(pl.multiple_of(at * WIDTH, WIDTH), WIDTH)] = rows

    dests = [(main, 1), (late_dest, 6)]
    final_body(strides, parts, dests, 7, got, *outs, *totals)


def late_dest(total, outs):
    out, query, kv, router, one, two = outs
    half = kv.shape[0]
    out[...] = total[:half, :]
    query[...] = total[half : 2 * half, :]
    step = half // 4
    at = 2 * half
    for j in range(4):
        kv[j * step : (j + 1) * step, :] = total[at : at + step, j * 128 : (j + 1) * 128]
    at += step
    router[...] = total[at : at + router.shape[0], :half]
    one[...] = total[at + 8 : at + 9, :half]
    two[...] = total[at + 8 : at + 9, half:]


def place_body(rest, *refs):
    place = lax.axis_index("ctx") // rest
    out = refs[-1]
    local = out.shape[1]
    for k, ref in enumerate(refs[:-1]):
        begin = ref.shape[0] - local
        out[place ^ k] = ref[begin:, :].astype(F32)


def on_device(
    tokens,
    routes,
    block_order,
    norm_gain1,
    router_w,
    query_w,
    kv_w,
    out_w,
    norm_gain2,
    up_w,
    down_w,
    cotangent,
):
    size = lax.axis_size("ctx")
    count, local, dim = tokens.shape
    rest = size // count
    place = lax.axis_index("ctx") // rest
    total = count * local
    experts = router_w.shape[1]
    head = kv_w.shape[1] // 2
    feed = up_w.shape[1]

    Order.last = None
    tall = dim // 2
    keys = 2 * head
    router_t = router_w.T
    routes_t = routes.transpose(0, 2, 1)

    def core():
        return lax.axis_index("wsh")

    def here():
        return lax.axis_index("ctx") // rest

    tok_pieces = call(
        functools.partial(pack_body, count, rest),
        [((local + 8, dim), BF)] * (count - 1),
        far([tokens, routes_t]),
    )
    tok_x = [swap(tok_pieces[k - 1], k * rest, size) for k in range(1, count)]
    packed, tok_own, kv_own = call(
        pack_weights_body,
        [((tall + 8, experts * head + keys), BF)],
        far([query_w, kv_w, router_t]),
        ahead=[Ahead(tokens, (local, dim), lambda r: r.at[here()]), Ahead(kv_w)],
    )
    packed_x = trade(packed)
    gain_one, gain_two = after((norm_gain1, norm_gain2), packed)
    gains = jnp.stack([gain_one, gain_two])
    gains_x = trade(gains)

    steps = factors(rest)
    kv, normed, tok, gain_rows, wk, tails, query_own, router_own, *cot_pieces = call(
        functools.partial(keys_body, count, rest),
        [
            ((steps[0], total, keys), BF),
            ((total, dim), BF),
            ((total, dim), BF, 1),
            ((8, dim), F32, 1),
            ((dim, keys), BF, 1),
            ((8 * count, 128), F32),
        ],
        [tok_own, *tok_x, Far(routes_t), gains, gains_x, kv_own, packed_x],
        ahead=[Ahead(query_w), Ahead(router_t)]
        + [
            Ahead(cotangent, (local, dim), lambda r, k=k: r.at[here() ^ k])
            for k in range(1, count)
        ],
    )
    stride = 1
    for i, step in enumerate(steps):
        if i > 0:
            kv = jnp.broadcast_to(kv[None], (step,) + kv.shape)
        kv = exchange(kv, stride, size).reshape(-1, total, keys)
        stride *= step
    cot_x = [swap(cot_pieces[k - 1], k * rest, size) for k in range(1, count)]
    qt, qt_far, normed_t, gates, gates_far, route, route_far, wq, wr = call(
        functools.partial(project_body, count, experts, head),
        [
            ((TWO * head, total), BF),
            ((TWO * head, total), BF, 1),
            ((dim, total), BF, 1),
            ((TWO, total), F32),
            ((TWO, total), F32, 1),
            ((8, total), F32),
            ((8, total), F32, 1),
            ((dim, experts * head), BF, 1),
            ((128, dim), F32, 1),
        ],
        [normed, tails, query_own, router_own, packed_x],
    )
    up_w2, down_w2, out_w2, _ = lax.optimization_barrier((up_w, down_w, out_w, normed))
    out_x, up_x, down_x = trade(out_w2), trade(up_w2), trade(down_w2)
    span = rest * total
    wide = feed // 2

    def lanes(which):
        def view(ref):
            side = which()
            return ref.at[:, pl.ds(pl.multiple_of(side * wide, wide), wide)]

        return view

    att, logs, mixed, hidden, two, two_t, kv_far, wo, cot_own, up_first = call(
        functools.partial(attend_body, count, rest, experts, head),
        [
            ((TWO * head, total), F32, 1),
            ((TWO, total), F32, 1),
            ((experts * head, total), BF, 1),
            ((total, dim), F32),
            ((total, dim), BF),
            ((dim, total), BF),
            ((rest, total, keys), BF, 1),
            ((experts * head, dim), BF, 1),
        ],
        [block_order, kv, qt, gates, route, *far([tok, gain_rows, out_w]), out_x],
        scratch=[((keys, span), BF)],
        smem=(0,),
        late=(5, 6, 7),
        ahead=[
            Ahead(cotangent, (local, dim), lambda r: r.at[here()]),
            Ahead(up_w, (tall, wide), lanes(lambda: 1 - core())),
        ],
    )

    tile = 256
    upper = wide * tall // dim
    layer, back_two, send_one, keep_one, cots, cots_far, send_up, up_second, down_own = call(
        functools.partial(feed_body, count, rest, True, tile),
        [
            ((total, dim), F32),
            ((total, dim), F32),
            ((wide, dim), BF),
            ((upper, dim), BF, 1),
            ((total, dim), BF),
            ((total, dim), BF, 1),
            ((upper, dim), BF),
        ],
        [two, two_t, cot_own, *cot_x, up_first, up_x, down_x, hidden],
        scratch=[((dim, wide), BF)],
        ahead=[Ahead(up_w, (tall, wide), lanes(core)), Ahead(down_w)],
    )
    recv_down, recv_up = trade(send_one), trade(send_up)
    *layer_pieces, back_two, keep_down, keep_two, send_two, cots, wo, gain_near, gates, route, att = call(
        functools.partial(feed_body, count, rest, False, tile),
        [((local, dim), F32, 1)]
        + [((local, dim), BF, 1)] * (count - 1)
        + [
            ((total, dim), F32),
            ((wide, dim), BF, 1),
            ((upper, dim), BF, 1),
            ((upper, dim), BF, 1),
        ],
        [two, two_t, cots, up_second, up_x, down_own, layer, back_two],
        scratch=[((dim, wide), BF), ((total, dim), F32)],
        ahead=[
            Ahead(a)
            for a in (cots_far, wo, gain_rows, gates_far, route_far, att)
        ],
    )
    recv_two = trade(send_two)
    layer_got = [layer_pieces[0]] + [swap(layer_pieces[k], k * rest, size) for k in range(1, count)]

    strides = []
    stride = 1
    for step in [*steps, count]:
        strides.append((stride, step))
        stride *= step
    last = len(strides) - 1
    unit = 8 * size
    first = strides[0][1]
    early_rows = -(-(wide + tall) // unit) * unit
    main_rows = -(-(2 * upper - tall) // unit) * unit
    small = tall // 4 + 16
    late_rows = -(-(small + 2 * tall) // unit) * unit

    def bulk(args, layout, height, ahead=()):
        pieces, *near = call(
            functools.partial(start_body, layout, True, 1, first, len(args)),
            [((first, height // first, WIDTH), BF)],
            args,
            scratch=[((height, WIDTH), F32)],
            ahead=ahead,
        )
        return exchange(pieces, 1, size), near

    def inner(terms, height, riders=()):
        height //= first
        for at in range(1, last + 1):
            more = riders if at == last else ()
            terms = cut_up([terms], [height], strides, at, size, more)
            height //= strides[at][1]
        return terms

    def outer(got):
        for at in reversed(range(1, last)):
            got = spread(jnp.concatenate(got, axis=0), strides, at, size)
        return got

    def ready(got, ahead=()):
        rows = got[0].shape[0]
        copies, *near = call(
            functools.partial(copies_body, [(0, rows)], len(got)),
            [((first, rows * len(got), WIDTH), BF)],
            got,
            ahead=ahead,
        )
        return exchange(copies, 1, size), near

    back_hidden, branch, grad_att, delta, logit, gain_two = call(
        functools.partial(turn_body, count, rest, experts, head),
        [
            ((total, dim), F32, 1),
            ((total, dim), BF, 1),
            ((TWO * head, total), BF, 1),
            ((TWO, total), F32, 1),
            ((experts, total), F32, 1),
            ((8, dim), F32, 1),
        ],
        [hidden, back_two, cots, wo, gain_near, gates, route, att],
    )
    early, (kv_near, qt_near, logs_near, grad_att, delta) = bulk(
        [Far(keep_down), recv_down, Far(keep_two), recv_up],
        [[(0, 0, wide), (1, 0, wide)], [(2, 0, tall), (3, 0, tall)]],
        early_rows,
        [Ahead(a) for a in (kv_far, qt_far, logs, grad_att, delta)],
    )
    split = steps[-1]
    share = span // split
    grad_q, *kv_terms = call(
        functools.partial(attend_back_body, count, rest, head, split),
        [((TWO * head, total), BF), ((share, keys), F32, 1)] + [((share, keys), BF, 1)] * (split - 1),
        [block_order, kv_near, qt_near, grad_att, logs_near, delta],
        scratch=[
            ((keys, span), BF),
            ((2 * TWO, keys, total), BF),
            ((2 * TWO, total, keys), BF),
            ((span, keys), F32),
            ((TWO * head, total), F32),
        ],
        smem=(0,),
        ahead=[Ahead(a) for a in (normed_t, route_far, mixed, branch, wq, wr, logit, tok)],
    )
    kv_terms, ahead = kv_terms[:split], kv_terms[split:]
    stride = rest
    for i, step in reversed(list(enumerate(steps))):
        stride //= step
        if i + 1 < len(steps):
            summed = functools.reduce(lambda a, b: a + b.astype(F32), terms)
            parts = summed.reshape(step, -1, keys)
            digit = (lax.axis_index("ctx") // stride) % step
            kv_terms = [pick(parts, digit ^ j) for j in range(step)]
        terms = [kv_terms[0]] + [
            swap(kv_terms[j].astype(BF), j * stride, size) for j in range(1, step)
        ]
    grad_q = after(grad_q, *layer_got[1:])
    keep_out, keep_query, send_main, back_part, unit_rows, scale_rows, routers, *near = call(
        functools.partial(query_body, experts, head),
        [
            ((tall, dim), BF, 1),
            ((tall, dim), BF, 1),
            ((2 * tall, dim), BF, 1),
            ((total, dim), F32),
            ((total, dim), F32),
            ((total, 128), F32),
            ((experts, dim), F32),
        ],
        [grad_q, *ahead],
        scratch=[((experts * head, total), BF)],
        ahead=[Ahead(a) for a in (normed_t, back_hidden, wk, gain_rows, gain_two, terms[0])],
    )
    *near, term = near
    *input_pieces, keep_late, send_late = call(
        functools.partial(unproject_body, count, len(terms)),
        [((local, dim), F32, 1)]
        + [((local, dim), BF, 1)] * (count - 1)
        + [((small, dim), F32, 1), ((small + 2 * tall, dim), BF)],
        [term, *terms[1:], back_part, unit_rows, scale_rows, routers, *near, Far(send_main)],
        scratch=[((8, dim), F32)],
    )
    recv_late = trade(send_late)
    main, _ = bulk(
        [*far([keep_two]), recv_up, *far([keep_one]), recv_two],
        [
            [(0, tall, upper - tall), (1, tall, upper - tall)],
            [(2, 0, upper), (3, 0, upper)],
        ],
        main_rows,
    )
    early_terms = inner([early], early_rows)
    pieces = call(
        functools.partial(
            start_body,
            [
                [(0, 0, tall), (1, 0, tall)],
                [(0, tall, tall), (2, 0, tall)],
                [(0, 2 * tall, small), (3, 0, small)],
            ],
            False,
            1,
            first,
            4,
        ),
        [((late_rows // first, WIDTH), F32)] + [((late_rows // first, WIDTH), BF)] * (first - 1),
        [recv_late, *far([keep_out, keep_query, keep_late])],
        scratch=[((late_rows, WIDTH), F32)],
    )
    late = pieces[:1] + [swap(pieces[j], j, size) for j in range(1, first)]
    early_got = outer(spread(settle(early_terms), strides, last, size))
    heights = [main_rows // first, late_rows // first]
    chunks = [[main], late]
    for at in range(1, last):
        chunks = [cut_up([c], [h], strides, at, size) for c, h in zip(chunks, heights)]
        heights = [h // strides[at][1] for h in heights]
    both_terms = cut_up(chunks, heights, strides, last, size)
    heights = [h // count for h in heights]
    early_last, _ = ready(early_got)
    both_got = spread(settle(both_terms), strides, last, size)
    slices = [(0, heights[0]), (heights[0], heights[1])]
    for stage in reversed(range(1, last)):
        moved = []
        for begin, h in slices:
            piece = jnp.concatenate([g[begin : begin + h] for g in both_got], axis=0)
            moved.append(spread(piece, strides, stage, size))
        both_got = [jnp.concatenate([m[j] for m in moved], axis=0) for j in range(strides[stage][1])]
        tops = [m[0].shape[0] for m in moved]
        slices = [(0, tops[0]), (tops[0], tops[1])]
    tall_rows = sum(h for _, h in slices) * len(both_got)
    (copies,) = call(
        functools.partial(copies_body, slices, len(both_got)),
        [((first, tall_rows, WIDTH), BF)],
        both_got,
    )
    both_last = exchange(copies, 1, size)
    input_pieces = after(tuple(input_pieces), both_got[0])
    input_got = [input_pieces[0]] + [swap(input_pieces[k], k * rest, size) for k in range(1, count)]
    (layer_out,) = call(
        functools.partial(place_body, rest),
        [((count, local, dim), F32, 1)],
        [Far(layer_got[0]), *layer_got[1:]],
    )
    grad_down, up_tile = call(
        functools.partial(final_body, strides, [early_rows // first], [(early_dest, 2)], 2),
        [((wide, dim), F32, 1), ((tall, WIDTH), F32)],
        [early_last],
        scratch=[((early_rows, WIDTH), F32)],
    )
    (input_grad,) = call(
        functools.partial(place_body, rest),
        [((count, local, dim), F32, 1)],
        [Far(input_got[0]), *input_got[1:]],
    )
    grad_up, grad_out, grad_query, grad_kv, grad_router, grad_one, grad_two = call(
        functools.partial(both_final_body, strides, [main_rows // first, late_rows // first]),
        [
            ((tall, feed), F32, 1),
            ((tall, dim), F32, 1),
            ((tall, experts * head), F32, 1),
            ((tall, keys), F32, 1),
            ((experts, tall), F32, 1),
            ((1, tall), F32, 1),
            ((1, tall), F32, 1),
        ],
        [both_last, up_tile],
        scratch=[((main_rows, WIDTH), F32), ((late_rows, WIDTH), F32)],
    )
    return (
        layer_out,
        input_grad,
        grad_one.reshape(tall),
        grad_router.T,
        grad_query,
        grad_kv,
        grad_out,
        grad_two.reshape(tall),
        grad_up,
        grad_down,
    )


def solution(mesh):
    placed = (
        P("wsh", "ctx", None),
        P("wsh", "ctx", None),
        P(),
        P("wsh"),
        P("wsh", None),
        P("wsh", None),
        P("wsh", None),
        P("wsh", None),
        P("wsh"),
        P("wsh", None),
        P("wsh", None),
        P("wsh", "ctx", None),
    )
    return jax.shard_map(
        on_device,
        mesh=mesh,
        in_specs=placed,
        out_specs=(
            P("wsh", "ctx", None),
            P("wsh", "ctx", None),
            P("wsh"),
            P("wsh", None),
            P("wsh", None),
            P("wsh", None),
            P("wsh", None),
            P("wsh"),
            P("wsh", None),
            P("wsh", None),
        ),
        check_vma=False,
    )
```

```python
import functools
import math

import jax
import jax.numpy as jnp
from jax import lax
from jax.experimental import pallas as pl
from jax.experimental.pallas import tpu as pltpu
from jax.sharding import PartitionSpec as P

BF = jnp.bfloat16
F32 = jnp.float32
I32 = jnp.int32
NONE = -1e30
TWO = 2


def factors(size):
    out = []
    while size > 1:
        step = 4 if size % 4 == 0 else 2
        out.append(step)
        size //= step
    return out


def swap(values, mask, size):
    return lax.ppermute(values, "ctx", [(i, i ^ mask) for i in range(size)])


def groups_of(stride, step, size):
    out = []
    for i in range(size):
        if (i // stride) % step == 0:
            out.append([i + j * stride for j in range(step)])
    return out


def exchange(parts, stride, size):
    step = parts.shape[0]
    groups = groups_of(stride, step, size)
    return lax.all_to_all(parts, "ctx", 0, 0, tiled=True, axis_index_groups=groups)


def trade(values):
    return lax.ppermute(values, "wsh", [(0, 1), (1, 0)])


def pick(parts, index):
    return lax.dynamic_index_in_dim(parts, index, 0, False)


def mm(a, b, left=1, right=0):
    return lax.dot_general(a, b, (((left,), (right,)), ((), ())), preferred_element_type=F32)


class Order:
    last = None
    rest = None
    leave = None


def after(value, *earlier):
    return lax.optimization_barrier((value, *earlier))[0]


class Far:
    def __init__(self, value):
        self.value = value


class Ahead:
    def __init__(self, value, shape=None, view=None):
        self.value, self.view = value, view
        self.shape = value.shape if shape is None else shape


def loading_body(body, plan, n_out, far_out, late, views, n_scratch, *refs):
    n_in, n_pre = len(plan), len(views)
    ins, pre_in = list(refs[:n_in]), refs[n_in : n_in + n_pre]
    at = n_in + n_pre
    outs, pre_out = list(refs[at : at + n_out]), refs[at + n_out : at + n_out + n_pre]
    at += n_out + n_pre
    own = refs[at : at + n_scratch]
    held, sems = refs[at + n_scratch : -1], refs[-1]
    first, second, ahead, slot = [], [], [], 0
    for i in range(n_in):
        if plan[i]:
            copy = pltpu.make_async_copy(ins[i], held[slot], sems.at[slot])
            (second if i in late else first).append(copy)
            ins[i] = held[slot]
            slot += 1
    leaving = {}
    for i in range(n_out):
        if far_out[i]:
            leaving[i] = pltpu.make_async_copy(held[slot], outs[i], sems.at[slot])
            outs[i] = held[slot]
            slot += 1
    for view, source, target in zip(views, pre_in, pre_out):
        source = source if view is None else view(source)
        ahead.append(pltpu.make_async_copy(source, target, sems.at[slot]))
        slot += 1
    for copy in first + second + ahead:
        copy.start()
    for copy in first:
        copy.wait()

    def rest():
        for copy in second:
            copy.wait()

    gone = []

    def leave(*which):
        for i in which:
            if far_out[i]:
                gone.append(i)
                leaving[i].start()

    Order.rest, Order.leave = rest, leave
    body(*ins, *outs, *own)
    leave(*[i for i in range(n_out) if i not in gone])
    for i in gone:
        leaving[i].wait()
    for copy in ahead:
        copy.wait()


def call(body, outs, args, scratch=(), smem=(), late=(), ahead=(), mib=14):
    whole = pl.BlockSpec(memory_space=pltpu.VMEM)
    scalars = pl.BlockSpec(memory_space=pltpu.SMEM)
    distant = pl.BlockSpec(memory_space=pltpu.HBM)
    plan = [isinstance(a, Far) for a in args]
    args = [
        pltpu.with_memory_space_constraint(a.value, pltpu.HBM) if isinstance(a, Far) else a
        for a in args
    ]
    far_out = [len(o) > 2 for o in outs]
    if Order.last is not None:
        args[0] = after(args[0], Order.last)
    held = [(a.shape, a.dtype) for a, far in zip(args, plan) if far]
    held += [o[:2] for o, far in zip(outs, far_out) if far]
    need = sum(math.prod(s) * jnp.dtype(d).itemsize for s, d in [*held, *scratch])
    run = pl.pallas_call(
        functools.partial(
            loading_body,
            body,
            plan,
            len(outs),
            far_out,
            late,
            [a.view for a in ahead],
            len(scratch),
        ),
        out_shape=[
            pltpu.HBM(o[0], o[1]) if far else jax.ShapeDtypeStruct(o[0], o[1])
            for o, far in zip(outs, far_out)
        ]
        + [jax.ShapeDtypeStruct(a.shape, a.value.dtype) for a in ahead],
        in_specs=[
            scalars if i in smem else distant if plan[i] else whole for i in range(len(args))
        ]
        + [distant] * len(ahead),
        out_specs=[distant if far else whole for far in far_out] + [whole] * len(ahead),
        scratch_shapes=[pltpu.VMEM(s, d) for s, d in [*scratch, *held]]
        + [pltpu.SemaphoreType.DMA((max(len(held) + len(ahead), 1),))],
        compiler_params=pltpu.CompilerParams(vmem_limit_bytes=(mib << 20) + need),
        cost_estimate=pl.CostEstimate(flops=1, bytes_accessed=1, transcendentals=0),
    )
    moved = [pltpu.with_memory_space_constraint(a.value, pltpu.HBM) for a in ahead]
    got = list(run(*args, *moved))
    Order.last = got[0]
    return got


def far(values):
    return [Far(v) for v in values]


def join(slots):
    half = slots[0].shape[0] // 2
    return jnp.concatenate([s[:half] for s in slots] + [s[half:] for s in slots], axis=0)


def slot_rows(rows, k, count):
    half = rows.shape[0] // (2 * count)
    low = k * half
    high = rows.shape[0] // 2 + k * half
    return jnp.concatenate([rows[low : low + half], rows[high : high + half]], axis=0)


def centred(rows):
    centre = rows - jnp.mean(rows, axis=-1, keepdims=True)
    scale = lax.rsqrt(jnp.mean(centre * centre, axis=-1, keepdims=True) + 1e-05)
    return centre * scale, scale


def fill(scratch, own, other, core):
    half = own.shape[0]
    scratch[pl.ds(pl.multiple_of(core * half, half), half), :] = own[...]
    scratch[pl.ds(pl.multiple_of((1 - core) * half, half), half), :] = other[...]


def pick_gain(own, other, which, core):
    a = own[which : which + 1, :].astype(F32)
    b = other[which : which + 1, :].astype(F32)
    first = jnp.where(core == 0, a, b)
    second = jnp.where(core == 0, b, a)
    return jnp.concatenate([first, second], axis=1)


def route_rows(pieces):
    lane = lax.broadcasted_iota(I32, (8, 128), 1)
    low = lane < 64
    rolled = [pltpu.roll(p, 64, 1) for p in pieces]
    count = len(pieces)
    front = [jnp.where(low, pieces[i], rolled[i + 1]) for i in range(0, count, 2)]
    back = [jnp.where(low, rolled[i], pieces[i + 1]) for i in range(0, count, 2)]
    return jnp.concatenate(front + back, axis=1)


def pack_body(count, rest, *refs):
    tok, routes = refs[:2]
    place = lax.axis_index("ctx") // rest
    local, dim = tok.shape[1:]
    for k, out in enumerate(refs[2:]):
        out[:local, :] = tok[place ^ (k + 1)]
        out[local:, :] = jnp.zeros((8, dim), BF)
        out[local : local + TWO, :128] = routes[place ^ (k + 1)].astype(F32).astype(BF)


def pack_all_body(count, rest, *refs):
    tok, routes, query, kv, router, out = refs[:6]
    pieces, packed = refs[6:-1], refs[-1]
    pack_body(count, rest, tok, routes, *pieces)
    Order.rest()
    half, cols = query.shape
    keys = kv.shape[1]
    packed[half:, :] = jnp.zeros((8, packed.shape[1]), BF)
    packed[:half, :cols] = query[...]
    packed[:half, cols : cols + keys] = kv[...]
    packed[:half, cols + keys :] = out[...]
    packed[half:, :half] = router[...]


def fill_router(wr, own, packed, core):
    half = own.shape[1]
    wr[...] = jnp.zeros_like(wr)
    experts = own.shape[0]
    mine = pl.ds(pl.multiple_of(core * half, half), half)
    theirs = pl.ds(pl.multiple_of((1 - core) * half, half), half)
    wr[:experts, mine] = own[...].astype(F32)
    wr[:experts, theirs] = packed[half:, :half].astype(F32)


def keys_body(count, rest, *refs):
    toks = refs[:count]
    routes, g_own, g_other, k_own, packed = refs[count : count + 5]
    kv_out, normed_out, tok_out, gain_out, wk, tail_out = refs[count + 5 :]
    core = lax.axis_index("wsh")
    place = lax.axis_index("ctx") // rest
    half = k_own.shape[0]
    local = toks[0].shape[0]
    keys = k_own.shape[1]
    cols = packed.shape[1] - keys - toks[0].shape[1]
    fill(wk, k_own, packed.at[:half, cols : cols + keys], core)
    rows = join([t[:local] for t in toks])
    tok_out[...] = rows
    Order.leave(2, 4)
    tail_out[...] = jnp.zeros_like(tail_out)
    tail_out[:TWO, :] = routes[place].astype(F32)
    for k in range(1, count):
        tail_out[8 * k : 8 * k + 8, :] = toks[k][local : local + 8, :128].astype(F32)
    rows = rows.astype(F32)
    unit, _ = centred(rows)
    gain_out[...] = jnp.zeros_like(gain_out)
    for which in range(TWO):
        gain_out[which : which + 1, :] = pick_gain(g_own, g_other, which, core)
    normed = (unit * gain_out[0:1, :]).astype(BF)
    normed_out[...] = normed
    Order.leave(1, 3)
    kv = mm(normed, wk[...]).astype(BF)
    for i in range(kv_out.shape[0]):
        kv_out[i] = kv


def project_body(count, experts, head, *refs):
    normed_ref, tails, q_own, r_own, o_own, packed = refs[:6]
    qt_out, nt_out, gate_out, gate_far, route_out, route_far, wq, wr, wo = refs[6:]
    core = lax.axis_index("wsh")
    half, cols = q_own.shape
    normed = normed_ref[...]
    nt_out[...] = normed.T
    Order.leave(1)
    Order.rest()
    fill(wq, q_own, packed.at[:half, :cols], core)
    fill_router(wr, r_own, packed, core)
    fill(wo, o_own, packed.at[:half, packed.shape[1] - o_own.shape[1] :], core)
    Order.leave(6, 7, 8)
    routes = route_rows([tails[8 * k : 8 * k + 8, :] for k in range(count)])
    route_out[...] = routes
    route_far[...] = routes
    logits = mm(wr[...].astype(BF), normed, 1, 1)
    queries = mm(wq[...], normed, 0, 1) * 0.125
    chosen = []
    for s in range(TWO):
        route = routes[s : s + 1]
        total = jnp.zeros((head, normed.shape[0]), F32)
        value = jnp.zeros((1, normed.shape[0]), F32)
        for e in range(experts):
            here = route == e
            total = jnp.where(here, queries[e * head : (e + 1) * head], total)
            value = jnp.where(here, logits[e : e + 1], value)
        qt_out[s * head : (s + 1) * head, :] = total.astype(BF)
        chosen.append(value)
    top = jnp.maximum(chosen[0], chosen[1])
    raised = [jnp.exp(c - top) for c in chosen]
    total = raised[0] + raised[1]
    gate_out[...] = jnp.concatenate([r / total for r in raised], axis=0)
    gate_far[...] = gate_out[...]


def places(order, count, rest, block, width, part):
    me = lax.axis_index("ctx")
    place, other = me // rest, me % rest
    size = count * rest
    lane = lax.broadcasted_iota(I32, (1, width), 1)
    out = jnp.zeros((1, width), I32)
    for k in range(count):
        first = order[(place ^ k) * rest + other]
        base = jnp.where(part == 0, first, 2 * size - 1 - first) * block
        out = jnp.where(lane // block == k, lane - k * block + base, out)
    return out


def key_bases(order, count, rest, block, chunk, part):
    me = lax.axis_index("ctx")
    place = me // rest
    size = count * rest
    out = []
    for k in range(count):
        first = order[(place ^ k) * rest + chunk]
        out.append((first if part == 0 else 2 * size - 1 - first) * block)
    return out


def masked(scores, gap, bases, block):
    parts = [
        jnp.where(gap <= -base, scores[k * block : (k + 1) * block], NONE)
        for k, base in enumerate(bases)
    ]
    return jnp.concatenate(parts, axis=0)


def scored(kv, side, h, gap, order, count, rest, block, chunk, half):
    first = mm(kv[:half], side)
    if h == 0:
        return masked(first, gap, key_bases(order, count, rest, block, chunk, 0), block)
    second = mm(kv[half:], side)
    second = masked(second, gap, key_bases(order, count, rest, block, chunk, 1), block)
    return jnp.concatenate([first, second], axis=0)


def turn_keys(kv, kv_turned):
    rows = kv.shape[1]
    for c in range(kv.shape[0]):
        kv_turned[:, c * rows : (c + 1) * rows] = kv[c].T


def both_slots(rows, head, cols):
    return jnp.concatenate([rows[s * head : (s + 1) * head, cols] for s in range(TWO)], axis=1)


def gap_rows(order, count, rest, block, half, h):
    gap = lax.broadcasted_iota(I32, (block, half), 0) - places(order, count, rest, block, half, h)
    return jnp.concatenate([gap] * TWO, axis=1)


def attend_body(count, rest, experts, head, *refs):
    order, kv_ref, qt, gates, routes = refs[:5]
    tok, gains, wo = refs[5:8]
    att_out, log_out, mixed_out, hidden_out, two_out, turned_out, kv_out, kv_turned = refs[8:]
    kv_out[...] = kv_ref[...]
    Order.leave(6)
    other = lax.axis_index("ctx") % rest
    total = qt.shape[1]
    half = total // 2
    block = half // count
    turn_keys(kv_ref, kv_turned)
    sides, gaps = [], []
    for h in range(2):
        side = both_slots(qt, head, slice(h * half, (h + 1) * half))
        sides.append(jnp.concatenate([side, jnp.zeros_like(side)], axis=0))
        gaps.append(gap_rows(order, count, rest, block, half, h))

    def step(turn, carry):
        chunk = turn ^ other
        at = pl.multiple_of(chunk * total, total)
        kv = kv_ref[chunk]
        scores = [
            scored(kv, sides[h], h, gaps[h], order, count, rest, block, chunk, half)
            for h in range(2)
        ]
        out = []
        for h in range(2):
            top, norm, summed = carry[h]
            fresh = jnp.maximum(top, jnp.max(scores[h], axis=0, keepdims=True))
            shares = jnp.exp(scores[h] - fresh)
            fade = jnp.exp(top - fresh)
            norm = norm * fade + jnp.sum(shares, axis=0, keepdims=True)
            values = kv_turned[head:, pl.ds(at, half * (h + 1))]
            out.append((fresh, norm, summed * fade + mm(values, shares.astype(BF))))
        return tuple(out)

    start = (
        jnp.full((1, TWO * half), NONE, F32),
        jnp.zeros((1, TWO * half), F32),
        jnp.zeros((head, TWO * half), F32),
    )
    done = lax.fori_loop(0, rest, step, (start, start), unroll=rest <= 4)
    for h in range(2):
        top, norm, summed = done[h]
        logs, attended = top + jnp.log(norm), summed / norm
        for s in range(TWO):
            here, cols = slice(h * half, (h + 1) * half), slice(s * half, (s + 1) * half)
            log_out[s : s + 1, here] = logs[:, cols]
            att_out[s * head : (s + 1) * head, here] = attended[:, cols]
    Order.rest()
    Order.leave(0, 1)
    for e in range(experts):
        part = jnp.zeros((head, total), F32)
        for s in range(TWO):
            gate = jnp.where(routes[s : s + 1] == e, gates[s : s + 1], 0.0)
            part = part + gate * att_out[s * head : (s + 1) * head, :]
        mixed_out[e * head : (e + 1) * head, :] = part.astype(BF)
    Order.leave(2)
    hidden = tok[...].astype(F32) + mm(mixed_out[...].T, wo[...])
    hidden_out[...] = hidden
    unit, _ = centred(hidden)
    two = (unit * gains[1:2, :]).astype(BF)
    two_out[...] = two
    turned_out[...] = two.T


def feed_body(count, rest, first, tile, *refs):
    two, turned = refs[:2]
    if first:
        slots = refs[2 : 2 + count]
        u_own, u_other, down, layer_in = refs[2 + count : 6 + count]
        layer_out, back_out, send, keep, cots, cot_far, send_up, up = refs[6 + count :]
    else:
        cots, u_own, u_other, down, layer_in, back_in = refs[2:8]
        outs = refs[8 : 12 + count]
        layer_pieces, back_out, keep_down, keep, send = outs[:count], *outs[count:]
        up, layer_out = refs[12 + count :]
    core = lax.axis_index("wsh")
    side = (1 - core) if first else core
    width = down.shape[0]
    half = u_own.shape[0]
    lanes = pl.ds(pl.multiple_of(side * width, width), width)
    up[pl.ds(pl.multiple_of(core * half, half), half), :] = u_own[...]
    up[pl.ds(pl.multiple_of((1 - core) * half, half), half), :] = u_other[:, lanes]
    if first:
        cots[...] = join([o[...] for o in slots])
        cot_far[...] = cots[...]
        Order.leave(5)
    layer_out[...] = layer_in[...]
    if first:
        back_out[...] = jnp.zeros_like(back_out)
    else:
        back_out[...] = back_in[...]
    mine = pl.ds(pl.multiple_of(core * half, half), half)
    theirs = pl.ds(pl.multiple_of((1 - core) * half, half), half)
    dim = up.shape[0]
    per = dim // tile

    def step(j, carry):
        cols = pl.ds(pl.multiple_of(j * tile, tile), tile)
        up_j = up[:, cols]
        down_j = down[cols, :]
        pre = mm(two[...], up_j)
        back = mm(cots[...], down_j, 1, 1)
        phi = 0.5 * (1.0 + lax.erf(pre * math.sqrt(0.5)))
        bell = jnp.exp(pre * pre * -0.5) * (1.0 / math.sqrt(2.0 * math.pi))
        act = (pre * phi).astype(BF)
        back_pre = (back * (phi + pre * bell)).astype(BF)
        layer_out[...] += mm(act, down_j)
        back_out[...] += mm(back_pre, up_j, 1, 1)
        grad = mm(act.T, cots[...]).astype(BF)
        grad_mine = mm(turned[mine, :], back_pre).astype(BF)
        grad_theirs = mm(turned[theirs, :], back_pre).astype(BF)
        rows = pl.ds(pl.multiple_of((j // per) * half, half), half)
        lane = pl.ds(pl.multiple_of((j % per) * tile, tile), tile)
        keep[rows, lane] = grad_mine
        if first:
            send[cols, :] = grad
            send_up[rows, lane] = grad_theirs
        else:
            keep_down[cols, :] = grad
            send[rows, lane] = grad_theirs
        return carry

    lax.fori_loop(0, width // tile, step, 0)
    if not first:
        for k in range(count):
            layer_pieces[k][...] = slot_rows(layer_out[...], k, count).astype(layer_pieces[k].dtype)


def turn_body(count, rest, experts, head, *refs):
    hidden, back_two, cot, wo, gain, gates, routes, att = refs[:8]
    back_hidden_out, branch_out, grad_att_out, delta_out, logit_out, gain_out = refs[8:]
    unit, scale = centred(hidden[...])
    back = back_two[...]
    side = back * gain[1:2, :]
    part = scale * (
        side
        - jnp.mean(side, axis=-1, keepdims=True)
        - unit * jnp.mean(side * unit, axis=-1, keepdims=True)
    )
    gain_out[...] = jnp.broadcast_to(jnp.sum(back * unit, axis=0, keepdims=True), gain_out.shape)
    back_hidden = cot[...].astype(F32) + part
    back_hidden_out[...] = back_hidden
    branch = back_hidden.astype(BF)
    branch_out[...] = branch
    Order.leave(0, 1, 5)
    back_mixed = mm(wo[...], branch, 1, 1)
    grads = []
    for s in range(TWO):
        total = jnp.zeros((head, branch.shape[0]), F32)
        for e in range(experts):
            total = jnp.where(routes[s : s + 1] == e, back_mixed[e * head : (e + 1) * head], total)
        att_s = att[s * head : (s + 1) * head, :]
        grads.append(jnp.sum(total * att_s, axis=0, keepdims=True))
        low = (gates[s : s + 1] * total).astype(BF)
        grad_att_out[s * head : (s + 1) * head, :] = low
        delta_out[s : s + 1, :] = jnp.sum(low.astype(F32) * att_s, axis=0, keepdims=True)
    mean = gates[0:1] * grads[0] + gates[1:2] * grads[1]
    row = lax.broadcasted_iota(I32, logit_out.shape, 0)
    logit = jnp.zeros(logit_out.shape, F32)
    for s in range(TWO):
        value = gates[s : s + 1] * (grads[s] - mean)
        logit = logit + jnp.where(row.astype(F32) == routes[s : s + 1], value, 0.0)
    logit_out[...] = logit


def turn_start_body(count, rest, experts, head, layout, step, *refs):
    ins, early, outs, pieces = refs[:8], refs[8:12], refs[12:18], refs[18]
    turn_body(count, rest, experts, head, *ins, *outs)
    Order.rest()
    start_body(layout, True, 1, step, len(early), *early, pieces, None)


def attend_back_body(count, rest, head, split, *refs):
    order, kv_ref, qt, grad_att, logs, delta, grad_q_out = refs[:7]
    outs = refs[7 : 7 + split]
    kv_turned, sides, turned, grad_kv, grad_q = refs[7 + split :]
    total = qt.shape[1]
    half = total // 2
    block = half // count
    wide = TWO * half
    turn_keys(kv_ref, kv_turned)
    blank = jnp.zeros((head, wide), BF)
    for h in range(2):
        cols = slice(h * half, (h + 1) * half)
        q_side = jnp.concatenate([both_slots(qt, head, cols), blank], axis=0)
        g_side = jnp.concatenate([blank, both_slots(grad_att, head, cols)], axis=0)
        sides[2 * h], sides[2 * h + 1] = q_side, g_side
        turned[h, :wide, :], turned[h, wide:, :] = q_side.T, g_side.T
    grad_q[...] = jnp.zeros_like(grad_q)
    gaps = [gap_rows(order, count, rest, block, half, h) for h in range(2)]
    log_rows = [both_slots(logs, 1, slice(h * half, (h + 1) * half)) for h in range(2)]
    delta_rows = [both_slots(delta, 1, slice(h * half, (h + 1) * half)) for h in range(2)]

    def step(chunk, carry):
        at = pl.multiple_of(chunk * total, total)
        kv = kv_ref[chunk]
        grads = []
        for h in range(2):
            reach = half * (h + 1)
            scores = scored(
                kv, sides[2 * h], h, gaps[h], order, count, rest, block, chunk, half
            )
            shares = jnp.exp(scores - log_rows[h])
            back_shares = mm(kv[:reach], sides[2 * h + 1])
            back_scores = (shares * (back_shares - delta_rows[h])).astype(BF)
            both = jnp.concatenate([back_scores, shares.astype(BF)], axis=1)
            grads.append(mm(both, turned[h]))
            grad_q[h] += mm(kv_turned[:head, pl.ds(at, reach)], back_scores)
        grad_kv[pl.ds(at, half), :] = grads[0] + grads[1][:half]
        grad_kv[pl.ds(at + half, half), :] = grads[1][half:]
        return carry

    lax.fori_loop(0, rest, step, 0, unroll=rest <= 4)
    for h in range(2):
        for s in range(TWO):
            here, cols = slice(h * half, (h + 1) * half), slice(s * half, (s + 1) * half)
            grad_q_out[s * head : (s + 1) * head, here] = grad_q[h, :, cols].astype(BF)
    rows = outs[0].shape[0]
    digit = (lax.axis_index("ctx") % rest) // (rest // split)
    for i, out in enumerate(outs):
        begin = pl.multiple_of((digit ^ i) * rows, rows)
        out[...] = grad_kv[pl.ds(begin, rows), :].astype(out.dtype)


def query_body(experts, head, *refs):
    grad_q, normed_t, routes, mixed, branch, wq, wr, logit, tok = refs[:9]
    keep_out, keep, send, back_out, unit_out, scale_out, routers, bqt = refs[9:]
    core = lax.axis_index("wsh")
    total = grad_q.shape[1]
    for e in range(experts):
        part = jnp.zeros((head, total), F32)
        for s in range(TWO):
            value = grad_q[s * head : (s + 1) * head, :].astype(F32) * 0.125
            part = jnp.where(routes[s : s + 1] == e, value, part)
        bqt[e * head : (e + 1) * head, :] = part.astype(BF)
    back_q = bqt[...].T
    half = keep.shape[0]
    mine = pl.ds(pl.multiple_of(core * half, half), half)
    theirs = pl.ds(pl.multiple_of((1 - core) * half, half), half)
    send[:half, :] = mm(mixed[theirs, :], branch[...]).astype(BF)
    send[half:, :] = mm(normed_t[theirs, :], back_q).astype(BF)
    keep_out[...] = mm(mixed[mine, :], branch[...]).astype(BF)
    keep[...] = mm(normed_t[mine, :], back_q).astype(BF)
    parts = []
    left = logit[...]
    for _ in range(3):
        low = left.astype(BF)
        parts.append(low)
        left = left - low.astype(F32)
    routers[...] = parts_dot(parts, normed_t[...])
    back = mm(back_q, wq[...], 1, 1)
    wr_turned = wr[...].astype(BF)
    for low in parts:
        padded = jnp.concatenate([low.astype(F32), jnp.zeros((120, total), F32)], axis=0)
        back = back + mm(padded.T.astype(BF), wr_turned)
    back_out[...] = back
    unit, scale = centred(tok[...].astype(F32))
    unit_out[...] = unit
    scale_out[...] = jnp.broadcast_to(scale, scale_out.shape)


def unproject_body(count, terms, *refs):
    kv_terms = refs[:terms]
    back_part, unit_ref, scale_ref, routers, normed_t, back_hidden, wk, gain, gain_two, sent = refs[
        terms : terms + 10
    ]
    at = terms + 10
    pieces = refs[at : at + count]
    keep, send, gains = refs[at + count :]
    core = lax.axis_index("wsh")
    half = back_part.shape[1] // 2
    back_kv = kv_terms[0][...].astype(F32)
    for term in kv_terms[1:]:
        back_kv = back_kv + term[...].astype(F32)
    back_kv = back_kv.astype(BF)
    back = back_part[...] + mm(back_kv, wk[...], 1, 1)
    unit, scale = unit_ref[...], scale_ref[:, 0:1]
    side = back * gain[0:1, :]
    grad = back_hidden[...] + scale * (
        side
        - jnp.mean(side, axis=-1, keepdims=True)
        - unit * jnp.mean(side * unit, axis=-1, keepdims=True)
    )
    gains[0:1, :] = jnp.sum(back * unit, axis=0, keepdims=True)
    gains[1:2, :] = gain_two[0:1, :]
    step = half // 4
    experts = routers.shape[0]
    high = sent.shape[0]
    Order.rest()
    send[:high, :] = sent[...]
    for out, which in ((keep, core), (send.at[high:, :], 1 - core)):
        mine = pl.ds(pl.multiple_of(which * half, half), half)
        grad_k = mm(normed_t[mine, :], back_kv).astype(out.dtype)
        for j in range(4):
            out[:step, j * 128 : (j + 1) * 128] = grad_k[j * step : (j + 1) * step]
        blank = jnp.zeros((experts, half), F32)
        out[step : step + 8, :] = jnp.concatenate([routers[:, mine], blank], axis=1).astype(out.dtype)
        gain_pair = jnp.concatenate([gains[0:1, mine], gains[1:2, mine]], axis=1)
        out[step + 8 :, :] = jnp.broadcast_to(gain_pair, (8, 2 * half)).astype(out.dtype)
    for k in range(count):
        pieces[k][...] = slot_rows(grad, k, count).astype(pieces[k].dtype)


def parts_dot(parts, normed_t):
    out = None
    for low in parts:
        value = mm(low, normed_t, 1, 1)
        out = value if out is None else out + value
    return out


def sum_layout(layout, ins, total):
    at = 0
    for terms in layout:
        height = terms[0][2]
        value = None
        for index, begin, count in terms:
            part = ins[index][begin : begin + count, :].astype(F32)
            value = part if value is None else value + part
        total[at : at + height, :] = value
        at += height
    if at < total.shape[0]:
        total[at:, :] = jnp.zeros((total.shape[0] - at, total.shape[1]), F32)


def cut_rows(total, outs, stride, step):
    rows = outs[0].shape[0]
    digit = (lax.axis_index("ctx") // stride) % step
    for j in range(step):
        begin = pl.multiple_of((digit ^ j) * rows, 8)
        outs[j][...] = total[pl.ds(begin, rows), :].astype(outs[j].dtype)


def start_body(layout, whole, stride, step, n_in, *refs):
    ins, outs, total = refs[:n_in], refs[n_in:-1], refs[-1]
    if whole:
        rows = outs[0].shape[1]
        at = 0
        for terms in layout:
            height, done = terms[0][2], 0
            while done < height:
                j, low = (at + done) // rows, (at + done) % rows
                take = min(height - done, rows - low)
                value = None
                for index, begin, _ in terms:
                    part = ins[index][begin + done : begin + done + take, :].astype(F32)
                    value = part if value is None else value + part
                outs[0][j, low : low + take, :] = value.astype(BF)
                done += take
            at += height
        while at < rows * step:
            j, low = at // rows, at % rows
            outs[0][j, low:, :] = jnp.zeros((rows - low, outs[0].shape[2]), BF)
            at += rows - low
    else:
        sum_layout(layout, ins, total)
        cut_rows(total, outs, stride, step)


def terms_of(ref):
    return [ref.at[j] for j in range(ref.shape[0])] if len(ref.shape) == 3 else [ref]


def middle_body(chunks, stride, step, n_in, riders, *refs):
    ins, riding = refs[:n_in], refs[n_in : n_in + riders]
    refs = refs[n_in + riders :]
    outs, totals = refs[:step], refs[step:]
    digit = (lax.axis_index("ctx") // stride) % step
    at, low = 0, 0
    for count, total in zip(chunks, totals):
        value = None
        for ref in ins[at : at + count]:
            for term in terms_of(ref):
                part = term[...].astype(F32)
                value = part if value is None else value + part
        total[...] = value
        rows = total.shape[0] // step
        for j in range(step):
            begin = pl.multiple_of((digit ^ j) * rows, 8)
            outs[j][low : low + rows, :] = total[pl.ds(begin, rows), :].astype(outs[j].dtype)
        low += rows
        at += count
    for j in range(1, step if riders else 1):
        outs[j][low:, :] = riding[j - 1][...]


def copies_body(slices, n_in, *refs):
    ins, out = refs[:n_in], refs[-1]
    for j in range(out.shape[0]):
        at = 0
        for begin, rows in slices:
            for ref in ins:
                out[j, at : at + rows, :] = ref[begin : begin + rows, :]
                at += rows


def final_body(strides, parts, dests, n_out, *refs):
    got, outs, totals = refs[0], refs[1 : 1 + n_out], refs[1 + n_out :]
    me = lax.axis_index("ctx")
    shift, per = 0, 1
    for stride, step in strides[1:]:
        shift = shift * step + (me // stride) % step
        per *= step
    at, used = 0, 0
    for height, total, (dest, many) in zip(parts, totals, dests):
        rows = height // per
        for i in range(got.shape[0]):
            for b in range(per):
                begin = pl.multiple_of((i * per + (b ^ shift)) * rows, 8)
                piece = got[i, at + b * rows : at + (b + 1) * rows, :]
                total[pl.ds(begin, rows), :] = piece.astype(F32)
        at += height
        dest(total, outs[used : used + many])
        Order.leave(*range(used, used + many))
        used += many


WIDTH = 512


def cut_up(chunks, heights, strides, at, size, riders=()):
    stride, step = strides[at]
    total = sum(heights) // step
    more = riders[0].shape[0] if riders else 0
    n_in = sum(len(c) for c in chunks)
    pieces = call(
        functools.partial(middle_body, [len(c) for c in chunks], stride, step, n_in, len(riders)),
        [((total, WIDTH), F32)] + [((total + more, WIDTH), BF)] * (step - 1),
        [t for c in chunks for t in c] + far(riders),
        scratch=[((h, WIDTH), F32) for h in heights],
    )
    return pieces[:1] + [swap(pieces[j], j * stride, size) for j in range(1, step)]


def spread(done, strides, at, size):
    stride, step = strides[at]
    return [done] + [swap(done, j * stride, size) for j in range(1, step)]


def settle(terms):
    return call(add_body, [(terms[0].shape, BF)], terms)[0]


def add_body(*refs):
    rows = refs[-1].shape[0]
    value = refs[0][:rows, :].astype(F32)
    for ref in refs[1:-1]:
        value = value + ref[:rows, :].astype(F32)
    refs[-1][...] = value.astype(refs[-1].dtype)


def early_dest(total, outs):
    down, tile = outs
    wide = down.shape[0]
    down[...] = total[:wide, :]
    tile[...] = total[wide : wide + tile.shape[0], :]


def both_final_body(strides, parts, got, tile, *refs):
    outs, totals = refs[:7], refs[7:]

    def main(total, outs):
        (up,) = outs
        half = up.shape[0]
        core = lax.axis_index("wsh")
        tiles = up.shape[1] // WIDTH
        for i in range(tiles):
            side, inner = i // (tiles // 2), i % (tiles // 2)
            at = (core if side == 0 else 1 - core) * (tiles // 2) + inner
            rows = tile[...] if i == 0 else total[(i - 1) * half : i * half, :]
            up[:, pl.ds(pl.multiple_of(at * WIDTH, WIDTH), WIDTH)] = rows

    dests = [(main, 1), (late_dest, 6)]
    final_body(strides, parts, dests, 7, got, *outs, *totals)


def late_dest(total, outs):
    out, query, kv, router, one, two = outs
    half = kv.shape[0]
    out[...] = total[:half, :]
    query[...] = total[half : 2 * half, :]
    step = half // 4
    at = 2 * half
    for j in range(4):
        kv[j * step : (j + 1) * step, :] = total[at : at + step, j * 128 : (j + 1) * 128]
    at += step
    router[...] = total[at : at + router.shape[0], :half]
    one[...] = total[at + 8 : at + 9, :half]
    two[...] = total[at + 8 : at + 9, half:]


def place_body(rest, *refs):
    place = lax.axis_index("ctx") // rest
    out = refs[-1]
    local = out.shape[1]
    for k, ref in enumerate(refs[:-1]):
        begin = ref.shape[0] - local
        out[place ^ k] = ref[begin:, :].astype(F32)


def on_device(
    tokens,
    routes,
    block_order,
    norm_gain1,
    router_w,
    query_w,
    kv_w,
    out_w,
    norm_gain2,
    up_w,
    down_w,
    cotangent,
):
    size = lax.axis_size("ctx")
    count, local, dim = tokens.shape
    rest = size // count
    place = lax.axis_index("ctx") // rest
    total = count * local
    experts = router_w.shape[1]
    head = kv_w.shape[1] // 2
    feed = up_w.shape[1]

    Order.last = None
    tall = dim // 2
    keys = 2 * head
    router_t = router_w.T
    routes_t = routes.transpose(0, 2, 1)

    def core():
        return lax.axis_index("wsh")

    def here():
        return lax.axis_index("ctx") // rest

    got = call(
        functools.partial(pack_all_body, count, rest),
        [((local + 8, dim), BF)] * (count - 1) + [((tall + 8, experts * head + keys + dim), BF)],
        far([tokens, routes_t, query_w, kv_w, router_t, out_w]),
        late=(2, 3, 4, 5),
        ahead=[Ahead(tokens, (local, dim), lambda r: r.at[here()]), Ahead(kv_w)]
        + [
            Ahead(cotangent, (local, dim), lambda r, k=k: r.at[here() ^ k])
            for k in range(1, count)
        ],
    )
    tok_pieces, (packed, tok_own, kv_own), cot_pieces = got[: count - 1], got[count - 1 : count + 2], got[count + 2 :]
    tok_x = [swap(tok_pieces[k - 1], k * rest, size) for k in range(1, count)]
    packed_x = trade(packed)
    gain_one, gain_two = after((norm_gain1, norm_gain2), packed)
    gains = jnp.stack([gain_one, gain_two])
    gains_x = trade(gains)

    steps = factors(rest)
    kv, normed, tok, gain_rows, wk, tails = call(
        functools.partial(keys_body, count, rest),
        [
            ((steps[0], total, keys), BF, 1),
            ((total, dim), BF, 1),
            ((total, dim), BF, 1),
            ((8, dim), F32, 1),
            ((dim, keys), BF, 1),
            ((8 * count, 128), F32),
        ],
        [tok_own, *tok_x, Far(routes_t), gains, gains_x, kv_own, packed_x],
    )
    stride = 1
    for i, step in enumerate(steps):
        if i > 0:
            kv = jnp.broadcast_to(kv[None], (step,) + kv.shape)
        kv = exchange(kv, stride, size).reshape(-1, total, keys)
        stride *= step
    cot_pieces = after(tuple(cot_pieces), normed)
    cot_x = [swap(cot_pieces[k - 1], k * rest, size) for k in range(1, count)]
    qt, normed_t, gates, gates_far, route, route_far, wq, wr, wo = call(
        functools.partial(project_body, count, experts, head),
        [
            ((TWO * head, total), BF, 1),
            ((dim, total), BF, 1),
            ((TWO, total), F32),
            ((TWO, total), F32, 1),
            ((8, total), F32),
            ((8, total), F32, 1),
            ((dim, experts * head), BF, 1),
            ((128, dim), F32, 1),
            ((experts * head, dim), BF, 1),
        ],
        [Far(normed), tails, *far([query_w, router_t, out_w]), packed_x],
        late=(2, 3, 4),
    )
    up_w2, down_w2, _ = lax.optimization_barrier((up_w, down_w, normed))
    up_x, down_x = trade(up_w2), trade(down_w2)
    span = rest * total
    wide = feed // 2

    def lanes(which):
        def view(ref):
            side = which()
            return ref.at[:, pl.ds(pl.multiple_of(side * wide, wide), wide)]

        return view

    att, logs, mixed, hidden, two, two_t, kv_far, cot_own, up_first = call(
        functools.partial(attend_body, count, rest, experts, head),
        [
            ((TWO * head, total), F32, 1),
            ((TWO, total), F32, 1),
            ((experts * head, total), BF, 1),
            ((total, dim), F32),
            ((total, dim), BF),
            ((dim, total), BF),
            ((rest, total, keys), BF, 1),
        ],
        [block_order, kv, Far(qt), gates, route, *far([tok, gain_rows, wo])],
        scratch=[((keys, span), BF)],
        smem=(0,),
        late=(5, 6, 7),
        ahead=[
            Ahead(cotangent, (local, dim), lambda r: r.at[here()]),
            Ahead(up_w, (tall, wide), lanes(lambda: 1 - core())),
        ],
    )

    tile = 256
    upper = wide * tall // dim
    layer, back_two, send_one, keep_one, cots, cots_far, send_up, up_second, down_own = call(
        functools.partial(feed_body, count, rest, True, tile),
        [
            ((total, dim), F32),
            ((total, dim), F32),
            ((wide, dim), BF),
            ((upper, dim), BF, 1),
            ((total, dim), BF),
            ((total, dim), BF, 1),
            ((upper, dim), BF),
        ],
        [two, two_t, cot_own, *cot_x, up_first, up_x, down_x, hidden],
        scratch=[((dim, wide), BF)],
        ahead=[Ahead(up_w, (tall, wide), lanes(core)), Ahead(down_w)],
    )
    recv_down, recv_up = trade(send_one), trade(send_up)
    *layer_pieces, back_two, keep_down, keep_two, send_two, cots, wo, gain_near, gates, route, att = call(
        functools.partial(feed_body, count, rest, False, tile),
        [((local, dim), F32, 1)]
        + [((local, dim), BF, 1)] * (count - 1)
        + [
            ((total, dim), F32),
            ((wide, dim), BF, 1),
            ((upper, dim), BF, 1),
            ((upper, dim), BF, 1),
        ],
        [two, two_t, cots, up_second, up_x, down_own, layer, back_two],
        scratch=[((dim, wide), BF), ((total, dim), F32)],
        ahead=[
            Ahead(a)
            for a in (cots_far, wo, gain_rows, gates_far, route_far, att)
        ],
    )
    recv_two = trade(send_two)
    layer_got = [layer_pieces[0]] + [swap(layer_pieces[k], k * rest, size) for k in range(1, count)]

    strides = []
    stride = 1
    for step in [*steps, count]:
        strides.append((stride, step))
        stride *= step
    last = len(strides) - 1
    unit = 8 * size
    first = strides[0][1]
    early_rows = -(-(wide + tall) // unit) * unit
    main_rows = -(-(2 * upper - tall) // unit) * unit
    small = tall // 4 + 16
    late_rows = -(-(small + 2 * tall) // unit) * unit

    def bulk(args, layout, height, ahead=()):
        pieces, *near = call(
            functools.partial(start_body, layout, True, 1, first, len(args)),
            [((first, height // first, WIDTH), BF)],
            args,
            scratch=[((8, WIDTH), F32)],
            ahead=ahead,
        )
        return exchange(pieces, 1, size), near

    def inner(terms, height, riders=()):
        height //= first
        for at in range(1, last + 1):
            more = riders if at == last else ()
            terms = cut_up([terms], [height], strides, at, size, more)
            height //= strides[at][1]
        return terms

    def outer(got):
        for at in reversed(range(1, last)):
            got = spread(jnp.concatenate(got, axis=0), strides, at, size)
        return got

    def ready(got, ahead=()):
        rows = got[0].shape[0]
        copies, *near = call(
            functools.partial(copies_body, [(0, rows)], len(got)),
            [((first, rows * len(got), WIDTH), BF)],
            got,
            ahead=ahead,
        )
        return exchange(copies, 1, size), near

    back_hidden, branch, grad_att, delta, logit, gain_two, early, kv_near, qt_near, logs_near = call(
        functools.partial(
            turn_start_body,
            count,
            rest,
            experts,
            head,
            [[(0, 0, wide), (1, 0, wide)], [(2, 0, tall), (3, 0, tall)]],
            first,
        ),
        [
            ((total, dim), F32, 1),
            ((total, dim), BF, 1),
            ((TWO * head, total), BF),
            ((TWO, total), F32),
            ((experts, total), F32, 1),
            ((8, dim), F32, 1),
            ((first, early_rows // first, WIDTH), BF),
        ],
        [
            hidden,
            back_two,
            cots,
            wo,
            gain_near,
            gates,
            route,
            att,
            Far(keep_down),
            recv_down,
            Far(keep_two),
            recv_up,
        ],
        late=(8, 10),
        ahead=[Ahead(a) for a in (kv_far, qt, logs)],
    )
    early = exchange(early, 1, size)
    split = steps[-1]
    share = span // split
    grad_q, *kv_terms = call(
        functools.partial(attend_back_body, count, rest, head, split),
        [((TWO * head, total), BF), ((share, keys), F32, 1)] + [((share, keys), BF, 1)] * (split - 1),
        [block_order, kv_near, qt_near, grad_att, logs_near, delta],
        scratch=[
            ((keys, span), BF),
            ((4, keys, total), BF),
            ((2, 2 * total, keys), BF),
            ((span, keys), F32),
            ((2, head, total), F32),
        ],
        smem=(0,),
        ahead=[Ahead(a) for a in (normed_t, route_far, mixed, branch, wq, wr, logit, tok)],
    )
    kv_terms, ahead = kv_terms[:split], kv_terms[split:]
    stride = rest
    for i, step in reversed(list(enumerate(steps))):
        stride //= step
        if i + 1 < len(steps):
            summed = functools.reduce(lambda a, b: a + b.astype(F32), terms)
            parts = summed.reshape(step, -1, keys)
            digit = (lax.axis_index("ctx") // stride) % step
            kv_terms = [pick(parts, digit ^ j) for j in range(step)]
        terms = [kv_terms[0]] + [
            swap(kv_terms[j].astype(BF), j * stride, size) for j in range(1, step)
        ]
    grad_q = after(grad_q, *layer_got[1:])
    keep_out, keep_query, send_main, back_part, unit_rows, scale_rows, routers, *near = call(
        functools.partial(query_body, experts, head),
        [
            ((tall, dim), BF, 1),
            ((tall, dim), BF, 1),
            ((2 * tall, dim), BF, 1),
            ((total, dim), F32),
            ((total, dim), F32),
            ((total, 128), F32),
            ((experts, dim), F32),
        ],
        [grad_q, *ahead],
        scratch=[((experts * head, total), BF)],
        ahead=[Ahead(a) for a in (normed_t, back_hidden, wk, gain_rows, gain_two, terms[0])],
    )
    *near, term = near
    *input_pieces, keep_late, send_late, keep_two, keep_one = call(
        functools.partial(unproject_body, count, len(terms)),
        [((local, dim), F32, 1)]
        + [((local, dim), BF, 1)] * (count - 1)
        + [((small, dim), F32, 1), ((small + 2 * tall, dim), BF)],
        [term, *terms[1:], back_part, unit_rows, scale_rows, routers, *near, Far(send_main)],
        scratch=[((8, dim), F32)],
        late=(len(terms) + 9,),
        ahead=[Ahead(a) for a in (keep_two, keep_one)],
    )
    recv_late = trade(send_late)
    main, _ = bulk(
        [keep_two, recv_up, keep_one, recv_two],
        [
            [(0, tall, upper - tall), (1, tall, upper - tall)],
            [(2, 0, upper), (3, 0, upper)],
        ],
        main_rows,
    )
    early_terms = inner([early], early_rows)
    pieces = call(
        functools.partial(
            start_body,
            [
                [(0, 0, tall), (1, 0, tall)],
                [(0, tall, tall), (2, 0, tall)],
                [(0, 2 * tall, small), (3, 0, small)],
            ],
            False,
            1,
            first,
            4,
        ),
        [((late_rows // first, WIDTH), F32)] + [((late_rows // first, WIDTH), BF)] * (first - 1),
        [recv_late, *far([keep_out, keep_query, keep_late])],
        scratch=[((late_rows, WIDTH), F32)],
    )
    late = pieces[:1] + [swap(pieces[j], j, size) for j in range(1, first)]
    early_got = outer(spread(settle(early_terms), strides, last, size))
    heights = [main_rows // first, late_rows // first]
    chunks = [[main], late]
    for at in range(1, last):
        chunks = [cut_up([c], [h], strides, at, size) for c, h in zip(chunks, heights)]
        heights = [h // strides[at][1] for h in heights]
    both_terms = cut_up(chunks, heights, strides, last, size)
    heights = [h // count for h in heights]
    early_last, _ = ready(early_got)
    both_got = spread(settle(both_terms), strides, last, size)
    slices = [(0, heights[0]), (heights[0], heights[1])]
    for stage in reversed(range(1, last)):
        moved = []
        for begin, h in slices:
            piece = jnp.concatenate([g[begin : begin + h] for g in both_got], axis=0)
            moved.append(spread(piece, strides, stage, size))
        both_got = [jnp.concatenate([m[j] for m in moved], axis=0) for j in range(strides[stage][1])]
        tops = [m[0].shape[0] for m in moved]
        slices = [(0, tops[0]), (tops[0], tops[1])]
    tall_rows = sum(h for _, h in slices) * len(both_got)
    (copies,) = call(
        functools.partial(copies_body, slices, len(both_got)),
        [((first, tall_rows, WIDTH), BF)],
        both_got,
    )
    both_last = exchange(copies, 1, size)
    input_pieces = after(tuple(input_pieces), both_got[0])
    input_got = [input_pieces[0]] + [swap(input_pieces[k], k * rest, size) for k in range(1, count)]
    (layer_out,) = call(
        functools.partial(place_body, rest),
        [((count, local, dim), F32, 1)],
        [Far(layer_got[0]), *layer_got[1:]],
    )
    grad_down, up_tile = call(
        functools.partial(final_body, strides, [early_rows // first], [(early_dest, 2)], 2),
        [((wide, dim), F32, 1), ((tall, WIDTH), F32)],
        [early_last],
        scratch=[((early_rows, WIDTH), F32)],
    )
    (input_grad,) = call(
        functools.partial(place_body, rest),
        [((count, local, dim), F32, 1)],
        [Far(input_got[0]), *input_got[1:]],
    )
    grad_up, grad_out, grad_query, grad_kv, grad_router, grad_one, grad_two = call(
        functools.partial(both_final_body, strides, [main_rows // first, late_rows // first]),
        [
            ((tall, feed), F32, 1),
            ((tall, dim), F32, 1),
            ((tall, experts * head), F32, 1),
            ((tall, keys), F32, 1),
            ((experts, tall), F32, 1),
            ((1, tall), F32, 1),
            ((1, tall), F32, 1),
        ],
        [both_last, up_tile],
        scratch=[((main_rows, WIDTH), F32), ((late_rows, WIDTH), F32)],
    )
    return (
        layer_out,
        input_grad,
        grad_one.reshape(tall),
        grad_router.T,
        grad_query,
        grad_kv,
        grad_out,
        grad_two.reshape(tall),
        grad_up,
        grad_down,
    )


def solution(mesh):
    placed = (
        P("wsh", "ctx", None),
        P("wsh", "ctx", None),
        P(),
        P("wsh"),
        P("wsh", None),
        P("wsh", None),
        P("wsh", None),
        P("wsh", None),
        P("wsh"),
        P("wsh", None),
        P("wsh", None),
        P("wsh", "ctx", None),
    )
    return jax.shard_map(
        on_device,
        mesh=mesh,
        in_specs=placed,
        out_specs=(
            P("wsh", "ctx", None),
            P("wsh", "ctx", None),
            P("wsh"),
            P("wsh", None),
            P("wsh", None),
            P("wsh", None),
            P("wsh", None),
            P("wsh"),
            P("wsh", None),
            P("wsh", None),
        ),
        check_vma=False,
    )
```

```python
import functools
import math

import jax
import jax.numpy as jnp
from jax import lax
from jax.experimental import pallas as pl
from jax.experimental.pallas import tpu as pltpu
from jax.sharding import PartitionSpec as P

BF = jnp.bfloat16
F32 = jnp.float32
I32 = jnp.int32
NONE = -1e30
TWO = 2


def factors(size):
    out = []
    while size > 1:
        step = 4 if size % 4 == 0 else 2
        out.append(step)
        size //= step
    return out


def swap(values, mask, size):
    return lax.ppermute(values, "ctx", [(i, i ^ mask) for i in range(size)])


def groups_of(stride, step, size):
    out = []
    for i in range(size):
        if (i // stride) % step == 0:
            out.append([i + j * stride for j in range(step)])
    return out


def exchange(parts, stride, size):
    step = parts.shape[0]
    groups = groups_of(stride, step, size)
    return lax.all_to_all(parts, "ctx", 0, 0, tiled=True, axis_index_groups=groups)


def trade(values):
    return lax.ppermute(values, "wsh", [(0, 1), (1, 0)])


def pick(parts, index):
    return lax.dynamic_index_in_dim(parts, index, 0, False)


def mm(a, b, left=1, right=0):
    return lax.dot_general(a, b, (((left,), (right,)), ((), ())), preferred_element_type=F32)


class Order:
    last = None
    rest = None
    leave = None


def after(value, *earlier):
    return lax.optimization_barrier((value, *earlier))[0]


class Far:
    def __init__(self, value):
        self.value = value


class Ahead:
    def __init__(self, value, shape=None, view=None):
        self.value, self.view = value, view
        self.shape = value.shape if shape is None else shape


def loading_body(body, plan, n_out, far_out, late, views, n_scratch, *refs):
    n_in, n_pre = len(plan), len(views)
    ins, pre_in = list(refs[:n_in]), refs[n_in : n_in + n_pre]
    at = n_in + n_pre
    outs, pre_out = list(refs[at : at + n_out]), refs[at + n_out : at + n_out + n_pre]
    at += n_out + n_pre
    own = refs[at : at + n_scratch]
    held, sems = refs[at + n_scratch : -1], refs[-1]
    first, second, ahead, slot = [], [], [], 0
    for i in range(n_in):
        if plan[i]:
            copy = pltpu.make_async_copy(ins[i], held[slot], sems.at[slot])
            (second if i in late else first).append(copy)
            ins[i] = held[slot]
            slot += 1
    leaving = {}
    for i in range(n_out):
        if far_out[i]:
            leaving[i] = pltpu.make_async_copy(held[slot], outs[i], sems.at[slot])
            outs[i] = held[slot]
            slot += 1
    for view, source, target in zip(views, pre_in, pre_out):
        source = source if view is None else view(source)
        ahead.append(pltpu.make_async_copy(source, target, sems.at[slot]))
        slot += 1
    for copy in first + second + ahead:
        copy.start()
    for copy in first:
        copy.wait()

    def rest():
        for copy in second:
            copy.wait()

    gone = []

    def leave(*which):
        for i in which:
            if far_out[i]:
                gone.append(i)
                leaving[i].start()

    Order.rest, Order.leave = rest, leave
    body(*ins, *outs, *own)
    leave(*[i for i in range(n_out) if i not in gone])
    for i in gone:
        leaving[i].wait()
    for copy in ahead:
        copy.wait()


def call(body, outs, args, scratch=(), smem=(), late=(), ahead=(), mib=14):
    whole = pl.BlockSpec(memory_space=pltpu.VMEM)
    scalars = pl.BlockSpec(memory_space=pltpu.SMEM)
    distant = pl.BlockSpec(memory_space=pltpu.HBM)
    plan = [isinstance(a, Far) for a in args]
    args = [
        pltpu.with_memory_space_constraint(a.value, pltpu.HBM) if isinstance(a, Far) else a
        for a in args
    ]
    far_out = [len(o) > 2 for o in outs]
    if Order.last is not None:
        args[0] = after(args[0], Order.last)
    held = [(a.shape, a.dtype) for a, far in zip(args, plan) if far]
    held += [o[:2] for o, far in zip(outs, far_out) if far]
    need = sum(math.prod(s) * jnp.dtype(d).itemsize for s, d in [*held, *scratch])
    run = pl.pallas_call(
        functools.partial(
            loading_body,
            body,
            plan,
            len(outs),
            far_out,
            late,
            [a.view for a in ahead],
            len(scratch),
        ),
        out_shape=[
            pltpu.HBM(o[0], o[1]) if far else jax.ShapeDtypeStruct(o[0], o[1])
            for o, far in zip(outs, far_out)
        ]
        + [jax.ShapeDtypeStruct(a.shape, a.value.dtype) for a in ahead],
        in_specs=[
            scalars if i in smem else distant if plan[i] else whole for i in range(len(args))
        ]
        + [distant] * len(ahead),
        out_specs=[distant if far else whole for far in far_out] + [whole] * len(ahead),
        scratch_shapes=[pltpu.VMEM(s, d) for s, d in [*scratch, *held]]
        + [pltpu.SemaphoreType.DMA((max(len(held) + len(ahead), 1),))],
        compiler_params=pltpu.CompilerParams(vmem_limit_bytes=(mib << 20) + need),
        cost_estimate=pl.CostEstimate(flops=1, bytes_accessed=1, transcendentals=0),
    )
    moved = [pltpu.with_memory_space_constraint(a.value, pltpu.HBM) for a in ahead]
    got = list(run(*args, *moved))
    Order.last = got[0]
    return got


def far(values):
    return [Far(v) for v in values]


def join(slots):
    half = slots[0].shape[0] // 2
    return jnp.concatenate([s[:half] for s in slots] + [s[half:] for s in slots], axis=0)


def slot_rows(rows, k, count):
    half = rows.shape[0] // (2 * count)
    low = k * half
    high = rows.shape[0] // 2 + k * half
    return jnp.concatenate([rows[low : low + half], rows[high : high + half]], axis=0)


def centred(rows):
    centre = rows - jnp.mean(rows, axis=-1, keepdims=True)
    scale = lax.rsqrt(jnp.mean(centre * centre, axis=-1, keepdims=True) + 1e-05)
    return centre * scale, scale


def fill(scratch, own, other, core):
    half = own.shape[0]
    scratch[pl.ds(pl.multiple_of(core * half, half), half), :] = own[...]
    scratch[pl.ds(pl.multiple_of((1 - core) * half, half), half), :] = other[...]


def pick_gain(own, other, which, core):
    a = own[which : which + 1, :].astype(F32)
    b = other[which : which + 1, :].astype(F32)
    first = jnp.where(core == 0, a, b)
    second = jnp.where(core == 0, b, a)
    return jnp.concatenate([first, second], axis=1)


def route_rows(pieces):
    lane = lax.broadcasted_iota(I32, (8, 128), 1)
    low = lane < 64
    rolled = [pltpu.roll(p, 64, 1) for p in pieces]
    count = len(pieces)
    front = [jnp.where(low, pieces[i], rolled[i + 1]) for i in range(0, count, 2)]
    back = [jnp.where(low, rolled[i], pieces[i + 1]) for i in range(0, count, 2)]
    return jnp.concatenate(front + back, axis=1)


def pack_body(count, rest, *refs):
    tok, routes = refs[:2]
    place = lax.axis_index("ctx") // rest
    local, dim = tok.shape[1:]
    for k, out in enumerate(refs[2:]):
        out[:local, :] = tok[place ^ (k + 1)]
        out[local:, :] = jnp.zeros((8, dim), BF)
        out[local : local + TWO, :128] = routes[place ^ (k + 1)].astype(F32).astype(BF)


def pack_all_body(count, rest, *refs):
    tok, routes, query, kv, router, out = refs[:6]
    pieces, packed = refs[6:-1], refs[-1]
    pack_body(count, rest, tok, routes, *pieces)
    Order.rest()
    half, cols = query.shape
    keys = kv.shape[1]
    packed[half:, :] = jnp.zeros((8, packed.shape[1]), BF)
    packed[:half, :cols] = query[...]
    packed[:half, cols : cols + keys] = kv[...]
    packed[:half, cols + keys :] = out[...]
    packed[half:, :half] = router[...]


def fill_router(wr, own, packed, core):
    half = own.shape[1]
    wr[...] = jnp.zeros_like(wr)
    experts = own.shape[0]
    mine = pl.ds(pl.multiple_of(core * half, half), half)
    theirs = pl.ds(pl.multiple_of((1 - core) * half, half), half)
    wr[:experts, mine] = own[...].astype(F32)
    wr[:experts, theirs] = packed[half:, :half].astype(F32)


def keys_body(count, rest, *refs):
    toks = refs[:count]
    routes, g_own, g_other, k_own, packed = refs[count : count + 5]
    kv_out, normed_out, tok_out, gain_out, wk, tail_out = refs[count + 5 :]
    core = lax.axis_index("wsh")
    place = lax.axis_index("ctx") // rest
    half = k_own.shape[0]
    local = toks[0].shape[0]
    keys = k_own.shape[1]
    cols = packed.shape[1] - keys - toks[0].shape[1]
    fill(wk, k_own, packed.at[:half, cols : cols + keys], core)
    rows = join([t[:local] for t in toks])
    tok_out[...] = rows
    Order.leave(2, 4)
    tail_out[...] = jnp.zeros_like(tail_out)
    tail_out[:TWO, :] = routes[place].astype(F32)
    for k in range(1, count):
        tail_out[8 * k : 8 * k + 8, :] = toks[k][local : local + 8, :128].astype(F32)
    rows = rows.astype(F32)
    unit, _ = centred(rows)
    gain_out[...] = jnp.zeros_like(gain_out)
    for which in range(TWO):
        gain_out[which : which + 1, :] = pick_gain(g_own, g_other, which, core)
    normed = (unit * gain_out[0:1, :]).astype(BF)
    normed_out[...] = normed
    Order.leave(1, 3)
    kv = mm(normed, wk[...]).astype(BF)
    for i in range(kv_out.shape[0]):
        kv_out[i] = kv


def project_body(count, experts, head, *refs):
    normed_ref, tails, q_own, r_own, o_own, packed = refs[:6]
    qt_out, nt_out, gate_out, gate_far, route_out, route_far, wq, wr, wo = refs[6:]
    core = lax.axis_index("wsh")
    half, cols = q_own.shape
    normed = normed_ref[...]
    nt_out[...] = normed.T
    Order.leave(1)
    Order.rest()
    fill(wq, q_own, packed.at[:half, :cols], core)
    fill_router(wr, r_own, packed, core)
    fill(wo, o_own, packed.at[:half, packed.shape[1] - o_own.shape[1] :], core)
    Order.leave(6, 7, 8)
    routes = route_rows([tails[8 * k : 8 * k + 8, :] for k in range(count)])
    route_out[...] = routes
    route_far[...] = routes
    logits = mm(wr[...].astype(BF), normed, 1, 1)
    queries = mm(wq[...], normed, 0, 1) * 0.125
    chosen = []
    for s in range(TWO):
        route = routes[s : s + 1]
        total = jnp.zeros((head, normed.shape[0]), F32)
        value = jnp.zeros((1, normed.shape[0]), F32)
        for e in range(experts):
            here = route == e
            total = jnp.where(here, queries[e * head : (e + 1) * head], total)
            value = jnp.where(here, logits[e : e + 1], value)
        qt_out[s * head : (s + 1) * head, :] = total.astype(BF)
        chosen.append(value)
    top = jnp.maximum(chosen[0], chosen[1])
    raised = [jnp.exp(c - top) for c in chosen]
    total = raised[0] + raised[1]
    gate_out[...] = jnp.concatenate([r / total for r in raised], axis=0)
    gate_far[...] = gate_out[...]


def places(order, count, rest, block, width, part):
    me = lax.axis_index("ctx")
    place, other = me // rest, me % rest
    size = count * rest
    lane = lax.broadcasted_iota(I32, (1, width), 1)
    out = jnp.zeros((1, width), I32)
    for k in range(count):
        first = order[(place ^ k) * rest + other]
        base = jnp.where(part == 0, first, 2 * size - 1 - first) * block
        out = jnp.where(lane // block == k, lane - k * block + base, out)
    return out


def key_bases(order, count, rest, block, chunk, part):
    me = lax.axis_index("ctx")
    place = me // rest
    size = count * rest
    out = []
    for k in range(count):
        first = order[(place ^ k) * rest + chunk]
        out.append((first if part == 0 else 2 * size - 1 - first) * block)
    return out


def masked(scores, gap, bases, block):
    parts = [
        jnp.where(gap <= -base, scores[k * block : (k + 1) * block], NONE)
        for k, base in enumerate(bases)
    ]
    return jnp.concatenate(parts, axis=0)


def scored(kv, side, h, gap, order, count, rest, block, chunk, half):
    first = mm(kv[:half], side)
    if h == 0:
        return masked(first, gap, key_bases(order, count, rest, block, chunk, 0), block)
    second = mm(kv[half:], side)
    second = masked(second, gap, key_bases(order, count, rest, block, chunk, 1), block)
    return jnp.concatenate([first, second], axis=0)


def turn_keys(kv, kv_turned):
    rows = kv.shape[1]
    for c in range(kv.shape[0]):
        kv_turned[:, c * rows : (c + 1) * rows] = kv[c].T


def both_slots(rows, head, cols):
    return jnp.concatenate([rows[s * head : (s + 1) * head, cols] for s in range(TWO)], axis=1)


def gap_rows(order, count, rest, block, half, h):
    gap = lax.broadcasted_iota(I32, (block, half), 0) - places(order, count, rest, block, half, h)
    return jnp.concatenate([gap] * TWO, axis=1)


def attend_body(count, rest, experts, head, *refs):
    order, kv_ref, qt, gates, routes = refs[:5]
    tok, gains, wo = refs[5:8]
    att_out, log_out, mixed_out, hidden_out, two_out, turned_out, kv_out, kv_turned = refs[8:]
    kv_out[...] = kv_ref[...]
    Order.leave(6)
    other = lax.axis_index("ctx") % rest
    total = qt.shape[1]
    half = total // 2
    block = half // count
    turn_keys(kv_ref, kv_turned)
    sides, gaps = [], []
    for h in range(2):
        side = both_slots(qt, head, slice(h * half, (h + 1) * half))
        sides.append(jnp.concatenate([side, jnp.zeros_like(side)], axis=0))
        gaps.append(gap_rows(order, count, rest, block, half, h))

    def step(turn, carry):
        chunk = turn ^ other
        at = pl.multiple_of(chunk * total, total)
        kv = kv_ref[chunk]
        scores = [
            scored(kv, sides[h], h, gaps[h], order, count, rest, block, chunk, half)
            for h in range(2)
        ]
        out = []
        for h in range(2):
            top, norm, summed = carry[h]
            fresh = jnp.maximum(top, jnp.max(scores[h], axis=0, keepdims=True))
            shares = jnp.exp(scores[h] - fresh)
            fade = jnp.exp(top - fresh)
            norm = norm * fade + jnp.sum(shares, axis=0, keepdims=True)
            values = kv_turned[head:, pl.ds(at, half * (h + 1))]
            out.append((fresh, norm, summed * fade + mm(values, shares.astype(BF))))
        return tuple(out)

    start = (
        jnp.full((1, TWO * half), NONE, F32),
        jnp.zeros((1, TWO * half), F32),
        jnp.zeros((head, TWO * half), F32),
    )
    done = lax.fori_loop(0, rest, step, (start, start), unroll=rest <= 4)
    for h in range(2):
        top, norm, summed = done[h]
        logs, attended = top + jnp.log(norm), summed / norm
        for s in range(TWO):
            here, cols = slice(h * half, (h + 1) * half), slice(s * half, (s + 1) * half)
            log_out[s : s + 1, here] = logs[:, cols]
            att_out[s * head : (s + 1) * head, here] = attended[:, cols]
    Order.rest()
    Order.leave(0, 1)
    for e in range(experts):
        part = jnp.zeros((head, total), F32)
        for s in range(TWO):
            gate = jnp.where(routes[s : s + 1] == e, gates[s : s + 1], 0.0)
            part = part + gate * att_out[s * head : (s + 1) * head, :]
        mixed_out[e * head : (e + 1) * head, :] = part.astype(BF)
    Order.leave(2)
    hidden = tok[...].astype(F32) + mm(mixed_out[...].T, wo[...])
    hidden_out[...] = hidden
    unit, _ = centred(hidden)
    two = (unit * gains[1:2, :]).astype(BF)
    two_out[...] = two
    turned_out[...] = two.T


def feed_body(count, rest, first, tile, *refs):
    two, turned = refs[:2]
    if first:
        slots = refs[2 : 2 + count]
        u_own, u_other, down, layer_in = refs[2 + count : 6 + count]
        layer_out, back_out, send, keep, cots, cot_far, send_up, up = refs[6 + count :]
    else:
        cots, u_own, u_other, down, layer_in, back_in = refs[2:8]
        outs = refs[8 : 12 + count]
        layer_pieces, back_out, keep_down, keep, send = outs[:count], *outs[count:]
        up, layer_out = refs[12 + count :]
    core = lax.axis_index("wsh")
    side = (1 - core) if first else core
    width = down.shape[0]
    half = u_own.shape[0]
    lanes = pl.ds(pl.multiple_of(side * width, width), width)
    up[pl.ds(pl.multiple_of(core * half, half), half), :] = u_own[...]
    up[pl.ds(pl.multiple_of((1 - core) * half, half), half), :] = u_other[:, lanes]
    if first:
        cots[...] = join([o[...] for o in slots])
        cot_far[...] = cots[...]
        Order.leave(5)
    layer_out[...] = layer_in[...]
    if first:
        back_out[...] = jnp.zeros_like(back_out)
    else:
        back_out[...] = back_in[...]
    mine = pl.ds(pl.multiple_of(core * half, half), half)
    theirs = pl.ds(pl.multiple_of((1 - core) * half, half), half)
    dim = up.shape[0]
    per = dim // tile

    def step(j, carry):
        cols = pl.ds(pl.multiple_of(j * tile, tile), tile)
        up_j = up[:, cols]
        down_j = down[cols, :]
        pre = mm(two[...], up_j)
        back = mm(cots[...], down_j, 1, 1)
        phi = 0.5 * (1.0 + lax.erf(pre * math.sqrt(0.5)))
        bell = jnp.exp(pre * pre * -0.5) * (1.0 / math.sqrt(2.0 * math.pi))
        act = (pre * phi).astype(BF)
        back_pre = (back * (phi + pre * bell)).astype(BF)
        layer_out[...] += mm(act, down_j)
        back_out[...] += mm(back_pre, up_j, 1, 1)
        grad = mm(act.T, cots[...]).astype(BF)
        grad_mine = mm(turned[mine, :], back_pre).astype(BF)
        grad_theirs = mm(turned[theirs, :], back_pre).astype(BF)
        rows = pl.ds(pl.multiple_of((j // per) * half, half), half)
        lane = pl.ds(pl.multiple_of((j % per) * tile, tile), tile)
        keep[rows, lane] = grad_mine
        if first:
            send[cols, :] = grad
            send_up[rows, lane] = grad_theirs
        else:
            keep_down[cols, :] = grad
            send[rows, lane] = grad_theirs
        return carry

    lax.fori_loop(0, width // tile, step, 0)
    if not first:
        for k in range(count):
            layer_pieces[k][...] = slot_rows(layer_out[...], k, count).astype(layer_pieces[k].dtype)


def turn_body(count, rest, experts, head, *refs):
    hidden, back_two, cot, wo, gain, gates, routes, att = refs[:8]
    back_hidden_out, branch_out, grad_att_out, delta_out, logit_out, gain_out = refs[8:]
    unit, scale = centred(hidden[...])
    back = back_two[...]
    side = back * gain[1:2, :]
    part = scale * (
        side
        - jnp.mean(side, axis=-1, keepdims=True)
        - unit * jnp.mean(side * unit, axis=-1, keepdims=True)
    )
    gain_out[...] = jnp.broadcast_to(jnp.sum(back * unit, axis=0, keepdims=True), gain_out.shape)
    back_hidden = cot[...].astype(F32) + part
    back_hidden_out[...] = back_hidden
    branch = back_hidden.astype(BF)
    branch_out[...] = branch
    Order.leave(0, 1, 5)
    back_mixed = mm(wo[...], branch, 1, 1)
    grads = []
    for s in range(TWO):
        total = jnp.zeros((head, branch.shape[0]), F32)
        for e in range(experts):
            total = jnp.where(routes[s : s + 1] == e, back_mixed[e * head : (e + 1) * head], total)
        att_s = att[s * head : (s + 1) * head, :]
        grads.append(jnp.sum(total * att_s, axis=0, keepdims=True))
        low = (gates[s : s + 1] * total).astype(BF)
        grad_att_out[s * head : (s + 1) * head, :] = low
        delta_out[s : s + 1, :] = jnp.sum(low.astype(F32) * att_s, axis=0, keepdims=True)
    mean = gates[0:1] * grads[0] + gates[1:2] * grads[1]
    row = lax.broadcasted_iota(I32, logit_out.shape, 0)
    logit = jnp.zeros(logit_out.shape, F32)
    for s in range(TWO):
        value = gates[s : s + 1] * (grads[s] - mean)
        logit = logit + jnp.where(row.astype(F32) == routes[s : s + 1], value, 0.0)
    logit_out[...] = logit


def turn_start_body(count, rest, experts, head, layout, step, *refs):
    ins, early, outs, pieces = refs[:8], refs[8:12], refs[12:18], refs[18]
    turn_body(count, rest, experts, head, *ins, *outs)
    Order.rest()
    start_body(layout, True, 1, step, len(early), *early, pieces, None)


def attend_back_body(count, rest, head, split, *refs):
    order, kv_ref, qt, grad_att, logs, delta, grad_q_out = refs[:7]
    outs = refs[7 : 7 + split]
    kv_turned, sides, turned, grad_kv, grad_q = refs[7 + split :]
    total = qt.shape[1]
    half = total // 2
    block = half // count
    wide = TWO * half
    turn_keys(kv_ref, kv_turned)
    blank = jnp.zeros((head, wide), BF)
    for h in range(2):
        cols = slice(h * half, (h + 1) * half)
        q_side = jnp.concatenate([both_slots(qt, head, cols), blank], axis=0)
        g_side = jnp.concatenate([blank, both_slots(grad_att, head, cols)], axis=0)
        sides[2 * h], sides[2 * h + 1] = q_side, g_side
        turned[h, :wide, :], turned[h, wide:, :] = q_side.T, g_side.T
    grad_q[...] = jnp.zeros_like(grad_q)
    gaps = [gap_rows(order, count, rest, block, half, h) for h in range(2)]
    log_rows = [both_slots(logs, 1, slice(h * half, (h + 1) * half)) for h in range(2)]
    delta_rows = [both_slots(delta, 1, slice(h * half, (h + 1) * half)) for h in range(2)]

    def step(chunk, carry):
        at = pl.multiple_of(chunk * total, total)
        kv = kv_ref[chunk]
        grads = []
        for h in range(2):
            reach = half * (h + 1)
            scores = scored(
                kv, sides[2 * h], h, gaps[h], order, count, rest, block, chunk, half
            )
            shares = jnp.exp(scores - log_rows[h])
            back_shares = mm(kv[:reach], sides[2 * h + 1])
            back_scores = (shares * (back_shares - delta_rows[h])).astype(BF)
            both = jnp.concatenate([back_scores, shares.astype(BF)], axis=1)
            grads.append(mm(both, turned[h]))
            grad_q[h] += mm(kv_turned[:head, pl.ds(at, reach)], back_scores)
        grad_kv[pl.ds(at, half), :] = grads[0] + grads[1][:half]
        grad_kv[pl.ds(at + half, half), :] = grads[1][half:]
        return carry

    lax.fori_loop(0, rest, step, 0, unroll=rest <= 4)
    for h in range(2):
        for s in range(TWO):
            here, cols = slice(h * half, (h + 1) * half), slice(s * half, (s + 1) * half)
            grad_q_out[s * head : (s + 1) * head, here] = grad_q[h, :, cols].astype(BF)
    rows = outs[0].shape[0]
    digit = (lax.axis_index("ctx") % rest) // (rest // split)
    for i, out in enumerate(outs):
        begin = pl.multiple_of((digit ^ i) * rows, rows)
        out[...] = grad_kv[pl.ds(begin, rows), :].astype(out.dtype)


def query_body(experts, head, *refs):
    grad_q, normed_t, routes, mixed, branch, wq, wr, logit, tok = refs[:9]
    keep_out, keep, send, back_out, unit_out, scale_out, routers, bqt = refs[9:]
    core = lax.axis_index("wsh")
    total = grad_q.shape[1]
    for e in range(experts):
        part = jnp.zeros((head, total), F32)
        for s in range(TWO):
            value = grad_q[s * head : (s + 1) * head, :].astype(F32) * 0.125
            part = jnp.where(routes[s : s + 1] == e, value, part)
        bqt[e * head : (e + 1) * head, :] = part.astype(BF)
    back_q = bqt[...].T
    half = keep.shape[0]
    mine = pl.ds(pl.multiple_of(core * half, half), half)
    theirs = pl.ds(pl.multiple_of((1 - core) * half, half), half)
    send[:half, :] = mm(mixed[theirs, :], branch[...]).astype(BF)
    send[half:, :] = mm(normed_t[theirs, :], back_q).astype(BF)
    keep_out[...] = mm(mixed[mine, :], branch[...]).astype(BF)
    keep[...] = mm(normed_t[mine, :], back_q).astype(BF)
    parts = []
    left = logit[...]
    for _ in range(3):
        low = left.astype(BF)
        parts.append(low)
        left = left - low.astype(F32)
    routers[...] = parts_dot(parts, normed_t[...])
    back = mm(back_q, wq[...], 1, 1)
    wr_turned = wr[...].astype(BF)
    for low in parts:
        padded = jnp.concatenate([low.astype(F32), jnp.zeros((120, total), F32)], axis=0)
        back = back + mm(padded.T.astype(BF), wr_turned)
    back_out[...] = back
    unit, scale = centred(tok[...].astype(F32))
    unit_out[...] = unit
    scale_out[...] = jnp.broadcast_to(scale, scale_out.shape)


def unproject_body(count, terms, *refs):
    kv_terms = refs[:terms]
    back_part, unit_ref, scale_ref, routers, normed_t, back_hidden, wk, gain, gain_two, sent = refs[
        terms : terms + 10
    ]
    at = terms + 10
    pieces = refs[at : at + count]
    keep, send, gains = refs[at + count :]
    core = lax.axis_index("wsh")
    half = back_part.shape[1] // 2
    back_kv = kv_terms[0][...].astype(F32)
    for term in kv_terms[1:]:
        back_kv = back_kv + term[...].astype(F32)
    back_kv = back_kv.astype(BF)
    back = back_part[...] + mm(back_kv, wk[...], 1, 1)
    unit, scale = unit_ref[...], scale_ref[:, 0:1]
    side = back * gain[0:1, :]
    grad = back_hidden[...] + scale * (
        side
        - jnp.mean(side, axis=-1, keepdims=True)
        - unit * jnp.mean(side * unit, axis=-1, keepdims=True)
    )
    gains[0:1, :] = jnp.sum(back * unit, axis=0, keepdims=True)
    gains[1:2, :] = gain_two[0:1, :]
    step = half // 4
    experts = routers.shape[0]
    high = sent.shape[0]
    Order.rest()
    send[:high, :] = sent[...]
    for out, which in ((keep, core), (send.at[high:, :], 1 - core)):
        mine = pl.ds(pl.multiple_of(which * half, half), half)
        grad_k = mm(normed_t[mine, :], back_kv).astype(out.dtype)
        for j in range(4):
            out[:step, j * 128 : (j + 1) * 128] = grad_k[j * step : (j + 1) * step]
        blank = jnp.zeros((experts, half), F32)
        out[step : step + 8, :] = jnp.concatenate([routers[:, mine], blank], axis=1).astype(out.dtype)
        gain_pair = jnp.concatenate([gains[0:1, mine], gains[1:2, mine]], axis=1)
        out[step + 8 :, :] = jnp.broadcast_to(gain_pair, (8, 2 * half)).astype(out.dtype)
    for k in range(count):
        pieces[k][...] = slot_rows(grad, k, count).astype(pieces[k].dtype)


def parts_dot(parts, normed_t):
    out = None
    for low in parts:
        value = mm(low, normed_t, 1, 1)
        out = value if out is None else out + value
    return out


def sum_layout(layout, ins, total):
    at = 0
    for terms in layout:
        height = terms[0][2]
        value = None
        for index, begin, count in terms:
            part = ins[index][begin : begin + count, :].astype(F32)
            value = part if value is None else value + part
        total[at : at + height, :] = value
        at += height
    if at < total.shape[0]:
        total[at:, :] = jnp.zeros((total.shape[0] - at, total.shape[1]), F32)


def cut_rows(total, outs, stride, step):
    rows = outs[0].shape[0]
    digit = (lax.axis_index("ctx") // stride) % step
    for j in range(step):
        begin = pl.multiple_of((digit ^ j) * rows, 8)
        outs[j][...] = total[pl.ds(begin, rows), :].astype(outs[j].dtype)


def start_body(layout, whole, stride, step, n_in, *refs):
    ins, outs, total = refs[:n_in], refs[n_in:-1], refs[-1]
    if whole:
        rows = outs[0].shape[1]
        at = 0
        for terms in layout:
            height, done = terms[0][2], 0
            while done < height:
                j, low = (at + done) // rows, (at + done) % rows
                take = min(height - done, rows - low)
                value = None
                for index, begin, _ in terms:
                    part = ins[index][begin + done : begin + done + take, :].astype(F32)
                    value = part if value is None else value + part
                outs[0][j, low : low + take, :] = value.astype(BF)
                done += take
            at += height
        while at < rows * step:
            j, low = at // rows, at % rows
            outs[0][j, low:, :] = jnp.zeros((rows - low, outs[0].shape[2]), BF)
            at += rows - low
    else:
        sum_layout(layout, ins, total)
        cut_rows(total, outs, stride, step)


def terms_of(ref):
    return [ref.at[j] for j in range(ref.shape[0])] if len(ref.shape) == 3 else [ref]


def middle_body(chunks, stride, step, n_in, riders, *refs):
    ins, riding = refs[:n_in], refs[n_in : n_in + riders]
    refs = refs[n_in + riders :]
    outs, totals = refs[:step], refs[step:]
    digit = (lax.axis_index("ctx") // stride) % step
    at, low = 0, 0
    for count, total in zip(chunks, totals):
        value = None
        for ref in ins[at : at + count]:
            for term in terms_of(ref):
                part = term[...].astype(F32)
                value = part if value is None else value + part
        total[...] = value
        rows = total.shape[0] // step
        for j in range(step):
            begin = pl.multiple_of((digit ^ j) * rows, 8)
            outs[j][low : low + rows, :] = total[pl.ds(begin, rows), :].astype(outs[j].dtype)
        low += rows
        at += count
    for j in range(1, step if riders else 1):
        outs[j][low:, :] = riding[j - 1][...]


def copies_body(slices, n_in, *refs):
    ins, out = refs[:n_in], refs[-1]
    for j in range(out.shape[0]):
        at = 0
        for begin, rows in slices:
            for ref in ins:
                out[j, at : at + rows, :] = ref[begin : begin + rows, :]
                at += rows


def final_body(strides, parts, dests, n_out, *refs):
    got, outs, totals = refs[0], refs[1 : 1 + n_out], refs[1 + n_out :]
    me = lax.axis_index("ctx")
    shift, per = 0, 1
    for stride, step in strides[1:]:
        shift = shift * step + (me // stride) % step
        per *= step
    at, used = 0, 0
    for height, total, (dest, many) in zip(parts, totals, dests):
        rows = height // per
        swapped = isinstance(got, tuple)
        digit = me % strides[0][1] if swapped else 0
        for i in range(len(got) if swapped else got.shape[0]):
            for b in range(per):
                begin = pl.multiple_of(((i ^ digit) * per + (b ^ shift)) * rows, 8)
                source = got[i].at[0] if swapped else got.at[i]
                piece = source[at + b * rows : at + (b + 1) * rows, :]
                total[pl.ds(begin, rows), :] = piece.astype(F32)
        at += height
        dest(total, outs[used : used + many])
        Order.leave(*range(used, used + many))
        used += many


WIDTH = 512


def cut_up(chunks, heights, strides, at, size, riders=()):
    stride, step = strides[at]
    total = sum(heights) // step
    more = riders[0].shape[0] if riders else 0
    n_in = sum(len(c) for c in chunks)
    pieces = call(
        functools.partial(middle_body, [len(c) for c in chunks], stride, step, n_in, len(riders)),
        [((total, WIDTH), F32)] + [((total + more, WIDTH), BF)] * (step - 1),
        [t for c in chunks for t in c] + far(riders),
        scratch=[((h, WIDTH), F32) for h in heights],
    )
    return pieces[:1] + [swap(pieces[j], j * stride, size) for j in range(1, step)]


def spread(done, strides, at, size):
    stride, step = strides[at]
    return [done] + [swap(done, j * stride, size) for j in range(1, step)]


def settle(terms):
    return call(add_body, [(terms[0].shape, BF)], terms)[0]


def add_body(*refs):
    rows = refs[-1].shape[0]
    value = refs[0][:rows, :].astype(F32)
    for ref in refs[1:-1]:
        value = value + ref[:rows, :].astype(F32)
    refs[-1][...] = value.astype(refs[-1].dtype)


def early_dest(total, outs):
    down, tile = outs
    wide = down.shape[0]
    down[...] = total[:wide, :]
    tile[...] = total[wide : wide + tile.shape[0], :]


def both_final_body(strides, parts, n_in, *refs):
    got, tile = refs[:n_in], refs[n_in]
    outs, totals = refs[n_in + 1 : n_in + 8], refs[n_in + 8 :]

    def main(total, outs):
        (up,) = outs
        half = up.shape[0]
        core = lax.axis_index("wsh")
        tiles = up.shape[1] // WIDTH
        for i in range(tiles):
            side, inner = i // (tiles // 2), i % (tiles // 2)
            at = (core if side == 0 else 1 - core) * (tiles // 2) + inner
            rows = tile[...] if i == 0 else total[(i - 1) * half : i * half, :]
            up[:, pl.ds(pl.multiple_of(at * WIDTH, WIDTH), WIDTH)] = rows

    dests = [(main, 1), (late_dest, 6)]
    final_body(strides, parts, dests, 7, got, *outs, *totals)


def late_dest(total, outs):
    out, query, kv, router, one, two = outs
    half = kv.shape[0]
    out[...] = total[:half, :]
    query[...] = total[half : 2 * half, :]
    step = half // 4
    at = 2 * half
    for j in range(4):
        kv[j * step : (j + 1) * step, :] = total[at : at + step, j * 128 : (j + 1) * 128]
    at += step
    router[...] = total[at : at + router.shape[0], :half]
    one[...] = total[at + 8 : at + 9, :half]
    two[...] = total[at + 8 : at + 9, half:]


def place_body(rest, *refs):
    place = lax.axis_index("ctx") // rest
    out = refs[-1]
    local = out.shape[1]
    for k, ref in enumerate(refs[:-1]):
        begin = ref.shape[0] - local
        out[place ^ k] = ref[begin:, :].astype(F32)


def close_body(rest, count, strides, parts, n_in, *refs):
    main, moved = refs[: n_in + 1], refs[n_in + 1 : n_in + 1 + count]
    outs, totals = refs[n_in + 1 + count : n_in + 9 + count], refs[n_in + 9 + count :]
    place_body(rest, *moved, outs[7])
    Order.leave(7)
    both_final_body(strides, parts, n_in, *main, *outs[:7], *totals)


def on_device(
    tokens,
    routes,
    block_order,
    norm_gain1,
    router_w,
    query_w,
    kv_w,
    out_w,
    norm_gain2,
    up_w,
    down_w,
    cotangent,
):
    size = lax.axis_size("ctx")
    count, local, dim = tokens.shape
    rest = size // count
    place = lax.axis_index("ctx") // rest
    total = count * local
    experts = router_w.shape[1]
    head = kv_w.shape[1] // 2
    feed = up_w.shape[1]

    Order.last = None
    tall = dim // 2
    keys = 2 * head
    router_t = router_w.T
    routes_t = routes.transpose(0, 2, 1)

    def core():
        return lax.axis_index("wsh")

    def here():
        return lax.axis_index("ctx") // rest

    got = call(
        functools.partial(pack_all_body, count, rest),
        [((local + 8, dim), BF)] * (count - 1) + [((tall + 8, experts * head + keys + dim), BF)],
        far([tokens, routes_t, query_w, kv_w, router_t, out_w]),
        late=(2, 3, 4, 5),
        ahead=[Ahead(tokens, (local, dim), lambda r: r.at[here()]), Ahead(kv_w)]
        + [
            Ahead(cotangent, (local, dim), lambda r, k=k: r.at[here() ^ k])
            for k in range(1, count)
        ],
    )
    tok_pieces, (packed, tok_own, kv_own), cot_pieces = got[: count - 1], got[count - 1 : count + 2], got[count + 2 :]
    tok_x = [swap(tok_pieces[k - 1], k * rest, size) for k in range(1, count)]
    packed_x = trade(packed)
    gain_one, gain_two = after((norm_gain1, norm_gain2), packed)
    gains = jnp.stack([gain_one, gain_two])
    gains_x = trade(gains)

    steps = factors(rest)
    kv, normed, tok, gain_rows, wk, tails = call(
        functools.partial(keys_body, count, rest),
        [
            ((steps[0], total, keys), BF, 1),
            ((total, dim), BF, 1),
            ((total, dim), BF, 1),
            ((8, dim), F32, 1),
            ((dim, keys), BF, 1),
            ((8 * count, 128), F32),
        ],
        [tok_own, *tok_x, Far(routes_t), gains, gains_x, kv_own, packed_x],
    )
    stride = 1
    for i, step in enumerate(steps):
        if i > 0:
            kv = jnp.broadcast_to(kv[None], (step,) + kv.shape)
        kv = exchange(kv, stride, size).reshape(-1, total, keys)
        stride *= step
    cot_pieces = after(tuple(cot_pieces), normed)
    cot_x = [swap(cot_pieces[k - 1], k * rest, size) for k in range(1, count)]
    qt, normed_t, gates, gates_far, route, route_far, wq, wr, wo = call(
        functools.partial(project_body, count, experts, head),
        [
            ((TWO * head, total), BF, 1),
            ((dim, total), BF, 1),
            ((TWO, total), F32),
            ((TWO, total), F32, 1),
            ((8, total), F32),
            ((8, total), F32, 1),
            ((dim, experts * head), BF, 1),
            ((128, dim), F32, 1),
            ((experts * head, dim), BF, 1),
        ],
        [Far(normed), tails, *far([query_w, router_t, out_w]), packed_x],
        late=(2, 3, 4),
    )
    up_w2, down_w2, _ = lax.optimization_barrier((up_w, down_w, normed))
    up_x, down_x = trade(up_w2), trade(down_w2)
    span = rest * total
    wide = feed // 2

    def lanes(which):
        def view(ref):
            side = which()
            return ref.at[:, pl.ds(pl.multiple_of(side * wide, wide), wide)]

        return view

    att, logs, mixed, hidden, two, two_t, kv_far, cot_own, up_first = call(
        functools.partial(attend_body, count, rest, experts, head),
        [
            ((TWO * head, total), F32, 1),
            ((TWO, total), F32, 1),
            ((experts * head, total), BF, 1),
            ((total, dim), F32),
            ((total, dim), BF),
            ((dim, total), BF),
            ((rest, total, keys), BF, 1),
        ],
        [block_order, kv, Far(qt), gates, route, *far([tok, gain_rows, wo])],
        scratch=[((keys, span), BF)],
        smem=(0,),
        late=(5, 6, 7),
        ahead=[
            Ahead(cotangent, (local, dim), lambda r: r.at[here()]),
            Ahead(up_w, (tall, wide), lanes(lambda: 1 - core())),
        ],
    )

    tile = 256
    upper = wide * tall // dim
    layer, back_two, send_one, keep_one, cots, cots_far, send_up, up_second, down_own = call(
        functools.partial(feed_body, count, rest, True, tile),
        [
            ((total, dim), F32),
            ((total, dim), F32),
            ((wide, dim), BF),
            ((upper, dim), BF, 1),
            ((total, dim), BF),
            ((total, dim), BF, 1),
            ((upper, dim), BF),
        ],
        [two, two_t, cot_own, *cot_x, up_first, up_x, down_x, hidden],
        scratch=[((dim, wide), BF)],
        ahead=[Ahead(up_w, (tall, wide), lanes(core)), Ahead(down_w)],
    )
    recv_down, recv_up = trade(send_one), trade(send_up)
    *layer_pieces, back_two, keep_down, keep_two, send_two, cots, wo, gain_near, gates, route, att = call(
        functools.partial(feed_body, count, rest, False, tile),
        [((local, dim), F32, 1)]
        + [((local, dim), BF, 1)] * (count - 1)
        + [
            ((total, dim), F32),
            ((wide, dim), BF, 1),
            ((upper, dim), BF, 1),
            ((upper, dim), BF, 1),
        ],
        [two, two_t, cots, up_second, up_x, down_own, layer, back_two],
        scratch=[((dim, wide), BF), ((total, dim), F32)],
        ahead=[
            Ahead(a)
            for a in (cots_far, wo, gain_rows, gates_far, route_far, att)
        ],
    )
    recv_two = trade(send_two)
    layer_got = [layer_pieces[0]] + [swap(layer_pieces[k], k * rest, size) for k in range(1, count)]

    strides = []
    stride = 1
    for step in [*steps, count]:
        strides.append((stride, step))
        stride *= step
    last = len(strides) - 1
    unit = 8 * size
    first = strides[0][1]
    early_rows = -(-(wide + tall) // unit) * unit
    main_rows = -(-(2 * upper - tall) // unit) * unit
    small = tall // 4 + 16
    late_rows = -(-(small + 2 * tall) // unit) * unit

    def bulk(args, layout, height, ahead=()):
        pieces, *near = call(
            functools.partial(start_body, layout, True, 1, first, len(args)),
            [((first, height // first, WIDTH), BF)],
            args,
            scratch=[((8, WIDTH), F32)],
            ahead=ahead,
        )
        return exchange(pieces, 1, size), near

    def inner(terms, height, riders=()):
        height //= first
        for at in range(1, last + 1):
            more = riders if at == last else ()
            terms = cut_up([terms], [height], strides, at, size, more)
            height //= strides[at][1]
        return terms

    def outer(got):
        for at in reversed(range(1, last)):
            got = spread(jnp.concatenate(got, axis=0), strides, at, size)
        return got

    def ready(got, ahead=()):
        rows = got[0].shape[0]
        copies, *near = call(
            functools.partial(copies_body, [(0, rows)], len(got)),
            [((first, rows * len(got), WIDTH), BF)],
            got,
            ahead=ahead,
        )
        return exchange(copies, 1, size), near

    back_hidden, branch, grad_att, delta, logit, gain_two, early, kv_near, qt_near, logs_near = call(
        functools.partial(
            turn_start_body,
            count,
            rest,
            experts,
            head,
            [[(0, 0, wide), (1, 0, wide)], [(2, 0, tall), (3, 0, tall)]],
            first,
        ),
        [
            ((total, dim), F32, 1),
            ((total, dim), BF, 1),
            ((TWO * head, total), BF),
            ((TWO, total), F32),
            ((experts, total), F32, 1),
            ((8, dim), F32, 1),
            ((first, early_rows // first, WIDTH), BF),
        ],
        [
            hidden,
            back_two,
            cots,
            wo,
            gain_near,
            gates,
            route,
            att,
            Far(keep_down),
            recv_down,
            Far(keep_two),
            recv_up,
        ],
        late=(8, 10),
        ahead=[Ahead(a) for a in (kv_far, qt, logs)],
    )
    early = exchange(early, 1, size)
    split = steps[-1]
    share = span // split
    grad_q, *kv_terms = call(
        functools.partial(attend_back_body, count, rest, head, split),
        [((TWO * head, total), BF), ((share, keys), F32, 1)] + [((share, keys), BF, 1)] * (split - 1),
        [block_order, kv_near, qt_near, grad_att, logs_near, delta],
        scratch=[
            ((keys, span), BF),
            ((4, keys, total), BF),
            ((2, 2 * total, keys), BF),
            ((span, keys), F32),
            ((2, head, total), F32),
        ],
        smem=(0,),
        ahead=[Ahead(a) for a in (normed_t, route_far, mixed, branch, wq, wr, logit, tok)],
    )
    kv_terms, ahead = kv_terms[:split], kv_terms[split:]
    stride = rest
    for i, step in reversed(list(enumerate(steps))):
        stride //= step
        if i + 1 < len(steps):
            summed = functools.reduce(lambda a, b: a + b.astype(F32), terms)
            parts = summed.reshape(step, -1, keys)
            digit = (lax.axis_index("ctx") // stride) % step
            kv_terms = [pick(parts, digit ^ j) for j in range(step)]
        terms = [kv_terms[0]] + [
            swap(kv_terms[j].astype(BF), j * stride, size) for j in range(1, step)
        ]
    grad_q = after(grad_q, *layer_got[1:])
    keep_out, keep_query, send_main, back_part, unit_rows, scale_rows, routers, *near = call(
        functools.partial(query_body, experts, head),
        [
            ((tall, dim), BF, 1),
            ((tall, dim), BF, 1),
            ((2 * tall, dim), BF, 1),
            ((total, dim), F32),
            ((total, dim), F32),
            ((total, 128), F32),
            ((experts, dim), F32),
        ],
        [grad_q, *ahead],
        scratch=[((experts * head, total), BF)],
        ahead=[Ahead(a) for a in (normed_t, back_hidden, wk, gain_rows, gain_two, terms[0])],
    )
    *near, term = near
    *input_pieces, keep_late, send_late, keep_two, keep_one = call(
        functools.partial(unproject_body, count, len(terms)),
        [((local, dim), F32, 1)]
        + [((local, dim), BF, 1)] * (count - 1)
        + [((small, dim), F32, 1), ((small + 2 * tall, dim), BF)],
        [term, *terms[1:], back_part, unit_rows, scale_rows, routers, *near, Far(send_main)],
        scratch=[((8, dim), F32)],
        late=(len(terms) + 9,),
        ahead=[Ahead(a) for a in (keep_two, keep_one)],
    )
    recv_late = trade(send_late)
    main, _ = bulk(
        [keep_two, recv_up, keep_one, recv_two],
        [
            [(0, tall, upper - tall), (1, tall, upper - tall)],
            [(2, 0, upper), (3, 0, upper)],
        ],
        main_rows,
    )
    early_terms = inner([early], early_rows)
    pieces = call(
        functools.partial(
            start_body,
            [
                [(0, 0, tall), (1, 0, tall)],
                [(0, tall, tall), (2, 0, tall)],
                [(0, 2 * tall, small), (3, 0, small)],
            ],
            False,
            1,
            first,
            4,
        ),
        [((late_rows // first, WIDTH), F32)] + [((late_rows // first, WIDTH), BF)] * (first - 1),
        [recv_late, *far([keep_out, keep_query, keep_late])],
        scratch=[((late_rows, WIDTH), F32)],
    )
    late = pieces[:1] + [swap(pieces[j], j, size) for j in range(1, first)]
    early_got = outer(spread(settle(early_terms), strides, last, size))
    heights = [main_rows // first, late_rows // first]
    chunks = [[main], late]
    for at in range(1, last):
        chunks = [cut_up([c], [h], strides, at, size) for c, h in zip(chunks, heights)]
        heights = [h // strides[at][1] for h in heights]
    both_terms = cut_up(chunks, heights, strides, last, size)
    heights = [h // count for h in heights]
    (layer_out,) = call(
        functools.partial(place_body, rest),
        [((count, local, dim), F32, 1)],
        [Far(layer_got[0]), *far(layer_got[1:])],
    )
    early_last, _ = ready(early_got)
    both_got = spread(settle(both_terms), strides, last, size)
    slices = [(0, heights[0]), (heights[0], heights[1])]
    for stage in reversed(range(1, last)):
        moved = []
        for begin, h in slices:
            piece = jnp.concatenate([g[begin : begin + h] for g in both_got], axis=0)
            moved.append(spread(piece, strides, stage, size))
        both_got = [jnp.concatenate([m[j] for m in moved], axis=0) for j in range(strides[stage][1])]
        tops = [m[0].shape[0] for m in moved]
        slices = [(0, tops[0]), (tops[0], tops[1])]
    tall_rows = sum(h for _, h in slices) * len(both_got)
    (both_own,) = call(
        functools.partial(copies_body, slices, len(both_got)),
        [((1, tall_rows, WIDTH), BF)],
        both_got,
    )
    both_last = spread(both_own, strides, 0, size)
    input_pieces = after(tuple(input_pieces), both_got[0])
    moved = {k: swap(input_pieces[k], k * rest, size) for k in reversed(range(1, count))}
    input_got = [input_pieces[0]] + [moved[k] for k in range(1, count)]
    grad_down, up_tile = call(
        functools.partial(final_body, strides, [early_rows // first], [(early_dest, 2)], 2),
        [((wide, dim), F32, 1), ((tall, WIDTH), F32)],
        [early_last],
        scratch=[((early_rows, WIDTH), F32)],
    )
    grad_up, grad_out, grad_query, grad_kv, grad_router, grad_one, grad_two, input_grad = call(
        functools.partial(
            close_body,
            rest,
            count,
            strides,
            [main_rows // first, late_rows // first],
            len(both_last),
        ),
        [
            ((tall, feed), F32, 1),
            ((tall, dim), F32, 1),
            ((tall, experts * head), F32, 1),
            ((tall, keys), F32, 1),
            ((experts, tall), F32, 1),
            ((1, tall), F32, 1),
            ((1, tall), F32, 1),
            ((count, local, dim), F32, 1),
        ],
        [*both_last, up_tile, *input_got],
        scratch=[((main_rows, WIDTH), F32), ((late_rows, WIDTH), F32)],
    )
    return (
        layer_out,
        input_grad,
        grad_one.reshape(tall),
        grad_router.T,
        grad_query,
        grad_kv,
        grad_out,
        grad_two.reshape(tall),
        grad_up,
        grad_down,
    )


def solution(mesh):
    placed = (
        P("wsh", "ctx", None),
        P("wsh", "ctx", None),
        P(),
        P("wsh"),
        P("wsh", None),
        P("wsh", None),
        P("wsh", None),
        P("wsh", None),
        P("wsh"),
        P("wsh", None),
        P("wsh", None),
        P("wsh", "ctx", None),
    )
    return jax.shard_map(
        on_device,
        mesh=mesh,
        in_specs=placed,
        out_specs=(
            P("wsh", "ctx", None),
            P("wsh", "ctx", None),
            P("wsh"),
            P("wsh", None),
            P("wsh", None),
            P("wsh", None),
            P("wsh", None),
            P("wsh"),
            P("wsh", None),
            P("wsh", None),
        ),
        check_vma=False,
    )
```

```python
import functools
import math

import jax
import jax.numpy as jnp
from jax import lax
from jax.experimental import pallas as pl
from jax.experimental.pallas import tpu as pltpu
from jax.sharding import PartitionSpec as P

BF = jnp.bfloat16
F32 = jnp.float32
I32 = jnp.int32
NONE = -1e30
TWO = 2


def factors(size):
    out = []
    while size > 1:
        step = 4 if size % 4 == 0 else 2
        out.append(step)
        size //= step
    return out


def swap(values, mask, size):
    return lax.ppermute(values, "ctx", [(i, i ^ mask) for i in range(size)])


def groups_of(stride, step, size):
    out = []
    for i in range(size):
        if (i // stride) % step == 0:
            out.append([i + j * stride for j in range(step)])
    return out


def exchange(parts, stride, size):
    step = parts.shape[0]
    groups = groups_of(stride, step, size)
    return lax.all_to_all(parts, "ctx", 0, 0, tiled=True, axis_index_groups=groups)


def trade(values):
    return lax.ppermute(values, "wsh", [(0, 1), (1, 0)])


def pick(parts, index):
    return lax.dynamic_index_in_dim(parts, index, 0, False)


def mm(a, b, left=1, right=0):
    return lax.dot_general(a, b, (((left,), (right,)), ((), ())), preferred_element_type=F32)


class Order:
    last = None
    rest = None
    leave = None


def after(value, *earlier):
    return lax.optimization_barrier((value, *earlier))[0]


class Far:
    def __init__(self, value):
        self.value = value


class Ahead:
    def __init__(self, value, shape=None, view=None):
        self.value, self.view = value, view
        self.shape = value.shape if shape is None else shape


def loading_body(body, plan, n_out, far_out, late, views, n_scratch, *refs):
    n_in, n_pre = len(plan), len(views)
    ins, pre_in = list(refs[:n_in]), refs[n_in : n_in + n_pre]
    at = n_in + n_pre
    outs, pre_out = list(refs[at : at + n_out]), refs[at + n_out : at + n_out + n_pre]
    at += n_out + n_pre
    own = refs[at : at + n_scratch]
    held, sems = refs[at + n_scratch : -1], refs[-1]
    first, second, ahead, slot = [], [], [], 0
    for i in range(n_in):
        if plan[i]:
            copy = pltpu.make_async_copy(ins[i], held[slot], sems.at[slot])
            (second if i in late else first).append(copy)
            ins[i] = held[slot]
            slot += 1
    leaving = {}
    for i in range(n_out):
        if far_out[i]:
            leaving[i] = pltpu.make_async_copy(held[slot], outs[i], sems.at[slot])
            outs[i] = held[slot]
            slot += 1
    for view, source, target in zip(views, pre_in, pre_out):
        source = source if view is None else view(source)
        ahead.append(pltpu.make_async_copy(source, target, sems.at[slot]))
        slot += 1
    for copy in first + second + ahead:
        copy.start()
    for copy in first:
        copy.wait()

    def rest():
        for copy in second:
            copy.wait()

    gone = []

    def leave(*which):
        for i in which:
            if far_out[i]:
                gone.append(i)
                leaving[i].start()

    Order.rest, Order.leave = rest, leave
    body(*ins, *outs, *own)
    leave(*[i for i in range(n_out) if i not in gone])
    for i in gone:
        leaving[i].wait()
    for copy in ahead:
        copy.wait()


def call(body, outs, args, scratch=(), smem=(), late=(), ahead=(), mib=14):
    whole = pl.BlockSpec(memory_space=pltpu.VMEM)
    scalars = pl.BlockSpec(memory_space=pltpu.SMEM)
    distant = pl.BlockSpec(memory_space=pltpu.HBM)
    plan = [isinstance(a, Far) for a in args]
    args = [
        pltpu.with_memory_space_constraint(a.value, pltpu.HBM) if isinstance(a, Far) else a
        for a in args
    ]
    far_out = [len(o) > 2 for o in outs]
    if Order.last is not None:
        args[0] = after(args[0], Order.last)
    held = [(a.shape, a.dtype) for a, far in zip(args, plan) if far]
    held += [o[:2] for o, far in zip(outs, far_out) if far]
    need = sum(math.prod(s) * jnp.dtype(d).itemsize for s, d in [*held, *scratch])
    run = pl.pallas_call(
        functools.partial(
            loading_body,
            body,
            plan,
            len(outs),
            far_out,
            late,
            [a.view for a in ahead],
            len(scratch),
        ),
        out_shape=[
            pltpu.HBM(o[0], o[1]) if far else jax.ShapeDtypeStruct(o[0], o[1])
            for o, far in zip(outs, far_out)
        ]
        + [jax.ShapeDtypeStruct(a.shape, a.value.dtype) for a in ahead],
        in_specs=[
            scalars if i in smem else distant if plan[i] else whole for i in range(len(args))
        ]
        + [distant] * len(ahead),
        out_specs=[distant if far else whole for far in far_out] + [whole] * len(ahead),
        scratch_shapes=[pltpu.VMEM(s, d) for s, d in [*scratch, *held]]
        + [pltpu.SemaphoreType.DMA((max(len(held) + len(ahead), 1),))],
        compiler_params=pltpu.CompilerParams(vmem_limit_bytes=(mib << 20) + need),
        cost_estimate=pl.CostEstimate(flops=1, bytes_accessed=1, transcendentals=0),
    )
    moved = [pltpu.with_memory_space_constraint(a.value, pltpu.HBM) for a in ahead]
    got = list(run(*args, *moved))
    Order.last = got[0]
    return got


def far(values):
    return [Far(v) for v in values]


def join(slots):
    half = slots[0].shape[0] // 2
    return jnp.concatenate([s[:half] for s in slots] + [s[half:] for s in slots], axis=0)


def slot_rows(rows, k, count):
    half = rows.shape[0] // (2 * count)
    low = k * half
    high = rows.shape[0] // 2 + k * half
    return jnp.concatenate([rows[low : low + half], rows[high : high + half]], axis=0)


def centred(rows):
    centre = rows - jnp.mean(rows, axis=-1, keepdims=True)
    scale = lax.rsqrt(jnp.mean(centre * centre, axis=-1, keepdims=True) + 1e-05)
    return centre * scale, scale


def fill(scratch, own, other, core):
    half = own.shape[0]
    scratch[pl.ds(pl.multiple_of(core * half, half), half), :] = own[...]
    scratch[pl.ds(pl.multiple_of((1 - core) * half, half), half), :] = other[...]


def pick_gain(own, other, which, core):
    a = own[which : which + 1, :].astype(F32)
    b = other[which : which + 1, :].astype(F32)
    first = jnp.where(core == 0, a, b)
    second = jnp.where(core == 0, b, a)
    return jnp.concatenate([first, second], axis=1)


def route_rows(pieces):
    lane = lax.broadcasted_iota(I32, (8, 128), 1)
    low = lane < 64
    rolled = [pltpu.roll(p, 64, 1) for p in pieces]
    count = len(pieces)
    front = [jnp.where(low, pieces[i], rolled[i + 1]) for i in range(0, count, 2)]
    back = [jnp.where(low, rolled[i], pieces[i + 1]) for i in range(0, count, 2)]
    return jnp.concatenate(front + back, axis=1)


def pack_body(count, rest, *refs):
    tok, routes = refs[:2]
    place = lax.axis_index("ctx") // rest
    local, dim = tok.shape[1:]
    for k, out in enumerate(refs[2:]):
        out[:local, :] = tok[place ^ (k + 1)]
        out[local:, :] = jnp.zeros((8, dim), BF)
        out[local : local + TWO, :128] = routes[place ^ (k + 1)].astype(F32).astype(BF)


def pack_all_body(count, rest, *refs):
    tok, routes, query, kv, router, out = refs[:6]
    pieces, packed = refs[6:-1], refs[-1]
    pack_body(count, rest, tok, routes, *pieces)
    Order.rest()
    half, cols = query.shape
    keys = kv.shape[1]
    packed[half:, :] = jnp.zeros((8, packed.shape[1]), BF)
    packed[:half, :cols] = query[...]
    packed[:half, cols : cols + keys] = kv[...]
    packed[:half, cols + keys :] = out[...]
    packed[half:, :half] = router[...]


def fill_router(wr, own, packed, core):
    half = own.shape[1]
    wr[...] = jnp.zeros_like(wr)
    experts = own.shape[0]
    mine = pl.ds(pl.multiple_of(core * half, half), half)
    theirs = pl.ds(pl.multiple_of((1 - core) * half, half), half)
    wr[:experts, mine] = own[...].astype(F32)
    wr[:experts, theirs] = packed[half:, :half].astype(F32)


def keys_body(count, rest, *refs):
    toks = refs[:count]
    routes, g_own, g_other, k_own, packed = refs[count : count + 5]
    kv_out, normed_out, tok_out, gain_out, wk, tail_out = refs[count + 5 :]
    core = lax.axis_index("wsh")
    place = lax.axis_index("ctx") // rest
    half = k_own.shape[0]
    local = toks[0].shape[0]
    keys = k_own.shape[1]
    cols = packed.shape[1] - keys - toks[0].shape[1]
    fill(wk, k_own, packed.at[:half, cols : cols + keys], core)
    rows = join([t[:local] for t in toks])
    tok_out[...] = rows
    Order.leave(2, 4)
    tail_out[...] = jnp.zeros_like(tail_out)
    tail_out[:TWO, :] = routes[place].astype(F32)
    for k in range(1, count):
        tail_out[8 * k : 8 * k + 8, :] = toks[k][local : local + 8, :128].astype(F32)
    rows = rows.astype(F32)
    unit, _ = centred(rows)
    gain_out[...] = jnp.zeros_like(gain_out)
    for which in range(TWO):
        gain_out[which : which + 1, :] = pick_gain(g_own, g_other, which, core)
    normed = (unit * gain_out[0:1, :]).astype(BF)
    normed_out[...] = normed
    Order.leave(1, 3)
    kv = mm(normed, wk[...]).astype(BF)
    for i in range(kv_out.shape[0]):
        kv_out[i] = kv


def project_body(count, experts, head, *refs):
    normed_ref, tails, q_own, r_own, o_own, packed = refs[:6]
    qt_out, nt_out, gate_out, gate_far, route_out, route_far, wq, wr, wo = refs[6:]
    core = lax.axis_index("wsh")
    half, cols = q_own.shape
    normed = normed_ref[...]
    nt_out[...] = normed.T
    Order.leave(1)
    Order.rest()
    fill(wq, q_own, packed.at[:half, :cols], core)
    fill_router(wr, r_own, packed, core)
    fill(wo, o_own, packed.at[:half, packed.shape[1] - o_own.shape[1] :], core)
    Order.leave(6, 7, 8)
    routes = route_rows([tails[8 * k : 8 * k + 8, :] for k in range(count)])
    route_out[...] = routes
    route_far[...] = routes
    logits = mm(wr[...].astype(BF), normed, 1, 1)
    queries = mm(wq[...], normed, 0, 1) * 0.125
    chosen = []
    for s in range(TWO):
        route = routes[s : s + 1]
        total = jnp.zeros((head, normed.shape[0]), F32)
        value = jnp.zeros((1, normed.shape[0]), F32)
        for e in range(experts):
            here = route == e
            total = jnp.where(here, queries[e * head : (e + 1) * head], total)
            value = jnp.where(here, logits[e : e + 1], value)
        qt_out[s * head : (s + 1) * head, :] = total.astype(BF)
        chosen.append(value)
    top = jnp.maximum(chosen[0], chosen[1])
    raised = [jnp.exp(c - top) for c in chosen]
    total = raised[0] + raised[1]
    gate_out[...] = jnp.concatenate([r / total for r in raised], axis=0)
    gate_far[...] = gate_out[...]


def places(order, count, rest, block, width, part):
    me = lax.axis_index("ctx")
    place, other = me // rest, me % rest
    size = count * rest
    lane = lax.broadcasted_iota(I32, (1, width), 1)
    out = jnp.zeros((1, width), I32)
    for k in range(count):
        first = order[(place ^ k) * rest + other]
        base = jnp.where(part == 0, first, 2 * size - 1 - first) * block
        out = jnp.where(lane // block == k, lane - k * block + base, out)
    return out


def key_bases(order, count, rest, block, chunk, part):
    me = lax.axis_index("ctx")
    place = me // rest
    size = count * rest
    out = []
    for k in range(count):
        first = order[(place ^ k) * rest + chunk]
        out.append((first if part == 0 else 2 * size - 1 - first) * block)
    return out


def masked(scores, gap, bases, block):
    parts = [
        jnp.where(gap <= -base, scores[k * block : (k + 1) * block], NONE)
        for k, base in enumerate(bases)
    ]
    return jnp.concatenate(parts, axis=0)


def scored(kv, side, h, gap, order, count, rest, block, chunk, half):
    first = mm(kv[:half], side)
    if h == 0:
        return masked(first, gap, key_bases(order, count, rest, block, chunk, 0), block)
    second = mm(kv[half:], side)
    second = masked(second, gap, key_bases(order, count, rest, block, chunk, 1), block)
    return jnp.concatenate([first, second], axis=0)


def turn_keys(kv, kv_turned):
    rows = kv.shape[1]
    for c in range(kv.shape[0]):
        kv_turned[:, c * rows : (c + 1) * rows] = kv[c].T


def both_slots(rows, head, cols):
    return jnp.concatenate([rows[s * head : (s + 1) * head, cols] for s in range(TWO)], axis=1)


def gap_rows(order, count, rest, block, half, h):
    gap = lax.broadcasted_iota(I32, (block, half), 0) - places(order, count, rest, block, half, h)
    return jnp.concatenate([gap] * TWO, axis=1)


def attend_body(count, rest, experts, head, *refs):
    order, kv_ref, qt, gates, routes = refs[:5]
    tok, gains, wo = refs[5:8]
    att_out, log_out, mixed_out, hidden_out, two_out, turned_out, kv_out, kv_turned = refs[8:]
    kv_out[...] = kv_ref[...]
    Order.leave(6)
    other = lax.axis_index("ctx") % rest
    total = qt.shape[1]
    half = total // 2
    block = half // count
    turn_keys(kv_ref, kv_turned)
    sides, gaps = [], []
    for h in range(2):
        side = both_slots(qt, head, slice(h * half, (h + 1) * half))
        sides.append(jnp.concatenate([side, jnp.zeros_like(side)], axis=0))
        gaps.append(gap_rows(order, count, rest, block, half, h))

    def step(turn, carry):
        chunk = turn ^ other
        at = pl.multiple_of(chunk * total, total)
        kv = kv_ref[chunk]
        scores = [
            scored(kv, sides[h], h, gaps[h], order, count, rest, block, chunk, half)
            for h in range(2)
        ]
        out = []
        for h in range(2):
            top, norm, summed = carry[h]
            fresh = jnp.maximum(top, jnp.max(scores[h], axis=0, keepdims=True))
            shares = jnp.exp(scores[h] - fresh)
            fade = jnp.exp(top - fresh)
            norm = norm * fade + jnp.sum(shares, axis=0, keepdims=True)
            values = kv_turned[head:, pl.ds(at, half * (h + 1))]
            out.append((fresh, norm, summed * fade + mm(values, shares.astype(BF))))
        return tuple(out)

    start = (
        jnp.full((1, TWO * half), NONE, F32),
        jnp.zeros((1, TWO * half), F32),
        jnp.zeros((head, TWO * half), F32),
    )
    done = lax.fori_loop(0, rest, step, (start, start), unroll=rest <= 4)
    for h in range(2):
        top, norm, summed = done[h]
        logs, attended = top + jnp.log(norm), summed / norm
        for s in range(TWO):
            here, cols = slice(h * half, (h + 1) * half), slice(s * half, (s + 1) * half)
            log_out[s : s + 1, here] = logs[:, cols]
            att_out[s * head : (s + 1) * head, here] = attended[:, cols]
    Order.rest()
    Order.leave(0, 1)
    for e in range(experts):
        part = jnp.zeros((head, total), F32)
        for s in range(TWO):
            gate = jnp.where(routes[s : s + 1] == e, gates[s : s + 1], 0.0)
            part = part + gate * att_out[s * head : (s + 1) * head, :]
        mixed_out[e * head : (e + 1) * head, :] = part.astype(BF)
    Order.leave(2)
    hidden = tok[...].astype(F32) + mm(mixed_out[...].T, wo[...])
    hidden_out[...] = hidden
    unit, _ = centred(hidden)
    two = (unit * gains[1:2, :]).astype(BF)
    two_out[...] = two
    turned_out[...] = two.T


def feed_body(count, rest, first, tile, *refs):
    two, turned = refs[:2]
    if first:
        slots = refs[2 : 2 + count]
        u_own, u_other, down, layer_in = refs[2 + count : 6 + count]
        layer_out, back_out, send, keep, cots, cot_far, send_up, up = refs[6 + count :]
    else:
        cots, u_own, u_other, down, layer_in, back_in = refs[2:8]
        outs = refs[8 : 12 + count]
        layer_pieces, back_out, keep_down, keep, send = outs[:count], *outs[count:]
        up, layer_out = refs[12 + count :]
    core = lax.axis_index("wsh")
    side = (1 - core) if first else core
    width = down.shape[0]
    half = u_own.shape[0]
    lanes = pl.ds(pl.multiple_of(side * width, width), width)
    up[pl.ds(pl.multiple_of(core * half, half), half), :] = u_own[...]
    up[pl.ds(pl.multiple_of((1 - core) * half, half), half), :] = u_other[:, lanes]
    if first:
        cots[...] = join([o[...] for o in slots])
        cot_far[...] = cots[...]
        Order.leave(5)
    layer_out[...] = layer_in[...]
    if first:
        back_out[...] = jnp.zeros_like(back_out)
    else:
        back_out[...] = back_in[...]
    mine = pl.ds(pl.multiple_of(core * half, half), half)
    theirs = pl.ds(pl.multiple_of((1 - core) * half, half), half)
    dim = up.shape[0]
    per = dim // tile

    def products(j):
        cols = slice(j * tile, (j + 1) * tile)
        return mm(two[...], up[:, cols]), mm(cots[...], down[cols, :], 1, 1)

    steps = width // tile
    ready = products(0)
    for j in range(steps):
        cols = slice(j * tile, (j + 1) * tile)
        pre, back = ready
        if j + 1 < steps:
            ready = products(j + 1)
        phi = 0.5 * (1.0 + lax.erf(pre * math.sqrt(0.5)))
        bell = jnp.exp(pre * pre * -0.5) * (1.0 / math.sqrt(2.0 * math.pi))
        act = (pre * phi).astype(BF)
        back_pre = (back * (phi + pre * bell)).astype(BF)
        layer_out[...] += mm(act, down[cols, :])
        back_out[...] += mm(back_pre, up[:, cols], 1, 1)
        grad = mm(act.T, cots[...]).astype(BF)
        grad_mine = mm(turned[mine, :], back_pre).astype(BF)
        grad_theirs = mm(turned[theirs, :], back_pre).astype(BF)
        rows = slice((j // per) * half, (j // per + 1) * half)
        lane = slice((j % per) * tile, (j % per + 1) * tile)
        keep[rows, lane] = grad_mine
        if first:
            send[cols, :] = grad
            send_up[rows, lane] = grad_theirs
        else:
            keep_down[cols, :] = grad
            send[rows, lane] = grad_theirs
    if not first:
        for k in range(count):
            layer_pieces[k][...] = slot_rows(layer_out[...], k, count).astype(layer_pieces[k].dtype)


def turn_body(count, rest, experts, head, *refs):
    hidden, back_two, cot, wo, gain, gates, routes, att = refs[:8]
    back_hidden_out, branch_out, grad_att_out, delta_out, logit_out, gain_out = refs[8:]
    unit, scale = centred(hidden[...])
    back = back_two[...]
    side = back * gain[1:2, :]
    part = scale * (
        side
        - jnp.mean(side, axis=-1, keepdims=True)
        - unit * jnp.mean(side * unit, axis=-1, keepdims=True)
    )
    gain_out[...] = jnp.broadcast_to(jnp.sum(back * unit, axis=0, keepdims=True), gain_out.shape)
    back_hidden = cot[...].astype(F32) + part
    back_hidden_out[...] = back_hidden
    branch = back_hidden.astype(BF)
    branch_out[...] = branch
    Order.leave(0, 1, 5)
    back_mixed = mm(wo[...], branch, 1, 1)
    grads = []
    for s in range(TWO):
        total = jnp.zeros((head, branch.shape[0]), F32)
        for e in range(experts):
            total = jnp.where(routes[s : s + 1] == e, back_mixed[e * head : (e + 1) * head], total)
        att_s = att[s * head : (s + 1) * head, :]
        grads.append(jnp.sum(total * att_s, axis=0, keepdims=True))
        low = (gates[s : s + 1] * total).astype(BF)
        grad_att_out[s * head : (s + 1) * head, :] = low
        delta_out[s : s + 1, :] = jnp.sum(low.astype(F32) * att_s, axis=0, keepdims=True)
    mean = gates[0:1] * grads[0] + gates[1:2] * grads[1]
    row = lax.broadcasted_iota(I32, logit_out.shape, 0)
    logit = jnp.zeros(logit_out.shape, F32)
    for s in range(TWO):
        value = gates[s : s + 1] * (grads[s] - mean)
        logit = logit + jnp.where(row.astype(F32) == routes[s : s + 1], value, 0.0)
    logit_out[...] = logit


def turn_start_body(count, rest, experts, head, layout, step, *refs):
    ins, early, outs, pieces = refs[:8], refs[8:12], refs[12:18], refs[18]
    turn_body(count, rest, experts, head, *ins, *outs)
    Order.rest()
    start_body(layout, True, 1, step, len(early), *early, pieces, None)


def attend_back_body(count, rest, head, split, *refs):
    order, kv_ref, qt, grad_att, logs, delta, grad_q_out = refs[:7]
    outs = refs[7 : 7 + split]
    kv_turned, sides, turned, grad_kv, grad_q = refs[7 + split :]
    total = qt.shape[1]
    half = total // 2
    block = half // count
    wide = TWO * half
    turn_keys(kv_ref, kv_turned)
    blank = jnp.zeros((head, wide), BF)
    for h in range(2):
        cols = slice(h * half, (h + 1) * half)
        q_side = jnp.concatenate([both_slots(qt, head, cols), blank], axis=0)
        g_side = jnp.concatenate([blank, both_slots(grad_att, head, cols)], axis=0)
        sides[2 * h], sides[2 * h + 1] = q_side, g_side
        turned[h, :wide, :], turned[h, wide:, :] = q_side.T, g_side.T
    grad_q[...] = jnp.zeros_like(grad_q)
    gaps = [gap_rows(order, count, rest, block, half, h) for h in range(2)]
    log_rows = [both_slots(logs, 1, slice(h * half, (h + 1) * half)) for h in range(2)]
    delta_rows = [both_slots(delta, 1, slice(h * half, (h + 1) * half)) for h in range(2)]

    def step(chunk, carry):
        at = pl.multiple_of(chunk * total, total)
        kv = kv_ref[chunk]
        grads = []
        for h in range(2):
            reach = half * (h + 1)
            scores = scored(
                kv, sides[2 * h], h, gaps[h], order, count, rest, block, chunk, half
            )
            shares = jnp.exp(scores - log_rows[h])
            back_shares = mm(kv[:reach], sides[2 * h + 1])
            back_scores = (shares * (back_shares - delta_rows[h])).astype(BF)
            both = jnp.concatenate([back_scores, shares.astype(BF)], axis=1)
            grads.append(mm(both, turned[h]))
            grad_q[h] += mm(kv_turned[:head, pl.ds(at, reach)], back_scores)
        grad_kv[pl.ds(at, half), :] = grads[0] + grads[1][:half]
        grad_kv[pl.ds(at + half, half), :] = grads[1][half:]
        return carry

    lax.fori_loop(0, rest, step, 0, unroll=rest <= 4)
    for h in range(2):
        for s in range(TWO):
            here, cols = slice(h * half, (h + 1) * half), slice(s * half, (s + 1) * half)
            grad_q_out[s * head : (s + 1) * head, here] = grad_q[h, :, cols].astype(BF)
    rows = outs[0].shape[0]
    digit = (lax.axis_index("ctx") % rest) // (rest // split)
    for i, out in enumerate(outs):
        begin = pl.multiple_of((digit ^ i) * rows, rows)
        out[...] = grad_kv[pl.ds(begin, rows), :].astype(out.dtype)


def query_body(experts, head, *refs):
    grad_q, normed_t, routes, mixed, branch, wq, wr, logit, tok = refs[:9]
    keep_out, keep, send, back_out, unit_out, scale_out, routers, bqt = refs[9:]
    core = lax.axis_index("wsh")
    total = grad_q.shape[1]
    for e in range(experts):
        part = jnp.zeros((head, total), F32)
        for s in range(TWO):
            value = grad_q[s * head : (s + 1) * head, :].astype(F32) * 0.125
            part = jnp.where(routes[s : s + 1] == e, value, part)
        bqt[e * head : (e + 1) * head, :] = part.astype(BF)
    back_q = bqt[...].T
    half = keep.shape[0]
    mine = pl.ds(pl.multiple_of(core * half, half), half)
    theirs = pl.ds(pl.multiple_of((1 - core) * half, half), half)
    send[:half, :] = mm(mixed[theirs, :], branch[...]).astype(BF)
    send[half:, :] = mm(normed_t[theirs, :], back_q).astype(BF)
    keep_out[...] = mm(mixed[mine, :], branch[...]).astype(BF)
    keep[...] = mm(normed_t[mine, :], back_q).astype(BF)
    parts = []
    left = logit[...]
    for _ in range(3):
        low = left.astype(BF)
        parts.append(low)
        left = left - low.astype(F32)
    routers[...] = parts_dot(parts, normed_t[...])
    back = mm(back_q, wq[...], 1, 1)
    wr_turned = wr[...].astype(BF)
    for low in parts:
        padded = jnp.concatenate([low.astype(F32), jnp.zeros((120, total), F32)], axis=0)
        back = back + mm(padded.T.astype(BF), wr_turned)
    back_out[...] = back
    unit, scale = centred(tok[...].astype(F32))
    unit_out[...] = unit
    scale_out[...] = jnp.broadcast_to(scale, scale_out.shape)


def unproject_body(count, terms, *refs):
    kv_terms = refs[:terms]
    back_part, unit_ref, scale_ref, routers, normed_t, back_hidden, wk, gain, gain_two, sent = refs[
        terms : terms + 10
    ]
    at = terms + 10
    pieces = refs[at : at + count]
    keep, send, gains = refs[at + count :]
    core = lax.axis_index("wsh")
    half = back_part.shape[1] // 2
    back_kv = kv_terms[0][...].astype(F32)
    for term in kv_terms[1:]:
        back_kv = back_kv + term[...].astype(F32)
    back_kv = back_kv.astype(BF)
    back = back_part[...] + mm(back_kv, wk[...], 1, 1)
    unit, scale = unit_ref[...], scale_ref[:, 0:1]
    side = back * gain[0:1, :]
    grad = back_hidden[...] + scale * (
        side
        - jnp.mean(side, axis=-1, keepdims=True)
        - unit * jnp.mean(side * unit, axis=-1, keepdims=True)
    )
    gains[0:1, :] = jnp.sum(back * unit, axis=0, keepdims=True)
    gains[1:2, :] = gain_two[0:1, :]
    step = half // 4
    experts = routers.shape[0]
    high = sent.shape[0]
    Order.rest()
    send[:high, :] = sent[...]
    for out, which in ((keep, core), (send.at[high:, :], 1 - core)):
        mine = pl.ds(pl.multiple_of(which * half, half), half)
        grad_k = mm(normed_t[mine, :], back_kv).astype(out.dtype)
        for j in range(4):
            out[:step, j * 128 : (j + 1) * 128] = grad_k[j * step : (j + 1) * step]
        blank = jnp.zeros((experts, half), F32)
        out[step : step + 8, :] = jnp.concatenate([routers[:, mine], blank], axis=1).astype(out.dtype)
        gain_pair = jnp.concatenate([gains[0:1, mine], gains[1:2, mine]], axis=1)
        out[step + 8 :, :] = jnp.broadcast_to(gain_pair, (8, 2 * half)).astype(out.dtype)
    for k in range(count):
        pieces[k][...] = slot_rows(grad, k, count).astype(pieces[k].dtype)


def parts_dot(parts, normed_t):
    out = None
    for low in parts:
        value = mm(low, normed_t, 1, 1)
        out = value if out is None else out + value
    return out


def sum_layout(layout, ins, total):
    at = 0
    for terms in layout:
        height = terms[0][2]
        value = None
        for index, begin, count in terms:
            part = ins[index][begin : begin + count, :].astype(F32)
            value = part if value is None else value + part
        total[at : at + height, :] = value
        at += height
    if at < total.shape[0]:
        total[at:, :] = jnp.zeros((total.shape[0] - at, total.shape[1]), F32)


def cut_rows(total, outs, stride, step):
    rows = outs[0].shape[0]
    digit = (lax.axis_index("ctx") // stride) % step
    for j in range(step):
        begin = pl.multiple_of((digit ^ j) * rows, 8)
        outs[j][...] = total[pl.ds(begin, rows), :].astype(outs[j].dtype)


def start_body(layout, whole, stride, step, n_in, *refs):
    ins, outs, total = refs[:n_in], refs[n_in:-1], refs[-1]
    if whole:
        rows = outs[0].shape[1]
        at = 0
        for terms in layout:
            height, done = terms[0][2], 0
            while done < height:
                j, low = (at + done) // rows, (at + done) % rows
                take = min(height - done, rows - low)
                value = None
                for index, begin, _ in terms:
                    part = ins[index][begin + done : begin + done + take, :].astype(F32)
                    value = part if value is None else value + part
                outs[0][j, low : low + take, :] = value.astype(BF)
                done += take
            at += height
        while at < rows * step:
            j, low = at // rows, at % rows
            outs[0][j, low:, :] = jnp.zeros((rows - low, outs[0].shape[2]), BF)
            at += rows - low
    else:
        sum_layout(layout, ins, total)
        cut_rows(total, outs, stride, step)


def terms_of(ref):
    return [ref.at[j] for j in range(ref.shape[0])] if len(ref.shape) == 3 else [ref]


def middle_body(chunks, stride, step, n_in, riders, *refs):
    ins, riding = refs[:n_in], refs[n_in : n_in + riders]
    refs = refs[n_in + riders :]
    outs, totals = refs[:step], refs[step:]
    digit = (lax.axis_index("ctx") // stride) % step
    at, low = 0, 0
    for count, total in zip(chunks, totals):
        value = None
        for ref in ins[at : at + count]:
            for term in terms_of(ref):
                part = term[...].astype(F32)
                value = part if value is None else value + part
        total[...] = value
        rows = total.shape[0] // step
        for j in range(step):
            begin = pl.multiple_of((digit ^ j) * rows, 8)
            outs[j][low : low + rows, :] = total[pl.ds(begin, rows), :].astype(outs[j].dtype)
        low += rows
        at += count
    for j in range(1, step if riders else 1):
        outs[j][low:, :] = riding[j - 1][...]


def copies_body(slices, n_in, *refs):
    ins, out = refs[:n_in], refs[-1]
    for j in range(out.shape[0]):
        at = 0
        for begin, rows in slices:
            for ref in ins:
                out[j, at : at + rows, :] = ref[begin : begin + rows, :]
                at += rows


def final_body(strides, parts, dests, n_out, *refs):
    got, outs, totals = refs[0], refs[1 : 1 + n_out], refs[1 + n_out :]
    me = lax.axis_index("ctx")
    shift, per = 0, 1
    for stride, step in strides[1:]:
        shift = shift * step + (me // stride) % step
        per *= step
    at, used = 0, 0
    for height, total, (dest, many) in zip(parts, totals, dests):
        rows = height // per
        swapped = isinstance(got, tuple)
        digit = me % strides[0][1] if swapped else 0
        for i in range(len(got) if swapped else got.shape[0]):
            for b in range(per):
                begin = pl.multiple_of(((i ^ digit) * per + (b ^ shift)) * rows, 8)
                source = got[i].at[0] if swapped else got.at[i]
                piece = source[at + b * rows : at + (b + 1) * rows, :]
                total[pl.ds(begin, rows), :] = piece.astype(F32)
        at += height
        dest(total, outs[used : used + many])
        Order.leave(*range(used, used + many))
        used += many


WIDTH = 512


def cut_up(chunks, heights, strides, at, size, riders=()):
    stride, step = strides[at]
    total = sum(heights) // step
    more = riders[0].shape[0] if riders else 0
    n_in = sum(len(c) for c in chunks)
    pieces = call(
        functools.partial(middle_body, [len(c) for c in chunks], stride, step, n_in, len(riders)),
        [((total, WIDTH), F32)] + [((total + more, WIDTH), BF)] * (step - 1),
        [t for c in chunks for t in c] + far(riders),
        scratch=[((h, WIDTH), F32) for h in heights],
    )
    return pieces[:1] + [swap(pieces[j], j * stride, size) for j in range(1, step)]


def spread(done, strides, at, size):
    stride, step = strides[at]
    return [done] + [swap(done, j * stride, size) for j in range(1, step)]


def settle(terms):
    return call(add_body, [(terms[0].shape, BF)], terms)[0]


def add_body(*refs):
    rows = refs[-1].shape[0]
    value = refs[0][:rows, :].astype(F32)
    for ref in refs[1:-1]:
        value = value + ref[:rows, :].astype(F32)
    refs[-1][...] = value.astype(refs[-1].dtype)


def early_dest(total, outs):
    down, tile = outs
    wide = down.shape[0]
    down[...] = total[:wide, :]
    tile[...] = total[wide : wide + tile.shape[0], :]


def both_final_body(strides, parts, n_in, *refs):
    got, tile = refs[:n_in], refs[n_in]
    outs, totals = refs[n_in + 1 : n_in + 8], refs[n_in + 8 :]

    def main(total, outs):
        (up,) = outs
        half = up.shape[0]
        core = lax.axis_index("wsh")
        tiles = up.shape[1] // WIDTH
        for i in range(tiles):
            side, inner = i // (tiles // 2), i % (tiles // 2)
            at = (core if side == 0 else 1 - core) * (tiles // 2) + inner
            rows = tile[...] if i == 0 else total[(i - 1) * half : i * half, :]
            up[:, pl.ds(pl.multiple_of(at * WIDTH, WIDTH), WIDTH)] = rows

    dests = [(main, 1), (late_dest, 6)]
    final_body(strides, parts, dests, 7, got, *outs, *totals)


def late_dest(total, outs):
    out, query, kv, router, one, two = outs
    half = kv.shape[0]
    out[...] = total[:half, :]
    query[...] = total[half : 2 * half, :]
    step = half // 4
    at = 2 * half
    for j in range(4):
        kv[j * step : (j + 1) * step, :] = total[at : at + step, j * 128 : (j + 1) * 128]
    at += step
    router[...] = total[at : at + router.shape[0], :half]
    one[...] = total[at + 8 : at + 9, :half]
    two[...] = total[at + 8 : at + 9, half:]


def place_body(rest, *refs):
    place = lax.axis_index("ctx") // rest
    out = refs[-1]
    local = out.shape[1]
    for k, ref in enumerate(refs[:-1]):
        begin = ref.shape[0] - local
        out[place ^ k] = ref[begin:, :].astype(F32)


def close_body(rest, count, strides, parts, n_in, *refs):
    main, moved = refs[: n_in + 1], refs[n_in + 1 : n_in + 1 + count]
    outs, totals = refs[n_in + 1 + count : n_in + 9 + count], refs[n_in + 9 + count :]
    place_body(rest, *moved, outs[7])
    Order.leave(7)
    both_final_body(strides, parts, n_in, *main, *outs[:7], *totals)


def on_device(
    tokens,
    routes,
    block_order,
    norm_gain1,
    router_w,
    query_w,
    kv_w,
    out_w,
    norm_gain2,
    up_w,
    down_w,
    cotangent,
):
    size = lax.axis_size("ctx")
    count, local, dim = tokens.shape
    rest = size // count
    place = lax.axis_index("ctx") // rest
    total = count * local
    experts = router_w.shape[1]
    head = kv_w.shape[1] // 2
    feed = up_w.shape[1]

    Order.last = None
    tall = dim // 2
    keys = 2 * head
    router_t = router_w.T
    routes_t = routes.transpose(0, 2, 1)

    def core():
        return lax.axis_index("wsh")

    def here():
        return lax.axis_index("ctx") // rest

    got = call(
        functools.partial(pack_all_body, count, rest),
        [((local + 8, dim), BF)] * (count - 1) + [((tall + 8, experts * head + keys + dim), BF)],
        far([tokens, routes_t, query_w, kv_w, router_t, out_w]),
        late=(2, 3, 4, 5),
        ahead=[Ahead(tokens, (local, dim), lambda r: r.at[here()]), Ahead(kv_w)]
        + [
            Ahead(cotangent, (local, dim), lambda r, k=k: r.at[here() ^ k])
            for k in range(1, count)
        ],
    )
    tok_pieces, (packed, tok_own, kv_own), cot_pieces = got[: count - 1], got[count - 1 : count + 2], got[count + 2 :]
    tok_x = [swap(tok_pieces[k - 1], k * rest, size) for k in range(1, count)]
    packed_x = trade(packed)
    gain_one, gain_two = after((norm_gain1, norm_gain2), packed)
    gains = jnp.stack([gain_one, gain_two])
    gains_x = trade(gains)

    steps = factors(rest)
    kv, normed, tok, gain_rows, wk, tails = call(
        functools.partial(keys_body, count, rest),
        [
            ((steps[0], total, keys), BF, 1),
            ((total, dim), BF, 1),
            ((total, dim), BF, 1),
            ((8, dim), F32, 1),
            ((dim, keys), BF, 1),
            ((8 * count, 128), F32),
        ],
        [tok_own, *tok_x, Far(routes_t), gains, gains_x, kv_own, packed_x],
    )
    stride = 1
    for i, step in enumerate(steps):
        if i > 0:
            kv = jnp.broadcast_to(kv[None], (step,) + kv.shape)
        kv = exchange(kv, stride, size).reshape(-1, total, keys)
        stride *= step
    cot_pieces = after(tuple(cot_pieces), normed)
    cot_x = [swap(cot_pieces[k - 1], k * rest, size) for k in range(1, count)]
    qt, normed_t, gates, gates_far, route, route_far, wq, wr, wo = call(
        functools.partial(project_body, count, experts, head),
        [
            ((TWO * head, total), BF, 1),
            ((dim, total), BF, 1),
            ((TWO, total), F32),
            ((TWO, total), F32, 1),
            ((8, total), F32),
            ((8, total), F32, 1),
            ((dim, experts * head), BF, 1),
            ((128, dim), F32, 1),
            ((experts * head, dim), BF, 1),
        ],
        [Far(normed), tails, *far([query_w, router_t, out_w]), packed_x],
        late=(2, 3, 4),
    )
    up_w2, down_w2, _ = lax.optimization_barrier((up_w, down_w, normed))
    up_x, down_x = trade(up_w2), trade(down_w2)
    span = rest * total
    wide = feed // 2

    def lanes(which):
        def view(ref):
            side = which()
            return ref.at[:, pl.ds(pl.multiple_of(side * wide, wide), wide)]

        return view

    att, logs, mixed, hidden, two, two_t, kv_far, cot_own, up_first = call(
        functools.partial(attend_body, count, rest, experts, head),
        [
            ((TWO * head, total), F32, 1),
            ((TWO, total), F32, 1),
            ((experts * head, total), BF, 1),
            ((total, dim), F32),
            ((total, dim), BF),
            ((dim, total), BF),
            ((rest, total, keys), BF, 1),
        ],
        [block_order, kv, Far(qt), gates, route, *far([tok, gain_rows, wo])],
        scratch=[((keys, span), BF)],
        smem=(0,),
        late=(5, 6, 7),
        ahead=[
            Ahead(cotangent, (local, dim), lambda r: r.at[here()]),
            Ahead(up_w, (tall, wide), lanes(lambda: 1 - core())),
        ],
    )

    tile = 512
    upper = wide * tall // dim
    layer, back_two, send_one, keep_one, cots, cots_far, send_up, up_second, down_own = call(
        functools.partial(feed_body, count, rest, True, tile),
        [
            ((total, dim), F32),
            ((total, dim), F32),
            ((wide, dim), BF),
            ((upper, dim), BF, 1),
            ((total, dim), BF),
            ((total, dim), BF, 1),
            ((upper, dim), BF),
        ],
        [two, two_t, cot_own, *cot_x, up_first, up_x, down_x, hidden],
        scratch=[((dim, wide), BF)],
        ahead=[Ahead(up_w, (tall, wide), lanes(core)), Ahead(down_w)],
    )
    recv_down, recv_up = trade(send_one), trade(send_up)
    *layer_pieces, back_two, keep_down, keep_two, send_two, cots, wo, gain_near, gates, route, att = call(
        functools.partial(feed_body, count, rest, False, tile),
        [((local, dim), F32, 1)]
        + [((local, dim), BF, 1)] * (count - 1)
        + [
            ((total, dim), F32),
            ((wide, dim), BF, 1),
            ((upper, dim), BF, 1),
            ((upper, dim), BF, 1),
        ],
        [two, two_t, cots, up_second, up_x, down_own, layer, back_two],
        scratch=[((dim, wide), BF), ((total, dim), F32)],
        ahead=[
            Ahead(a)
            for a in (cots_far, wo, gain_rows, gates_far, route_far, att)
        ],
    )
    recv_two = trade(send_two)
    layer_got = [layer_pieces[0]] + [swap(layer_pieces[k], k * rest, size) for k in range(1, count)]

    strides = []
    stride = 1
    for step in [*steps, count]:
        strides.append((stride, step))
        stride *= step
    last = len(strides) - 1
    unit = 8 * size
    first = strides[0][1]
    early_rows = -(-(wide + tall) // unit) * unit
    main_rows = -(-(2 * upper - tall) // unit) * unit
    small = tall // 4 + 16
    late_rows = -(-(small + 2 * tall) // unit) * unit

    def bulk(args, layout, height, ahead=()):
        pieces, *near = call(
            functools.partial(start_body, layout, True, 1, first, len(args)),
            [((first, height // first, WIDTH), BF)],
            args,
            scratch=[((8, WIDTH), F32)],
            ahead=ahead,
        )
        return exchange(pieces, 1, size), near

    def inner(terms, height, riders=()):
        height //= first
        for at in range(1, last + 1):
            more = riders if at == last else ()
            terms = cut_up([terms], [height], strides, at, size, more)
            height //= strides[at][1]
        return terms

    def outer(got):
        for at in reversed(range(1, last)):
            got = spread(jnp.concatenate(got, axis=0), strides, at, size)
        return got

    def ready(got, ahead=()):
        rows = got[0].shape[0]
        copies, *near = call(
            functools.partial(copies_body, [(0, rows)], len(got)),
            [((first, rows * len(got), WIDTH), BF)],
            got,
            ahead=ahead,
        )
        return exchange(copies, 1, size), near

    back_hidden, branch, grad_att, delta, logit, gain_two, early, kv_near, qt_near, logs_near = call(
        functools.partial(
            turn_start_body,
            count,
            rest,
            experts,
            head,
            [[(0, 0, wide), (1, 0, wide)], [(2, 0, tall), (3, 0, tall)]],
            first,
        ),
        [
            ((total, dim), F32, 1),
            ((total, dim), BF, 1),
            ((TWO * head, total), BF),
            ((TWO, total), F32),
            ((experts, total), F32, 1),
            ((8, dim), F32, 1),
            ((first, early_rows // first, WIDTH), BF),
        ],
        [
            hidden,
            back_two,
            cots,
            wo,
            gain_near,
            gates,
            route,
            att,
            Far(keep_down),
            recv_down,
            Far(keep_two),
            recv_up,
        ],
        late=(8, 10),
        ahead=[Ahead(a) for a in (kv_far, qt, logs)],
    )
    early = exchange(early, 1, size)
    split = steps[-1]
    share = span // split
    grad_q, *kv_terms = call(
        functools.partial(attend_back_body, count, rest, head, split),
        [((TWO * head, total), BF), ((share, keys), F32, 1)] + [((share, keys), BF, 1)] * (split - 1),
        [block_order, kv_near, qt_near, grad_att, logs_near, delta],
        scratch=[
            ((keys, span), BF),
            ((4, keys, total), BF),
            ((2, 2 * total, keys), BF),
            ((span, keys), F32),
            ((2, head, total), F32),
        ],
        smem=(0,),
        ahead=[Ahead(a) for a in (normed_t, route_far, mixed, branch, wq, wr, logit, tok)],
    )
    kv_terms, ahead = kv_terms[:split], kv_terms[split:]
    stride = rest
    for i, step in reversed(list(enumerate(steps))):
        stride //= step
        if i + 1 < len(steps):
            summed = functools.reduce(lambda a, b: a + b.astype(F32), terms)
            parts = summed.reshape(step, -1, keys)
            digit = (lax.axis_index("ctx") // stride) % step
            kv_terms = [pick(parts, digit ^ j) for j in range(step)]
        terms = [kv_terms[0]] + [
            swap(kv_terms[j].astype(BF), j * stride, size) for j in range(1, step)
        ]
    grad_q = after(grad_q, *layer_got[1:])
    keep_out, keep_query, send_main, back_part, unit_rows, scale_rows, routers, *near = call(
        functools.partial(query_body, experts, head),
        [
            ((tall, dim), BF, 1),
            ((tall, dim), BF, 1),
            ((2 * tall, dim), BF, 1),
            ((total, dim), F32),
            ((total, dim), F32),
            ((total, 128), F32),
            ((experts, dim), F32),
        ],
        [grad_q, *ahead],
        scratch=[((experts * head, total), BF)],
        ahead=[Ahead(a) for a in (normed_t, back_hidden, wk, gain_rows, gain_two, terms[0])],
    )
    *near, term = near
    *input_pieces, keep_late, send_late, keep_two, keep_one = call(
        functools.partial(unproject_body, count, len(terms)),
        [((local, dim), F32, 1)]
        + [((local, dim), BF, 1)] * (count - 1)
        + [((small, dim), F32, 1), ((small + 2 * tall, dim), BF)],
        [term, *terms[1:], back_part, unit_rows, scale_rows, routers, *near, Far(send_main)],
        scratch=[((8, dim), F32)],
        late=(len(terms) + 9,),
        ahead=[Ahead(a) for a in (keep_two, keep_one)],
    )
    recv_late = trade(send_late)
    main, _ = bulk(
        [keep_two, recv_up, keep_one, recv_two],
        [
            [(0, tall, upper - tall), (1, tall, upper - tall)],
            [(2, 0, upper), (3, 0, upper)],
        ],
        main_rows,
    )
    early_terms = inner([early], early_rows)
    pieces = call(
        functools.partial(
            start_body,
            [
                [(0, 0, tall), (1, 0, tall)],
                [(0, tall, tall), (2, 0, tall)],
                [(0, 2 * tall, small), (3, 0, small)],
            ],
            False,
            1,
            first,
            4,
        ),
        [((late_rows // first, WIDTH), F32)] + [((late_rows // first, WIDTH), BF)] * (first - 1),
        [recv_late, *far([keep_out, keep_query, keep_late])],
        scratch=[((late_rows, WIDTH), F32)],
    )
    late = pieces[:1] + [swap(pieces[j], j, size) for j in range(1, first)]
    early_got = outer(spread(settle(early_terms), strides, last, size))
    heights = [main_rows // first, late_rows // first]
    chunks = [[main], late]
    for at in range(1, last):
        chunks = [cut_up([c], [h], strides, at, size) for c, h in zip(chunks, heights)]
        heights = [h // strides[at][1] for h in heights]
    both_terms = cut_up(chunks, heights, strides, last, size)
    heights = [h // count for h in heights]
    (layer_out,) = call(
        functools.partial(place_body, rest),
        [((count, local, dim), F32, 1)],
        [Far(layer_got[0]), *far(layer_got[1:])],
    )
    early_last, _ = ready(early_got)
    both_got = spread(settle(both_terms), strides, last, size)
    slices = [(0, heights[0]), (heights[0], heights[1])]
    for stage in reversed(range(1, last)):
        moved = []
        for begin, h in slices:
            piece = jnp.concatenate([g[begin : begin + h] for g in both_got], axis=0)
            moved.append(spread(piece, strides, stage, size))
        both_got = [jnp.concatenate([m[j] for m in moved], axis=0) for j in range(strides[stage][1])]
        tops = [m[0].shape[0] for m in moved]
        slices = [(0, tops[0]), (tops[0], tops[1])]
    tall_rows = sum(h for _, h in slices) * len(both_got)
    (both_own,) = call(
        functools.partial(copies_body, slices, len(both_got)),
        [((1, tall_rows, WIDTH), BF)],
        both_got,
    )
    both_last = spread(both_own, strides, 0, size)
    input_pieces = after(tuple(input_pieces), both_got[0])
    moved = {k: swap(input_pieces[k], k * rest, size) for k in reversed(range(1, count))}
    input_got = [input_pieces[0]] + [moved[k] for k in range(1, count)]
    grad_down, up_tile = call(
        functools.partial(final_body, strides, [early_rows // first], [(early_dest, 2)], 2),
        [((wide, dim), F32, 1), ((tall, WIDTH), F32)],
        [early_last],
        scratch=[((early_rows, WIDTH), F32)],
    )
    grad_up, grad_out, grad_query, grad_kv, grad_router, grad_one, grad_two, input_grad = call(
        functools.partial(
            close_body,
            rest,
            count,
            strides,
            [main_rows // first, late_rows // first],
            len(both_last),
        ),
        [
            ((tall, feed), F32, 1),
            ((tall, dim), F32, 1),
            ((tall, experts * head), F32, 1),
            ((tall, keys), F32, 1),
            ((experts, tall), F32, 1),
            ((1, tall), F32, 1),
            ((1, tall), F32, 1),
            ((count, local, dim), F32, 1),
        ],
        [*both_last, up_tile, *input_got],
        scratch=[((main_rows, WIDTH), F32), ((late_rows, WIDTH), F32)],
    )
    return (
        layer_out,
        input_grad,
        grad_one.reshape(tall),
        grad_router.T,
        grad_query,
        grad_kv,
        grad_out,
        grad_two.reshape(tall),
        grad_up,
        grad_down,
    )


def solution(mesh):
    placed = (
        P("wsh", "ctx", None),
        P("wsh", "ctx", None),
        P(),
        P("wsh"),
        P("wsh", None),
        P("wsh", None),
        P("wsh", None),
        P("wsh", None),
        P("wsh"),
        P("wsh", None),
        P("wsh", None),
        P("wsh", "ctx", None),
    )
    return jax.shard_map(
        on_device,
        mesh=mesh,
        in_specs=placed,
        out_specs=(
            P("wsh", "ctx", None),
            P("wsh", "ctx", None),
            P("wsh"),
            P("wsh", None),
            P("wsh", None),
            P("wsh", None),
            P("wsh", None),
            P("wsh"),
            P("wsh", None),
            P("wsh", None),
        ),
        check_vma=False,
    )
```

```python
import functools
import math

import jax
import jax.numpy as jnp
from jax import lax
from jax.experimental import pallas as pl
from jax.experimental.pallas import tpu as pltpu
from jax.sharding import PartitionSpec as P

BF = jnp.bfloat16
F32 = jnp.float32
I32 = jnp.int32
NONE = -1e30
TWO = 2


def factors(size):
    out = []
    while size > 1:
        step = 4 if size % 4 == 0 else 2
        out.append(step)
        size //= step
    return out


def swap(values, mask, size):
    return lax.ppermute(values, "ctx", [(i, i ^ mask) for i in range(size)])


def groups_of(stride, step, size):
    out = []
    for i in range(size):
        if (i // stride) % step == 0:
            out.append([i + j * stride for j in range(step)])
    return out


def exchange(parts, stride, size):
    step = parts.shape[0]
    groups = groups_of(stride, step, size)
    return lax.all_to_all(parts, "ctx", 0, 0, tiled=True, axis_index_groups=groups)


def trade(values):
    return lax.ppermute(values, "wsh", [(0, 1), (1, 0)])


def pick(parts, index):
    return lax.dynamic_index_in_dim(parts, index, 0, False)


def mm(a, b, left=1, right=0):
    return lax.dot_general(a, b, (((left,), (right,)), ((), ())), preferred_element_type=F32)


class Order:
    last = None
    rest = None
    leave = None


def after(value, *earlier):
    return lax.optimization_barrier((value, *earlier))[0]


class Far:
    def __init__(self, value):
        self.value = value


class Ahead:
    def __init__(self, value, shape=None, view=None):
        self.value, self.view = value, view
        self.shape = value.shape if shape is None else shape


def loading_body(body, plan, n_out, far_out, late, views, n_scratch, *refs):
    n_in, n_pre = len(plan), len(views)
    ins, pre_in = list(refs[:n_in]), refs[n_in : n_in + n_pre]
    at = n_in + n_pre
    outs, pre_out = list(refs[at : at + n_out]), refs[at + n_out : at + n_out + n_pre]
    at += n_out + n_pre
    own = refs[at : at + n_scratch]
    held, sems = refs[at + n_scratch : -1], refs[-1]
    first, second, ahead, slot = [], [], [], 0
    for i in range(n_in):
        if plan[i]:
            copy = pltpu.make_async_copy(ins[i], held[slot], sems.at[slot])
            (second if i in late else first).append(copy)
            ins[i] = held[slot]
            slot += 1
    leaving = {}
    for i in range(n_out):
        if far_out[i]:
            leaving[i] = pltpu.make_async_copy(held[slot], outs[i], sems.at[slot])
            outs[i] = held[slot]
            slot += 1
    for view, source, target in zip(views, pre_in, pre_out):
        source = source if view is None else view(source)
        ahead.append(pltpu.make_async_copy(source, target, sems.at[slot]))
        slot += 1
    for copy in first + second + ahead:
        copy.start()
    for copy in first:
        copy.wait()

    def rest():
        for copy in second:
            copy.wait()

    gone = []

    def leave(*which):
        for i in which:
            if far_out[i]:
                gone.append(i)
                leaving[i].start()

    Order.rest, Order.leave = rest, leave
    body(*ins, *outs, *own)
    leave(*[i for i in range(n_out) if i not in gone])
    for i in gone:
        leaving[i].wait()
    for copy in ahead:
        copy.wait()


def call(body, outs, args, scratch=(), smem=(), late=(), ahead=(), mib=14):
    whole = pl.BlockSpec(memory_space=pltpu.VMEM)
    scalars = pl.BlockSpec(memory_space=pltpu.SMEM)
    distant = pl.BlockSpec(memory_space=pltpu.HBM)
    plan = [isinstance(a, Far) for a in args]
    args = [
        pltpu.with_memory_space_constraint(a.value, pltpu.HBM) if isinstance(a, Far) else a
        for a in args
    ]
    far_out = [len(o) > 2 for o in outs]
    if Order.last is not None:
        args[0] = after(args[0], Order.last)
    held = [(a.shape, a.dtype) for a, far in zip(args, plan) if far]
    held += [o[:2] for o, far in zip(outs, far_out) if far]
    need = sum(math.prod(s) * jnp.dtype(d).itemsize for s, d in [*held, *scratch])
    run = pl.pallas_call(
        functools.partial(
            loading_body,
            body,
            plan,
            len(outs),
            far_out,
            late,
            [a.view for a in ahead],
            len(scratch),
        ),
        out_shape=[
            pltpu.HBM(o[0], o[1]) if far else jax.ShapeDtypeStruct(o[0], o[1])
            for o, far in zip(outs, far_out)
        ]
        + [jax.ShapeDtypeStruct(a.shape, a.value.dtype) for a in ahead],
        in_specs=[
            scalars if i in smem else distant if plan[i] else whole for i in range(len(args))
        ]
        + [distant] * len(ahead),
        out_specs=[distant if far else whole for far in far_out] + [whole] * len(ahead),
        scratch_shapes=[pltpu.VMEM(s, d) for s, d in [*scratch, *held]]
        + [pltpu.SemaphoreType.DMA((max(len(held) + len(ahead), 1),))],
        compiler_params=pltpu.CompilerParams(vmem_limit_bytes=(mib << 20) + need),
        cost_estimate=pl.CostEstimate(flops=1, bytes_accessed=1, transcendentals=0),
    )
    moved = [pltpu.with_memory_space_constraint(a.value, pltpu.HBM) for a in ahead]
    got = list(run(*args, *moved))
    Order.last = got[0]
    return got


def far(values):
    return [Far(v) for v in values]


def join(slots):
    half = slots[0].shape[0] // 2
    return jnp.concatenate([s[:half] for s in slots] + [s[half:] for s in slots], axis=0)


def slot_rows(rows, k, count):
    half = rows.shape[0] // (2 * count)
    low = k * half
    high = rows.shape[0] // 2 + k * half
    return jnp.concatenate([rows[low : low + half], rows[high : high + half]], axis=0)


def centred(rows):
    centre = rows - jnp.mean(rows, axis=-1, keepdims=True)
    scale = lax.rsqrt(jnp.mean(centre * centre, axis=-1, keepdims=True) + 1e-05)
    return centre * scale, scale


def fill(scratch, own, other, core):
    half = own.shape[0]
    scratch[pl.ds(pl.multiple_of(core * half, half), half), :] = own[...]
    scratch[pl.ds(pl.multiple_of((1 - core) * half, half), half), :] = other[...]


def pick_gain(own, other, which, core):
    a = own[which : which + 1, :].astype(F32)
    b = other[which : which + 1, :].astype(F32)
    first = jnp.where(core == 0, a, b)
    second = jnp.where(core == 0, b, a)
    return jnp.concatenate([first, second], axis=1)


def route_rows(pieces):
    lane = lax.broadcasted_iota(I32, (8, 128), 1)
    low = lane < 64
    rolled = [pltpu.roll(p, 64, 1) for p in pieces]
    count = len(pieces)
    front = [jnp.where(low, pieces[i], rolled[i + 1]) for i in range(0, count, 2)]
    back = [jnp.where(low, rolled[i], pieces[i + 1]) for i in range(0, count, 2)]
    return jnp.concatenate(front + back, axis=1)


def pack_body(count, rest, *refs):
    tok, routes = refs[:2]
    place = lax.axis_index("ctx") // rest
    local, dim = tok.shape[1:]
    for k, out in enumerate(refs[2:]):
        out[:local, :] = tok[place ^ (k + 1)]
        out[local:, :] = jnp.zeros((8, dim), BF)
        out[local : local + TWO, :128] = routes[place ^ (k + 1)].astype(F32).astype(BF)


def pack_all_body(count, rest, *refs):
    tok, routes, query, kv, router, out = refs[:6]
    pieces, packed = refs[6:-1], refs[-1]
    pack_body(count, rest, tok, routes, *pieces)
    Order.rest()
    half, cols = query.shape
    keys = kv.shape[1]
    packed[half:, :] = jnp.zeros((8, packed.shape[1]), BF)
    packed[:half, :cols] = query[...]
    packed[:half, cols : cols + keys] = kv[...]
    packed[:half, cols + keys :] = out[...]
    packed[half:, :half] = router[...]


def fill_router(wr, own, packed, core):
    half = own.shape[1]
    wr[...] = jnp.zeros_like(wr)
    experts = own.shape[0]
    mine = pl.ds(pl.multiple_of(core * half, half), half)
    theirs = pl.ds(pl.multiple_of((1 - core) * half, half), half)
    wr[:experts, mine] = own[...].astype(F32)
    wr[:experts, theirs] = packed[half:, :half].astype(F32)


def keys_body(count, rest, *refs):
    toks = refs[:count]
    routes, g_own, g_other, k_own, packed = refs[count : count + 5]
    kv_out, normed_out, tok_out, gain_out, wk, tail_out = refs[count + 5 :]
    core = lax.axis_index("wsh")
    place = lax.axis_index("ctx") // rest
    half = k_own.shape[0]
    local = toks[0].shape[0]
    keys = k_own.shape[1]
    cols = packed.shape[1] - keys - toks[0].shape[1]
    fill(wk, k_own, packed.at[:half, cols : cols + keys], core)
    rows = join([t[:local] for t in toks])
    tok_out[...] = rows
    Order.leave(2, 4)
    tail_out[...] = jnp.zeros_like(tail_out)
    tail_out[:TWO, :] = routes[place].astype(F32)
    for k in range(1, count):
        tail_out[8 * k : 8 * k + 8, :] = toks[k][local : local + 8, :128].astype(F32)
    rows = rows.astype(F32)
    unit, _ = centred(rows)
    gain_out[...] = jnp.zeros_like(gain_out)
    for which in range(TWO):
        gain_out[which : which + 1, :] = pick_gain(g_own, g_other, which, core)
    normed = (unit * gain_out[0:1, :]).astype(BF)
    normed_out[...] = normed
    Order.leave(1, 3)
    kv = mm(normed, wk[...]).astype(BF)
    for i in range(kv_out.shape[0]):
        kv_out[i] = kv


def project_body(count, experts, head, *refs):
    normed_ref, tails, q_own, r_own, o_own, packed = refs[:6]
    qt_out, nt_out, gate_out, gate_far, route_out, route_far, wq, wr, wo = refs[6:]
    core = lax.axis_index("wsh")
    half, cols = q_own.shape
    normed = normed_ref[...]
    nt_out[...] = normed.T
    Order.leave(1)
    Order.rest()
    fill(wq, q_own, packed.at[:half, :cols], core)
    fill_router(wr, r_own, packed, core)
    fill(wo, o_own, packed.at[:half, packed.shape[1] - o_own.shape[1] :], core)
    Order.leave(6, 7, 8)
    routes = route_rows([tails[8 * k : 8 * k + 8, :] for k in range(count)])
    route_out[...] = routes
    route_far[...] = routes
    logits = mm(wr[...].astype(BF), normed, 1, 1)
    queries = mm(wq[...], normed, 0, 1) * 0.125
    chosen = []
    for s in range(TWO):
        route = routes[s : s + 1]
        total = jnp.zeros((head, normed.shape[0]), F32)
        value = jnp.zeros((1, normed.shape[0]), F32)
        for e in range(experts):
            here = route == e
            total = jnp.where(here, queries[e * head : (e + 1) * head], total)
            value = jnp.where(here, logits[e : e + 1], value)
        qt_out[s * head : (s + 1) * head, :] = total.astype(BF)
        chosen.append(value)
    top = jnp.maximum(chosen[0], chosen[1])
    raised = [jnp.exp(c - top) for c in chosen]
    total = raised[0] + raised[1]
    gate_out[...] = jnp.concatenate([r / total for r in raised], axis=0)
    gate_far[...] = gate_out[...]


def places(order, count, rest, block, width, part):
    me = lax.axis_index("ctx")
    place, other = me // rest, me % rest
    size = count * rest
    lane = lax.broadcasted_iota(I32, (1, width), 1)
    out = jnp.zeros((1, width), I32)
    for k in range(count):
        first = order[(place ^ k) * rest + other]
        base = jnp.where(part == 0, first, 2 * size - 1 - first) * block
        out = jnp.where(lane // block == k, lane - k * block + base, out)
    return out


def key_bases(order, count, rest, block, chunk, part):
    me = lax.axis_index("ctx")
    place = me // rest
    size = count * rest
    out = []
    for k in range(count):
        first = order[(place ^ k) * rest + chunk]
        out.append((first if part == 0 else 2 * size - 1 - first) * block)
    return out


def masked(scores, gap, bases, block):
    parts = [
        jnp.where(gap <= -base, scores[k * block : (k + 1) * block], NONE)
        for k, base in enumerate(bases)
    ]
    return jnp.concatenate(parts, axis=0)


def scored(kv, side, h, gap, order, count, rest, block, chunk, half):
    first = mm(kv[:half], side)
    if h == 0:
        return masked(first, gap, key_bases(order, count, rest, block, chunk, 0), block)
    second = mm(kv[half:], side)
    second = masked(second, gap, key_bases(order, count, rest, block, chunk, 1), block)
    return jnp.concatenate([first, second], axis=0)


def turn_keys(kv, kv_turned):
    rows = kv.shape[1]
    for c in range(kv.shape[0]):
        kv_turned[:, c * rows : (c + 1) * rows] = kv[c].T


def both_slots(rows, head, cols):
    return jnp.concatenate([rows[s * head : (s + 1) * head, cols] for s in range(TWO)], axis=1)


def gap_rows(order, count, rest, block, half, h):
    gap = lax.broadcasted_iota(I32, (block, half), 0) - places(order, count, rest, block, half, h)
    return jnp.concatenate([gap] * TWO, axis=1)


def attend_body(count, rest, experts, head, *refs):
    order, kv_ref, qt, gates, routes = refs[:5]
    tok, gains, wo = refs[5:8]
    att_out, log_out, mixed_out, hidden_out, two_out, turned_out, kv_out, kv_turned = refs[8:]
    kv_out[...] = kv_ref[...]
    Order.leave(6)
    other = lax.axis_index("ctx") % rest
    total = qt.shape[1]
    half = total // 2
    block = half // count
    turn_keys(kv_ref, kv_turned)
    sides, gaps = [], []
    for h in range(2):
        side = both_slots(qt, head, slice(h * half, (h + 1) * half))
        sides.append(jnp.concatenate([side, jnp.zeros_like(side)], axis=0))
        gaps.append(gap_rows(order, count, rest, block, half, h))

    def step(turn, carry):
        chunk = turn ^ other
        at = pl.multiple_of(chunk * total, total)
        kv = kv_ref[chunk]
        scores = [
            scored(kv, sides[h], h, gaps[h], order, count, rest, block, chunk, half)
            for h in range(2)
        ]
        out = []
        for h in range(2):
            top, norm, summed = carry[h]
            fresh = jnp.maximum(top, jnp.max(scores[h], axis=0, keepdims=True))
            shares = jnp.exp(scores[h] - fresh)
            fade = jnp.exp(top - fresh)
            norm = norm * fade + jnp.sum(shares, axis=0, keepdims=True)
            values = kv_turned[head:, pl.ds(at, half * (h + 1))]
            out.append((fresh, norm, summed * fade + mm(values, shares.astype(BF))))
        return tuple(out)

    start = (
        jnp.full((1, TWO * half), NONE, F32),
        jnp.zeros((1, TWO * half), F32),
        jnp.zeros((head, TWO * half), F32),
    )
    done = lax.fori_loop(0, rest, step, (start, start), unroll=rest <= 4)
    for h in range(2):
        top, norm, summed = done[h]
        logs, attended = top + jnp.log(norm), summed / norm
        for s in range(TWO):
            here, cols = slice(h * half, (h + 1) * half), slice(s * half, (s + 1) * half)
            log_out[s : s + 1, here] = logs[:, cols]
            att_out[s * head : (s + 1) * head, here] = attended[:, cols]
    Order.rest()
    Order.leave(0, 1)
    for e in range(experts):
        part = jnp.zeros((head, total), F32)
        for s in range(TWO):
            gate = jnp.where(routes[s : s + 1] == e, gates[s : s + 1], 0.0)
            part = part + gate * att_out[s * head : (s + 1) * head, :]
        mixed_out[e * head : (e + 1) * head, :] = part.astype(BF)
    Order.leave(2)
    hidden = tok[...].astype(F32) + mm(mixed_out[...].T, wo[...])
    hidden_out[...] = hidden
    unit, _ = centred(hidden)
    two = (unit * gains[1:2, :]).astype(BF)
    two_out[...] = two
    turned_out[...] = two.T


def feed_body(count, rest, first, tile, *refs):
    two, turned = refs[:2]
    if first:
        slots = refs[2 : 2 + count]
        u_own, u_other, down, layer_in = refs[2 + count : 6 + count]
        layer_out, back_out, send, keep, cots, cot_far, send_up, up = refs[6 + count :]
    else:
        cots, u_own, u_other, down, layer_in, back_in = refs[2:8]
        outs = refs[8 : 12 + count]
        layer_pieces, back_out, keep_down, keep, send = outs[:count], *outs[count:]
        up, layer_out = refs[12 + count :]
    core = lax.axis_index("wsh")
    side = (1 - core) if first else core
    width = down.shape[0]
    half = u_own.shape[0]
    lanes = pl.ds(pl.multiple_of(side * width, width), width)
    up[pl.ds(pl.multiple_of(core * half, half), half), :] = u_own[...]
    up[pl.ds(pl.multiple_of((1 - core) * half, half), half), :] = u_other[:, lanes]
    if first:
        cots[...] = join([o[...] for o in slots])
        cot_far[...] = cots[...]
        Order.leave(5)
    layer_out[...] = layer_in[...]
    if first:
        back_out[...] = jnp.zeros_like(back_out)
    else:
        back_out[...] = back_in[...]
    mine = pl.ds(pl.multiple_of(core * half, half), half)
    theirs = pl.ds(pl.multiple_of((1 - core) * half, half), half)
    dim = up.shape[0]
    per = dim // tile

    def products(j):
        cols = slice(j * tile, (j + 1) * tile)
        return mm(two[...], up[:, cols]), mm(cots[...], down[cols, :], 1, 1)

    steps = width // tile
    ready = products(0)
    for j in range(steps):
        cols = slice(j * tile, (j + 1) * tile)
        pre, back = ready
        if j + 1 < steps:
            ready = products(j + 1)
        phi = 0.5 * (1.0 + lax.erf(pre * math.sqrt(0.5)))
        bell = jnp.exp(pre * pre * -0.5) * (1.0 / math.sqrt(2.0 * math.pi))
        act = (pre * phi).astype(BF)
        back_pre = (back * (phi + pre * bell)).astype(BF)
        layer_out[...] += mm(act, down[cols, :])
        back_out[...] += mm(back_pre, up[:, cols], 1, 1)
        grad = mm(act.T, cots[...]).astype(BF)
        grad_mine = mm(turned[mine, :], back_pre).astype(BF)
        grad_theirs = mm(turned[theirs, :], back_pre).astype(BF)
        rows = slice((j // per) * half, (j // per + 1) * half)
        lane = slice((j % per) * tile, (j % per + 1) * tile)
        keep[rows, lane] = grad_mine
        if first:
            send[cols, :] = grad
            send_up[rows, lane] = grad_theirs
        else:
            keep_down[cols, :] = grad
            send[rows, lane] = grad_theirs
    if not first:
        for k in range(count):
            layer_pieces[k][...] = slot_rows(layer_out[...], k, count).astype(layer_pieces[k].dtype)


def turn_body(count, rest, experts, head, *refs):
    hidden, back_two, cot, wo, gain, gates, routes, att = refs[:8]
    back_hidden_out, branch_out, grad_att_out, delta_out, logit_out, gain_out = refs[8:]
    unit, scale = centred(hidden[...])
    back = back_two[...]
    side = back * gain[1:2, :]
    part = scale * (
        side
        - jnp.mean(side, axis=-1, keepdims=True)
        - unit * jnp.mean(side * unit, axis=-1, keepdims=True)
    )
    gain_out[...] = jnp.broadcast_to(jnp.sum(back * unit, axis=0, keepdims=True), gain_out.shape)
    back_hidden = cot[...].astype(F32) + part
    back_hidden_out[...] = back_hidden
    branch = back_hidden.astype(BF)
    branch_out[...] = branch
    Order.leave(0, 1, 5)
    back_mixed = mm(wo[...], branch, 1, 1)
    grads = []
    for s in range(TWO):
        total = jnp.zeros((head, branch.shape[0]), F32)
        for e in range(experts):
            total = jnp.where(routes[s : s + 1] == e, back_mixed[e * head : (e + 1) * head], total)
        att_s = att[s * head : (s + 1) * head, :]
        grads.append(jnp.sum(total * att_s, axis=0, keepdims=True))
        low = (gates[s : s + 1] * total).astype(BF)
        grad_att_out[s * head : (s + 1) * head, :] = low
        delta_out[s : s + 1, :] = jnp.sum(low.astype(F32) * att_s, axis=0, keepdims=True)
    mean = gates[0:1] * grads[0] + gates[1:2] * grads[1]
    row = lax.broadcasted_iota(I32, logit_out.shape, 0)
    logit = jnp.zeros(logit_out.shape, F32)
    for s in range(TWO):
        value = gates[s : s + 1] * (grads[s] - mean)
        logit = logit + jnp.where(row.astype(F32) == routes[s : s + 1], value, 0.0)
    logit_out[...] = logit


def turn_start_body(count, rest, experts, head, layout, step, *refs):
    ins, early, outs, pieces = refs[:8], refs[8:12], refs[12:18], refs[18]
    turn_body(count, rest, experts, head, *ins, *outs)
    Order.rest()
    start_body(layout, True, 1, step, len(early), *early, pieces, None)


def attend_back_body(count, rest, head, split, *refs):
    order, kv_ref, qt, grad_att, logs, delta, grad_q_out = refs[:7]
    outs = refs[7 : 7 + split]
    kv_turned, sides, turned, grad_kv, grad_q = refs[7 + split :]
    total = qt.shape[1]
    half = total // 2
    block = half // count
    wide = TWO * half
    turn_keys(kv_ref, kv_turned)
    blank = jnp.zeros((head, wide), BF)
    for h in range(2):
        cols = slice(h * half, (h + 1) * half)
        q_side = jnp.concatenate([both_slots(qt, head, cols), blank], axis=0)
        g_side = jnp.concatenate([blank, both_slots(grad_att, head, cols)], axis=0)
        sides[2 * h], sides[2 * h + 1] = q_side, g_side
        turned[h, :wide, :], turned[h, wide:, :] = q_side.T, g_side.T
    grad_q[...] = jnp.zeros_like(grad_q)
    gaps = [gap_rows(order, count, rest, block, half, h) for h in range(2)]
    log_rows = [both_slots(logs, 1, slice(h * half, (h + 1) * half)) for h in range(2)]
    delta_rows = [both_slots(delta, 1, slice(h * half, (h + 1) * half)) for h in range(2)]

    def step(chunk, carry):
        at = pl.multiple_of(chunk * total, total)
        kv = kv_ref[chunk]
        grads = []
        for h in range(2):
            reach = half * (h + 1)
            scores = scored(
                kv, sides[2 * h], h, gaps[h], order, count, rest, block, chunk, half
            )
            shares = jnp.exp(scores - log_rows[h])
            back_shares = mm(kv[:reach], sides[2 * h + 1])
            back_scores = (shares * (back_shares - delta_rows[h])).astype(BF)
            both = jnp.concatenate([back_scores, shares.astype(BF)], axis=1)
            grads.append(mm(both, turned[h]))
            grad_q[h] += mm(kv_turned[:head, pl.ds(at, reach)], back_scores)
        grad_kv[pl.ds(at, half), :] = grads[0] + grads[1][:half]
        grad_kv[pl.ds(at + half, half), :] = grads[1][half:]
        return carry

    lax.fori_loop(0, rest, step, 0, unroll=rest <= 4)
    for h in range(2):
        for s in range(TWO):
            here, cols = slice(h * half, (h + 1) * half), slice(s * half, (s + 1) * half)
            grad_q_out[s * head : (s + 1) * head, here] = grad_q[h, :, cols].astype(BF)
    rows = outs[0].shape[0]
    digit = (lax.axis_index("ctx") % rest) // (rest // split)
    for i, out in enumerate(outs):
        begin = pl.multiple_of((digit ^ i) * rows, rows)
        out[...] = grad_kv[pl.ds(begin, rows), :].astype(out.dtype)


def query_body(experts, head, *refs):
    grad_q, normed_t, routes, mixed, branch, wq, wr, logit, tok = refs[:9]
    keep_out, keep, send, back_out, unit_out, scale_out, routers, bqt = refs[9:]
    core = lax.axis_index("wsh")
    total = grad_q.shape[1]
    for e in range(experts):
        part = jnp.zeros((head, total), F32)
        for s in range(TWO):
            value = grad_q[s * head : (s + 1) * head, :].astype(F32) * 0.125
            part = jnp.where(routes[s : s + 1] == e, value, part)
        bqt[e * head : (e + 1) * head, :] = part.astype(BF)
    back_q = bqt[...].T
    half = keep.shape[0]
    mine = pl.ds(pl.multiple_of(core * half, half), half)
    theirs = pl.ds(pl.multiple_of((1 - core) * half, half), half)
    send[:half, :] = mm(mixed[theirs, :], branch[...]).astype(BF)
    send[half:, :] = mm(normed_t[theirs, :], back_q).astype(BF)
    keep_out[...] = mm(mixed[mine, :], branch[...]).astype(BF)
    keep[...] = mm(normed_t[mine, :], back_q).astype(BF)
    parts = []
    left = logit[...]
    for _ in range(3):
        low = left.astype(BF)
        parts.append(low)
        left = left - low.astype(F32)
    routers[...] = parts_dot(parts, normed_t[...])
    back = mm(back_q, wq[...], 1, 1)
    wr_turned = wr[...].astype(BF)
    for low in parts:
        padded = jnp.concatenate([low.astype(F32), jnp.zeros((120, total), F32)], axis=0)
        back = back + mm(padded.T.astype(BF), wr_turned)
    back_out[...] = back
    unit, scale = centred(tok[...].astype(F32))
    unit_out[...] = unit
    scale_out[...] = jnp.broadcast_to(scale, scale_out.shape)


def unproject_body(count, terms, *refs):
    kv_terms = refs[:terms]
    back_part, unit_ref, scale_ref, routers, normed_t, back_hidden, wk, gain, gain_two, sent = refs[
        terms : terms + 10
    ]
    at = terms + 10
    pieces = refs[at : at + count]
    keep, send, gains = refs[at + count :]
    core = lax.axis_index("wsh")
    half = back_part.shape[1] // 2
    back_kv = kv_terms[0][...].astype(F32)
    for term in kv_terms[1:]:
        back_kv = back_kv + term[...].astype(F32)
    back_kv = back_kv.astype(BF)
    back = back_part[...] + mm(back_kv, wk[...], 1, 1)
    unit, scale = unit_ref[...], scale_ref[:, 0:1]
    side = back * gain[0:1, :]
    grad = back_hidden[...] + scale * (
        side
        - jnp.mean(side, axis=-1, keepdims=True)
        - unit * jnp.mean(side * unit, axis=-1, keepdims=True)
    )
    gains[0:1, :] = jnp.sum(back * unit, axis=0, keepdims=True)
    gains[1:2, :] = gain_two[0:1, :]
    step = half // 4
    experts = routers.shape[0]
    high = sent.shape[0]
    Order.rest()
    send[:high, :] = sent[...]
    for out, which in ((keep, core), (send.at[high:, :], 1 - core)):
        mine = pl.ds(pl.multiple_of(which * half, half), half)
        grad_k = mm(normed_t[mine, :], back_kv).astype(out.dtype)
        for j in range(4):
            out[:step, j * 128 : (j + 1) * 128] = grad_k[j * step : (j + 1) * step]
        blank = jnp.zeros((experts, half), F32)
        out[step : step + 8, :] = jnp.concatenate([routers[:, mine], blank], axis=1).astype(out.dtype)
        gain_pair = jnp.concatenate([gains[0:1, mine], gains[1:2, mine]], axis=1)
        out[step + 8 :, :] = jnp.broadcast_to(gain_pair, (8, 2 * half)).astype(out.dtype)
    for k in range(count):
        pieces[k][...] = slot_rows(grad, k, count).astype(pieces[k].dtype)


def parts_dot(parts, normed_t):
    out = None
    for low in parts:
        value = mm(low, normed_t, 1, 1)
        out = value if out is None else out + value
    return out


def sum_layout(layout, ins, total):
    at = 0
    for terms in layout:
        height = terms[0][2]
        value = None
        for index, begin, count in terms:
            part = ins[index][begin : begin + count, :].astype(F32)
            value = part if value is None else value + part
        total[at : at + height, :] = value
        at += height
    if at < total.shape[0]:
        total[at:, :] = jnp.zeros((total.shape[0] - at, total.shape[1]), F32)


def cut_rows(total, outs, stride, step):
    rows = outs[0].shape[0]
    digit = (lax.axis_index("ctx") // stride) % step
    for j in range(step):
        begin = pl.multiple_of((digit ^ j) * rows, 8)
        outs[j][...] = total[pl.ds(begin, rows), :].astype(outs[j].dtype)


def start_body(layout, whole, stride, step, n_in, *refs):
    ins, outs, total = refs[:n_in], refs[n_in:-1], refs[-1]
    if whole:
        rows = outs[0].shape[1]
        at = 0
        for terms in layout:
            height, done = terms[0][2], 0
            while done < height:
                j, low = (at + done) // rows, (at + done) % rows
                take = min(height - done, rows - low)
                value = None
                for index, begin, _ in terms:
                    part = ins[index][begin + done : begin + done + take, :].astype(F32)
                    value = part if value is None else value + part
                outs[0][j, low : low + take, :] = value.astype(BF)
                done += take
            at += height
        while at < rows * step:
            j, low = at // rows, at % rows
            outs[0][j, low:, :] = jnp.zeros((rows - low, outs[0].shape[2]), BF)
            at += rows - low
    else:
        sum_layout(layout, ins, total)
        cut_rows(total, outs, stride, step)


def terms_of(ref):
    return [ref.at[j] for j in range(ref.shape[0])] if len(ref.shape) == 3 else [ref]


def middle_body(chunks, stride, step, n_in, riders, *refs):
    ins, riding = refs[:n_in], refs[n_in : n_in + riders]
    refs = refs[n_in + riders :]
    outs, totals = refs[:step], refs[step:]
    digit = (lax.axis_index("ctx") // stride) % step
    at, low = 0, 0
    for count, total in zip(chunks, totals):
        value = None
        for ref in ins[at : at + count]:
            for term in terms_of(ref):
                part = term[...].astype(F32)
                value = part if value is None else value + part
        total[...] = value
        rows = total.shape[0] // step
        for j in range(step):
            begin = pl.multiple_of((digit ^ j) * rows, 8)
            outs[j][low : low + rows, :] = total[pl.ds(begin, rows), :].astype(outs[j].dtype)
        low += rows
        at += count
    for j in range(1, step if riders else 1):
        outs[j][low:, :] = riding[j - 1][...]


def copies_body(slices, n_in, *refs):
    ins, out = refs[:n_in], refs[-1]
    for j in range(out.shape[0]):
        at = 0
        for begin, rows in slices:
            for ref in ins:
                out[j, at : at + rows, :] = ref[begin : begin + rows, :]
                at += rows


def final_body(strides, parts, dests, n_out, *refs):
    got, outs, totals = refs[0], refs[1 : 1 + n_out], refs[1 + n_out :]
    me = lax.axis_index("ctx")
    shift, per = 0, 1
    for stride, step in strides[1:]:
        shift = shift * step + (me // stride) % step
        per *= step
    at, used = 0, 0
    for height, total, (dest, many) in zip(parts, totals, dests):
        rows = height // per
        swapped = isinstance(got, tuple)
        digit = me % strides[0][1] if swapped else 0
        for i in range(len(got) if swapped else got.shape[0]):
            for b in range(per):
                begin = pl.multiple_of(((i ^ digit) * per + (b ^ shift)) * rows, 8)
                source = got[i].at[0] if swapped else got.at[i]
                piece = source[at + b * rows : at + (b + 1) * rows, :]
                total[pl.ds(begin, rows), :] = piece.astype(F32)
        at += height
        dest(total, outs[used : used + many])
        Order.leave(*range(used, used + many))
        used += many


WIDTH = 512


def cut_up(chunks, heights, strides, at, size, riders=()):
    stride, step = strides[at]
    total = sum(heights) // step
    more = riders[0].shape[0] if riders else 0
    n_in = sum(len(c) for c in chunks)
    pieces = call(
        functools.partial(middle_body, [len(c) for c in chunks], stride, step, n_in, len(riders)),
        [((total, WIDTH), F32)] + [((total + more, WIDTH), BF)] * (step - 1),
        [t for c in chunks for t in c] + far(riders),
        scratch=[((h, WIDTH), F32) for h in heights],
    )
    return pieces[:1] + [swap(pieces[j], j * stride, size) for j in range(1, step)]


def spread(done, strides, at, size):
    stride, step = strides[at]
    return [done] + [swap(done, j * stride, size) for j in range(1, step)]


def settle(terms):
    return call(add_body, [(terms[0].shape, BF)], terms)[0]


def add_body(*refs):
    rows = refs[-1].shape[0]
    value = refs[0][:rows, :].astype(F32)
    for ref in refs[1:-1]:
        value = value + ref[:rows, :].astype(F32)
    refs[-1][...] = value.astype(refs[-1].dtype)


def early_dest(total, outs):
    down, tile = outs
    wide = down.shape[0]
    down[...] = total[:wide, :]
    tile[...] = total[wide : wide + tile.shape[0], :]


def both_final_body(strides, parts, n_in, *refs):
    got, tile = refs[:n_in], refs[n_in]
    outs, totals = refs[n_in + 1 : n_in + 8], refs[n_in + 8 :]

    def main(total, outs):
        (up,) = outs
        half = up.shape[0]
        core = lax.axis_index("wsh")
        tiles = up.shape[1] // WIDTH
        for i in range(tiles):
            side, inner = i // (tiles // 2), i % (tiles // 2)
            at = (core if side == 0 else 1 - core) * (tiles // 2) + inner
            rows = tile[...] if i == 0 else total[(i - 1) * half : i * half, :]
            up[:, pl.ds(pl.multiple_of(at * WIDTH, WIDTH), WIDTH)] = rows

    dests = [(main, 1), (late_dest, 6)]
    final_body(strides, parts, dests, 7, got, *outs, *totals)


def late_dest(total, outs):
    out, query, kv, router, one, two = outs
    half = kv.shape[0]
    out[...] = total[:half, :]
    query[...] = total[half : 2 * half, :]
    step = half // 4
    at = 2 * half
    for j in range(4):
        kv[j * step : (j + 1) * step, :] = total[at : at + step, j * 128 : (j + 1) * 128]
    at += step
    router[...] = total[at : at + router.shape[0], :half]
    one[...] = total[at + 8 : at + 9, :half]
    two[...] = total[at + 8 : at + 9, half:]


def place_body(rest, *refs):
    place = lax.axis_index("ctx") // rest
    out = refs[-1]
    local = out.shape[1]
    for k, ref in enumerate(refs[:-1]):
        begin = ref.shape[0] - local
        out[place ^ k] = ref[begin:, :].astype(F32)


def close_body(rest, count, strides, parts, n_in, *refs):
    main, moved = refs[: n_in + 1], refs[n_in + 1 : n_in + 1 + count]
    outs, totals = refs[n_in + 1 + count : n_in + 9 + count], refs[n_in + 9 + count :]
    place_body(rest, *moved, outs[7])
    Order.leave(7)
    both_final_body(strides, parts, n_in, *main, *outs[:7], *totals)


def on_device(
    tokens,
    routes,
    block_order,
    norm_gain1,
    router_w,
    query_w,
    kv_w,
    out_w,
    norm_gain2,
    up_w,
    down_w,
    cotangent,
):
    size = lax.axis_size("ctx")
    count, local, dim = tokens.shape
    rest = size // count
    place = lax.axis_index("ctx") // rest
    total = count * local
    experts = router_w.shape[1]
    head = kv_w.shape[1] // 2
    feed = up_w.shape[1]

    Order.last = None
    tall = dim // 2
    keys = 2 * head
    router_t = router_w.T
    routes_t = routes.transpose(0, 2, 1)

    def core():
        return lax.axis_index("wsh")

    def here():
        return lax.axis_index("ctx") // rest

    got = call(
        functools.partial(pack_all_body, count, rest),
        [((local + 8, dim), BF)] * (count - 1) + [((tall + 8, experts * head + keys + dim), BF)],
        far([tokens, routes_t, query_w, kv_w, router_t, out_w]),
        late=(2, 3, 4, 5),
        ahead=[Ahead(tokens, (local, dim), lambda r: r.at[here()]), Ahead(kv_w)]
        + [
            Ahead(cotangent, (local, dim), lambda r, k=k: r.at[here() ^ k])
            for k in range(1, count)
        ],
    )
    tok_pieces, (packed, tok_own, kv_own), cot_pieces = got[: count - 1], got[count - 1 : count + 2], got[count + 2 :]
    tok_x = [swap(tok_pieces[k - 1], k * rest, size) for k in range(1, count)]
    packed_x = trade(packed)
    gain_one, gain_two = after((norm_gain1, norm_gain2), packed)
    gains = jnp.stack([gain_one, gain_two])
    gains_x = trade(gains)

    steps = factors(rest)
    kv, normed, tok, gain_rows, wk, tails = call(
        functools.partial(keys_body, count, rest),
        [
            ((steps[0], total, keys), BF, 1),
            ((total, dim), BF, 1),
            ((total, dim), BF, 1),
            ((8, dim), F32, 1),
            ((dim, keys), BF, 1),
            ((8 * count, 128), F32),
        ],
        [tok_own, *tok_x, Far(routes_t), gains, gains_x, kv_own, packed_x],
    )
    stride = 1
    for i, step in enumerate(steps):
        if i > 0:
            kv = jnp.broadcast_to(kv[None], (step,) + kv.shape)
        kv = exchange(kv, stride, size).reshape(-1, total, keys)
        stride *= step
    cot_pieces = after(tuple(cot_pieces), normed)
    cot_x = [swap(cot_pieces[k - 1], k * rest, size) for k in range(1, count)]
    qt, normed_t, gates, gates_far, route, route_far, wq, wr, wo = call(
        functools.partial(project_body, count, experts, head),
        [
            ((TWO * head, total), BF, 1),
            ((dim, total), BF, 1),
            ((TWO, total), F32),
            ((TWO, total), F32, 1),
            ((8, total), F32),
            ((8, total), F32, 1),
            ((dim, experts * head), BF, 1),
            ((128, dim), F32, 1),
            ((experts * head, dim), BF, 1),
        ],
        [Far(normed), tails, *far([query_w, router_t, out_w]), packed_x],
        late=(2, 3, 4),
    )
    up_w2, down_w2, _ = lax.optimization_barrier((up_w, down_w, normed))
    up_x, down_x = trade(up_w2), trade(down_w2)
    span = rest * total
    wide = feed // 2

    def lanes(which):
        def view(ref):
            side = which()
            return ref.at[:, pl.ds(pl.multiple_of(side * wide, wide), wide)]

        return view

    att, logs, mixed, hidden, two, two_t, kv_far, cot_own, up_first = call(
        functools.partial(attend_body, count, rest, experts, head),
        [
            ((TWO * head, total), F32, 1),
            ((TWO, total), F32, 1),
            ((experts * head, total), BF, 1),
            ((total, dim), F32),
            ((total, dim), BF),
            ((dim, total), BF),
            ((rest, total, keys), BF, 1),
        ],
        [block_order, kv, Far(qt), gates, route, *far([tok, gain_rows, wo])],
        scratch=[((keys, span), BF)],
        smem=(0,),
        late=(5, 6, 7),
        ahead=[
            Ahead(cotangent, (local, dim), lambda r: r.at[here()]),
            Ahead(up_w, (tall, wide), lanes(lambda: 1 - core())),
        ],
    )

    tile = 512
    upper = wide * tall // dim
    layer, back_two, send_one, keep_one, cots, cots_far, send_up, up_second, down_own = call(
        functools.partial(feed_body, count, rest, True, tile),
        [
            ((total, dim), F32),
            ((total, dim), F32),
            ((wide, dim), BF),
            ((upper, dim), BF, 1),
            ((total, dim), BF),
            ((total, dim), BF, 1),
            ((upper, dim), BF),
        ],
        [two, two_t, cot_own, *cot_x, up_first, up_x, down_x, hidden],
        scratch=[((dim, wide), BF)],
        ahead=[Ahead(up_w, (tall, wide), lanes(core)), Ahead(down_w)],
    )
    recv_down, recv_up = trade(send_one), trade(send_up)
    *layer_pieces, back_two, keep_down, keep_two, send_two, cots, wo, gain_near, gates, route, att = call(
        functools.partial(feed_body, count, rest, False, tile),
        [((local, dim), F32, 1)]
        + [((local, dim), BF, 1)] * (count - 1)
        + [
            ((total, dim), F32),
            ((wide, dim), BF, 1),
            ((upper, dim), BF, 1),
            ((upper, dim), BF, 1),
        ],
        [two, two_t, cots, up_second, up_x, down_own, layer, back_two],
        scratch=[((dim, wide), BF), ((total, dim), F32)],
        ahead=[
            Ahead(a)
            for a in (cots_far, wo, gain_rows, gates_far, route_far, att)
        ],
    )
    recv_two = trade(send_two)
    layer_got = [layer_pieces[0]] + [swap(layer_pieces[k], k * rest, size) for k in range(1, count)]

    strides = []
    stride = 1
    for step in [*steps, count]:
        strides.append((stride, step))
        stride *= step
    last = len(strides) - 1
    unit = 8 * size
    first = strides[0][1]
    early_rows = -(-(wide + tall) // unit) * unit
    main_rows = -(-(2 * upper - tall) // unit) * unit
    small = tall // 4 + 16
    late_rows = -(-(small + 2 * tall) // unit) * unit

    def bulk(args, layout, height, ahead=()):
        pieces, *near = call(
            functools.partial(start_body, layout, True, 1, first, len(args)),
            [((first, height // first, WIDTH), BF)],
            args,
            scratch=[((8, WIDTH), F32)],
            ahead=ahead,
        )
        return exchange(pieces, 1, size), near

    def inner(terms, height, riders=()):
        height //= first
        for at in range(1, last + 1):
            more = riders if at == last else ()
            terms = cut_up([terms], [height], strides, at, size, more)
            height //= strides[at][1]
        return terms

    def outer(got):
        for at in reversed(range(1, last)):
            got = spread(jnp.concatenate(got, axis=0), strides, at, size)
        return got

    def ready(got, ahead=()):
        rows = got[0].shape[0]
        copies, *near = call(
            functools.partial(copies_body, [(0, rows)], len(got)),
            [((first, rows * len(got), WIDTH), BF)],
            got,
            ahead=ahead,
        )
        return exchange(copies, 1, size), near

    back_hidden, branch, grad_att, delta, logit, gain_two, early, kv_near, qt_near, logs_near = call(
        functools.partial(
            turn_start_body,
            count,
            rest,
            experts,
            head,
            [[(0, 0, wide), (1, 0, wide)], [(2, 0, tall), (3, 0, tall)]],
            first,
        ),
        [
            ((total, dim), F32, 1),
            ((total, dim), BF, 1),
            ((TWO * head, total), BF),
            ((TWO, total), F32),
            ((experts, total), F32, 1),
            ((8, dim), F32, 1),
            ((first, early_rows // first, WIDTH), BF),
        ],
        [
            hidden,
            back_two,
            cots,
            wo,
            gain_near,
            gates,
            route,
            att,
            Far(keep_down),
            recv_down,
            Far(keep_two),
            recv_up,
        ],
        late=(8, 10),
        ahead=[Ahead(a) for a in (kv_far, qt, logs)],
    )
    early = exchange(early, 1, size)
    split = steps[-1]
    share = span // split
    grad_q, *kv_terms = call(
        functools.partial(attend_back_body, count, rest, head, split),
        [((TWO * head, total), BF), ((share, keys), F32, 1)] + [((share, keys), BF, 1)] * (split - 1),
        [block_order, kv_near, qt_near, grad_att, logs_near, delta],
        scratch=[
            ((keys, span), BF),
            ((4, keys, total), BF),
            ((2, 2 * total, keys), BF),
            ((span, keys), F32),
            ((2, head, total), F32),
        ],
        smem=(0,),
        ahead=[Ahead(a) for a in (normed_t, route_far, mixed, branch, wq, wr, logit, tok)],
    )
    kv_terms, ahead = kv_terms[:split], kv_terms[split:]
    stride = rest
    for i, step in reversed(list(enumerate(steps))):
        stride //= step
        if i + 1 < len(steps):
            summed = functools.reduce(lambda a, b: a + b.astype(F32), terms)
            parts = summed.reshape(step, -1, keys)
            digit = (lax.axis_index("ctx") // stride) % step
            kv_terms = [pick(parts, digit ^ j) for j in range(step)]
        terms = [kv_terms[0]] + [
            swap(kv_terms[j].astype(BF), j * stride, size) for j in range(1, step)
        ]
    grad_q = after(grad_q, *layer_got[1:])
    keep_out, keep_query, send_main, back_part, unit_rows, scale_rows, routers, *near = call(
        functools.partial(query_body, experts, head),
        [
            ((tall, dim), BF, 1),
            ((tall, dim), BF, 1),
            ((2 * tall, dim), BF, 1),
            ((total, dim), F32),
            ((total, dim), F32),
            ((total, 128), F32),
            ((experts, dim), F32),
        ],
        [grad_q, *ahead],
        scratch=[((experts * head, total), BF)],
        ahead=[Ahead(a) for a in (normed_t, back_hidden, wk, gain_rows, gain_two, terms[0])],
    )
    *near, term = near
    *input_pieces, keep_late, send_late, keep_two, keep_one = call(
        functools.partial(unproject_body, count, len(terms)),
        [((local, dim), F32, 1)]
        + [((local, dim), BF, 1)] * (count - 1)
        + [((small, dim), F32, 1), ((small + 2 * tall, dim), BF)],
        [term, *terms[1:], back_part, unit_rows, scale_rows, routers, *near, Far(send_main)],
        scratch=[((8, dim), F32)],
        late=(len(terms) + 9,),
        ahead=[Ahead(a) for a in (keep_two, keep_one)],
    )
    recv_late = trade(send_late)
    main, _ = bulk(
        [keep_two, recv_up, keep_one, recv_two],
        [
            [(0, tall, upper - tall), (1, tall, upper - tall)],
            [(2, 0, upper), (3, 0, upper)],
        ],
        main_rows,
    )
    pieces = call(
        functools.partial(
            start_body,
            [
                [(0, 0, tall), (1, 0, tall)],
                [(0, tall, tall), (2, 0, tall)],
                [(0, 2 * tall, small), (3, 0, small)],
            ],
            False,
            1,
            first,
            4,
        ),
        [((late_rows // first, WIDTH), F32)] + [((late_rows // first, WIDTH), BF)] * (first - 1),
        [recv_late, *far([keep_out, keep_query, keep_late])],
        scratch=[((late_rows, WIDTH), F32)],
    )
    late = pieces[:1] + [swap(pieces[j], j, size) for j in range(1, first)]
    early_terms = inner([early], early_rows)
    early_got = outer(spread(settle(early_terms), strides, last, size))
    heights = [main_rows // first, late_rows // first]
    chunks = [[main], late]
    for at in range(1, last):
        chunks = [cut_up([c], [h], strides, at, size) for c, h in zip(chunks, heights)]
        heights = [h // strides[at][1] for h in heights]
    both_terms = cut_up(chunks, heights, strides, last, size)
    heights = [h // count for h in heights]
    (layer_out,) = call(
        functools.partial(place_body, rest),
        [((count, local, dim), F32, 1)],
        [Far(layer_got[0]), *far(layer_got[1:])],
    )
    early_last, _ = ready(early_got)
    both_got = spread(settle(both_terms), strides, last, size)
    slices = [(0, heights[0]), (heights[0], heights[1])]
    for stage in reversed(range(1, last)):
        moved = []
        for begin, h in slices:
            piece = jnp.concatenate([g[begin : begin + h] for g in both_got], axis=0)
            moved.append(spread(piece, strides, stage, size))
        both_got = [jnp.concatenate([m[j] for m in moved], axis=0) for j in range(strides[stage][1])]
        tops = [m[0].shape[0] for m in moved]
        slices = [(0, tops[0]), (tops[0], tops[1])]
    tall_rows = sum(h for _, h in slices) * len(both_got)
    (both_own,) = call(
        functools.partial(copies_body, slices, len(both_got)),
        [((1, tall_rows, WIDTH), BF)],
        both_got,
    )
    both_last = spread(both_own, strides, 0, size)
    input_pieces = after(tuple(input_pieces), both_got[0])
    moved = {k: swap(input_pieces[k], k * rest, size) for k in reversed(range(1, count))}
    input_got = [input_pieces[0]] + [moved[k] for k in range(1, count)]
    grad_down, up_tile = call(
        functools.partial(final_body, strides, [early_rows // first], [(early_dest, 2)], 2),
        [((wide, dim), F32, 1), ((tall, WIDTH), F32)],
        [early_last],
        scratch=[((early_rows, WIDTH), F32)],
    )
    grad_up, grad_out, grad_query, grad_kv, grad_router, grad_one, grad_two, input_grad = call(
        functools.partial(
            close_body,
            rest,
            count,
            strides,
            [main_rows // first, late_rows // first],
            len(both_last),
        ),
        [
            ((tall, feed), F32, 1),
            ((tall, dim), F32, 1),
            ((tall, experts * head), F32, 1),
            ((tall, keys), F32, 1),
            ((experts, tall), F32, 1),
            ((1, tall), F32, 1),
            ((1, tall), F32, 1),
            ((count, local, dim), F32, 1),
        ],
        [*both_last, up_tile, *input_got],
        scratch=[((main_rows, WIDTH), F32), ((late_rows, WIDTH), F32)],
    )
    return (
        layer_out,
        input_grad,
        grad_one.reshape(tall),
        grad_router.T,
        grad_query,
        grad_kv,
        grad_out,
        grad_two.reshape(tall),
        grad_up,
        grad_down,
    )


def solution(mesh):
    placed = (
        P("wsh", "ctx", None),
        P("wsh", "ctx", None),
        P(),
        P("wsh"),
        P("wsh", None),
        P("wsh", None),
        P("wsh", None),
        P("wsh", None),
        P("wsh"),
        P("wsh", None),
        P("wsh", None),
        P("wsh", "ctx", None),
    )
    return jax.shard_map(
        on_device,
        mesh=mesh,
        in_specs=placed,
        out_specs=(
            P("wsh", "ctx", None),
            P("wsh", "ctx", None),
            P("wsh"),
            P("wsh", None),
            P("wsh", None),
            P("wsh", None),
            P("wsh", None),
            P("wsh"),
            P("wsh", None),
            P("wsh", None),
        ),
        check_vma=False,
    )
```

```python
import functools
import math

import jax
import jax.numpy as jnp
from jax import lax
from jax.experimental import pallas as pl
from jax.experimental.pallas import tpu as pltpu
from jax.sharding import PartitionSpec as P

BF = jnp.bfloat16
F32 = jnp.float32
I32 = jnp.int32
NONE = -1e30
TWO = 2


def factors(size):
    out = []
    while size > 1:
        step = 4 if size % 4 == 0 else 2
        out.append(step)
        size //= step
    return out


def swap(values, mask, size):
    return lax.ppermute(values, "ctx", [(i, i ^ mask) for i in range(size)])


def groups_of(stride, step, size):
    out = []
    for i in range(size):
        if (i // stride) % step == 0:
            out.append([i + j * stride for j in range(step)])
    return out


def exchange(parts, stride, size):
    step = parts.shape[0]
    groups = groups_of(stride, step, size)
    return lax.all_to_all(parts, "ctx", 0, 0, tiled=True, axis_index_groups=groups)


def trade(values):
    return lax.ppermute(values, "wsh", [(0, 1), (1, 0)])


def pick(parts, index):
    return lax.dynamic_index_in_dim(parts, index, 0, False)


def mm(a, b, left=1, right=0):
    return lax.dot_general(a, b, (((left,), (right,)), ((), ())), preferred_element_type=F32)


class Order:
    last = None
    rest = None
    leave = None


def after(value, *earlier):
    return lax.optimization_barrier((value, *earlier))[0]


class Far:
    def __init__(self, value):
        self.value = value


class Ahead:
    def __init__(self, value, shape=None, view=None):
        self.value, self.view = value, view
        self.shape = value.shape if shape is None else shape


def loading_body(body, plan, n_out, far_out, late, views, n_scratch, *refs):
    n_in, n_pre = len(plan), len(views)
    ins, pre_in = list(refs[:n_in]), refs[n_in : n_in + n_pre]
    at = n_in + n_pre
    outs, pre_out = list(refs[at : at + n_out]), refs[at + n_out : at + n_out + n_pre]
    at += n_out + n_pre
    own = refs[at : at + n_scratch]
    held, sems = refs[at + n_scratch : -1], refs[-1]
    first, second, ahead, slot = [], [], [], 0
    for i in range(n_in):
        if plan[i]:
            copy = pltpu.make_async_copy(ins[i], held[slot], sems.at[slot])
            (second if i in late else first).append(copy)
            ins[i] = held[slot]
            slot += 1
    leaving = {}
    for i in range(n_out):
        if far_out[i]:
            leaving[i] = pltpu.make_async_copy(held[slot], outs[i], sems.at[slot])
            outs[i] = held[slot]
            slot += 1
    for view, source, target in zip(views, pre_in, pre_out):
        source = source if view is None else view(source)
        ahead.append(pltpu.make_async_copy(source, target, sems.at[slot]))
        slot += 1
    for copy in first + second + ahead:
        copy.start()
    for copy in first:
        copy.wait()

    def rest():
        for copy in second:
            copy.wait()

    gone = []

    def leave(*which):
        for i in which:
            if far_out[i]:
                gone.append(i)
                leaving[i].start()

    Order.rest, Order.leave = rest, leave
    body(*ins, *outs, *own)
    leave(*[i for i in range(n_out) if i not in gone])
    for i in gone:
        leaving[i].wait()
    for copy in ahead:
        copy.wait()


def call(body, outs, args, scratch=(), smem=(), late=(), ahead=(), mib=14):
    whole = pl.BlockSpec(memory_space=pltpu.VMEM)
    scalars = pl.BlockSpec(memory_space=pltpu.SMEM)
    distant = pl.BlockSpec(memory_space=pltpu.HBM)
    plan = [isinstance(a, Far) for a in args]
    args = [
        pltpu.with_memory_space_constraint(a.value, pltpu.HBM) if isinstance(a, Far) else a
        for a in args
    ]
    far_out = [len(o) > 2 for o in outs]
    if Order.last is not None:
        args[0] = after(args[0], Order.last)
    held = [(a.shape, a.dtype) for a, far in zip(args, plan) if far]
    held += [o[:2] for o, far in zip(outs, far_out) if far]
    need = sum(math.prod(s) * jnp.dtype(d).itemsize for s, d in [*held, *scratch])
    run = pl.pallas_call(
        functools.partial(
            loading_body,
            body,
            plan,
            len(outs),
            far_out,
            late,
            [a.view for a in ahead],
            len(scratch),
        ),
        out_shape=[
            pltpu.HBM(o[0], o[1]) if far else jax.ShapeDtypeStruct(o[0], o[1])
            for o, far in zip(outs, far_out)
        ]
        + [jax.ShapeDtypeStruct(a.shape, a.value.dtype) for a in ahead],
        in_specs=[
            scalars if i in smem else distant if plan[i] else whole for i in range(len(args))
        ]
        + [distant] * len(ahead),
        out_specs=[distant if far else whole for far in far_out] + [whole] * len(ahead),
        scratch_shapes=[pltpu.VMEM(s, d) for s, d in [*scratch, *held]]
        + [pltpu.SemaphoreType.DMA((max(len(held) + len(ahead), 1),))],
        compiler_params=pltpu.CompilerParams(vmem_limit_bytes=(mib << 20) + need),
        cost_estimate=pl.CostEstimate(flops=1, bytes_accessed=1, transcendentals=0),
    )
    moved = [pltpu.with_memory_space_constraint(a.value, pltpu.HBM) for a in ahead]
    got = list(run(*args, *moved))
    Order.last = got[0]
    return got


def far(values):
    return [Far(v) for v in values]


def join(slots):
    half = slots[0].shape[0] // 2
    return jnp.concatenate([s[:half] for s in slots] + [s[half:] for s in slots], axis=0)


def slot_rows(rows, k, count):
    half = rows.shape[0] // (2 * count)
    low = k * half
    high = rows.shape[0] // 2 + k * half
    return jnp.concatenate([rows[low : low + half], rows[high : high + half]], axis=0)


def centred(rows):
    centre = rows - jnp.mean(rows, axis=-1, keepdims=True)
    scale = lax.rsqrt(jnp.mean(centre * centre, axis=-1, keepdims=True) + 1e-05)
    return centre * scale, scale


def fill(scratch, own, other, core):
    half = own.shape[0]
    scratch[pl.ds(pl.multiple_of(core * half, half), half), :] = own[...]
    scratch[pl.ds(pl.multiple_of((1 - core) * half, half), half), :] = other[...]


def pick_gain(own, other, which, core):
    a = own[which : which + 1, :].astype(F32)
    b = other[which : which + 1, :].astype(F32)
    first = jnp.where(core == 0, a, b)
    second = jnp.where(core == 0, b, a)
    return jnp.concatenate([first, second], axis=1)


def route_rows(pieces):
    lane = lax.broadcasted_iota(I32, (8, 128), 1)
    low = lane < 64
    rolled = [pltpu.roll(p, 64, 1) for p in pieces]
    count = len(pieces)
    front = [jnp.where(low, pieces[i], rolled[i + 1]) for i in range(0, count, 2)]
    back = [jnp.where(low, rolled[i], pieces[i + 1]) for i in range(0, count, 2)]
    return jnp.concatenate(front + back, axis=1)


def pack_body(count, rest, *refs):
    tok, routes = refs[:2]
    place = lax.axis_index("ctx") // rest
    local, dim = tok.shape[1:]
    for k, out in enumerate(refs[2:]):
        out[:local, :] = tok[place ^ (k + 1)]
        out[local:, :] = jnp.zeros((8, dim), BF)
        out[local : local + TWO, :128] = routes[place ^ (k + 1)].astype(F32).astype(BF)


def pack_all_body(count, rest, *refs):
    tok, routes, query, kv, router, out = refs[:6]
    pieces, packed = refs[6:-1], refs[-1]
    pack_body(count, rest, tok, routes, *pieces)
    Order.rest()
    half, cols = query.shape
    keys = kv.shape[1]
    packed[half:, :] = jnp.zeros((8, packed.shape[1]), BF)
    packed[:half, :cols] = query[...]
    packed[:half, cols : cols + keys] = kv[...]
    packed[:half, cols + keys :] = out[...]
    packed[half:, :half] = router[...]


def fill_router(wr, own, packed, core):
    half = own.shape[1]
    wr[...] = jnp.zeros_like(wr)
    experts = own.shape[0]
    mine = pl.ds(pl.multiple_of(core * half, half), half)
    theirs = pl.ds(pl.multiple_of((1 - core) * half, half), half)
    wr[:experts, mine] = own[...].astype(F32)
    wr[:experts, theirs] = packed[half:, :half].astype(F32)


def keys_body(count, rest, *refs):
    toks = refs[:count]
    routes, g_own, g_other, k_own, packed = refs[count : count + 5]
    kv_out, normed_out, tok_out, gain_out, wk, tail_out = refs[count + 5 :]
    core = lax.axis_index("wsh")
    place = lax.axis_index("ctx") // rest
    half = k_own.shape[0]
    local = toks[0].shape[0]
    keys = k_own.shape[1]
    cols = packed.shape[1] - keys - toks[0].shape[1]
    fill(wk, k_own, packed.at[:half, cols : cols + keys], core)
    rows = join([t[:local] for t in toks])
    tok_out[...] = rows
    Order.leave(2, 4)
    tail_out[...] = jnp.zeros_like(tail_out)
    tail_out[:TWO, :] = routes[place].astype(F32)
    for k in range(1, count):
        tail_out[8 * k : 8 * k + 8, :] = toks[k][local : local + 8, :128].astype(F32)
    rows = rows.astype(F32)
    unit, _ = centred(rows)
    gain_out[...] = jnp.zeros_like(gain_out)
    for which in range(TWO):
        gain_out[which : which + 1, :] = pick_gain(g_own, g_other, which, core)
    normed = (unit * gain_out[0:1, :]).astype(BF)
    normed_out[...] = normed
    Order.leave(1, 3)
    kv = mm(normed, wk[...]).astype(BF)
    for i in range(kv_out.shape[0]):
        kv_out[i] = kv


def project_body(count, experts, head, *refs):
    normed_ref, tails, q_own, r_own, o_own, packed = refs[:6]
    qt_out, nt_out, gate_out, gate_far, route_out, route_far, wq, wr, wo = refs[6:]
    core = lax.axis_index("wsh")
    half, cols = q_own.shape
    normed = normed_ref[...]
    nt_out[...] = normed.T
    Order.leave(1)
    Order.rest()
    fill(wq, q_own, packed.at[:half, :cols], core)
    fill_router(wr, r_own, packed, core)
    fill(wo, o_own, packed.at[:half, packed.shape[1] - o_own.shape[1] :], core)
    Order.leave(6, 7, 8)
    routes = route_rows([tails[8 * k : 8 * k + 8, :] for k in range(count)])
    route_out[...] = routes
    route_far[...] = routes
    logits = mm(wr[...].astype(BF), normed, 1, 1)
    queries = mm(wq[...], normed, 0, 1) * 0.125
    chosen = []
    for s in range(TWO):
        route = routes[s : s + 1]
        total = jnp.zeros((head, normed.shape[0]), F32)
        value = jnp.zeros((1, normed.shape[0]), F32)
        for e in range(experts):
            here = route == e
            total = jnp.where(here, queries[e * head : (e + 1) * head], total)
            value = jnp.where(here, logits[e : e + 1], value)
        qt_out[s * head : (s + 1) * head, :] = total.astype(BF)
        chosen.append(value)
    top = jnp.maximum(chosen[0], chosen[1])
    raised = [jnp.exp(c - top) for c in chosen]
    total = raised[0] + raised[1]
    gate_out[...] = jnp.concatenate([r / total for r in raised], axis=0)
    gate_far[...] = gate_out[...]


def places(order, count, rest, block, width, part):
    me = lax.axis_index("ctx")
    place, other = me // rest, me % rest
    size = count * rest
    lane = lax.broadcasted_iota(I32, (1, width), 1)
    out = jnp.zeros((1, width), I32)
    for k in range(count):
        first = order[(place ^ k) * rest + other]
        base = jnp.where(part == 0, first, 2 * size - 1 - first) * block
        out = jnp.where(lane // block == k, lane - k * block + base, out)
    return out


def key_bases(order, count, rest, block, chunk, part):
    me = lax.axis_index("ctx")
    place = me // rest
    size = count * rest
    out = []
    for k in range(count):
        first = order[(place ^ k) * rest + chunk]
        out.append((first if part == 0 else 2 * size - 1 - first) * block)
    return out


def masked(scores, gap, bases, block):
    parts = [
        jnp.where(gap <= -base, scores[k * block : (k + 1) * block], NONE)
        for k, base in enumerate(bases)
    ]
    return jnp.concatenate(parts, axis=0)


def scored(kv, side, h, gap, order, count, rest, block, chunk, half):
    first = mm(kv[:half], side)
    if h == 0:
        return masked(first, gap, key_bases(order, count, rest, block, chunk, 0), block)
    second = mm(kv[half:], side)
    second = masked(second, gap, key_bases(order, count, rest, block, chunk, 1), block)
    return jnp.concatenate([first, second], axis=0)


def turn_keys(kv, kv_turned):
    rows = kv.shape[1]
    for c in range(kv.shape[0]):
        kv_turned[:, c * rows : (c + 1) * rows] = kv[c].T


def both_slots(rows, head, cols):
    return jnp.concatenate([rows[s * head : (s + 1) * head, cols] for s in range(TWO)], axis=1)


def gap_rows(order, count, rest, block, half, h):
    gap = lax.broadcasted_iota(I32, (block, half), 0) - places(order, count, rest, block, half, h)
    return jnp.concatenate([gap] * TWO, axis=1)


def attend_body(count, rest, experts, head, *refs):
    order, kv_ref, qt, gates, routes = refs[:5]
    tok, gains, wo = refs[5:8]
    att_out, log_out, mixed_out, hidden_out, two_out, turned_out, kv_out, kv_turned = refs[8:]
    kv_out[...] = kv_ref[...]
    Order.leave(6)
    other = lax.axis_index("ctx") % rest
    total = qt.shape[1]
    half = total // 2
    block = half // count
    turn_keys(kv_ref, kv_turned)
    sides, gaps = [], []
    for h in range(2):
        side = both_slots(qt, head, slice(h * half, (h + 1) * half))
        sides.append(jnp.concatenate([side, jnp.zeros_like(side)], axis=0))
        gaps.append(gap_rows(order, count, rest, block, half, h))

    def step(turn, carry):
        chunk = turn ^ other
        at = pl.multiple_of(chunk * total, total)
        kv = kv_ref[chunk]
        scores = [
            scored(kv, sides[h], h, gaps[h], order, count, rest, block, chunk, half)
            for h in range(2)
        ]
        out = []
        for h in range(2):
            top, norm, summed = carry[h]
            fresh = jnp.maximum(top, jnp.max(scores[h], axis=0, keepdims=True))
            shares = jnp.exp(scores[h] - fresh)
            fade = jnp.exp(top - fresh)
            norm = norm * fade + jnp.sum(shares, axis=0, keepdims=True)
            values = kv_turned[head:, pl.ds(at, half * (h + 1))]
            out.append((fresh, norm, summed * fade + mm(values, shares.astype(BF))))
        return tuple(out)

    start = (
        jnp.full((1, TWO * half), NONE, F32),
        jnp.zeros((1, TWO * half), F32),
        jnp.zeros((head, TWO * half), F32),
    )
    done = lax.fori_loop(0, rest, step, (start, start), unroll=rest <= 4)
    for h in range(2):
        top, norm, summed = done[h]
        logs, attended = top + jnp.log(norm), summed / norm
        for s in range(TWO):
            here, cols = slice(h * half, (h + 1) * half), slice(s * half, (s + 1) * half)
            log_out[s : s + 1, here] = logs[:, cols]
            att_out[s * head : (s + 1) * head, here] = attended[:, cols]
    Order.rest()
    Order.leave(0, 1)
    for e in range(experts):
        part = jnp.zeros((head, total), F32)
        for s in range(TWO):
            gate = jnp.where(routes[s : s + 1] == e, gates[s : s + 1], 0.0)
            part = part + gate * att_out[s * head : (s + 1) * head, :]
        mixed_out[e * head : (e + 1) * head, :] = part.astype(BF)
    Order.leave(2)
    hidden = tok[...].astype(F32) + mm(mixed_out[...].T, wo[...])
    hidden_out[...] = hidden
    unit, _ = centred(hidden)
    two = (unit * gains[1:2, :]).astype(BF)
    two_out[...] = two
    turned_out[...] = two.T


def feed_body(count, rest, first, tile, *refs):
    two, turned = refs[:2]
    if first:
        slots = refs[2 : 2 + count]
        u_own, u_other, down, layer_in = refs[2 + count : 6 + count]
        layer_out, back_out, send, keep, cots, cot_far, send_up, up = refs[6 + count :]
    else:
        cots, u_own, u_other, down, layer_in, back_in = refs[2:8]
        outs = refs[8 : 12 + count]
        layer_pieces, back_out, keep_down, keep, send = outs[:count], *outs[count:]
        up, layer_out = refs[12 + count :]
    core = lax.axis_index("wsh")
    side = (1 - core) if first else core
    width = down.shape[0]
    half = u_own.shape[0]
    lanes = pl.ds(pl.multiple_of(side * width, width), width)
    up[pl.ds(pl.multiple_of(core * half, half), half), :] = u_own[...]
    up[pl.ds(pl.multiple_of((1 - core) * half, half), half), :] = u_other[:, lanes]
    if first:
        cots[...] = join([o[...] for o in slots])
        cot_far[...] = cots[...]
        Order.leave(5)
    layer_out[...] = layer_in[...]
    if first:
        back_out[...] = jnp.zeros_like(back_out)
    else:
        back_out[...] = back_in[...]
    mine = pl.ds(pl.multiple_of(core * half, half), half)
    theirs = pl.ds(pl.multiple_of((1 - core) * half, half), half)
    dim = up.shape[0]
    per = dim // tile

    def products(j):
        cols = slice(j * tile, (j + 1) * tile)
        return mm(two[...], up[:, cols]), mm(cots[...], down[cols, :], 1, 1)

    steps = width // tile
    ready = products(0)
    for j in range(steps):
        cols = slice(j * tile, (j + 1) * tile)
        pre, back = ready
        if j + 1 < steps:
            ready = products(j + 1)
        phi = 0.5 * (1.0 + lax.erf(pre * math.sqrt(0.5)))
        bell = jnp.exp(pre * pre * -0.5) * (1.0 / math.sqrt(2.0 * math.pi))
        act = (pre * phi).astype(BF)
        back_pre = (back * (phi + pre * bell)).astype(BF)
        layer_out[...] += mm(act, down[cols, :])
        back_out[...] += mm(back_pre, up[:, cols], 1, 1)
        grad = mm(act.T, cots[...]).astype(BF)
        grad_mine = mm(turned[mine, :], back_pre).astype(BF)
        grad_theirs = mm(turned[theirs, :], back_pre).astype(BF)
        rows = slice((j // per) * half, (j // per + 1) * half)
        lane = slice((j % per) * tile, (j % per + 1) * tile)
        keep[rows, lane] = grad_mine
        if first:
            send[cols, :] = grad
            send_up[rows, lane] = grad_theirs
        else:
            keep_down[cols, :] = grad
            send[rows, lane] = grad_theirs
    if not first:
        Order.leave(count + 1, count + 2, count + 3)
        for k in range(count):
            layer_pieces[k][...] = slot_rows(layer_out[...], k, count).astype(layer_pieces[k].dtype)


def turn_body(count, rest, experts, head, *refs):
    hidden, back_two, cot, wo, gain, gates, routes, att = refs[:8]
    back_hidden_out, branch_out, grad_att_out, delta_out, logit_out, gain_out = refs[8:]
    unit, scale = centred(hidden[...])
    back = back_two[...]
    side = back * gain[1:2, :]
    part = scale * (
        side
        - jnp.mean(side, axis=-1, keepdims=True)
        - unit * jnp.mean(side * unit, axis=-1, keepdims=True)
    )
    gain_out[...] = jnp.broadcast_to(jnp.sum(back * unit, axis=0, keepdims=True), gain_out.shape)
    back_hidden = cot[...].astype(F32) + part
    back_hidden_out[...] = back_hidden
    branch = back_hidden.astype(BF)
    branch_out[...] = branch
    Order.leave(0, 1, 5)
    back_mixed = mm(wo[...], branch, 1, 1)
    grads = []
    for s in range(TWO):
        total = jnp.zeros((head, branch.shape[0]), F32)
        for e in range(experts):
            total = jnp.where(routes[s : s + 1] == e, back_mixed[e * head : (e + 1) * head], total)
        att_s = att[s * head : (s + 1) * head, :]
        grads.append(jnp.sum(total * att_s, axis=0, keepdims=True))
        low = (gates[s : s + 1] * total).astype(BF)
        grad_att_out[s * head : (s + 1) * head, :] = low
        delta_out[s : s + 1, :] = jnp.sum(low.astype(F32) * att_s, axis=0, keepdims=True)
    mean = gates[0:1] * grads[0] + gates[1:2] * grads[1]
    row = lax.broadcasted_iota(I32, logit_out.shape, 0)
    logit = jnp.zeros(logit_out.shape, F32)
    for s in range(TWO):
        value = gates[s : s + 1] * (grads[s] - mean)
        logit = logit + jnp.where(row.astype(F32) == routes[s : s + 1], value, 0.0)
    logit_out[...] = logit


def turn_start_body(count, rest, experts, head, layout, step, *refs):
    ins, early, outs, pieces = refs[:8], refs[8:12], refs[12:18], refs[18]
    turn_body(count, rest, experts, head, *ins, *outs)
    Order.rest()
    start_body(layout, True, 1, step, len(early), *early, pieces, None)


def attend_back_body(count, rest, head, split, *refs):
    order, kv_ref, qt, grad_att, logs, delta, grad_q_out = refs[:7]
    outs = refs[7 : 7 + split]
    kv_turned, sides, turned, grad_kv, grad_q = refs[7 + split :]
    total = qt.shape[1]
    half = total // 2
    block = half // count
    wide = TWO * half
    turn_keys(kv_ref, kv_turned)
    blank = jnp.zeros((head, wide), BF)
    for h in range(2):
        cols = slice(h * half, (h + 1) * half)
        q_side = jnp.concatenate([both_slots(qt, head, cols), blank], axis=0)
        g_side = jnp.concatenate([blank, both_slots(grad_att, head, cols)], axis=0)
        sides[2 * h], sides[2 * h + 1] = q_side, g_side
        turned[h, :wide, :], turned[h, wide:, :] = q_side.T, g_side.T
    grad_q[...] = jnp.zeros_like(grad_q)
    gaps = [gap_rows(order, count, rest, block, half, h) for h in range(2)]
    log_rows = [both_slots(logs, 1, slice(h * half, (h + 1) * half)) for h in range(2)]
    delta_rows = [both_slots(delta, 1, slice(h * half, (h + 1) * half)) for h in range(2)]

    def step(chunk, carry):
        at = pl.multiple_of(chunk * total, total)
        kv = kv_ref[chunk]
        grads = []
        for h in range(2):
            reach = half * (h + 1)
            scores = scored(
                kv, sides[2 * h], h, gaps[h], order, count, rest, block, chunk, half
            )
            shares = jnp.exp(scores - log_rows[h])
            back_shares = mm(kv[:reach], sides[2 * h + 1])
            back_scores = (shares * (back_shares - delta_rows[h])).astype(BF)
            both = jnp.concatenate([back_scores, shares.astype(BF)], axis=1)
            grads.append(mm(both, turned[h]))
            grad_q[h] += mm(kv_turned[:head, pl.ds(at, reach)], back_scores)
        grad_kv[pl.ds(at, half), :] = grads[0] + grads[1][:half]
        grad_kv[pl.ds(at + half, half), :] = grads[1][half:]
        return carry

    lax.fori_loop(0, rest, step, 0, unroll=rest <= 4)
    for h in range(2):
        for s in range(TWO):
            here, cols = slice(h * half, (h + 1) * half), slice(s * half, (s + 1) * half)
            grad_q_out[s * head : (s + 1) * head, here] = grad_q[h, :, cols].astype(BF)
    rows = outs[0].shape[0]
    digit = (lax.axis_index("ctx") % rest) // (rest // split)
    for i, out in enumerate(outs):
        begin = pl.multiple_of((digit ^ i) * rows, rows)
        out[...] = grad_kv[pl.ds(begin, rows), :].astype(out.dtype)


def query_body(experts, head, *refs):
    grad_q, normed_t, routes, mixed, branch, wq, wr, logit, tok = refs[:9]
    keep_out, keep, send, back_out, unit_out, scale_out, routers, bqt = refs[9:]
    core = lax.axis_index("wsh")
    total = grad_q.shape[1]
    for e in range(experts):
        part = jnp.zeros((head, total), F32)
        for s in range(TWO):
            value = grad_q[s * head : (s + 1) * head, :].astype(F32) * 0.125
            part = jnp.where(routes[s : s + 1] == e, value, part)
        bqt[e * head : (e + 1) * head, :] = part.astype(BF)
    back_q = bqt[...].T
    half = keep.shape[0]
    mine = pl.ds(pl.multiple_of(core * half, half), half)
    theirs = pl.ds(pl.multiple_of((1 - core) * half, half), half)
    send[:half, :] = mm(mixed[theirs, :], branch[...]).astype(BF)
    send[half:, :] = mm(normed_t[theirs, :], back_q).astype(BF)
    keep_out[...] = mm(mixed[mine, :], branch[...]).astype(BF)
    keep[...] = mm(normed_t[mine, :], back_q).astype(BF)
    Order.leave(0, 1, 2)
    parts = []
    left = logit[...]
    for _ in range(3):
        low = left.astype(BF)
        parts.append(low)
        left = left - low.astype(F32)
    routers[...] = parts_dot(parts, normed_t[...])
    back = mm(back_q, wq[...], 1, 1)
    wr_turned = wr[...].astype(BF)
    for low in parts:
        padded = jnp.concatenate([low.astype(F32), jnp.zeros((120, total), F32)], axis=0)
        back = back + mm(padded.T.astype(BF), wr_turned)
    back_out[...] = back
    unit, scale = centred(tok[...].astype(F32))
    unit_out[...] = unit
    scale_out[...] = jnp.broadcast_to(scale, scale_out.shape)


def unproject_body(count, terms, *refs):
    kv_terms = refs[:terms]
    back_part, unit_ref, scale_ref, routers, normed_t, back_hidden, wk, gain, gain_two, sent = refs[
        terms : terms + 10
    ]
    at = terms + 10
    pieces = refs[at : at + count]
    keep, send, gains = refs[at + count :]
    core = lax.axis_index("wsh")
    half = back_part.shape[1] // 2
    back_kv = kv_terms[0][...].astype(F32)
    for term in kv_terms[1:]:
        back_kv = back_kv + term[...].astype(F32)
    back_kv = back_kv.astype(BF)
    back = back_part[...] + mm(back_kv, wk[...], 1, 1)
    unit, scale = unit_ref[...], scale_ref[:, 0:1]
    side = back * gain[0:1, :]
    grad = back_hidden[...] + scale * (
        side
        - jnp.mean(side, axis=-1, keepdims=True)
        - unit * jnp.mean(side * unit, axis=-1, keepdims=True)
    )
    gains[0:1, :] = jnp.sum(back * unit, axis=0, keepdims=True)
    gains[1:2, :] = gain_two[0:1, :]
    step = half // 4
    experts = routers.shape[0]
    high = sent.shape[0]
    Order.rest()
    send[:high, :] = sent[...]
    for out, which in ((keep, core), (send.at[high:, :], 1 - core)):
        mine = pl.ds(pl.multiple_of(which * half, half), half)
        grad_k = mm(normed_t[mine, :], back_kv).astype(out.dtype)
        for j in range(4):
            out[:step, j * 128 : (j + 1) * 128] = grad_k[j * step : (j + 1) * step]
        blank = jnp.zeros((experts, half), F32)
        out[step : step + 8, :] = jnp.concatenate([routers[:, mine], blank], axis=1).astype(out.dtype)
        gain_pair = jnp.concatenate([gains[0:1, mine], gains[1:2, mine]], axis=1)
        out[step + 8 :, :] = jnp.broadcast_to(gain_pair, (8, 2 * half)).astype(out.dtype)
    Order.leave(count, count + 1)
    for k in range(count):
        pieces[k][...] = slot_rows(grad, k, count).astype(pieces[k].dtype)


def parts_dot(parts, normed_t):
    out = None
    for low in parts:
        value = mm(low, normed_t, 1, 1)
        out = value if out is None else out + value
    return out


def sum_layout(layout, ins, total):
    at = 0
    for terms in layout:
        height = terms[0][2]
        value = None
        for index, begin, count in terms:
            part = ins[index][begin : begin + count, :].astype(F32)
            value = part if value is None else value + part
        total[at : at + height, :] = value
        at += height
    if at < total.shape[0]:
        total[at:, :] = jnp.zeros((total.shape[0] - at, total.shape[1]), F32)


def cut_rows(total, outs, stride, step):
    rows = outs[0].shape[0]
    digit = (lax.axis_index("ctx") // stride) % step
    for j in range(step):
        begin = pl.multiple_of((digit ^ j) * rows, 8)
        outs[j][...] = total[pl.ds(begin, rows), :].astype(outs[j].dtype)


def start_body(layout, whole, stride, step, n_in, *refs):
    ins, outs, total = refs[:n_in], refs[n_in:-1], refs[-1]
    if whole:
        rows = outs[0].shape[1]
        at = 0
        for terms in layout:
            height, done = terms[0][2], 0
            while done < height:
                j, low = (at + done) // rows, (at + done) % rows
                take = min(height - done, rows - low)
                value = None
                for index, begin, _ in terms:
                    part = ins[index][begin + done : begin + done + take, :].astype(F32)
                    value = part if value is None else value + part
                outs[0][j, low : low + take, :] = value.astype(BF)
                done += take
            at += height
        while at < rows * step:
            j, low = at // rows, at % rows
            outs[0][j, low:, :] = jnp.zeros((rows - low, outs[0].shape[2]), BF)
            at += rows - low
    else:
        sum_layout(layout, ins, total)
        cut_rows(total, outs, stride, step)


def terms_of(ref):
    return [ref.at[j] for j in range(ref.shape[0])] if len(ref.shape) == 3 else [ref]


def middle_body(chunks, stride, step, n_in, riders, *refs):
    ins, riding = refs[:n_in], refs[n_in : n_in + riders]
    refs = refs[n_in + riders :]
    outs, totals = refs[:step], refs[step:]
    digit = (lax.axis_index("ctx") // stride) % step
    at, low = 0, 0
    for count, total in zip(chunks, totals):
        value = None
        for ref in ins[at : at + count]:
            for term in terms_of(ref):
                part = term[...].astype(F32)
                value = part if value is None else value + part
        total[...] = value
        rows = total.shape[0] // step
        for j in range(step):
            begin = pl.multiple_of((digit ^ j) * rows, 8)
            outs[j][low : low + rows, :] = total[pl.ds(begin, rows), :].astype(outs[j].dtype)
        low += rows
        at += count
    for j in range(1, step if riders else 1):
        outs[j][low:, :] = riding[j - 1][...]


def copies_body(slices, n_in, *refs):
    ins, out = refs[:n_in], refs[-1]
    for j in range(out.shape[0]):
        at = 0
        for begin, rows in slices:
            for ref in ins:
                out[j, at : at + rows, :] = ref[begin : begin + rows, :]
                at += rows


def final_body(strides, parts, dests, n_out, *refs):
    got, outs, totals = refs[0], refs[1 : 1 + n_out], refs[1 + n_out :]
    me = lax.axis_index("ctx")
    shift, per = 0, 1
    for stride, step in strides[1:]:
        shift = shift * step + (me // stride) % step
        per *= step
    at, used = 0, 0
    for height, total, (dest, many) in zip(parts, totals, dests):
        rows = height // per
        swapped = isinstance(got, tuple)
        digit = me % strides[0][1] if swapped else 0
        for i in range(len(got) if swapped else got.shape[0]):
            for b in range(per):
                begin = pl.multiple_of(((i ^ digit) * per + (b ^ shift)) * rows, 8)
                source = got[i].at[0] if swapped else got.at[i]
                piece = source[at + b * rows : at + (b + 1) * rows, :]
                total[pl.ds(begin, rows), :] = piece.astype(F32)
        at += height
        dest(total, outs[used : used + many])
        Order.leave(*range(used, used + many))
        used += many


WIDTH = 512


def cut_up(chunks, heights, strides, at, size, riders=()):
    stride, step = strides[at]
    total = sum(heights) // step
    more = riders[0].shape[0] if riders else 0
    n_in = sum(len(c) for c in chunks)
    pieces = call(
        functools.partial(middle_body, [len(c) for c in chunks], stride, step, n_in, len(riders)),
        [((total, WIDTH), F32)] + [((total + more, WIDTH), BF)] * (step - 1),
        [t for c in chunks for t in c] + far(riders),
        scratch=[((h, WIDTH), F32) for h in heights],
    )
    return pieces[:1] + [swap(pieces[j], j * stride, size) for j in range(1, step)]


def spread(done, strides, at, size):
    stride, step = strides[at]
    return [done] + [swap(done, j * stride, size) for j in range(1, step)]


def settle(terms):
    return call(add_body, [(terms[0].shape, BF)], terms)[0]


def add_body(*refs):
    rows = refs[-1].shape[0]
    value = refs[0][:rows, :].astype(F32)
    for ref in refs[1:-1]:
        value = value + ref[:rows, :].astype(F32)
    refs[-1][...] = value.astype(refs[-1].dtype)


def early_dest(total, outs):
    down, tile = outs
    wide = down.shape[0]
    down[...] = total[:wide, :]
    tile[...] = total[wide : wide + tile.shape[0], :]


def both_final_body(strides, parts, n_in, *refs):
    got, tile = refs[:n_in], refs[n_in]
    outs, totals = refs[n_in + 1 : n_in + 8], refs[n_in + 8 :]

    def main(total, outs):
        (up,) = outs
        half = up.shape[0]
        core = lax.axis_index("wsh")
        tiles = up.shape[1] // WIDTH
        for i in range(tiles):
            side, inner = i // (tiles // 2), i % (tiles // 2)
            at = (core if side == 0 else 1 - core) * (tiles // 2) + inner
            rows = tile[...] if i == 0 else total[(i - 1) * half : i * half, :]
            up[:, pl.ds(pl.multiple_of(at * WIDTH, WIDTH), WIDTH)] = rows

    dests = [(main, 1), (late_dest, 6)]
    final_body(strides, parts, dests, 7, got, *outs, *totals)


def late_dest(total, outs):
    out, query, kv, router, one, two = outs
    half = kv.shape[0]
    out[...] = total[:half, :]
    query[...] = total[half : 2 * half, :]
    step = half // 4
    at = 2 * half
    for j in range(4):
        kv[j * step : (j + 1) * step, :] = total[at : at + step, j * 128 : (j + 1) * 128]
    at += step
    router[...] = total[at : at + router.shape[0], :half]
    one[...] = total[at + 8 : at + 9, :half]
    two[...] = total[at + 8 : at + 9, half:]


def place_body(rest, *refs):
    place = lax.axis_index("ctx") // rest
    out = refs[-1]
    local = out.shape[1]
    for k, ref in enumerate(refs[:-1]):
        begin = ref.shape[0] - local
        out[place ^ k] = ref[begin:, :].astype(F32)


def close_body(rest, count, strides, parts, n_in, *refs):
    main, moved = refs[: n_in + 1], refs[n_in + 1 : n_in + 1 + count]
    outs, totals = refs[n_in + 1 + count : n_in + 9 + count], refs[n_in + 9 + count :]
    place_body(rest, *moved, outs[7])
    Order.leave(7)
    both_final_body(strides, parts, n_in, *main, *outs[:7], *totals)


def on_device(
    tokens,
    routes,
    block_order,
    norm_gain1,
    router_w,
    query_w,
    kv_w,
    out_w,
    norm_gain2,
    up_w,
    down_w,
    cotangent,
):
    size = lax.axis_size("ctx")
    count, local, dim = tokens.shape
    rest = size // count
    place = lax.axis_index("ctx") // rest
    total = count * local
    experts = router_w.shape[1]
    head = kv_w.shape[1] // 2
    feed = up_w.shape[1]

    Order.last = None
    tall = dim // 2
    keys = 2 * head
    router_t = router_w.T
    routes_t = routes.transpose(0, 2, 1)

    def core():
        return lax.axis_index("wsh")

    def here():
        return lax.axis_index("ctx") // rest

    got = call(
        functools.partial(pack_all_body, count, rest),
        [((local + 8, dim), BF)] * (count - 1) + [((tall + 8, experts * head + keys + dim), BF)],
        far([tokens, routes_t, query_w, kv_w, router_t, out_w]),
        late=(2, 3, 4, 5),
        ahead=[Ahead(tokens, (local, dim), lambda r: r.at[here()]), Ahead(kv_w)]
        + [
            Ahead(cotangent, (local, dim), lambda r, k=k: r.at[here() ^ k])
            for k in range(1, count)
        ],
    )
    tok_pieces, (packed, tok_own, kv_own), cot_pieces = got[: count - 1], got[count - 1 : count + 2], got[count + 2 :]
    tok_x = [swap(tok_pieces[k - 1], k * rest, size) for k in range(1, count)]
    packed_x = trade(packed)
    gain_one, gain_two = after((norm_gain1, norm_gain2), packed)
    gains = jnp.stack([gain_one, gain_two])
    gains_x = trade(gains)

    steps = factors(rest)
    kv, normed, tok, gain_rows, wk, tails = call(
        functools.partial(keys_body, count, rest),
        [
            ((steps[0], total, keys), BF, 1),
            ((total, dim), BF, 1),
            ((total, dim), BF, 1),
            ((8, dim), F32, 1),
            ((dim, keys), BF, 1),
            ((8 * count, 128), F32),
        ],
        [tok_own, *tok_x, Far(routes_t), gains, gains_x, kv_own, packed_x],
    )
    stride = 1
    for i, step in enumerate(steps):
        if i > 0:
            kv = jnp.broadcast_to(kv[None], (step,) + kv.shape)
        kv = exchange(kv, stride, size).reshape(-1, total, keys)
        stride *= step
    cot_pieces = after(tuple(cot_pieces), normed)
    cot_x = [swap(cot_pieces[k - 1], k * rest, size) for k in range(1, count)]
    qt, normed_t, gates, gates_far, route, route_far, wq, wr, wo = call(
        functools.partial(project_body, count, experts, head),
        [
            ((TWO * head, total), BF, 1),
            ((dim, total), BF, 1),
            ((TWO, total), F32),
            ((TWO, total), F32, 1),
            ((8, total), F32),
            ((8, total), F32, 1),
            ((dim, experts * head), BF, 1),
            ((128, dim), F32, 1),
            ((experts * head, dim), BF, 1),
        ],
        [Far(normed), tails, *far([query_w, router_t, out_w]), packed_x],
        late=(2, 3, 4),
    )
    up_w2, down_w2, _ = lax.optimization_barrier((up_w, down_w, normed))
    up_x, down_x = trade(up_w2), trade(down_w2)
    span = rest * total
    wide = feed // 2

    def lanes(which):
        def view(ref):
            side = which()
            return ref.at[:, pl.ds(pl.multiple_of(side * wide, wide), wide)]

        return view

    att, logs, mixed, hidden, two, two_t, kv_far, cot_own, up_first = call(
        functools.partial(attend_body, count, rest, experts, head),
        [
            ((TWO * head, total), F32, 1),
            ((TWO, total), F32, 1),
            ((experts * head, total), BF, 1),
            ((total, dim), F32),
            ((total, dim), BF),
            ((dim, total), BF),
            ((rest, total, keys), BF, 1),
        ],
        [block_order, kv, Far(qt), gates, route, *far([tok, gain_rows, wo])],
        scratch=[((keys, span), BF)],
        smem=(0,),
        late=(5, 6, 7),
        ahead=[
            Ahead(cotangent, (local, dim), lambda r: r.at[here()]),
            Ahead(up_w, (tall, wide), lanes(lambda: 1 - core())),
        ],
    )

    tile = 512
    upper = wide * tall // dim
    layer, back_two, send_one, keep_one, cots, cots_far, send_up, up_second, down_own = call(
        functools.partial(feed_body, count, rest, True, tile),
        [
            ((total, dim), F32),
            ((total, dim), F32),
            ((wide, dim), BF),
            ((upper, dim), BF, 1),
            ((total, dim), BF),
            ((total, dim), BF, 1),
            ((upper, dim), BF),
        ],
        [two, two_t, cot_own, *cot_x, up_first, up_x, down_x, hidden],
        scratch=[((dim, wide), BF)],
        ahead=[Ahead(up_w, (tall, wide), lanes(core)), Ahead(down_w)],
    )
    recv_down, recv_up = trade(send_one), trade(send_up)
    *layer_pieces, back_two, keep_down, keep_two, send_two, cots, wo, gain_near, gates, route, att = call(
        functools.partial(feed_body, count, rest, False, tile),
        [((local, dim), F32, 1)]
        + [((local, dim), BF, 1)] * (count - 1)
        + [
            ((total, dim), F32),
            ((wide, dim), BF, 1),
            ((upper, dim), BF, 1),
            ((upper, dim), BF, 1),
        ],
        [two, two_t, cots, up_second, up_x, down_own, layer, back_two],
        scratch=[((dim, wide), BF), ((total, dim), F32)],
        ahead=[
            Ahead(a)
            for a in (cots_far, wo, gain_rows, gates_far, route_far, att)
        ],
    )
    recv_two = trade(send_two)
    layer_got = [layer_pieces[0]] + [swap(layer_pieces[k], k * rest, size) for k in range(1, count)]

    strides = []
    stride = 1
    for step in [*steps, count]:
        strides.append((stride, step))
        stride *= step
    last = len(strides) - 1
    unit = 8 * size
    first = strides[0][1]
    early_rows = -(-(wide + tall) // unit) * unit
    main_rows = -(-(2 * upper - tall) // unit) * unit
    small = tall // 4 + 16
    late_rows = -(-(small + 2 * tall) // unit) * unit

    def bulk(args, layout, height, ahead=()):
        pieces, *near = call(
            functools.partial(start_body, layout, True, 1, first, len(args)),
            [((first, height // first, WIDTH), BF)],
            args,
            scratch=[((8, WIDTH), F32)],
            ahead=ahead,
        )
        return exchange(pieces, 1, size), near

    def inner(terms, height, riders=()):
        height //= first
        for at in range(1, last + 1):
            more = riders if at == last else ()
            terms = cut_up([terms], [height], strides, at, size, more)
            height //= strides[at][1]
        return terms

    def outer(got):
        for at in reversed(range(1, last)):
            got = spread(jnp.concatenate(got, axis=0), strides, at, size)
        return got

    def ready(got, ahead=()):
        rows = got[0].shape[0]
        copies, *near = call(
            functools.partial(copies_body, [(0, rows)], len(got)),
            [((first, rows * len(got), WIDTH), BF)],
            got,
            ahead=ahead,
        )
        return exchange(copies, 1, size), near

    back_hidden, branch, grad_att, delta, logit, gain_two, early, kv_near, qt_near, logs_near = call(
        functools.partial(
            turn_start_body,
            count,
            rest,
            experts,
            head,
            [[(0, 0, wide), (1, 0, wide)], [(2, 0, tall), (3, 0, tall)]],
            first,
        ),
        [
            ((total, dim), F32, 1),
            ((total, dim), BF, 1),
            ((TWO * head, total), BF),
            ((TWO, total), F32),
            ((experts, total), F32, 1),
            ((8, dim), F32, 1),
            ((first, early_rows // first, WIDTH), BF),
        ],
        [
            hidden,
            back_two,
            cots,
            wo,
            gain_near,
            gates,
            route,
            att,
            Far(keep_down),
            recv_down,
            Far(keep_two),
            recv_up,
        ],
        late=(8, 10),
        ahead=[Ahead(a) for a in (kv_far, qt, logs)],
    )
    early = exchange(early, 1, size)
    split = steps[-1]
    share = span // split
    grad_q, *kv_terms = call(
        functools.partial(attend_back_body, count, rest, head, split),
        [((TWO * head, total), BF), ((share, keys), F32, 1)] + [((share, keys), BF, 1)] * (split - 1),
        [block_order, kv_near, qt_near, grad_att, logs_near, delta],
        scratch=[
            ((keys, span), BF),
            ((4, keys, total), BF),
            ((2, 2 * total, keys), BF),
            ((span, keys), F32),
            ((2, head, total), F32),
        ],
        smem=(0,),
        ahead=[Ahead(a) for a in (normed_t, route_far, mixed, branch, wq, wr, logit, tok)],
    )
    kv_terms, ahead = kv_terms[:split], kv_terms[split:]
    stride = rest
    for i, step in reversed(list(enumerate(steps))):
        stride //= step
        if i + 1 < len(steps):
            summed = functools.reduce(lambda a, b: a + b.astype(F32), terms)
            parts = summed.reshape(step, -1, keys)
            digit = (lax.axis_index("ctx") // stride) % step
            kv_terms = [pick(parts, digit ^ j) for j in range(step)]
        terms = [kv_terms[0]] + [
            swap(kv_terms[j].astype(BF), j * stride, size) for j in range(1, step)
        ]
    grad_q = after(grad_q, *layer_got[1:])
    keep_out, keep_query, send_main, back_part, unit_rows, scale_rows, routers, *near = call(
        functools.partial(query_body, experts, head),
        [
            ((tall, dim), BF, 1),
            ((tall, dim), BF, 1),
            ((2 * tall, dim), BF, 1),
            ((total, dim), F32),
            ((total, dim), F32),
            ((total, 128), F32),
            ((experts, dim), F32),
        ],
        [grad_q, *ahead],
        scratch=[((experts * head, total), BF)],
        ahead=[Ahead(a) for a in (normed_t, back_hidden, wk, gain_rows, gain_two, terms[0])],
    )
    *near, term = near
    *input_pieces, keep_late, send_late, keep_two, keep_one = call(
        functools.partial(unproject_body, count, len(terms)),
        [((local, dim), F32, 1)]
        + [((local, dim), BF, 1)] * (count - 1)
        + [((small, dim), F32, 1), ((small + 2 * tall, dim), BF)],
        [term, *terms[1:], back_part, unit_rows, scale_rows, routers, *near, Far(send_main)],
        scratch=[((8, dim), F32)],
        late=(len(terms) + 9,),
        ahead=[Ahead(a) for a in (keep_two, keep_one)],
    )
    recv_late = trade(send_late)
    main, _ = bulk(
        [keep_two, recv_up, keep_one, recv_two],
        [
            [(0, tall, upper - tall), (1, tall, upper - tall)],
            [(2, 0, upper), (3, 0, upper)],
        ],
        main_rows,
    )
    pieces = call(
        functools.partial(
            start_body,
            [
                [(0, 0, tall), (1, 0, tall)],
                [(0, tall, tall), (2, 0, tall)],
                [(0, 2 * tall, small), (3, 0, small)],
            ],
            False,
            1,
            first,
            4,
        ),
        [((late_rows // first, WIDTH), F32)] + [((late_rows // first, WIDTH), BF)] * (first - 1),
        [recv_late, *far([keep_out, keep_query, keep_late])],
        scratch=[((late_rows, WIDTH), F32)],
    )
    late = pieces[:1] + [swap(pieces[j], j, size) for j in range(1, first)]
    early_terms = inner([early], early_rows)
    early_got = outer(spread(settle(early_terms), strides, last, size))
    heights = [main_rows // first, late_rows // first]
    chunks = [[main], late]
    for at in range(1, last):
        chunks = [cut_up([c], [h], strides, at, size) for c, h in zip(chunks, heights)]
        heights = [h // strides[at][1] for h in heights]
    both_terms = cut_up(chunks, heights, strides, last, size)
    heights = [h // count for h in heights]
    (layer_out,) = call(
        functools.partial(place_body, rest),
        [((count, local, dim), F32, 1)],
        [Far(layer_got[0]), *far(layer_got[1:])],
    )
    early_last, _ = ready(early_got)
    both_got = spread(settle(both_terms), strides, last, size)
    slices = [(0, heights[0]), (heights[0], heights[1])]
    for stage in reversed(range(1, last)):
        moved = []
        for begin, h in slices:
            piece = jnp.concatenate([g[begin : begin + h] for g in both_got], axis=0)
            moved.append(spread(piece, strides, stage, size))
        both_got = [jnp.concatenate([m[j] for m in moved], axis=0) for j in range(strides[stage][1])]
        tops = [m[0].shape[0] for m in moved]
        slices = [(0, tops[0]), (tops[0], tops[1])]
    tall_rows = sum(h for _, h in slices) * len(both_got)
    (both_own,) = call(
        functools.partial(copies_body, slices, len(both_got)),
        [((1, tall_rows, WIDTH), BF)],
        both_got,
    )
    both_last = spread(both_own, strides, 0, size)
    input_pieces = after(tuple(input_pieces), both_got[0])
    moved = {k: swap(input_pieces[k], k * rest, size) for k in reversed(range(1, count))}
    input_got = [input_pieces[0]] + [moved[k] for k in range(1, count)]
    grad_down, up_tile = call(
        functools.partial(final_body, strides, [early_rows // first], [(early_dest, 2)], 2),
        [((wide, dim), F32, 1), ((tall, WIDTH), F32)],
        [early_last],
        scratch=[((early_rows, WIDTH), F32)],
    )
    grad_up, grad_out, grad_query, grad_kv, grad_router, grad_one, grad_two, input_grad = call(
        functools.partial(
            close_body,
            rest,
            count,
            strides,
            [main_rows // first, late_rows // first],
            len(both_last),
        ),
        [
            ((tall, feed), F32, 1),
            ((tall, dim), F32, 1),
            ((tall, experts * head), F32, 1),
            ((tall, keys), F32, 1),
            ((experts, tall), F32, 1),
            ((1, tall), F32, 1),
            ((1, tall), F32, 1),
            ((count, local, dim), F32, 1),
        ],
        [*both_last, up_tile, *input_got],
        scratch=[((main_rows, WIDTH), F32), ((late_rows, WIDTH), F32)],
    )
    return (
        layer_out,
        input_grad,
        grad_one.reshape(tall),
        grad_router.T,
        grad_query,
        grad_kv,
        grad_out,
        grad_two.reshape(tall),
        grad_up,
        grad_down,
    )


def solution(mesh):
    placed = (
        P("wsh", "ctx", None),
        P("wsh", "ctx", None),
        P(),
        P("wsh"),
        P("wsh", None),
        P("wsh", None),
        P("wsh", None),
        P("wsh", None),
        P("wsh"),
        P("wsh", None),
        P("wsh", None),
        P("wsh", "ctx", None),
    )
    return jax.shard_map(
        on_device,
        mesh=mesh,
        in_specs=placed,
        out_specs=(
            P("wsh", "ctx", None),
            P("wsh", "ctx", None),
            P("wsh"),
            P("wsh", None),
            P("wsh", None),
            P("wsh", None),
            P("wsh", None),
            P("wsh"),
            P("wsh", None),
            P("wsh", None),
        ),
        check_vma=False,
    )
```

```python
import functools
import math

import jax
import jax.numpy as jnp
from jax import lax
from jax.experimental import pallas as pl
from jax.experimental.pallas import tpu as pltpu
from jax.sharding import PartitionSpec as P

BF = jnp.bfloat16
F32 = jnp.float32
I32 = jnp.int32
NONE = -1e30
TWO = 2


def factors(size):
    out = []
    while size > 1:
        step = 4 if size % 4 == 0 else 2
        out.append(step)
        size //= step
    return out


def swap(values, mask, size):
    return lax.ppermute(values, "ctx", [(i, i ^ mask) for i in range(size)])


def groups_of(stride, step, size):
    out = []
    for i in range(size):
        if (i // stride) % step == 0:
            out.append([i + j * stride for j in range(step)])
    return out


def exchange(parts, stride, size):
    step = parts.shape[0]
    groups = groups_of(stride, step, size)
    return lax.all_to_all(parts, "ctx", 0, 0, tiled=True, axis_index_groups=groups)


def trade(values):
    return lax.ppermute(values, "wsh", [(0, 1), (1, 0)])


def pick(parts, index):
    return lax.dynamic_index_in_dim(parts, index, 0, False)


def mm(a, b, left=1, right=0):
    return lax.dot_general(a, b, (((left,), (right,)), ((), ())), preferred_element_type=F32)


class Order:
    last = None
    rest = None
    leave = None


def after(value, *earlier):
    return lax.optimization_barrier((value, *earlier))[0]


class Far:
    def __init__(self, value):
        self.value = value


class Ahead:
    def __init__(self, value, shape=None, view=None):
        self.value, self.view = value, view
        self.shape = value.shape if shape is None else shape


def loading_body(body, plan, n_out, far_out, late, views, n_scratch, *refs):
    n_in, n_pre = len(plan), len(views)
    ins, pre_in = list(refs[:n_in]), refs[n_in : n_in + n_pre]
    at = n_in + n_pre
    outs, pre_out = list(refs[at : at + n_out]), refs[at + n_out : at + n_out + n_pre]
    at += n_out + n_pre
    own = refs[at : at + n_scratch]
    held, sems = refs[at + n_scratch : -1], refs[-1]
    first, second, ahead, slot = [], [], [], 0
    for i in range(n_in):
        if plan[i]:
            copy = pltpu.make_async_copy(ins[i], held[slot], sems.at[slot])
            (second if i in late else first).append(copy)
            ins[i] = held[slot]
            slot += 1
    leaving = {}
    for i in range(n_out):
        if far_out[i]:
            leaving[i] = pltpu.make_async_copy(held[slot], outs[i], sems.at[slot])
            outs[i] = held[slot]
            slot += 1
    for view, source, target in zip(views, pre_in, pre_out):
        source = source if view is None else view(source)
        ahead.append(pltpu.make_async_copy(source, target, sems.at[slot]))
        slot += 1
    for copy in first + second + ahead:
        copy.start()
    for copy in first:
        copy.wait()

    def rest():
        for copy in second:
            copy.wait()

    gone = []

    def leave(*which):
        for i in which:
            if far_out[i]:
                gone.append(i)
                leaving[i].start()

    Order.rest, Order.leave = rest, leave
    body(*ins, *outs, *own)
    leave(*[i for i in range(n_out) if i not in gone])
    for i in gone:
        leaving[i].wait()
    for copy in ahead:
        copy.wait()


def call(body, outs, args, scratch=(), smem=(), late=(), ahead=(), mib=14):
    whole = pl.BlockSpec(memory_space=pltpu.VMEM)
    scalars = pl.BlockSpec(memory_space=pltpu.SMEM)
    distant = pl.BlockSpec(memory_space=pltpu.HBM)
    plan = [isinstance(a, Far) for a in args]
    args = [
        pltpu.with_memory_space_constraint(a.value, pltpu.HBM) if isinstance(a, Far) else a
        for a in args
    ]
    far_out = [len(o) > 2 for o in outs]
    if Order.last is not None:
        args[0] = after(args[0], Order.last)
    held = [(a.shape, a.dtype) for a, far in zip(args, plan) if far]
    held += [o[:2] for o, far in zip(outs, far_out) if far]
    need = sum(math.prod(s) * jnp.dtype(d).itemsize for s, d in [*held, *scratch])
    run = pl.pallas_call(
        functools.partial(
            loading_body,
            body,
            plan,
            len(outs),
            far_out,
            late,
            [a.view for a in ahead],
            len(scratch),
        ),
        out_shape=[
            pltpu.HBM(o[0], o[1]) if far else jax.ShapeDtypeStruct(o[0], o[1])
            for o, far in zip(outs, far_out)
        ]
        + [jax.ShapeDtypeStruct(a.shape, a.value.dtype) for a in ahead],
        in_specs=[
            scalars if i in smem else distant if plan[i] else whole for i in range(len(args))
        ]
        + [distant] * len(ahead),
        out_specs=[distant if far else whole for far in far_out] + [whole] * len(ahead),
        scratch_shapes=[pltpu.VMEM(s, d) for s, d in [*scratch, *held]]
        + [pltpu.SemaphoreType.DMA((max(len(held) + len(ahead), 1),))],
        compiler_params=pltpu.CompilerParams(vmem_limit_bytes=(mib << 20) + need),
        cost_estimate=pl.CostEstimate(flops=1, bytes_accessed=1, transcendentals=0),
    )
    moved = [pltpu.with_memory_space_constraint(a.value, pltpu.HBM) for a in ahead]
    got = list(run(*args, *moved))
    Order.last = got[0]
    return got


def far(values):
    return [Far(v) for v in values]


def join(slots):
    half = slots[0].shape[0] // 2
    return jnp.concatenate([s[:half] for s in slots] + [s[half:] for s in slots], axis=0)


def slot_rows(rows, k, count):
    half = rows.shape[0] // (2 * count)
    low = k * half
    high = rows.shape[0] // 2 + k * half
    return jnp.concatenate([rows[low : low + half], rows[high : high + half]], axis=0)


def centred(rows):
    centre = rows - jnp.mean(rows, axis=-1, keepdims=True)
    scale = lax.rsqrt(jnp.mean(centre * centre, axis=-1, keepdims=True) + 1e-05)
    return centre * scale, scale


def fill(scratch, own, other, core):
    half = own.shape[0]
    scratch[pl.ds(pl.multiple_of(core * half, half), half), :] = own[...]
    scratch[pl.ds(pl.multiple_of((1 - core) * half, half), half), :] = other[...]


def pick_gain(own, other, which, core):
    a = own[which : which + 1, :].astype(F32)
    b = other[which : which + 1, :].astype(F32)
    first = jnp.where(core == 0, a, b)
    second = jnp.where(core == 0, b, a)
    return jnp.concatenate([first, second], axis=1)


def route_rows(pieces):
    lane = lax.broadcasted_iota(I32, (8, 128), 1)
    low = lane < 64
    rolled = [pltpu.roll(p, 64, 1) for p in pieces]
    count = len(pieces)
    front = [jnp.where(low, pieces[i], rolled[i + 1]) for i in range(0, count, 2)]
    back = [jnp.where(low, rolled[i], pieces[i + 1]) for i in range(0, count, 2)]
    return jnp.concatenate(front + back, axis=1)


def pack_body(count, rest, *refs):
    tok, routes = refs[:2]
    place = lax.axis_index("ctx") // rest
    local, dim = tok.shape[1:]
    for k, out in enumerate(refs[2:]):
        out[:local, :] = tok[place ^ (k + 1)]
        out[local:, :] = jnp.zeros((8, dim), BF)
        out[local : local + TWO, :128] = routes[place ^ (k + 1)].astype(F32).astype(BF)


def pack_all_body(count, rest, *refs):
    tok, routes, query, kv, router, out = refs[:6]
    pieces, packed = refs[6:-1], refs[-1]
    pack_body(count, rest, tok, routes, *pieces)
    Order.rest()
    half, cols = query.shape
    keys = kv.shape[1]
    packed[half:, :] = jnp.zeros((8, packed.shape[1]), BF)
    packed[:half, :cols] = query[...]
    packed[:half, cols : cols + keys] = kv[...]
    packed[:half, cols + keys :] = out[...]
    packed[half:, :half] = router[...]


def fill_router(wr, own, packed, core):
    half = own.shape[1]
    wr[...] = jnp.zeros_like(wr)
    experts = own.shape[0]
    mine = pl.ds(pl.multiple_of(core * half, half), half)
    theirs = pl.ds(pl.multiple_of((1 - core) * half, half), half)
    wr[:experts, mine] = own[...].astype(F32)
    wr[:experts, theirs] = packed[half:, :half].astype(F32)


def keys_body(count, rest, *refs):
    toks = refs[:count]
    routes, g_own, g_other, k_own, packed = refs[count : count + 5]
    kv_out, normed_out, tok_out, gain_out, wk, tail_out = refs[count + 5 :]
    core = lax.axis_index("wsh")
    place = lax.axis_index("ctx") // rest
    half = k_own.shape[0]
    local = toks[0].shape[0]
    keys = k_own.shape[1]
    cols = packed.shape[1] - keys - toks[0].shape[1]
    fill(wk, k_own, packed.at[:half, cols : cols + keys], core)
    rows = join([t[:local] for t in toks])
    tok_out[...] = rows
    Order.leave(2, 4)
    tail_out[...] = jnp.zeros_like(tail_out)
    tail_out[:TWO, :] = routes[place].astype(F32)
    for k in range(1, count):
        tail_out[8 * k : 8 * k + 8, :] = toks[k][local : local + 8, :128].astype(F32)
    rows = rows.astype(F32)
    unit, _ = centred(rows)
    gain_out[...] = jnp.zeros_like(gain_out)
    for which in range(TWO):
        gain_out[which : which + 1, :] = pick_gain(g_own, g_other, which, core)
    normed = (unit * gain_out[0:1, :]).astype(BF)
    normed_out[...] = normed
    Order.leave(1, 3)
    kv = mm(normed, wk[...]).astype(BF)
    for i in range(kv_out.shape[0]):
        kv_out[i] = kv


def project_body(count, experts, head, *refs):
    normed_ref, tails, q_own, r_own, o_own, packed = refs[:6]
    qt_out, nt_out, gate_out, gate_far, route_out, route_far, wq, wr, wo = refs[6:]
    core = lax.axis_index("wsh")
    half, cols = q_own.shape
    normed = normed_ref[...]
    nt_out[...] = normed.T
    Order.leave(1)
    Order.rest()
    fill(wq, q_own, packed.at[:half, :cols], core)
    fill_router(wr, r_own, packed, core)
    fill(wo, o_own, packed.at[:half, packed.shape[1] - o_own.shape[1] :], core)
    Order.leave(6, 7, 8)
    routes = route_rows([tails[8 * k : 8 * k + 8, :] for k in range(count)])
    route_out[...] = routes
    route_far[...] = routes
    logits = mm(wr[...].astype(BF), normed, 1, 1)
    queries = mm(wq[...], normed, 0, 1) * 0.125
    chosen = []
    for s in range(TWO):
        route = routes[s : s + 1]
        total = jnp.zeros((head, normed.shape[0]), F32)
        value = jnp.zeros((1, normed.shape[0]), F32)
        for e in range(experts):
            here = route == e
            total = jnp.where(here, queries[e * head : (e + 1) * head], total)
            value = jnp.where(here, logits[e : e + 1], value)
        qt_out[s * head : (s + 1) * head, :] = total.astype(BF)
        chosen.append(value)
    top = jnp.maximum(chosen[0], chosen[1])
    raised = [jnp.exp(c - top) for c in chosen]
    total = raised[0] + raised[1]
    gate_out[...] = jnp.concatenate([r / total for r in raised], axis=0)
    gate_far[...] = gate_out[...]


def places(order, count, rest, block, width, part):
    me = lax.axis_index("ctx")
    place, other = me // rest, me % rest
    size = count * rest
    lane = lax.broadcasted_iota(I32, (1, width), 1)
    out = jnp.zeros((1, width), I32)
    for k in range(count):
        first = order[(place ^ k) * rest + other]
        base = jnp.where(part == 0, first, 2 * size - 1 - first) * block
        out = jnp.where(lane // block == k, lane - k * block + base, out)
    return out


def key_bases(order, count, rest, block, chunk, part):
    me = lax.axis_index("ctx")
    place = me // rest
    size = count * rest
    out = []
    for k in range(count):
        first = order[(place ^ k) * rest + chunk]
        out.append((first if part == 0 else 2 * size - 1 - first) * block)
    return out


def masked(scores, gap, bases, block):
    parts = [
        jnp.where(gap <= -base, scores[k * block : (k + 1) * block], NONE)
        for k, base in enumerate(bases)
    ]
    return jnp.concatenate(parts, axis=0)


def scored(kv, side, h, gap, order, count, rest, block, chunk, half):
    first = mm(kv[:half], side)
    if h == 0:
        return masked(first, gap, key_bases(order, count, rest, block, chunk, 0), block)
    second = mm(kv[half:], side)
    second = masked(second, gap, key_bases(order, count, rest, block, chunk, 1), block)
    return jnp.concatenate([first, second], axis=0)


def turn_keys(kv, kv_turned):
    rows = kv.shape[1]
    for c in range(kv.shape[0]):
        kv_turned[:, c * rows : (c + 1) * rows] = kv[c].T


def both_slots(rows, head, cols):
    return jnp.concatenate([rows[s * head : (s + 1) * head, cols] for s in range(TWO)], axis=1)


def gap_rows(order, count, rest, block, half, h):
    gap = lax.broadcasted_iota(I32, (block, half), 0) - places(order, count, rest, block, half, h)
    return jnp.concatenate([gap] * TWO, axis=1)


def attend_body(count, rest, experts, head, *refs):
    order, kv_ref, qt, gates, routes = refs[:5]
    tok, gains, wo = refs[5:8]
    att_out, log_out, mixed_out, hidden_out, two_out, turned_out, kv_out, kv_turned = refs[8:]
    kv_out[...] = kv_ref[...]
    Order.leave(6)
    other = lax.axis_index("ctx") % rest
    total = qt.shape[1]
    half = total // 2
    block = half // count
    turn_keys(kv_ref, kv_turned)
    sides, gaps = [], []
    for h in range(2):
        side = both_slots(qt, head, slice(h * half, (h + 1) * half))
        sides.append(jnp.concatenate([side, jnp.zeros_like(side)], axis=0))
        gaps.append(gap_rows(order, count, rest, block, half, h))

    def step(turn, carry):
        chunk = turn ^ other
        at = pl.multiple_of(chunk * total, total)
        kv = kv_ref[chunk]
        scores = [
            scored(kv, sides[h], h, gaps[h], order, count, rest, block, chunk, half)
            for h in range(2)
        ]
        out = []
        for h in range(2):
            top, norm, summed = carry[h]
            fresh = jnp.maximum(top, jnp.max(scores[h], axis=0, keepdims=True))
            shares = jnp.exp(scores[h] - fresh)
            fade = jnp.exp(top - fresh)
            norm = norm * fade + jnp.sum(shares, axis=0, keepdims=True)
            values = kv_turned[head:, pl.ds(at, half * (h + 1))]
            out.append((fresh, norm, summed * fade + mm(values, shares.astype(BF))))
        return tuple(out)

    start = (
        jnp.full((1, TWO * half), NONE, F32),
        jnp.zeros((1, TWO * half), F32),
        jnp.zeros((head, TWO * half), F32),
    )
    done = lax.fori_loop(0, rest, step, (start, start), unroll=rest <= 4)
    for h in range(2):
        top, norm, summed = done[h]
        logs, attended = top + jnp.log(norm), summed / norm
        for s in range(TWO):
            here, cols = slice(h * half, (h + 1) * half), slice(s * half, (s + 1) * half)
            log_out[s : s + 1, here] = logs[:, cols]
            att_out[s * head : (s + 1) * head, here] = attended[:, cols]
    Order.rest()
    Order.leave(0, 1)
    for e in range(experts):
        part = jnp.zeros((head, total), F32)
        for s in range(TWO):
            gate = jnp.where(routes[s : s + 1] == e, gates[s : s + 1], 0.0)
            part = part + gate * att_out[s * head : (s + 1) * head, :]
        mixed_out[e * head : (e + 1) * head, :] = part.astype(BF)
    Order.leave(2)
    hidden = tok[...].astype(F32) + mm(mixed_out[...].T, wo[...])
    hidden_out[...] = hidden
    unit, _ = centred(hidden)
    two = (unit * gains[1:2, :]).astype(BF)
    two_out[...] = two
    turned_out[...] = two.T


def feed_body(count, rest, first, tile, *refs):
    two, turned = refs[:2]
    if first:
        slots = refs[2 : 2 + count]
        u_own, u_other, down, layer_in = refs[2 + count : 6 + count]
        layer_out, back_out, send, keep, cots, cot_far, send_up, up = refs[6 + count :]
    else:
        cots, u_own, u_other, down, layer_in, back_in = refs[2:8]
        outs = refs[8 : 12 + count]
        layer_pieces, back_out, keep_down, keep, send = outs[:count], *outs[count:]
        up, layer_out = refs[12 + count :]
    core = lax.axis_index("wsh")
    side = (1 - core) if first else core
    width = down.shape[0]
    half = u_own.shape[0]
    lanes = pl.ds(pl.multiple_of(side * width, width), width)
    up[pl.ds(pl.multiple_of(core * half, half), half), :] = u_own[...]
    up[pl.ds(pl.multiple_of((1 - core) * half, half), half), :] = u_other[:, lanes]
    if first:
        cots[...] = join([o[...] for o in slots])
        cot_far[...] = cots[...]
        Order.leave(5)
    layer_out[...] = layer_in[...]
    if first:
        back_out[...] = jnp.zeros_like(back_out)
    else:
        back_out[...] = back_in[...]
    mine = pl.ds(pl.multiple_of(core * half, half), half)
    theirs = pl.ds(pl.multiple_of((1 - core) * half, half), half)
    dim = up.shape[0]
    per = dim // tile

    def products(j):
        cols = slice(j * tile, (j + 1) * tile)
        return mm(two[...], up[:, cols]), mm(cots[...], down[cols, :], 1, 1)

    steps = width // tile
    ready = products(0)
    for j in range(steps):
        cols = slice(j * tile, (j + 1) * tile)
        pre, back = ready
        if j + 1 < steps:
            ready = products(j + 1)
        phi = 0.5 * (1.0 + lax.erf(pre * math.sqrt(0.5)))
        bell = jnp.exp(pre * pre * -0.5) * (1.0 / math.sqrt(2.0 * math.pi))
        act = (pre * phi).astype(BF)
        back_pre = (back * (phi + pre * bell)).astype(BF)
        layer_out[...] += mm(act, down[cols, :])
        back_out[...] += mm(back_pre, up[:, cols], 1, 1)
        grad = mm(act.T, cots[...]).astype(BF)
        grad_mine = mm(turned[mine, :], back_pre).astype(BF)
        grad_theirs = mm(turned[theirs, :], back_pre).astype(BF)
        rows = slice((j // per) * half, (j // per + 1) * half)
        lane = slice((j % per) * tile, (j % per + 1) * tile)
        keep[rows, lane] = grad_mine
        if first:
            send[cols, :] = grad
            send_up[rows, lane] = grad_theirs
        else:
            keep_down[cols, :] = grad
            send[rows, lane] = grad_theirs
    if not first:
        Order.leave(count + 1, count + 2, count + 3)
        for k in range(count):
            layer_pieces[k][...] = slot_rows(layer_out[...], k, count).astype(layer_pieces[k].dtype)


def turn_body(count, rest, experts, head, *refs):
    hidden, back_two, cot, wo, gain, gates, routes, att = refs[:8]
    back_hidden_out, branch_out, grad_att_out, delta_out, logit_out, gain_out = refs[8:]
    unit, scale = centred(hidden[...])
    back = back_two[...]
    side = back * gain[1:2, :]
    part = scale * (
        side
        - jnp.mean(side, axis=-1, keepdims=True)
        - unit * jnp.mean(side * unit, axis=-1, keepdims=True)
    )
    gain_out[...] = jnp.broadcast_to(jnp.sum(back * unit, axis=0, keepdims=True), gain_out.shape)
    back_hidden = cot[...].astype(F32) + part
    back_hidden_out[...] = back_hidden
    branch = back_hidden.astype(BF)
    branch_out[...] = branch
    Order.leave(0, 1, 5)
    back_mixed = mm(wo[...], branch, 1, 1)
    grads = []
    for s in range(TWO):
        total = jnp.zeros((head, branch.shape[0]), F32)
        for e in range(experts):
            total = jnp.where(routes[s : s + 1] == e, back_mixed[e * head : (e + 1) * head], total)
        att_s = att[s * head : (s + 1) * head, :]
        grads.append(jnp.sum(total * att_s, axis=0, keepdims=True))
        low = (gates[s : s + 1] * total).astype(BF)
        grad_att_out[s * head : (s + 1) * head, :] = low
        delta_out[s : s + 1, :] = jnp.sum(low.astype(F32) * att_s, axis=0, keepdims=True)
    mean = gates[0:1] * grads[0] + gates[1:2] * grads[1]
    row = lax.broadcasted_iota(I32, logit_out.shape, 0)
    logit = jnp.zeros(logit_out.shape, F32)
    for s in range(TWO):
        value = gates[s : s + 1] * (grads[s] - mean)
        logit = logit + jnp.where(row.astype(F32) == routes[s : s + 1], value, 0.0)
    logit_out[...] = logit


def turn_start_body(count, rest, experts, head, layout, step, *refs):
    ins, early, outs, pieces = refs[:8], refs[8:12], refs[12:18], refs[18]
    turn_body(count, rest, experts, head, *ins, *outs)
    Order.rest()
    start_body(layout, True, 1, step, len(early), *early, pieces, None)


def attend_back_body(count, rest, head, split, *refs):
    order, kv_ref, qt, grad_att, logs, delta, grad_q_out = refs[:7]
    outs = refs[7 : 7 + split]
    kv_turned, sides, turned, grad_kv, grad_q = refs[7 + split :]
    total = qt.shape[1]
    half = total // 2
    block = half // count
    wide = TWO * half
    turn_keys(kv_ref, kv_turned)
    blank = jnp.zeros((head, wide), BF)
    for h in range(2):
        cols = slice(h * half, (h + 1) * half)
        q_side = jnp.concatenate([both_slots(qt, head, cols), blank], axis=0)
        g_side = jnp.concatenate([blank, both_slots(grad_att, head, cols)], axis=0)
        sides[2 * h], sides[2 * h + 1] = q_side, g_side
        turned[h, :wide, :], turned[h, wide:, :] = q_side.T, g_side.T
    grad_q[...] = jnp.zeros_like(grad_q)
    gaps = [gap_rows(order, count, rest, block, half, h) for h in range(2)]
    log_rows = [both_slots(logs, 1, slice(h * half, (h + 1) * half)) for h in range(2)]
    delta_rows = [both_slots(delta, 1, slice(h * half, (h + 1) * half)) for h in range(2)]

    def step(chunk, carry):
        at = pl.multiple_of(chunk * total, total)
        kv = kv_ref[chunk]
        grads = []
        for h in range(2):
            reach = half * (h + 1)
            scores = scored(
                kv, sides[2 * h], h, gaps[h], order, count, rest, block, chunk, half
            )
            shares = jnp.exp(scores - log_rows[h])
            back_shares = mm(kv[:reach], sides[2 * h + 1])
            back_scores = (shares * (back_shares - delta_rows[h])).astype(BF)
            both = jnp.concatenate([back_scores, shares.astype(BF)], axis=1)
            grads.append(mm(both, turned[h]))
            grad_q[h] += mm(kv_turned[:head, pl.ds(at, reach)], back_scores)
        grad_kv[pl.ds(at, half), :] = grads[0] + grads[1][:half]
        grad_kv[pl.ds(at + half, half), :] = grads[1][half:]
        return carry

    lax.fori_loop(0, rest, step, 0, unroll=rest <= 4)
    rows = outs[0].shape[0]
    digit = (lax.axis_index("ctx") % rest) // (rest // split)
    for i, out in enumerate(outs):
        begin = pl.multiple_of((digit ^ i) * rows, rows)
        out[...] = grad_kv[pl.ds(begin, rows), :].astype(out.dtype)
        Order.leave(i + 1)
    for h in range(2):
        for s in range(TWO):
            here, cols = slice(h * half, (h + 1) * half), slice(s * half, (s + 1) * half)
            grad_q_out[s * head : (s + 1) * head, here] = grad_q[h, :, cols].astype(BF)


def query_body(experts, head, *refs):
    grad_q, normed_t, routes, mixed, branch, wq, wr, logit, tok = refs[:9]
    keep_out, keep, send, back_out, unit_out, scale_out, routers, bqt = refs[9:]
    core = lax.axis_index("wsh")
    total = grad_q.shape[1]
    for e in range(experts):
        part = jnp.zeros((head, total), F32)
        for s in range(TWO):
            value = grad_q[s * head : (s + 1) * head, :].astype(F32) * 0.125
            part = jnp.where(routes[s : s + 1] == e, value, part)
        bqt[e * head : (e + 1) * head, :] = part.astype(BF)
    back_q = bqt[...].T
    half = keep.shape[0]
    mine = pl.ds(pl.multiple_of(core * half, half), half)
    theirs = pl.ds(pl.multiple_of((1 - core) * half, half), half)
    send[:half, :] = mm(mixed[theirs, :], branch[...]).astype(BF)
    send[half:, :] = mm(normed_t[theirs, :], back_q).astype(BF)
    keep_out[...] = mm(mixed[mine, :], branch[...]).astype(BF)
    keep[...] = mm(normed_t[mine, :], back_q).astype(BF)
    Order.leave(0, 1, 2)
    parts = []
    left = logit[...]
    for _ in range(3):
        low = left.astype(BF)
        parts.append(low)
        left = left - low.astype(F32)
    routers[...] = parts_dot(parts, normed_t[...])
    back = mm(back_q, wq[...], 1, 1)
    wr_turned = wr[...].astype(BF)
    for low in parts:
        padded = jnp.concatenate([low.astype(F32), jnp.zeros((120, total), F32)], axis=0)
        back = back + mm(padded.T.astype(BF), wr_turned)
    back_out[...] = back
    unit, scale = centred(tok[...].astype(F32))
    unit_out[...] = unit
    scale_out[...] = jnp.broadcast_to(scale, scale_out.shape)


def unproject_body(count, terms, *refs):
    kv_terms = refs[:terms]
    back_part, unit_ref, scale_ref, routers, normed_t, back_hidden, wk, gain, gain_two, sent = refs[
        terms : terms + 10
    ]
    at = terms + 10
    pieces = refs[at : at + count]
    keep, send, gains = refs[at + count :]
    core = lax.axis_index("wsh")
    half = back_part.shape[1] // 2
    back_kv = kv_terms[0][...].astype(F32)
    for term in kv_terms[1:]:
        back_kv = back_kv + term[...].astype(F32)
    back_kv = back_kv.astype(BF)
    back = back_part[...] + mm(back_kv, wk[...], 1, 1)
    unit, scale = unit_ref[...], scale_ref[:, 0:1]
    side = back * gain[0:1, :]
    grad = back_hidden[...] + scale * (
        side
        - jnp.mean(side, axis=-1, keepdims=True)
        - unit * jnp.mean(side * unit, axis=-1, keepdims=True)
    )
    gains[0:1, :] = jnp.sum(back * unit, axis=0, keepdims=True)
    gains[1:2, :] = gain_two[0:1, :]
    step = half // 4
    experts = routers.shape[0]
    high = sent.shape[0]
    Order.rest()
    send[:high, :] = sent[...]
    for out, which in ((keep, core), (send.at[high:, :], 1 - core)):
        mine = pl.ds(pl.multiple_of(which * half, half), half)
        grad_k = mm(normed_t[mine, :], back_kv).astype(out.dtype)
        for j in range(4):
            out[:step, j * 128 : (j + 1) * 128] = grad_k[j * step : (j + 1) * step]
        blank = jnp.zeros((experts, half), F32)
        out[step : step + 8, :] = jnp.concatenate([routers[:, mine], blank], axis=1).astype(out.dtype)
        gain_pair = jnp.concatenate([gains[0:1, mine], gains[1:2, mine]], axis=1)
        out[step + 8 :, :] = jnp.broadcast_to(gain_pair, (8, 2 * half)).astype(out.dtype)
    Order.leave(count, count + 1)
    for k in range(count):
        pieces[k][...] = slot_rows(grad, k, count).astype(pieces[k].dtype)


def parts_dot(parts, normed_t):
    out = None
    for low in parts:
        value = mm(low, normed_t, 1, 1)
        out = value if out is None else out + value
    return out


def sum_layout(layout, ins, total):
    at = 0
    for terms in layout:
        height = terms[0][2]
        value = None
        for index, begin, count in terms:
            part = ins[index][begin : begin + count, :].astype(F32)
            value = part if value is None else value + part
        total[at : at + height, :] = value
        at += height
    if at < total.shape[0]:
        total[at:, :] = jnp.zeros((total.shape[0] - at, total.shape[1]), F32)


def cut_rows(total, outs, stride, step):
    rows = outs[0].shape[0]
    digit = (lax.axis_index("ctx") // stride) % step
    for j in range(step):
        begin = pl.multiple_of((digit ^ j) * rows, 8)
        outs[j][...] = total[pl.ds(begin, rows), :].astype(outs[j].dtype)


def start_body(layout, whole, stride, step, n_in, *refs):
    ins, outs, total = refs[:n_in], refs[n_in:-1], refs[-1]
    if whole:
        rows = outs[0].shape[1]
        at = 0
        for terms in layout:
            height, done = terms[0][2], 0
            while done < height:
                j, low = (at + done) // rows, (at + done) % rows
                take = min(height - done, rows - low)
                value = None
                for index, begin, _ in terms:
                    part = ins[index][begin + done : begin + done + take, :].astype(F32)
                    value = part if value is None else value + part
                outs[0][j, low : low + take, :] = value.astype(BF)
                done += take
            at += height
        while at < rows * step:
            j, low = at // rows, at % rows
            outs[0][j, low:, :] = jnp.zeros((rows - low, outs[0].shape[2]), BF)
            at += rows - low
    else:
        sum_layout(layout, ins, total)
        cut_rows(total, outs, stride, step)


def terms_of(ref):
    return [ref.at[j] for j in range(ref.shape[0])] if len(ref.shape) == 3 else [ref]


def middle_body(chunks, stride, step, n_in, riders, *refs):
    ins, riding = refs[:n_in], refs[n_in : n_in + riders]
    refs = refs[n_in + riders :]
    outs, totals = refs[:step], refs[step:]
    digit = (lax.axis_index("ctx") // stride) % step
    at, low = 0, 0
    for count, total in zip(chunks, totals):
        value = None
        for ref in ins[at : at + count]:
            for term in terms_of(ref):
                part = term[...].astype(F32)
                value = part if value is None else value + part
        total[...] = value
        rows = total.shape[0] // step
        for j in range(step):
            begin = pl.multiple_of((digit ^ j) * rows, 8)
            outs[j][low : low + rows, :] = total[pl.ds(begin, rows), :].astype(outs[j].dtype)
        low += rows
        at += count
    for j in range(1, step if riders else 1):
        outs[j][low:, :] = riding[j - 1][...]


def copies_body(slices, n_in, *refs):
    ins, out = refs[:n_in], refs[-1]
    for j in range(out.shape[0]):
        at = 0
        for begin, rows in slices:
            for ref in ins:
                out[j, at : at + rows, :] = ref[begin : begin + rows, :]
                at += rows


def final_body(strides, parts, dests, n_out, *refs):
    got, outs, totals = refs[0], refs[1 : 1 + n_out], refs[1 + n_out :]
    me = lax.axis_index("ctx")
    shift, per = 0, 1
    for stride, step in strides[1:]:
        shift = shift * step + (me // stride) % step
        per *= step
    at, used = 0, 0
    for height, total, (dest, many) in zip(parts, totals, dests):
        rows = height // per
        swapped = isinstance(got, tuple)
        digit = me % strides[0][1] if swapped else 0
        for i in range(len(got) if swapped else got.shape[0]):
            for b in range(per):
                begin = pl.multiple_of(((i ^ digit) * per + (b ^ shift)) * rows, 8)
                source = got[i].at[0] if swapped else got.at[i]
                piece = source[at + b * rows : at + (b + 1) * rows, :]
                total[pl.ds(begin, rows), :] = piece.astype(F32)
        at += height
        dest(total, outs[used : used + many])
        Order.leave(*range(used, used + many))
        used += many


WIDTH = 512


def cut_up(chunks, heights, strides, at, size, riders=()):
    stride, step = strides[at]
    total = sum(heights) // step
    more = riders[0].shape[0] if riders else 0
    n_in = sum(len(c) for c in chunks)
    pieces = call(
        functools.partial(middle_body, [len(c) for c in chunks], stride, step, n_in, len(riders)),
        [((total, WIDTH), F32)] + [((total + more, WIDTH), BF)] * (step - 1),
        [t for c in chunks for t in c] + far(riders),
        scratch=[((h, WIDTH), F32) for h in heights],
    )
    return pieces[:1] + [swap(pieces[j], j * stride, size) for j in range(1, step)]


def spread(done, strides, at, size):
    stride, step = strides[at]
    return [done] + [swap(done, j * stride, size) for j in range(1, step)]


def settle(terms):
    return call(add_body, [(terms[0].shape, BF)], terms)[0]


def add_body(*refs):
    rows = refs[-1].shape[0]
    value = refs[0][:rows, :].astype(F32)
    for ref in refs[1:-1]:
        value = value + ref[:rows, :].astype(F32)
    refs[-1][...] = value.astype(refs[-1].dtype)


def early_dest(total, outs):
    down, tile = outs
    wide = down.shape[0]
    down[...] = total[:wide, :]
    tile[...] = total[wide : wide + tile.shape[0], :]


def both_final_body(strides, parts, n_in, *refs):
    got, tile = refs[:n_in], refs[n_in]
    outs, totals = refs[n_in + 1 : n_in + 8], refs[n_in + 8 :]

    def main(total, outs):
        (up,) = outs
        half = up.shape[0]
        core = lax.axis_index("wsh")
        tiles = up.shape[1] // WIDTH
        for i in range(tiles):
            side, inner = i // (tiles // 2), i % (tiles // 2)
            at = (core if side == 0 else 1 - core) * (tiles // 2) + inner
            rows = tile[...] if i == 0 else total[(i - 1) * half : i * half, :]
            up[:, pl.ds(pl.multiple_of(at * WIDTH, WIDTH), WIDTH)] = rows

    dests = [(main, 1), (late_dest, 6)]
    final_body(strides, parts, dests, 7, got, *outs, *totals)


def late_dest(total, outs):
    out, query, kv, router, one, two = outs
    half = kv.shape[0]
    out[...] = total[:half, :]
    query[...] = total[half : 2 * half, :]
    step = half // 4
    at = 2 * half
    for j in range(4):
        kv[j * step : (j + 1) * step, :] = total[at : at + step, j * 128 : (j + 1) * 128]
    at += step
    router[...] = total[at : at + router.shape[0], :half]
    one[...] = total[at + 8 : at + 9, :half]
    two[...] = total[at + 8 : at + 9, half:]


def place_body(rest, *refs):
    place = lax.axis_index("ctx") // rest
    out = refs[-1]
    local = out.shape[1]
    for k, ref in enumerate(refs[:-1]):
        begin = ref.shape[0] - local
        out[place ^ k] = ref[begin:, :].astype(F32)


def close_body(rest, count, strides, parts, n_in, *refs):
    main, moved = refs[: n_in + 1], refs[n_in + 1 : n_in + 1 + count]
    outs, totals = refs[n_in + 1 + count : n_in + 9 + count], refs[n_in + 9 + count :]
    place_body(rest, *moved, outs[7])
    Order.leave(7)
    both_final_body(strides, parts, n_in, *main, *outs[:7], *totals)


def on_device(
    tokens,
    routes,
    block_order,
    norm_gain1,
    router_w,
    query_w,
    kv_w,
    out_w,
    norm_gain2,
    up_w,
    down_w,
    cotangent,
):
    size = lax.axis_size("ctx")
    count, local, dim = tokens.shape
    rest = size // count
    place = lax.axis_index("ctx") // rest
    total = count * local
    experts = router_w.shape[1]
    head = kv_w.shape[1] // 2
    feed = up_w.shape[1]

    Order.last = None
    tall = dim // 2
    keys = 2 * head
    router_t = router_w.T
    routes_t = routes.transpose(0, 2, 1)

    def core():
        return lax.axis_index("wsh")

    def here():
        return lax.axis_index("ctx") // rest

    got = call(
        functools.partial(pack_all_body, count, rest),
        [((local + 8, dim), BF)] * (count - 1) + [((tall + 8, experts * head + keys + dim), BF)],
        far([tokens, routes_t, query_w, kv_w, router_t, out_w]),
        late=(2, 3, 4, 5),
        ahead=[Ahead(tokens, (local, dim), lambda r: r.at[here()]), Ahead(kv_w)]
        + [
            Ahead(cotangent, (local, dim), lambda r, k=k: r.at[here() ^ k])
            for k in range(1, count)
        ],
    )
    tok_pieces, (packed, tok_own, kv_own), cot_pieces = got[: count - 1], got[count - 1 : count + 2], got[count + 2 :]
    tok_x = [swap(tok_pieces[k - 1], k * rest, size) for k in range(1, count)]
    packed_x = trade(packed)
    gain_one, gain_two = after((norm_gain1, norm_gain2), packed)
    gains = jnp.stack([gain_one, gain_two])
    gains_x = trade(gains)

    steps = factors(rest)
    kv, normed, tok, gain_rows, wk, tails = call(
        functools.partial(keys_body, count, rest),
        [
            ((steps[0], total, keys), BF, 1),
            ((total, dim), BF, 1),
            ((total, dim), BF, 1),
            ((8, dim), F32, 1),
            ((dim, keys), BF, 1),
            ((8 * count, 128), F32),
        ],
        [tok_own, *tok_x, Far(routes_t), gains, gains_x, kv_own, packed_x],
    )
    stride = 1
    for i, step in enumerate(steps):
        if i > 0:
            kv = jnp.broadcast_to(kv[None], (step,) + kv.shape)
        kv = exchange(kv, stride, size).reshape(-1, total, keys)
        stride *= step
    cot_pieces = after(tuple(cot_pieces), normed)
    cot_x = [swap(cot_pieces[k - 1], k * rest, size) for k in range(1, count)]
    qt, normed_t, gates, gates_far, route, route_far, wq, wr, wo = call(
        functools.partial(project_body, count, experts, head),
        [
            ((TWO * head, total), BF, 1),
            ((dim, total), BF, 1),
            ((TWO, total), F32),
            ((TWO, total), F32, 1),
            ((8, total), F32),
            ((8, total), F32, 1),
            ((dim, experts * head), BF, 1),
            ((128, dim), F32, 1),
            ((experts * head, dim), BF, 1),
        ],
        [Far(normed), tails, *far([query_w, router_t, out_w]), packed_x],
        late=(2, 3, 4),
    )
    up_w2, down_w2, _ = lax.optimization_barrier((up_w, down_w, normed))
    up_x, down_x = trade(up_w2), trade(down_w2)
    span = rest * total
    wide = feed // 2

    def lanes(which):
        def view(ref):
            side = which()
            return ref.at[:, pl.ds(pl.multiple_of(side * wide, wide), wide)]

        return view

    att, logs, mixed, hidden, two, two_t, kv_far, cot_own, up_first = call(
        functools.partial(attend_body, count, rest, experts, head),
        [
            ((TWO * head, total), F32, 1),
            ((TWO, total), F32, 1),
            ((experts * head, total), BF, 1),
            ((total, dim), F32),
            ((total, dim), BF),
            ((dim, total), BF),
            ((rest, total, keys), BF, 1),
        ],
        [block_order, kv, Far(qt), gates, route, *far([tok, gain_rows, wo])],
        scratch=[((keys, span), BF)],
        smem=(0,),
        late=(5, 6, 7),
        ahead=[
            Ahead(cotangent, (local, dim), lambda r: r.at[here()]),
            Ahead(up_w, (tall, wide), lanes(lambda: 1 - core())),
        ],
    )

    tile = 512
    upper = wide * tall // dim
    layer, back_two, send_one, keep_one, cots, cots_far, send_up, up_second, down_own = call(
        functools.partial(feed_body, count, rest, True, tile),
        [
            ((total, dim), F32),
            ((total, dim), F32),
            ((wide, dim), BF),
            ((upper, dim), BF, 1),
            ((total, dim), BF),
            ((total, dim), BF, 1),
            ((upper, dim), BF),
        ],
        [two, two_t, cot_own, *cot_x, up_first, up_x, down_x, hidden],
        scratch=[((dim, wide), BF)],
        ahead=[Ahead(up_w, (tall, wide), lanes(core)), Ahead(down_w)],
    )
    recv_down, recv_up = trade(send_one), trade(send_up)
    *layer_pieces, back_two, keep_down, keep_two, send_two, cots, wo, gain_near, gates, route, att = call(
        functools.partial(feed_body, count, rest, False, tile),
        [((local, dim), F32, 1)]
        + [((local, dim), BF, 1)] * (count - 1)
        + [
            ((total, dim), F32),
            ((wide, dim), BF, 1),
            ((upper, dim), BF, 1),
            ((upper, dim), BF, 1),
        ],
        [two, two_t, cots, up_second, up_x, down_own, layer, back_two],
        scratch=[((dim, wide), BF), ((total, dim), F32)],
        ahead=[
            Ahead(a)
            for a in (cots_far, wo, gain_rows, gates_far, route_far, att)
        ],
    )
    recv_two = trade(send_two)
    layer_got = [layer_pieces[0]] + [swap(layer_pieces[k], k * rest, size) for k in range(1, count)]

    strides = []
    stride = 1
    for step in [*steps, count]:
        strides.append((stride, step))
        stride *= step
    last = len(strides) - 1
    unit = 8 * size
    first = strides[0][1]
    early_rows = -(-(wide + tall) // unit) * unit
    main_rows = -(-(2 * upper - tall) // unit) * unit
    small = tall // 4 + 16
    late_rows = -(-(small + 2 * tall) // unit) * unit

    def bulk(args, layout, height, ahead=()):
        pieces, *near = call(
            functools.partial(start_body, layout, True, 1, first, len(args)),
            [((first, height // first, WIDTH), BF)],
            args,
            scratch=[((8, WIDTH), F32)],
            ahead=ahead,
        )
        return exchange(pieces, 1, size), near

    def inner(terms, height, riders=()):
        height //= first
        for at in range(1, last + 1):
            more = riders if at == last else ()
            terms = cut_up([terms], [height], strides, at, size, more)
            height //= strides[at][1]
        return terms

    def outer(got):
        for at in reversed(range(1, last)):
            got = spread(jnp.concatenate(got, axis=0), strides, at, size)
        return got

    def ready(got, ahead=()):
        rows = got[0].shape[0]
        copies, *near = call(
            functools.partial(copies_body, [(0, rows)], len(got)),
            [((first, rows * len(got), WIDTH), BF)],
            got,
            ahead=ahead,
        )
        return exchange(copies, 1, size), near

    back_hidden, branch, grad_att, delta, logit, gain_two, early, kv_near, qt_near, logs_near = call(
        functools.partial(
            turn_start_body,
            count,
            rest,
            experts,
            head,
            [[(0, 0, wide), (1, 0, wide)], [(2, 0, tall), (3, 0, tall)]],
            first,
        ),
        [
            ((total, dim), F32, 1),
            ((total, dim), BF, 1),
            ((TWO * head, total), BF),
            ((TWO, total), F32),
            ((experts, total), F32, 1),
            ((8, dim), F32, 1),
            ((first, early_rows // first, WIDTH), BF),
        ],
        [
            hidden,
            back_two,
            cots,
            wo,
            gain_near,
            gates,
            route,
            att,
            Far(keep_down),
            recv_down,
            Far(keep_two),
            recv_up,
        ],
        late=(8, 10),
        ahead=[Ahead(a) for a in (kv_far, qt, logs)],
    )
    early = exchange(early, 1, size)
    split = steps[-1]
    share = span // split
    grad_q, *kv_terms = call(
        functools.partial(attend_back_body, count, rest, head, split),
        [((TWO * head, total), BF), ((share, keys), F32, 1)] + [((share, keys), BF, 1)] * (split - 1),
        [block_order, kv_near, qt_near, grad_att, logs_near, delta],
        scratch=[
            ((keys, span), BF),
            ((4, keys, total), BF),
            ((2, 2 * total, keys), BF),
            ((span, keys), F32),
            ((2, head, total), F32),
        ],
        smem=(0,),
        ahead=[Ahead(a) for a in (normed_t, route_far, mixed, branch, wq, wr, logit, tok)],
    )
    kv_terms, ahead = kv_terms[:split], kv_terms[split:]
    stride = rest
    for i, step in reversed(list(enumerate(steps))):
        stride //= step
        if i + 1 < len(steps):
            summed = functools.reduce(lambda a, b: a + b.astype(F32), terms)
            parts = summed.reshape(step, -1, keys)
            digit = (lax.axis_index("ctx") // stride) % step
            kv_terms = [pick(parts, digit ^ j) for j in range(step)]
        terms = [kv_terms[0]] + [
            swap(kv_terms[j].astype(BF), j * stride, size) for j in range(1, step)
        ]
    grad_q = after(grad_q, *layer_got[1:])
    keep_out, keep_query, send_main, back_part, unit_rows, scale_rows, routers, *near = call(
        functools.partial(query_body, experts, head),
        [
            ((tall, dim), BF, 1),
            ((tall, dim), BF, 1),
            ((2 * tall, dim), BF, 1),
            ((total, dim), F32),
            ((total, dim), F32),
            ((total, 128), F32),
            ((experts, dim), F32),
        ],
        [grad_q, *ahead],
        scratch=[((experts * head, total), BF)],
        ahead=[Ahead(a) for a in (normed_t, back_hidden, wk, gain_rows, gain_two, terms[0])],
    )
    *near, term = near
    *input_pieces, keep_late, send_late, keep_two, keep_one = call(
        functools.partial(unproject_body, count, len(terms)),
        [((local, dim), F32, 1)]
        + [((local, dim), BF, 1)] * (count - 1)
        + [((small, dim), F32, 1), ((small + 2 * tall, dim), BF)],
        [term, *terms[1:], back_part, unit_rows, scale_rows, routers, *near, Far(send_main)],
        scratch=[((8, dim), F32)],
        late=(len(terms) + 9,),
        ahead=[Ahead(a) for a in (keep_two, keep_one)],
    )
    recv_late = trade(send_late)
    main, _ = bulk(
        [keep_two, recv_up, keep_one, recv_two],
        [
            [(0, tall, upper - tall), (1, tall, upper - tall)],
            [(2, 0, upper), (3, 0, upper)],
        ],
        main_rows,
    )
    pieces = call(
        functools.partial(
            start_body,
            [
                [(0, 0, tall), (1, 0, tall)],
                [(0, tall, tall), (2, 0, tall)],
                [(0, 2 * tall, small), (3, 0, small)],
            ],
            False,
            1,
            first,
            4,
        ),
        [((late_rows // first, WIDTH), F32)] + [((late_rows // first, WIDTH), BF)] * (first - 1),
        [recv_late, *far([keep_out, keep_query, keep_late])],
        scratch=[((late_rows, WIDTH), F32)],
    )
    late = pieces[:1] + [swap(pieces[j], j, size) for j in range(1, first)]
    early_terms = inner([early], early_rows)
    early_got = outer(spread(settle(early_terms), strides, last, size))
    heights = [main_rows // first, late_rows // first]
    chunks = [[main], late]
    for at in range(1, last):
        chunks = [cut_up([c], [h], strides, at, size) for c, h in zip(chunks, heights)]
        heights = [h // strides[at][1] for h in heights]
    both_terms = cut_up(chunks, heights, strides, last, size)
    heights = [h // count for h in heights]
    (layer_out,) = call(
        functools.partial(place_body, rest),
        [((count, local, dim), F32, 1)],
        [Far(layer_got[0]), *far(layer_got[1:])],
    )
    early_last, _ = ready(early_got)
    both_got = spread(settle(both_terms), strides, last, size)
    slices = [(0, heights[0]), (heights[0], heights[1])]
    for stage in reversed(range(1, last)):
        moved = []
        for begin, h in slices:
            piece = jnp.concatenate([g[begin : begin + h] for g in both_got], axis=0)
            moved.append(spread(piece, strides, stage, size))
        both_got = [jnp.concatenate([m[j] for m in moved], axis=0) for j in range(strides[stage][1])]
        tops = [m[0].shape[0] for m in moved]
        slices = [(0, tops[0]), (tops[0], tops[1])]
    tall_rows = sum(h for _, h in slices) * len(both_got)
    (both_own,) = call(
        functools.partial(copies_body, slices, len(both_got)),
        [((1, tall_rows, WIDTH), BF)],
        both_got,
    )
    both_last = spread(both_own, strides, 0, size)
    input_pieces = after(tuple(input_pieces), both_got[0])
    moved = {k: swap(input_pieces[k], k * rest, size) for k in reversed(range(1, count))}
    input_got = [input_pieces[0]] + [moved[k] for k in range(1, count)]
    grad_down, up_tile = call(
        functools.partial(final_body, strides, [early_rows // first], [(early_dest, 2)], 2),
        [((wide, dim), F32, 1), ((tall, WIDTH), F32)],
        [early_last],
        scratch=[((early_rows, WIDTH), F32)],
    )
    grad_up, grad_out, grad_query, grad_kv, grad_router, grad_one, grad_two, input_grad = call(
        functools.partial(
            close_body,
            rest,
            count,
            strides,
            [main_rows // first, late_rows // first],
            len(both_last),
        ),
        [
            ((tall, feed), F32, 1),
            ((tall, dim), F32, 1),
            ((tall, experts * head), F32, 1),
            ((tall, keys), F32, 1),
            ((experts, tall), F32, 1),
            ((1, tall), F32, 1),
            ((1, tall), F32, 1),
            ((count, local, dim), F32, 1),
        ],
        [*both_last, up_tile, *input_got],
        scratch=[((main_rows, WIDTH), F32), ((late_rows, WIDTH), F32)],
    )
    return (
        layer_out,
        input_grad,
        grad_one.reshape(tall),
        grad_router.T,
        grad_query,
        grad_kv,
        grad_out,
        grad_two.reshape(tall),
        grad_up,
        grad_down,
    )


def solution(mesh):
    placed = (
        P("wsh", "ctx", None),
        P("wsh", "ctx", None),
        P(),
        P("wsh"),
        P("wsh", None),
        P("wsh", None),
        P("wsh", None),
        P("wsh", None),
        P("wsh"),
        P("wsh", None),
        P("wsh", None),
        P("wsh", "ctx", None),
    )
    return jax.shard_map(
        on_device,
        mesh=mesh,
        in_specs=placed,
        out_specs=(
            P("wsh", "ctx", None),
            P("wsh", "ctx", None),
            P("wsh"),
            P("wsh", None),
            P("wsh", None),
            P("wsh", None),
            P("wsh", None),
            P("wsh"),
            P("wsh", None),
            P("wsh", None),
        ),
        check_vma=False,
    )
```

```python
import functools
import math

import jax
import jax.numpy as jnp
from jax import lax
from jax.experimental import pallas as pl
from jax.experimental.pallas import tpu as pltpu
from jax.sharding import PartitionSpec as P

BF = jnp.bfloat16
F32 = jnp.float32
I32 = jnp.int32
NONE = -1e30
TWO = 2


def factors(size):
    out = []
    while size > 1:
        step = 4 if size % 4 == 0 else 2
        out.append(step)
        size //= step
    return out


def swap(values, mask, size):
    return lax.ppermute(values, "ctx", [(i, i ^ mask) for i in range(size)])


def groups_of(stride, step, size):
    out = []
    for i in range(size):
        if (i // stride) % step == 0:
            out.append([i + j * stride for j in range(step)])
    return out


def exchange(parts, stride, size):
    step = parts.shape[0]
    groups = groups_of(stride, step, size)
    return lax.all_to_all(parts, "ctx", 0, 0, tiled=True, axis_index_groups=groups)


def trade(values):
    return lax.ppermute(values, "wsh", [(0, 1), (1, 0)])


def pick(parts, index):
    return lax.dynamic_index_in_dim(parts, index, 0, False)


def mm(a, b, left=1, right=0):
    return lax.dot_general(a, b, (((left,), (right,)), ((), ())), preferred_element_type=F32)


class Order:
    last = None
    rest = None
    leave = None


def after(value, *earlier):
    return lax.optimization_barrier((value, *earlier))[0]


class Far:
    def __init__(self, value):
        self.value = value


class Ahead:
    def __init__(self, value, shape=None, view=None):
        self.value, self.view = value, view
        self.shape = value.shape if shape is None else shape


def loading_body(body, plan, n_out, far_out, late, views, n_scratch, *refs):
    n_in, n_pre = len(plan), len(views)
    ins, pre_in = list(refs[:n_in]), refs[n_in : n_in + n_pre]
    at = n_in + n_pre
    outs, pre_out = list(refs[at : at + n_out]), refs[at + n_out : at + n_out + n_pre]
    at += n_out + n_pre
    own = refs[at : at + n_scratch]
    held, sems = refs[at + n_scratch : -1], refs[-1]
    first, second, ahead, slot = [], [], [], 0
    for i in range(n_in):
        if plan[i]:
            copy = pltpu.make_async_copy(ins[i], held[slot], sems.at[slot])
            (second if i in late else first).append(copy)
            ins[i] = held[slot]
            slot += 1
    leaving = {}
    for i in range(n_out):
        if far_out[i]:
            leaving[i] = pltpu.make_async_copy(held[slot], outs[i], sems.at[slot])
            outs[i] = held[slot]
            slot += 1
    for view, source, target in zip(views, pre_in, pre_out):
        source = source if view is None else view(source)
        ahead.append(pltpu.make_async_copy(source, target, sems.at[slot]))
        slot += 1
    for copy in first + second + ahead:
        copy.start()
    for copy in first:
        copy.wait()

    def rest():
        for copy in second:
            copy.wait()

    gone = []

    def leave(*which):
        for i in which:
            if far_out[i]:
                gone.append(i)
                leaving[i].start()

    Order.rest, Order.leave = rest, leave
    body(*ins, *outs, *own)
    leave(*[i for i in range(n_out) if i not in gone])
    for i in gone:
        leaving[i].wait()
    for copy in ahead:
        copy.wait()


def call(body, outs, args, scratch=(), smem=(), late=(), ahead=(), mib=14):
    whole = pl.BlockSpec(memory_space=pltpu.VMEM)
    scalars = pl.BlockSpec(memory_space=pltpu.SMEM)
    distant = pl.BlockSpec(memory_space=pltpu.HBM)
    plan = [isinstance(a, Far) for a in args]
    args = [
        pltpu.with_memory_space_constraint(a.value, pltpu.HBM) if isinstance(a, Far) else a
        for a in args
    ]
    far_out = [len(o) > 2 for o in outs]
    if Order.last is not None:
        args[0] = after(args[0], Order.last)
    held = [(a.shape, a.dtype) for a, far in zip(args, plan) if far]
    held += [o[:2] for o, far in zip(outs, far_out) if far]
    need = sum(math.prod(s) * jnp.dtype(d).itemsize for s, d in [*held, *scratch])
    run = pl.pallas_call(
        functools.partial(
            loading_body,
            body,
            plan,
            len(outs),
            far_out,
            late,
            [a.view for a in ahead],
            len(scratch),
        ),
        out_shape=[
            pltpu.HBM(o[0], o[1]) if far else jax.ShapeDtypeStruct(o[0], o[1])
            for o, far in zip(outs, far_out)
        ]
        + [jax.ShapeDtypeStruct(a.shape, a.value.dtype) for a in ahead],
        in_specs=[
            scalars if i in smem else distant if plan[i] else whole for i in range(len(args))
        ]
        + [distant] * len(ahead),
        out_specs=[distant if far else whole for far in far_out] + [whole] * len(ahead),
        scratch_shapes=[pltpu.VMEM(s, d) for s, d in [*scratch, *held]]
        + [pltpu.SemaphoreType.DMA((max(len(held) + len(ahead), 1),))],
        compiler_params=pltpu.CompilerParams(vmem_limit_bytes=(mib << 20) + need),
        cost_estimate=pl.CostEstimate(flops=1, bytes_accessed=1, transcendentals=0),
    )
    moved = [pltpu.with_memory_space_constraint(a.value, pltpu.HBM) for a in ahead]
    got = list(run(*args, *moved))
    Order.last = got[0]
    return got


def far(values):
    return [Far(v) for v in values]


def join(slots):
    half = slots[0].shape[0] // 2
    return jnp.concatenate([s[:half] for s in slots] + [s[half:] for s in slots], axis=0)


def slot_rows(rows, k, count):
    half = rows.shape[0] // (2 * count)
    low = k * half
    high = rows.shape[0] // 2 + k * half
    return jnp.concatenate([rows[low : low + half], rows[high : high + half]], axis=0)


def centred(rows):
    centre = rows - jnp.mean(rows, axis=-1, keepdims=True)
    scale = lax.rsqrt(jnp.mean(centre * centre, axis=-1, keepdims=True) + 1e-05)
    return centre * scale, scale


def fill(scratch, own, other, core):
    half = own.shape[0]
    scratch[pl.ds(pl.multiple_of(core * half, half), half), :] = own[...]
    scratch[pl.ds(pl.multiple_of((1 - core) * half, half), half), :] = other[...]


def pick_gain(own, other, which, core):
    a = own[which : which + 1, :].astype(F32)
    b = other[which : which + 1, :].astype(F32)
    first = jnp.where(core == 0, a, b)
    second = jnp.where(core == 0, b, a)
    return jnp.concatenate([first, second], axis=1)


def route_rows(pieces):
    lane = lax.broadcasted_iota(I32, (8, 128), 1)
    low = lane < 64
    rolled = [pltpu.roll(p, 64, 1) for p in pieces]
    count = len(pieces)
    front = [jnp.where(low, pieces[i], rolled[i + 1]) for i in range(0, count, 2)]
    back = [jnp.where(low, rolled[i], pieces[i + 1]) for i in range(0, count, 2)]
    return jnp.concatenate(front + back, axis=1)


def pack_body(count, rest, *refs):
    tok, routes = refs[:2]
    place = lax.axis_index("ctx") // rest
    local, dim = tok.shape[1:]
    for k, out in enumerate(refs[2:]):
        out[:local, :] = tok[place ^ (k + 1)]
        out[local:, :] = jnp.zeros((8, dim), BF)
        out[local : local + TWO, :128] = routes[place ^ (k + 1)].astype(F32).astype(BF)


def pack_all_body(count, rest, *refs):
    tok, routes, query, kv, router, out = refs[:6]
    pieces, packed = refs[6:-1], refs[-1]
    pack_body(count, rest, tok, routes, *pieces)
    Order.rest()
    half, cols = query.shape
    keys = kv.shape[1]
    packed[half:, :] = jnp.zeros((8, packed.shape[1]), BF)
    packed[:half, :cols] = query[...]
    packed[:half, cols : cols + keys] = kv[...]
    packed[:half, cols + keys :] = out[...]
    packed[half:, :half] = router[...]


def fill_router(wr, own, packed, core):
    half = own.shape[1]
    wr[...] = jnp.zeros_like(wr)
    experts = own.shape[0]
    mine = pl.ds(pl.multiple_of(core * half, half), half)
    theirs = pl.ds(pl.multiple_of((1 - core) * half, half), half)
    wr[:experts, mine] = own[...].astype(F32)
    wr[:experts, theirs] = packed[half:, :half].astype(F32)


def keys_body(count, rest, *refs):
    toks = refs[:count]
    routes, g_own, g_other, k_own, packed = refs[count : count + 5]
    kv_out, normed_out, tok_out, gain_out, wk, tail_out = refs[count + 5 :]
    core = lax.axis_index("wsh")
    place = lax.axis_index("ctx") // rest
    half = k_own.shape[0]
    local = toks[0].shape[0]
    keys = k_own.shape[1]
    cols = packed.shape[1] - keys - toks[0].shape[1]
    fill(wk, k_own, packed.at[:half, cols : cols + keys], core)
    rows = join([t[:local] for t in toks])
    tok_out[...] = rows
    Order.leave(2, 4)
    tail_out[...] = jnp.zeros_like(tail_out)
    tail_out[:TWO, :] = routes[place].astype(F32)
    for k in range(1, count):
        tail_out[8 * k : 8 * k + 8, :] = toks[k][local : local + 8, :128].astype(F32)
    rows = rows.astype(F32)
    unit, _ = centred(rows)
    gain_out[...] = jnp.zeros_like(gain_out)
    for which in range(TWO):
        gain_out[which : which + 1, :] = pick_gain(g_own, g_other, which, core)
    normed = (unit * gain_out[0:1, :]).astype(BF)
    normed_out[...] = normed
    Order.leave(1, 3)
    kv = mm(normed, wk[...]).astype(BF)
    for i in range(kv_out.shape[0]):
        kv_out[i] = kv


def project_body(count, experts, head, *refs):
    normed_ref, tails, q_own, r_own, o_own, packed = refs[:6]
    qt_out, nt_out, gate_out, gate_far, route_out, route_far, wq, wr, wo = refs[6:]
    core = lax.axis_index("wsh")
    half, cols = q_own.shape
    normed = normed_ref[...]
    nt_out[...] = normed.T
    Order.leave(1)
    Order.rest()
    fill(wq, q_own, packed.at[:half, :cols], core)
    fill_router(wr, r_own, packed, core)
    fill(wo, o_own, packed.at[:half, packed.shape[1] - o_own.shape[1] :], core)
    Order.leave(6, 7, 8)
    routes = route_rows([tails[8 * k : 8 * k + 8, :] for k in range(count)])
    route_out[...] = routes
    route_far[...] = routes
    logits = mm(wr[...].astype(BF), normed, 1, 1)
    queries = mm(wq[...], normed, 0, 1) * 0.125
    chosen = []
    for s in range(TWO):
        route = routes[s : s + 1]
        total = jnp.zeros((head, normed.shape[0]), F32)
        value = jnp.zeros((1, normed.shape[0]), F32)
        for e in range(experts):
            here = route == e
            total = jnp.where(here, queries[e * head : (e + 1) * head], total)
            value = jnp.where(here, logits[e : e + 1], value)
        qt_out[s * head : (s + 1) * head, :] = total.astype(BF)
        chosen.append(value)
    top = jnp.maximum(chosen[0], chosen[1])
    raised = [jnp.exp(c - top) for c in chosen]
    total = raised[0] + raised[1]
    gate_out[...] = jnp.concatenate([r / total for r in raised], axis=0)
    gate_far[...] = gate_out[...]


def places(order, count, rest, block, width, part):
    me = lax.axis_index("ctx")
    place, other = me // rest, me % rest
    size = count * rest
    lane = lax.broadcasted_iota(I32, (1, width), 1)
    out = jnp.zeros((1, width), I32)
    for k in range(count):
        first = order[(place ^ k) * rest + other]
        base = jnp.where(part == 0, first, 2 * size - 1 - first) * block
        out = jnp.where(lane // block == k, lane - k * block + base, out)
    return out


def key_bases(order, count, rest, block, chunk, part):
    me = lax.axis_index("ctx")
    place = me // rest
    size = count * rest
    out = []
    for k in range(count):
        first = order[(place ^ k) * rest + chunk]
        out.append((first if part == 0 else 2 * size - 1 - first) * block)
    return out


def masked(scores, gap, bases, block):
    parts = [
        jnp.where(gap <= -base, scores[k * block : (k + 1) * block], NONE)
        for k, base in enumerate(bases)
    ]
    return jnp.concatenate(parts, axis=0)


def scored(kv, side, h, gap, order, count, rest, block, chunk, half):
    first = mm(kv[:half], side)
    if h == 0:
        return masked(first, gap, key_bases(order, count, rest, block, chunk, 0), block)
    second = mm(kv[half:], side)
    second = masked(second, gap, key_bases(order, count, rest, block, chunk, 1), block)
    return jnp.concatenate([first, second], axis=0)


def turn_keys(kv, kv_turned):
    rows = kv.shape[1]
    for c in range(kv.shape[0]):
        kv_turned[:, c * rows : (c + 1) * rows] = kv[c].T


def both_slots(rows, head, cols):
    return jnp.concatenate([rows[s * head : (s + 1) * head, cols] for s in range(TWO)], axis=1)


def gap_rows(order, count, rest, block, half, h):
    gap = lax.broadcasted_iota(I32, (block, half), 0) - places(order, count, rest, block, half, h)
    return jnp.concatenate([gap] * TWO, axis=1)


def attend_body(count, rest, experts, head, *refs):
    order, kv_ref, qt, gates, routes = refs[:5]
    tok, gains, wo = refs[5:8]
    att_out, log_out, mixed_out, hidden_out, two_out, turned_out, kv_out, kv_turned = refs[8:]
    kv_out[...] = kv_ref[...]
    Order.leave(6)
    other = lax.axis_index("ctx") % rest
    total = qt.shape[1]
    half = total // 2
    block = half // count
    turn_keys(kv_ref, kv_turned)
    Order.rest()
    sides, gaps = [], []
    for h in range(2):
        side = both_slots(qt, head, slice(h * half, (h + 1) * half))
        sides.append(jnp.concatenate([side, jnp.zeros_like(side)], axis=0))
        gaps.append(gap_rows(order, count, rest, block, half, h))

    def step(turn, carry):
        chunk = turn ^ other
        at = pl.multiple_of(chunk * total, total)
        kv = kv_ref[chunk]
        scores = [
            scored(kv, sides[h], h, gaps[h], order, count, rest, block, chunk, half)
            for h in range(2)
        ]
        out = []
        for h in range(2):
            top, norm, summed = carry[h]
            fresh = jnp.maximum(top, jnp.max(scores[h], axis=0, keepdims=True))
            shares = jnp.exp(scores[h] - fresh)
            fade = jnp.exp(top - fresh)
            norm = norm * fade + jnp.sum(shares, axis=0, keepdims=True)
            values = kv_turned[head:, pl.ds(at, half * (h + 1))]
            out.append((fresh, norm, summed * fade + mm(values, shares.astype(BF))))
        return tuple(out)

    start = (
        jnp.full((1, TWO * half), NONE, F32),
        jnp.zeros((1, TWO * half), F32),
        jnp.zeros((head, TWO * half), F32),
    )
    done = lax.fori_loop(0, rest, step, (start, start), unroll=rest <= 4)
    for h in range(2):
        top, norm, summed = done[h]
        logs, attended = top + jnp.log(norm), summed / norm
        for s in range(TWO):
            here, cols = slice(h * half, (h + 1) * half), slice(s * half, (s + 1) * half)
            log_out[s : s + 1, here] = logs[:, cols]
            att_out[s * head : (s + 1) * head, here] = attended[:, cols]
    Order.leave(0, 1)
    for e in range(experts):
        part = jnp.zeros((head, total), F32)
        for s in range(TWO):
            gate = jnp.where(routes[s : s + 1] == e, gates[s : s + 1], 0.0)
            part = part + gate * att_out[s * head : (s + 1) * head, :]
        mixed_out[e * head : (e + 1) * head, :] = part.astype(BF)
    Order.leave(2)
    hidden = tok[...].astype(F32) + mm(mixed_out[...].T, wo[...])
    hidden_out[...] = hidden
    unit, _ = centred(hidden)
    two = (unit * gains[1:2, :]).astype(BF)
    two_out[...] = two
    turned_out[...] = two.T


def feed_body(count, rest, first, tile, *refs):
    two, turned = refs[:2]
    if first:
        slots = refs[2 : 2 + count]
        u_own, u_other, down, layer_in = refs[2 + count : 6 + count]
        layer_out, back_out, send, keep, cots, cot_far, send_up, up = refs[6 + count :]
    else:
        cots, u_own, u_other, down, layer_in, back_in = refs[2:8]
        outs = refs[8 : 12 + count]
        layer_pieces, back_out, keep_down, keep, send = outs[:count], *outs[count:]
        up, layer_out = refs[12 + count :]
    core = lax.axis_index("wsh")
    side = (1 - core) if first else core
    width = down.shape[0]
    half = u_own.shape[0]
    lanes = pl.ds(pl.multiple_of(side * width, width), width)
    up[pl.ds(pl.multiple_of(core * half, half), half), :] = u_own[...]
    up[pl.ds(pl.multiple_of((1 - core) * half, half), half), :] = u_other[:, lanes]
    if first:
        cots[...] = join([o[...] for o in slots])
        cot_far[...] = cots[...]
        Order.leave(5)
    layer_out[...] = layer_in[...]
    if first:
        back_out[...] = jnp.zeros_like(back_out)
    else:
        back_out[...] = back_in[...]
    mine = pl.ds(pl.multiple_of(core * half, half), half)
    theirs = pl.ds(pl.multiple_of((1 - core) * half, half), half)
    dim = up.shape[0]
    per = dim // tile

    def products(j):
        cols = slice(j * tile, (j + 1) * tile)
        return mm(two[...], up[:, cols]), mm(cots[...], down[cols, :], 1, 1)

    steps = width // tile
    ready = products(0)
    for j in range(steps):
        cols = slice(j * tile, (j + 1) * tile)
        pre, back = ready
        if j + 1 < steps:
            ready = products(j + 1)
        phi = 0.5 * (1.0 + lax.erf(pre * math.sqrt(0.5)))
        bell = jnp.exp(pre * pre * -0.5) * (1.0 / math.sqrt(2.0 * math.pi))
        act = (pre * phi).astype(BF)
        back_pre = (back * (phi + pre * bell)).astype(BF)
        layer_out[...] += mm(act, down[cols, :])
        back_out[...] += mm(back_pre, up[:, cols], 1, 1)
        grad = mm(act.T, cots[...]).astype(BF)
        grad_mine = mm(turned[mine, :], back_pre).astype(BF)
        grad_theirs = mm(turned[theirs, :], back_pre).astype(BF)
        rows = slice((j // per) * half, (j // per + 1) * half)
        lane = slice((j % per) * tile, (j % per + 1) * tile)
        keep[rows, lane] = grad_mine
        if first:
            send[cols, :] = grad
            send_up[rows, lane] = grad_theirs
        else:
            keep_down[cols, :] = grad
            send[rows, lane] = grad_theirs
    if not first:
        Order.leave(count + 1, count + 2, count + 3)
        for k in range(count):
            layer_pieces[k][...] = slot_rows(layer_out[...], k, count).astype(layer_pieces[k].dtype)


def turn_body(count, rest, experts, head, *refs):
    hidden, back_two, cot, wo, gain, gates, routes, att = refs[:8]
    back_hidden_out, branch_out, grad_att_out, delta_out, logit_out, gain_out = refs[8:]
    unit, scale = centred(hidden[...])
    back = back_two[...]
    side = back * gain[1:2, :]
    part = scale * (
        side
        - jnp.mean(side, axis=-1, keepdims=True)
        - unit * jnp.mean(side * unit, axis=-1, keepdims=True)
    )
    gain_out[...] = jnp.broadcast_to(jnp.sum(back * unit, axis=0, keepdims=True), gain_out.shape)
    back_hidden = cot[...].astype(F32) + part
    back_hidden_out[...] = back_hidden
    branch = back_hidden.astype(BF)
    branch_out[...] = branch
    Order.leave(0, 1, 5)
    back_mixed = mm(wo[...], branch, 1, 1)
    grads = []
    for s in range(TWO):
        total = jnp.zeros((head, branch.shape[0]), F32)
        for e in range(experts):
            total = jnp.where(routes[s : s + 1] == e, back_mixed[e * head : (e + 1) * head], total)
        att_s = att[s * head : (s + 1) * head, :]
        grads.append(jnp.sum(total * att_s, axis=0, keepdims=True))
        low = (gates[s : s + 1] * total).astype(BF)
        grad_att_out[s * head : (s + 1) * head, :] = low
        delta_out[s : s + 1, :] = jnp.sum(low.astype(F32) * att_s, axis=0, keepdims=True)
    mean = gates[0:1] * grads[0] + gates[1:2] * grads[1]
    row = lax.broadcasted_iota(I32, logit_out.shape, 0)
    logit = jnp.zeros(logit_out.shape, F32)
    for s in range(TWO):
        value = gates[s : s + 1] * (grads[s] - mean)
        logit = logit + jnp.where(row.astype(F32) == routes[s : s + 1], value, 0.0)
    logit_out[...] = logit


def turn_start_body(count, rest, experts, head, layout, step, *refs):
    ins, early, outs, pieces = refs[:8], refs[8:12], refs[12:18], refs[18]
    turn_body(count, rest, experts, head, *ins, *outs)
    Order.rest()
    start_body(layout, True, 1, step, len(early), *early, pieces, None)


def attend_back_body(count, rest, head, split, *refs):
    order, kv_ref, qt, grad_att, logs, delta, grad_q_out = refs[:7]
    outs = refs[7 : 7 + split]
    kv_turned, sides, turned, grad_kv, grad_q = refs[7 + split :]
    total = qt.shape[1]
    half = total // 2
    block = half // count
    wide = TWO * half
    turn_keys(kv_ref, kv_turned)
    blank = jnp.zeros((head, wide), BF)
    for h in range(2):
        cols = slice(h * half, (h + 1) * half)
        q_side = jnp.concatenate([both_slots(qt, head, cols), blank], axis=0)
        g_side = jnp.concatenate([blank, both_slots(grad_att, head, cols)], axis=0)
        sides[2 * h], sides[2 * h + 1] = q_side, g_side
        turned[h, :wide, :], turned[h, wide:, :] = q_side.T, g_side.T
    grad_q[...] = jnp.zeros_like(grad_q)
    gaps = [gap_rows(order, count, rest, block, half, h) for h in range(2)]
    log_rows = [both_slots(logs, 1, slice(h * half, (h + 1) * half)) for h in range(2)]
    delta_rows = [both_slots(delta, 1, slice(h * half, (h + 1) * half)) for h in range(2)]

    def step(chunk, carry):
        at = pl.multiple_of(chunk * total, total)
        kv = kv_ref[chunk]
        grads = []
        for h in range(2):
            reach = half * (h + 1)
            scores = scored(
                kv, sides[2 * h], h, gaps[h], order, count, rest, block, chunk, half
            )
            shares = jnp.exp(scores - log_rows[h])
            back_shares = mm(kv[:reach], sides[2 * h + 1])
            back_scores = (shares * (back_shares - delta_rows[h])).astype(BF)
            both = jnp.concatenate([back_scores, shares.astype(BF)], axis=1)
            grads.append(mm(both, turned[h]))
            grad_q[h] += mm(kv_turned[:head, pl.ds(at, reach)], back_scores)
        grad_kv[pl.ds(at, half), :] = grads[0] + grads[1][:half]
        grad_kv[pl.ds(at + half, half), :] = grads[1][half:]
        return carry

    lax.fori_loop(0, rest, step, 0, unroll=rest <= 4)
    for h in range(2):
        for s in range(TWO):
            here, cols = slice(h * half, (h + 1) * half), slice(s * half, (s + 1) * half)
            grad_q_out[s * head : (s + 1) * head, here] = grad_q[h, :, cols].astype(BF)
    rows = outs[0].shape[0]
    digit = (lax.axis_index("ctx") % rest) // (rest // split)
    for i, out in enumerate(outs):
        begin = pl.multiple_of((digit ^ i) * rows, rows)
        out[...] = grad_kv[pl.ds(begin, rows), :].astype(out.dtype)


def query_body(experts, head, *refs):
    grad_q, normed_t, routes, mixed, branch, wq, wr, logit, tok = refs[:9]
    keep_out, keep, send, back_out, unit_out, scale_out, routers, bqt = refs[9:]
    core = lax.axis_index("wsh")
    total = grad_q.shape[1]
    for e in range(experts):
        part = jnp.zeros((head, total), F32)
        for s in range(TWO):
            value = grad_q[s * head : (s + 1) * head, :].astype(F32) * 0.125
            part = jnp.where(routes[s : s + 1] == e, value, part)
        bqt[e * head : (e + 1) * head, :] = part.astype(BF)
    back_q = bqt[...].T
    half = keep.shape[0]
    mine = pl.ds(pl.multiple_of(core * half, half), half)
    theirs = pl.ds(pl.multiple_of((1 - core) * half, half), half)
    send[:half, :] = mm(mixed[theirs, :], branch[...]).astype(BF)
    send[half:, :] = mm(normed_t[theirs, :], back_q).astype(BF)
    keep_out[...] = mm(mixed[mine, :], branch[...]).astype(BF)
    keep[...] = mm(normed_t[mine, :], back_q).astype(BF)
    Order.leave(0, 1, 2)
    parts = []
    left = logit[...]
    for _ in range(3):
        low = left.astype(BF)
        parts.append(low)
        left = left - low.astype(F32)
    routers[...] = parts_dot(parts, normed_t[...])
    back = mm(back_q, wq[...], 1, 1)
    wr_turned = wr[...].astype(BF)
    for low in parts:
        padded = jnp.concatenate([low.astype(F32), jnp.zeros((120, total), F32)], axis=0)
        back = back + mm(padded.T.astype(BF), wr_turned)
    back_out[...] = back
    unit, scale = centred(tok[...].astype(F32))
    unit_out[...] = unit
    scale_out[...] = jnp.broadcast_to(scale, scale_out.shape)


def unproject_body(count, terms, *refs):
    kv_terms = refs[:terms]
    back_part, unit_ref, scale_ref, routers, normed_t, back_hidden, wk, gain, gain_two, sent = refs[
        terms : terms + 10
    ]
    at = terms + 10
    pieces = refs[at : at + count]
    keep, send, gains = refs[at + count :]
    core = lax.axis_index("wsh")
    half = back_part.shape[1] // 2
    back_kv = kv_terms[0][...].astype(F32)
    for term in kv_terms[1:]:
        back_kv = back_kv + term[...].astype(F32)
    back_kv = back_kv.astype(BF)
    back = back_part[...] + mm(back_kv, wk[...], 1, 1)
    unit, scale = unit_ref[...], scale_ref[:, 0:1]
    side = back * gain[0:1, :]
    grad = back_hidden[...] + scale * (
        side
        - jnp.mean(side, axis=-1, keepdims=True)
        - unit * jnp.mean(side * unit, axis=-1, keepdims=True)
    )
    gains[0:1, :] = jnp.sum(back * unit, axis=0, keepdims=True)
    gains[1:2, :] = gain_two[0:1, :]
    step = half // 4
    experts = routers.shape[0]
    high = sent.shape[0]
    Order.rest()
    send[:high, :] = sent[...]
    for out, which in ((keep, core), (send.at[high:, :], 1 - core)):
        mine = pl.ds(pl.multiple_of(which * half, half), half)
        grad_k = mm(normed_t[mine, :], back_kv).astype(out.dtype)
        for j in range(4):
            out[:step, j * 128 : (j + 1) * 128] = grad_k[j * step : (j + 1) * step]
        blank = jnp.zeros((experts, half), F32)
        out[step : step + 8, :] = jnp.concatenate([routers[:, mine], blank], axis=1).astype(out.dtype)
        gain_pair = jnp.concatenate([gains[0:1, mine], gains[1:2, mine]], axis=1)
        out[step + 8 :, :] = jnp.broadcast_to(gain_pair, (8, 2 * half)).astype(out.dtype)
    Order.leave(count, count + 1)
    for k in range(count):
        pieces[k][...] = slot_rows(grad, k, count).astype(pieces[k].dtype)


def parts_dot(parts, normed_t):
    out = None
    for low in parts:
        value = mm(low, normed_t, 1, 1)
        out = value if out is None else out + value
    return out


def sum_layout(layout, ins, total):
    at = 0
    for terms in layout:
        height = terms[0][2]
        value = None
        for index, begin, count in terms:
            part = ins[index][begin : begin + count, :].astype(F32)
            value = part if value is None else value + part
        total[at : at + height, :] = value
        at += height
    if at < total.shape[0]:
        total[at:, :] = jnp.zeros((total.shape[0] - at, total.shape[1]), F32)


def cut_rows(total, outs, stride, step):
    rows = outs[0].shape[0]
    digit = (lax.axis_index("ctx") // stride) % step
    for j in range(step):
        begin = pl.multiple_of((digit ^ j) * rows, 8)
        outs[j][...] = total[pl.ds(begin, rows), :].astype(outs[j].dtype)


def start_body(layout, whole, stride, step, n_in, *refs):
    ins, outs, total = refs[:n_in], refs[n_in:-1], refs[-1]
    if whole:
        rows = outs[0].shape[1]
        at = 0
        for terms in layout:
            height, done = terms[0][2], 0
            while done < height:
                j, low = (at + done) // rows, (at + done) % rows
                take = min(height - done, rows - low)
                value = None
                for index, begin, _ in terms:
                    part = ins[index][begin + done : begin + done + take, :].astype(F32)
                    value = part if value is None else value + part
                outs[0][j, low : low + take, :] = value.astype(BF)
                done += take
            at += height
        while at < rows * step:
            j, low = at // rows, at % rows
            outs[0][j, low:, :] = jnp.zeros((rows - low, outs[0].shape[2]), BF)
            at += rows - low
    else:
        sum_layout(layout, ins, total)
        cut_rows(total, outs, stride, step)


def terms_of(ref):
    return [ref.at[j] for j in range(ref.shape[0])] if len(ref.shape) == 3 else [ref]


def middle_body(chunks, stride, step, n_in, riders, *refs):
    ins, riding = refs[:n_in], refs[n_in : n_in + riders]
    refs = refs[n_in + riders :]
    outs, totals = refs[:step], refs[step:]
    digit = (lax.axis_index("ctx") // stride) % step
    at, low = 0, 0
    for count, total in zip(chunks, totals):
        value = None
        for ref in ins[at : at + count]:
            for term in terms_of(ref):
                part = term[...].astype(F32)
                value = part if value is None else value + part
        total[...] = value
        rows = total.shape[0] // step
        for j in range(step):
            begin = pl.multiple_of((digit ^ j) * rows, 8)
            outs[j][low : low + rows, :] = total[pl.ds(begin, rows), :].astype(outs[j].dtype)
        low += rows
        at += count
    for j in range(1, step if riders else 1):
        outs[j][low:, :] = riding[j - 1][...]


def copies_body(slices, n_in, *refs):
    ins, out = refs[:n_in], refs[-1]
    for j in range(out.shape[0]):
        at = 0
        for begin, rows in slices:
            for ref in ins:
                out[j, at : at + rows, :] = ref[begin : begin + rows, :]
                at += rows


def final_body(strides, parts, dests, n_out, *refs):
    got, outs, totals = refs[0], refs[1 : 1 + n_out], refs[1 + n_out :]
    me = lax.axis_index("ctx")
    shift, per = 0, 1
    for stride, step in strides[1:]:
        shift = shift * step + (me // stride) % step
        per *= step
    at, used = 0, 0
    for height, total, (dest, many) in zip(parts, totals, dests):
        rows = height // per
        swapped = isinstance(got, tuple)
        digit = me % strides[0][1] if swapped else 0
        for i in range(len(got) if swapped else got.shape[0]):
            for b in range(per):
                begin = pl.multiple_of(((i ^ digit) * per + (b ^ shift)) * rows, 8)
                source = got[i].at[0] if swapped else got.at[i]
                piece = source[at + b * rows : at + (b + 1) * rows, :]
                total[pl.ds(begin, rows), :] = piece.astype(F32)
        at += height
        dest(total, outs[used : used + many])
        Order.leave(*range(used, used + many))
        used += many


WIDTH = 512


def cut_up(chunks, heights, strides, at, size, riders=()):
    stride, step = strides[at]
    total = sum(heights) // step
    more = riders[0].shape[0] if riders else 0
    n_in = sum(len(c) for c in chunks)
    pieces = call(
        functools.partial(middle_body, [len(c) for c in chunks], stride, step, n_in, len(riders)),
        [((total, WIDTH), F32)] + [((total + more, WIDTH), BF)] * (step - 1),
        [t for c in chunks for t in c] + far(riders),
        scratch=[((h, WIDTH), F32) for h in heights],
    )
    return pieces[:1] + [swap(pieces[j], j * stride, size) for j in range(1, step)]


def spread(done, strides, at, size):
    stride, step = strides[at]
    return [done] + [swap(done, j * stride, size) for j in range(1, step)]


def settle(terms):
    return call(add_body, [(terms[0].shape, BF)], terms)[0]


def add_body(*refs):
    rows = refs[-1].shape[0]
    value = refs[0][:rows, :].astype(F32)
    for ref in refs[1:-1]:
        value = value + ref[:rows, :].astype(F32)
    refs[-1][...] = value.astype(refs[-1].dtype)


def early_dest(total, outs):
    down, tile = outs
    wide = down.shape[0]
    down[...] = total[:wide, :]
    tile[...] = total[wide : wide + tile.shape[0], :]


def both_final_body(strides, parts, n_in, *refs):
    got, tile = refs[:n_in], refs[n_in]
    outs, totals = refs[n_in + 1 : n_in + 8], refs[n_in + 8 :]

    def main(total, outs):
        (up,) = outs
        half = up.shape[0]
        core = lax.axis_index("wsh")
        tiles = up.shape[1] // WIDTH
        for i in range(tiles):
            side, inner = i // (tiles // 2), i % (tiles // 2)
            at = (core if side == 0 else 1 - core) * (tiles // 2) + inner
            rows = tile[...] if i == 0 else total[(i - 1) * half : i * half, :]
            up[:, pl.ds(pl.multiple_of(at * WIDTH, WIDTH), WIDTH)] = rows

    dests = [(main, 1), (late_dest, 6)]
    final_body(strides, parts, dests, 7, got, *outs, *totals)


def late_dest(total, outs):
    out, query, kv, router, one, two = outs
    half = kv.shape[0]
    out[...] = total[:half, :]
    query[...] = total[half : 2 * half, :]
    step = half // 4
    at = 2 * half
    for j in range(4):
        kv[j * step : (j + 1) * step, :] = total[at : at + step, j * 128 : (j + 1) * 128]
    at += step
    router[...] = total[at : at + router.shape[0], :half]
    one[...] = total[at + 8 : at + 9, :half]
    two[...] = total[at + 8 : at + 9, half:]


def place_body(rest, *refs):
    place = lax.axis_index("ctx") // rest
    out = refs[-1]
    local = out.shape[1]
    for k, ref in enumerate(refs[:-1]):
        begin = ref.shape[0] - local
        out[place ^ k] = ref[begin:, :].astype(F32)


def close_body(rest, count, strides, parts, n_in, *refs):
    main, moved = refs[: n_in + 1], refs[n_in + 1 : n_in + 1 + count]
    outs, totals = refs[n_in + 1 + count : n_in + 9 + count], refs[n_in + 9 + count :]
    place_body(rest, *moved, outs[7])
    Order.leave(7)
    both_final_body(strides, parts, n_in, *main, *outs[:7], *totals)


def on_device(
    tokens,
    routes,
    block_order,
    norm_gain1,
    router_w,
    query_w,
    kv_w,
    out_w,
    norm_gain2,
    up_w,
    down_w,
    cotangent,
):
    size = lax.axis_size("ctx")
    count, local, dim = tokens.shape
    rest = size // count
    place = lax.axis_index("ctx") // rest
    total = count * local
    experts = router_w.shape[1]
    head = kv_w.shape[1] // 2
    feed = up_w.shape[1]

    Order.last = None
    tall = dim // 2
    keys = 2 * head
    router_t = router_w.T
    routes_t = routes.transpose(0, 2, 1)

    def core():
        return lax.axis_index("wsh")

    def here():
        return lax.axis_index("ctx") // rest

    got = call(
        functools.partial(pack_all_body, count, rest),
        [((local + 8, dim), BF)] * (count - 1) + [((tall + 8, experts * head + keys + dim), BF)],
        far([tokens, routes_t, query_w, kv_w, router_t, out_w]),
        late=(2, 3, 4, 5),
        ahead=[Ahead(tokens, (local, dim), lambda r: r.at[here()]), Ahead(kv_w)]
        + [
            Ahead(cotangent, (local, dim), lambda r, k=k: r.at[here() ^ k])
            for k in range(1, count)
        ],
    )
    tok_pieces, (packed, tok_own, kv_own), cot_pieces = got[: count - 1], got[count - 1 : count + 2], got[count + 2 :]
    tok_x = [swap(tok_pieces[k - 1], k * rest, size) for k in range(1, count)]
    packed_x = trade(packed)
    gain_one, gain_two = after((norm_gain1, norm_gain2), packed)
    gains = jnp.stack([gain_one, gain_two])
    gains_x = trade(gains)

    steps = factors(rest)
    kv, normed, tok, gain_rows, wk, tails = call(
        functools.partial(keys_body, count, rest),
        [
            ((steps[0], total, keys), BF, 1),
            ((total, dim), BF, 1),
            ((total, dim), BF, 1),
            ((8, dim), F32, 1),
            ((dim, keys), BF, 1),
            ((8 * count, 128), F32),
        ],
        [tok_own, *tok_x, Far(routes_t), gains, gains_x, kv_own, packed_x],
    )
    stride = 1
    for i, step in enumerate(steps):
        if i > 0:
            kv = jnp.broadcast_to(kv[None], (step,) + kv.shape)
        kv = exchange(kv, stride, size).reshape(-1, total, keys)
        stride *= step
    cot_pieces = after(tuple(cot_pieces), normed)
    cot_x = [swap(cot_pieces[k - 1], k * rest, size) for k in range(1, count)]
    qt, normed_t, gates, gates_far, route, route_far, wq, wr, wo = call(
        functools.partial(project_body, count, experts, head),
        [
            ((TWO * head, total), BF, 1),
            ((dim, total), BF, 1),
            ((TWO, total), F32),
            ((TWO, total), F32, 1),
            ((8, total), F32),
            ((8, total), F32, 1),
            ((dim, experts * head), BF, 1),
            ((128, dim), F32, 1),
            ((experts * head, dim), BF, 1),
        ],
        [Far(normed), tails, *far([query_w, router_t, out_w]), packed_x],
        late=(2, 3, 4),
    )
    up_w2, down_w2, _ = lax.optimization_barrier((up_w, down_w, normed))
    up_x, down_x = trade(up_w2), trade(down_w2)
    span = rest * total
    wide = feed // 2

    def lanes(which):
        def view(ref):
            side = which()
            return ref.at[:, pl.ds(pl.multiple_of(side * wide, wide), wide)]

        return view

    att, logs, mixed, hidden, two, two_t, kv_far, cot_own, up_first = call(
        functools.partial(attend_body, count, rest, experts, head),
        [
            ((TWO * head, total), F32, 1),
            ((TWO, total), F32, 1),
            ((experts * head, total), BF, 1),
            ((total, dim), F32),
            ((total, dim), BF),
            ((dim, total), BF),
            ((rest, total, keys), BF, 1),
        ],
        [block_order, kv, Far(qt), gates, route, *far([tok, gain_rows, wo])],
        scratch=[((keys, span), BF)],
        smem=(0,),
        late=(2, 5, 6, 7),
        ahead=[
            Ahead(cotangent, (local, dim), lambda r: r.at[here()]),
            Ahead(up_w, (tall, wide), lanes(lambda: 1 - core())),
        ],
    )

    tile = 512
    upper = wide * tall // dim
    layer, back_two, send_one, keep_one, cots, cots_far, send_up, up_second, down_own = call(
        functools.partial(feed_body, count, rest, True, tile),
        [
            ((total, dim), F32),
            ((total, dim), F32),
            ((wide, dim), BF),
            ((upper, dim), BF, 1),
            ((total, dim), BF),
            ((total, dim), BF, 1),
            ((upper, dim), BF),
        ],
        [two, two_t, cot_own, *cot_x, up_first, up_x, down_x, hidden],
        scratch=[((dim, wide), BF)],
        ahead=[Ahead(up_w, (tall, wide), lanes(core)), Ahead(down_w)],
    )
    recv_down, recv_up = trade(send_one), trade(send_up)
    *layer_pieces, back_two, keep_down, keep_two, send_two, cots, wo, gain_near, gates, route, att = call(
        functools.partial(feed_body, count, rest, False, tile),
        [((local, dim), F32, 1)]
        + [((local, dim), BF, 1)] * (count - 1)
        + [
            ((total, dim), F32),
            ((wide, dim), BF, 1),
            ((upper, dim), BF, 1),
            ((upper, dim), BF, 1),
        ],
        [two, two_t, cots, up_second, up_x, down_own, layer, back_two],
        scratch=[((dim, wide), BF), ((total, dim), F32)],
        ahead=[
            Ahead(a)
            for a in (cots_far, wo, gain_rows, gates_far, route_far, att)
        ],
    )
    recv_two = trade(send_two)
    layer_got = [layer_pieces[0]] + [swap(layer_pieces[k], k * rest, size) for k in range(1, count)]

    strides = []
    stride = 1
    for step in [*steps, count]:
        strides.append((stride, step))
        stride *= step
    last = len(strides) - 1
    unit = 8 * size
    first = strides[0][1]
    early_rows = -(-(wide + tall) // unit) * unit
    main_rows = -(-(2 * upper - tall) // unit) * unit
    small = tall // 4 + 16
    late_rows = -(-(small + 2 * tall) // unit) * unit

    def bulk(args, layout, height, ahead=()):
        pieces, *near = call(
            functools.partial(start_body, layout, True, 1, first, len(args)),
            [((first, height // first, WIDTH), BF)],
            args,
            scratch=[((8, WIDTH), F32)],
            ahead=ahead,
        )
        return exchange(pieces, 1, size), near

    def inner(terms, height, riders=()):
        height //= first
        for at in range(1, last + 1):
            more = riders if at == last else ()
            terms = cut_up([terms], [height], strides, at, size, more)
            height //= strides[at][1]
        return terms

    def outer(got):
        for at in reversed(range(1, last)):
            got = spread(jnp.concatenate(got, axis=0), strides, at, size)
        return got

    def ready(got, ahead=()):
        rows = got[0].shape[0]
        copies, *near = call(
            functools.partial(copies_body, [(0, rows)], len(got)),
            [((first, rows * len(got), WIDTH), BF)],
            got,
            ahead=ahead,
        )
        return exchange(copies, 1, size), near

    back_hidden, branch, grad_att, delta, logit, gain_two, early, kv_near, qt_near, logs_near = call(
        functools.partial(
            turn_start_body,
            count,
            rest,
            experts,
            head,
            [[(0, 0, wide), (1, 0, wide)], [(2, 0, tall), (3, 0, tall)]],
            first,
        ),
        [
            ((total, dim), F32, 1),
            ((total, dim), BF, 1),
            ((TWO * head, total), BF),
            ((TWO, total), F32),
            ((experts, total), F32, 1),
            ((8, dim), F32, 1),
            ((first, early_rows // first, WIDTH), BF),
        ],
        [
            hidden,
            back_two,
            cots,
            wo,
            gain_near,
            gates,
            route,
            att,
            Far(keep_down),
            recv_down,
            Far(keep_two),
            recv_up,
        ],
        late=(8, 10),
        ahead=[Ahead(a) for a in (kv_far, qt, logs)],
    )
    early = exchange(early, 1, size)
    split = steps[-1]
    share = span // split
    grad_q, *kv_terms = call(
        functools.partial(attend_back_body, count, rest, head, split),
        [((TWO * head, total), BF), ((share, keys), F32, 1)] + [((share, keys), BF, 1)] * (split - 1),
        [block_order, kv_near, qt_near, grad_att, logs_near, delta],
        scratch=[
            ((keys, span), BF),
            ((4, keys, total), BF),
            ((2, 2 * total, keys), BF),
            ((span, keys), F32),
            ((2, head, total), F32),
        ],
        smem=(0,),
        ahead=[Ahead(a) for a in (normed_t, route_far, mixed, branch, wq, wr, logit, tok)],
    )
    kv_terms, ahead = kv_terms[:split], kv_terms[split:]
    stride = rest
    for i, step in reversed(list(enumerate(steps))):
        stride //= step
        if i + 1 < len(steps):
            summed = functools.reduce(lambda a, b: a + b.astype(F32), terms)
            parts = summed.reshape(step, -1, keys)
            digit = (lax.axis_index("ctx") // stride) % step
            kv_terms = [pick(parts, digit ^ j) for j in range(step)]
        terms = [kv_terms[0]] + [
            swap(kv_terms[j].astype(BF), j * stride, size) for j in range(1, step)
        ]
    grad_q = after(grad_q, *layer_got[1:])
    keep_out, keep_query, send_main, back_part, unit_rows, scale_rows, routers, *near = call(
        functools.partial(query_body, experts, head),
        [
            ((tall, dim), BF, 1),
            ((tall, dim), BF, 1),
            ((2 * tall, dim), BF, 1),
            ((total, dim), F32),
            ((total, dim), F32),
            ((total, 128), F32),
            ((experts, dim), F32),
        ],
        [grad_q, *ahead],
        scratch=[((experts * head, total), BF)],
        ahead=[Ahead(a) for a in (normed_t, back_hidden, wk, gain_rows, gain_two, terms[0])],
    )
    *near, term = near
    *input_pieces, keep_late, send_late, keep_two, keep_one = call(
        functools.partial(unproject_body, count, len(terms)),
        [((local, dim), F32, 1)]
        + [((local, dim), BF, 1)] * (count - 1)
        + [((small, dim), F32, 1), ((small + 2 * tall, dim), BF)],
        [term, *terms[1:], back_part, unit_rows, scale_rows, routers, *near, Far(send_main)],
        scratch=[((8, dim), F32)],
        late=(len(terms) + 9,),
        ahead=[Ahead(a) for a in (keep_two, keep_one)],
    )
    recv_late = trade(send_late)
    main, _ = bulk(
        [keep_two, recv_up, keep_one, recv_two],
        [
            [(0, tall, upper - tall), (1, tall, upper - tall)],
            [(2, 0, upper), (3, 0, upper)],
        ],
        main_rows,
    )
    pieces = call(
        functools.partial(
            start_body,
            [
                [(0, 0, tall), (1, 0, tall)],
                [(0, tall, tall), (2, 0, tall)],
                [(0, 2 * tall, small), (3, 0, small)],
            ],
            False,
            1,
            first,
            4,
        ),
        [((late_rows // first, WIDTH), F32)] + [((late_rows // first, WIDTH), BF)] * (first - 1),
        [recv_late, *far([keep_out, keep_query, keep_late])],
        scratch=[((late_rows, WIDTH), F32)],
    )
    late = pieces[:1] + [swap(pieces[j], j, size) for j in range(1, first)]
    early_terms = inner([early], early_rows)
    early_got = outer(spread(settle(early_terms), strides, last, size))
    heights = [main_rows // first, late_rows // first]
    chunks = [[main], late]
    for at in range(1, last):
        chunks = [cut_up([c], [h], strides, at, size) for c, h in zip(chunks, heights)]
        heights = [h // strides[at][1] for h in heights]
    both_terms = cut_up(chunks, heights, strides, last, size)
    heights = [h // count for h in heights]
    (layer_out,) = call(
        functools.partial(place_body, rest),
        [((count, local, dim), F32, 1)],
        [Far(layer_got[0]), *far(layer_got[1:])],
    )
    early_last, _ = ready(early_got)
    both_got = spread(settle(both_terms), strides, last, size)
    slices = [(0, heights[0]), (heights[0], heights[1])]
    for stage in reversed(range(1, last)):
        moved = []
        for begin, h in slices:
            piece = jnp.concatenate([g[begin : begin + h] for g in both_got], axis=0)
            moved.append(spread(piece, strides, stage, size))
        both_got = [jnp.concatenate([m[j] for m in moved], axis=0) for j in range(strides[stage][1])]
        tops = [m[0].shape[0] for m in moved]
        slices = [(0, tops[0]), (tops[0], tops[1])]
    tall_rows = sum(h for _, h in slices) * len(both_got)
    (both_own,) = call(
        functools.partial(copies_body, slices, len(both_got)),
        [((1, tall_rows, WIDTH), BF)],
        both_got,
    )
    both_last = spread(both_own, strides, 0, size)
    input_pieces = after(tuple(input_pieces), both_got[0])
    moved = {k: swap(input_pieces[k], k * rest, size) for k in reversed(range(1, count))}
    input_got = [input_pieces[0]] + [moved[k] for k in range(1, count)]
    grad_down, up_tile = call(
        functools.partial(final_body, strides, [early_rows // first], [(early_dest, 2)], 2),
        [((wide, dim), F32, 1), ((tall, WIDTH), F32)],
        [early_last],
        scratch=[((early_rows, WIDTH), F32)],
    )
    grad_up, grad_out, grad_query, grad_kv, grad_router, grad_one, grad_two, input_grad = call(
        functools.partial(
            close_body,
            rest,
            count,
            strides,
            [main_rows // first, late_rows // first],
            len(both_last),
        ),
        [
            ((tall, feed), F32, 1),
            ((tall, dim), F32, 1),
            ((tall, experts * head), F32, 1),
            ((tall, keys), F32, 1),
            ((experts, tall), F32, 1),
            ((1, tall), F32, 1),
            ((1, tall), F32, 1),
            ((count, local, dim), F32, 1),
        ],
        [*both_last, up_tile, *input_got],
        scratch=[((main_rows, WIDTH), F32), ((late_rows, WIDTH), F32)],
    )
    return (
        layer_out,
        input_grad,
        grad_one.reshape(tall),
        grad_router.T,
        grad_query,
        grad_kv,
        grad_out,
        grad_two.reshape(tall),
        grad_up,
        grad_down,
    )


def solution(mesh):
    placed = (
        P("wsh", "ctx", None),
        P("wsh", "ctx", None),
        P(),
        P("wsh"),
        P("wsh", None),
        P("wsh", None),
        P("wsh", None),
        P("wsh", None),
        P("wsh"),
        P("wsh", None),
        P("wsh", None),
        P("wsh", "ctx", None),
    )
    return jax.shard_map(
        on_device,
        mesh=mesh,
        in_specs=placed,
        out_specs=(
            P("wsh", "ctx", None),
            P("wsh", "ctx", None),
            P("wsh"),
            P("wsh", None),
            P("wsh", None),
            P("wsh", None),
            P("wsh", None),
            P("wsh"),
            P("wsh", None),
            P("wsh", None),
        ),
        check_vma=False,
    )
```
